32 devices in a mesh: query: 4 (over y, x), corpus: 8 (over z, core).
Axes of the slice: x: 2, y: 2, z: 4, core: 2. Of those that a mesh axis runs over, the one named last changes fastest.
Arguments:
- hidden_in: bfloat16 [512, 4096], P('query', 'corpus'), may hold values from -6 to 6
- lengths: int32 [16], P('query'), may hold values from 1 to 32, 320 in all
- gate_weight: bfloat16 [4096, 14336], P('query', 'corpus'), may hold values from -0.09375 to 0.09375
- up_weight: bfloat16 [4096, 14336], P('query', 'corpus'), may hold values from -0.09375 to 0.09375
- down_weight: bfloat16 [14336, 4096], P('corpus', 'query'), may hold values from -0.04175957 to 0.04175957
- code_weight: bfloat16 [4096, 1024], P('corpus'), may hold values from -0.03125 to 0.03125
- corpus_codes: bfloat16 [16384, 1024], P(('query', 'corpus')), may hold values from -1 to 1, as said below
Outputs:
- top_scores: float32 [16, 100], replicated
The draws below stay inside these ranges and needn't reach their ends.
Inputs may be any that keep to these rules, and one draw needn't show every extreme that they name: `corpus_codes`: every entry is +1 or -1. `lengths`: at least one query has all 32 slots real.
All inputs are finite; a program needn't handle non-finite values. No bound on the sum of `lengths` on one device may be relied on, other than what follows from the above.
Results may differ from the reference program's by a relative error of at most 0.00067.
Values may be sent and summed in bfloat16 or wider, within the bound.
A program may use at most 128 MiB of HBM per device.

```python
import math
import jax
import jax.numpy as jnp
import numpy as np
from jax import lax

D = 4096
FF = 14336
BITS = 1024
SEQ = 32
TOPK = 100
DOCS_DEV = 512
QUERIES = 16
TOKENS = 512
DOCS = 16384


def shared_parts(key):
    offset = 1.2 * jnp.clip(jax.random.normal(jax.random.fold_in(key, 101), (D,), jnp.float32), -2.5, 2.5)
    bound = 2.0 / max(8, D // 64)
    code_matrix = jax.random.uniform(jax.random.fold_in(key, 102), (D, BITS), jnp.float32, -bound, bound)
    return (offset, code_matrix)


def draw_code_weight(key, part):
    offset, code_matrix = shared_parts(key)
    return code_matrix.astype(jnp.bfloat16)


def draw_down_weight(key, part):
    unit_scale = FF ** (-0.5)
    noise_part = jnp.clip(jax.random.normal(jax.random.fold_in(key, 201), (FF, D), jnp.float32), -3.0, 3.0)
    sign_table = jnp.where(jax.random.uniform(jax.random.fold_in(key, 202), (FF, 1), jnp.float32) < 0.5, -1.0, 1.0)
    directions = jax.random.uniform(jax.random.fold_in(key, 203), (1, D), jnp.float32, -1.7, 1.7)
    common_part = sign_table * directions
    combined = (noise_part + common_part) * unit_scale
    return jnp.clip(combined, -5.0 * unit_scale, 5.0 * unit_scale).astype(jnp.bfloat16)


def draw_hidden_in(key, part):
    offset, code_matrix = shared_parts(key)
    noise_key = jax.random.fold_in(key, 103)
    noise = jnp.clip(jax.random.normal(noise_key, (TOKENS, D), jnp.float32), -4.0, 4.0)
    return jnp.clip(noise + offset[None, :], -6.0, 6.0).astype(jnp.bfloat16)


def draw_corpus_codes(key, part):
    offset, code_matrix = shared_parts(key)
    rounded = code_matrix.astype(jnp.bfloat16).astype(jnp.float32)
    direction = jnp.dot(offset, rounded, precision=lax.Precision.HIGHEST)
    sign_code = jnp.where(direction >= 0.0, 1.0, -1.0).astype(jnp.float32)
    flips = jax.random.uniform(jax.random.fold_in(key, 17), (DOCS, BITS), jnp.float32)
    chosen = jax.random.randint(jax.random.fold_in(key, 18), (), 0, DOCS // DOCS_DEV)
    placing = jax.random.permutation(jax.random.fold_in(key, 19), DOCS_DEV).astype(jnp.int32)
    rows = jnp.arange(DOCS, dtype=jnp.int32)
    planted = jnp.logical_and(rows // DOCS_DEV == chosen, placing[rows % DOCS_DEV] < TOPK // 2)
    rates = jax.random.uniform(jax.random.fold_in(key, 20), (DOCS, 1), jnp.float32, 0.2, 0.5)
    near_copy = sign_code[None, :] * jnp.where(flips < rates, -1.0, 1.0)
    drawn = jnp.where(flips < 0.5, 1.0, -1.0)
    return jnp.where(planted[:, None], near_copy, drawn).astype(jnp.float32).astype(jnp.bfloat16)


def steps_of(key, extent, cuts, smallest, largest):
    loudness = 1.0
    for dim, parts in cuts:
        draws = jax.random.uniform(jax.random.fold_in(jax.random.fold_in(key, 6), dim), (parts,), jnp.float32, smallest / len(cuts), largest / len(cuts))
        loudness = loudness * jnp.repeat(jnp.exp(draws), extent[dim] // parts).reshape((-1,) + (1,) * (len(extent) - 1 - dim))
    return loudness


def split_up(count, total, limit, skew):
    portions = [(1 << 20) // math.isqrt(standing ** skew) + 1 for standing in range(2, count + 1)]
    surplus, counts = total - limit - (count - 1), [1] * (count - 1)
    while surplus > 0:
        movable = [i for i in range(count - 1) if counts[i] < limit]
        mass, budget = sum([portions[i] for i in movable]), surplus
        for i in movable:
            addition = min(limit - counts[i], max(1, budget * portions[i] // mass), surplus)
            counts[i] = counts[i] + addition
            surplus = surplus - addition
    return np.array([limit] + counts)


def uneven_parts(rng, amount, total, most, lean):
    if amount == 2:
        one = jax.random.randint(rng, (), max(1, total - most), min(most, total - 1) + 1)
        return jnp.stack([one, total - one])
    sizes = jnp.asarray(split_up(amount, total, most, lean), jnp.int32)
    twos = (amount - 1) // 2
    giver, taker = sizes[1:1 + 2 * twos:2], sizes[2:2 + 2 * twos:2]
    margin = jnp.minimum(giver - 1, most - taker)
    shifted = jax.random.randint(jax.random.fold_in(rng, 1), (twos,), 0, 1 << 20) % (margin + 1)
    sizes = sizes.at[1:1 + 2 * twos:2].set(giver - shifted).at[2:2 + 2 * twos:2].set(taker + shifted)
    return sizes[jax.random.permutation(jax.random.fold_in(rng, 2), amount)]


def centred(own_key, shape, scale, reach, pieces=(), held_as=jnp.bfloat16):
    result = scale * jax.random.normal(own_key, shape, jnp.float32)
    if pieces:
        result = result * steps_of(own_key, shape, pieces, -0.22, 0.18)
    return jnp.clip(result, -reach, reach).astype(held_as)


def setup_inputs(seed: int = 0) -> dict:
    arg_keys = jax.random.split(jax.random.key(seed), 8)
    return {
        "hidden_in": draw_hidden_in(jax.random.fold_in(arg_keys[7], 71), 0),
        "lengths": uneven_parts(arg_keys[1], QUERIES, QUERIES * SEQ * 5 // 8, SEQ, 2).astype(jnp.int32),
        "gate_weight": centred(arg_keys[2], (D, FF), D ** -0.5, 0.09375, ((0, 4), (1, 8))),
        "up_weight": centred(arg_keys[3], (D, FF), D ** -0.5, 0.09375, ((0, 4), (1, 8))),
        "down_weight": draw_down_weight(jax.random.fold_in(arg_keys[7], 71), 0),
        "code_weight": draw_code_weight(jax.random.fold_in(arg_keys[7], 71), 0),
        "corpus_codes": draw_corpus_codes(jax.random.fold_in(arg_keys[7], 71), 0),
    }


epsilon = 1e-05

def keep_best(first, second):
    return lax.top_k(jnp.concatenate([first, second], axis=1), TOPK)[0]

def reference(hidden_in, lengths, gate_weight, up_weight, down_weight, code_weight, corpus_codes):
    widened = hidden_in.astype(jnp.float32)
    normed = (widened * lax.rsqrt(lax.optimization_barrier(jnp.mean(widened * widened, axis=1, keepdims=True)) + epsilon)).astype(jnp.bfloat16)
    gate_sum = jnp.dot(normed, gate_weight, preferred_element_type=jnp.float32)
    up_sum = jnp.dot(normed, up_weight, preferred_element_type=jnp.float32)
    hidden_units = (jax.nn.silu(gate_sum) * up_sum).astype(jnp.bfloat16)
    branch_out = jnp.dot(hidden_units, down_weight, preferred_element_type=jnp.float32)
    residual = widened + branch_out
    final_rows = residual * lax.rsqrt(lax.optimization_barrier(jnp.mean(residual * residual, axis=1, keepdims=True)) + epsilon)
    grouped = final_rows.reshape(QUERIES, SEQ, D)
    valid_mask = (jnp.arange(SEQ, dtype=jnp.int32)[None, :] < lengths[:, None]).astype(jnp.float32)
    pooled = lax.optimization_barrier(jnp.sum(grouped * valid_mask[:, :, None], axis=1)) / lengths[:, None].astype(jnp.float32)
    pooled = pooled.astype(jnp.bfloat16)
    query_codes = jnp.dot(pooled, code_weight, preferred_element_type=jnp.float32).astype(jnp.bfloat16)
    scale = 1.0 / math.sqrt(BITS)
    shards = corpus_codes.reshape(DOCS // DOCS_DEV, DOCS_DEV, BITS)

    def visit(carry, shard_codes):
        scores = lax.dot_general(query_codes, shard_codes, (((1,), (1,)), ((), ())), preferred_element_type=jnp.float32) * scale
        return (keep_best(carry, scores), None)
    start_best = jnp.full((QUERIES, TOPK), -1e+30, jnp.float32)
    top_scores, unused = lax.scan(visit, start_best, shards)
    return top_scores
```

```python
import functools
import math
import types

import jax
import jax.numpy as jnp
from jax import lax
from jax.experimental import pallas as pl
from jax.experimental.pallas import tpu as pltpu
from jax.sharding import PartitionSpec as P

SEQ = 32
LANES = 128
TOPK = 100
REAL_NUM, REAL_DEN = 5, 8
CHUNK = 256
PIECE = 32

epsilon = 1e-05
F32, BF16 = jnp.float32, jnp.bfloat16


def mm(a, b, precision=None):
    return lax.dot_general(a, b, (((1,), (0,)), ((), ())), precision=precision, preferred_element_type=F32)


def rcopy(src, dst, send, recv, dev):
    return pltpu.make_async_remote_copy(
        src_ref=src, dst_ref=dst, send_sem=send, recv_sem=recv,
        device_id=dev, device_id_type=pl.DeviceIdType.MESH)


def exchange(x, s, keep_max):
    bit = (lax.broadcasted_iota(jnp.int32, x.shape, 1) & s) != 0
    other = jnp.where(bit, pltpu.roll(x, s, 1), pltpu.roll(x, LANES - s, 1))
    return jnp.where(keep_max, jnp.maximum(x, other), jnp.minimum(x, other))


def sort_lanes(x):
    lane = lax.broadcasted_iota(jnp.int32, x.shape, 1)
    flip = (lax.broadcasted_iota(jnp.int32, x.shape, 0) >= x.shape[0] // 2).astype(jnp.int32)
    size = 2
    while size <= LANES:
        up = ((lane & size) != 0).astype(jnp.int32) if size < LANES else jnp.zeros_like(lane)
        s = size // 2
        while s:
            low = ((lane & s) != 0).astype(jnp.int32)
            x = exchange(x, s, (low ^ up ^ flip) == 0)
            s //= 2
        size *= 2
    return x


def merge_all(x, rows, lone):
    while x.shape[0] > rows:
        half = x.shape[0] // 2
        x = jnp.maximum(x[:half], x[half:])
        lane = lax.broadcasted_iota(jnp.int32, x.shape, 1)
        if half > rows:
            flip = (lax.broadcasted_iota(jnp.int32, x.shape, 0) >= half // 2).astype(jnp.int32)
        else:
            flip = jnp.zeros_like(lane) + jnp.asarray(lone, jnp.int32)
        s = LANES // 2
        while s:
            low = ((lane & s) != 0).astype(jnp.int32)
            x = exchange(x, s, (low ^ flip) == 0)
            s //= 2
    return x


def general_kernel(dims, hid, lens, gate_h, up_h, down_h, code_h, corp_h, out,
                 gate, up, down, code, corp, colbuf, lens_all, xall, psend, precv,
                 st_send, st_recv, inv_all, xn, pown, top_q, top_c, hall, acc, lsend, lrecv, gsend, grecv, t_send, t_recv,
                 pp, prc, pblk, cpart, crecv, codes,
                 w_s, a_s, a_r, l_s, l_r, ch_s, ch_r, la_s, la_r, p_s, p_r, st_s, st_r, iv_s, iv_r, tq_s, tq_r, tc_s, tc_r, h_s, h_r,
                 lr_s, lr_r, g_s, g_r, t_s, t_r, pp_s, pp_r, pb_s, pb_r, c_s, c_r, o_s, o_r):
    nq, nc, r, nreal, tq, tb, nch, cw, d_all = dims
    q = lax.axis_index("query")
    c = lax.axis_index("corpus")
    g = c // r
    j = lax.rem(c, r)
    slots, w = hid.shape[0], hid.shape[1]
    total = nq * slots
    nqueries = total // SEQ
    bw = code.shape[1] // nq

    loads = []
    for i, (s, d) in enumerate(((gate_h, gate), (up_h, up), (down_h, down), (code_h, code), (corp_h, corp))):
        cp = pltpu.make_async_copy(s, d, w_s.at[i])
        cp.start()
        loads.append(cp)

    def rq(k):
        return lax.rem(q + k, nq)

    def rc(k):
        return lax.rem(c + k, nc)

    def lane(k):
        return lax.rem(j + k, r)

    barrier = pltpu.get_barrier_semaphore()
    for k in range(1, nq):
        pl.semaphore_signal(barrier, inc=1, device_id=(rq(k), c), device_id_type=pl.DeviceIdType.MESH)
    for k in range(1, nc):
        pl.semaphore_signal(barrier, inc=1, device_id=(q, rc(k)), device_id_type=pl.DeviceIdType.MESH)
    pl.semaphore_wait(barrier, nq - 1 + nc - 1)

    for k in range(1, nq):
        rcopy(lens, lens_all.at[q], l_s.at[k], l_r.at[q], (rq(k), c)).start()

    @pl.when(q != g)
    def _():
        rcopy(hid, colbuf.at[q], a_s, a_r.at[q], (g, c)).start()

    squares = jnp.square(hid[...].astype(F32))
    st_send[...] = lax.dot_general(jnp.ones((8, w), F32), squares, (((1,), (1,)), ((), ())),
                                   precision=lax.Precision.HIGHEST, preferred_element_type=F32)
    for k in range(1, nc):
        rcopy(st_send, st_recv.at[c], st_s.at[k], st_r.at[c], (q, rc(k))).start()
    st_recv[c] = st_send[...]
    lens_all[q] = lens[...]
    for k in range(1, nq):
        s = rq(k)
        rcopy(lens, lens_all.at[s], l_s.at[k], l_r.at[s], (s, c)).wait_recv()
    lens_row = jnp.concatenate([lens_all[i] for i in range(nq)], axis=1)
    slot = lax.broadcasted_iota(jnp.int32, (8, total), 1)
    valid = lax.rem(slot, SEQ) < lens_row
    before = lax.broadcasted_iota(jnp.int32, (total, total), 0) < lax.broadcasted_iota(jnp.int32, (total, total), 1)
    pos = mm(valid.astype(F32).astype(BF16), before.astype(F32).astype(BF16)).astype(jnp.int32)
    pos = jnp.where(valid, pos, -1)[:1]

    for k in range(1, nc):
        s = rc(k)
        rcopy(st_send, st_recv.at[s], st_s.at[k], st_r.at[s], (q, s)).wait_recv()
    stat = st_recv[0]
    for i in range(1, nc):
        stat = stat + st_recv[i]
    inv_all[q] = lax.rsqrt(stat / d_all + epsilon)
    for k in range(1, nq):
        rcopy(inv_all.at[q], inv_all.at[q], iv_s.at[k], iv_r.at[q], (rq(k), c)).start()

    nb = ch_r.shape[0]
    ct = nreal // nb

    def chunk(i, slot_j):
        return xall.at[slot_j, pl.ds(i * ct, ct)]

    def down_chain(i):
        return rcopy(chunk(i, j), chunk(i, j), ch_s.at[0, i], ch_r.at[i], (q, jnp.maximum(c - r, 0)))

    def up_chain(i):
        return rcopy(chunk(i, j), chunk(i, j), ch_s.at[1, i], ch_r.at[i], (q, jnp.minimum(c + r, nc - 1)))

    sends_up = jnp.logical_and(g >= q, g < nc // r - 1)
    sends_down = jnp.logical_and(g <= q, g > 0)

    @pl.when(q == g)
    def _():
        colbuf[q] = hid[...]
        for k in range(1, nq):
            s = rq(k)
            rcopy(hid, colbuf.at[s], a_s, a_r.at[s], (s, c)).wait_recv()
        stacked = colbuf[...].reshape(total, w)
        for i in range(nq):
            row = lax.broadcasted_iota(jnp.int32, (tq, total), 0) + i * tq
            pick = (pos == row).astype(F32).astype(BF16)
            xall[j, i * tq:(i + 1) * tq, :] = mm(pick, stacked).astype(BF16)

    for i in range(nb):
        @pl.when(q != g)
        def _(i=i):
            up_chain(i).wait_recv()

        @pl.when(sends_up)
        def _(i=i):
            up_chain(i).start()

        @pl.when(sends_down)
        def _(i=i):
            down_chain(i).start()

        for k in range(1, r):
            rcopy(chunk(i, j), chunk(i, j), la_s.at[k, i], la_r.at[j, i], (q, g * r + lane(k))).start()
    for k in range(1, nq):
        s = rq(k)
        rcopy(inv_all.at[s], inv_all.at[s], iv_s.at[k], iv_r.at[s], (s, c)).wait_recv()
    inv_row = jnp.concatenate([inv_all[i] for i in range(nq)], axis=1)[:1]
    inv_cols = []
    for i in range(nq):
        row = lax.broadcasted_iota(jnp.int32, (tq, total), 0) + i * tq
        inv_cols.append(jnp.sum(jnp.where(pos == row, inv_row, 0.0), axis=1, keepdims=True))
    inv = jnp.concatenate(inv_cols, axis=0)
    for i in range(nb):
        for k in range(1, r):
            s = lane(k)
            rcopy(chunk(i, s), chunk(i, s), la_s.at[k, i], la_r.at[s, i], (q, g * r + s)).wait_recv()

    loads[0].wait()
    loads[1].wait()

    for i in range(r):
        xn[i] = (xall[i].astype(F32) * inv).astype(BF16)

    side_a = q + 1 - 2 * lax.rem(q, 2)
    side_b = q + 2 - 4 * (q // 2)
    far = nq - 1 - q

    def sides(n):
        odd = lax.rem(n, 2)
        return side_a + (side_b - side_a) * odd, side_b + (side_a - side_b) * odd

    def near_part(n):
        one, _ = sides(n)
        return rcopy(psend.at[n, one], precv.at[n, 0], p_s.at[n, 0], p_r.at[n, 0], (one, c))

    def far_part(n):
        one, _ = sides(n)
        return rcopy(psend.at[n, far], precv.at[n, 1], p_s.at[n, 1], p_r.at[n, 1], (one, c))

    def passed_part(n):
        _, two = sides(n)
        return rcopy(precv.at[n, 3], precv.at[n, 2], p_s.at[n, 2], p_r.at[n, 2], (two, c))

    def h_near(n, k):
        to = sides(n)[k]
        return rcopy(hall.at[n, q], hall.at[n, q], h_s.at[n, k], h_r.at[n, k], (to, c))

    def h_near_in(n, k):
        to = sides(n)[k]
        return rcopy(hall.at[n, to], hall.at[n, to], h_s.at[n, k], h_r.at[n, k], (to, c))

    def h_pass(n):
        one, two = sides(n)
        return rcopy(hall.at[n, one], hall.at[n, one], h_s.at[n, 2], h_r.at[n, 2], (two, c))

    def h_pass_in(n):
        _, two = sides(n)
        return rcopy(hall.at[n, far], hall.at[n, far], h_s.at[n, 2], h_r.at[n, 2], (two, c))

    def matmuls(n, carry):
        cols = pl.ds(pl.multiple_of(n * cw, cw), cw)
        for e, wref in enumerate((gate, up)):
            full = sum(mm(xn[i], wref[i * w:(i + 1) * w, cols]) for i in range(r))
            for i in range(nq):
                psend[n, i, e] = full[i * tq:(i + 1) * tq].astype(BF16)

                @pl.when(q == i)
                def _(i=i, e=e, full=full):
                    pown[n, e] = full[i * tq:(i + 1) * tq]
        far_part(n).start()
        near_part(n).start()
        return carry

    lax.fori_loop(0, nch, matmuls, 0)

    loads[2].wait()
    acc[...] = jnp.zeros_like(acc)

    def pass_chunk(n):
        _, two = sides(n)
        far_part(n).wait_recv()
        precv[n, 3] = (psend[n, two].astype(F32) + precv[n, 1].astype(F32)).astype(BF16)
        passed_part(n).start()

    def reduce_chunk(n):
        near_part(n).wait_recv()
        passed_part(n).wait_recv()
        gsum = pown[n, 0] + precv[n, 0, 0].astype(F32) + precv[n, 2, 0].astype(F32)
        usum = pown[n, 1] + precv[n, 0, 1].astype(F32) + precv[n, 2, 1].astype(F32)
        hall[n, q] = (gsum / (1.0 + jnp.exp(-gsum)) * usum).astype(BF16)
        h_near(n, 0).start()
        h_near(n, 1).start()

    def relay_chunk(n):
        h_near_in(n, 0).wait_recv()
        h_pass(n).start()

    def down_chunk(n):
        h_near_in(n, 1).wait_recv()
        h_pass_in(n).wait_recv()
        acc[...] += mm(hall[n].reshape(nreal, cw), down[pl.ds(pl.multiple_of(n * cw, cw), cw), :])

    def passes(n, carry):
        pass_chunk(n)
        return carry

    lax.fori_loop(0, nch, passes, 0)
    reduce_chunk(0)

    def reduces(n, carry):
        reduce_chunk(n)
        relay_chunk(n - 1)
        return carry

    lax.fori_loop(1, nch, reduces, 0)
    relay_chunk(nch - 1)

    def downs(n, carry):
        down_chunk(n)
        return carry

    lax.fori_loop(0, nch, downs, 0)

    ng = nc // r
    for gg in range(ng):
        for jj in range(r):
            b = gg * r + jj
            lsend[jj, gg] = acc[b * tb:(b + 1) * tb].astype(BF16)
    for k in range(1, r):
        t = lane(k)
        rcopy(lsend.at[t], lrecv.at[j], lr_s.at[k], lr_r.at[j], (q, g * r + t)).start()
    mine = lsend[j].astype(F32)
    for k in range(1, r):
        s = lane(k)
        rcopy(lsend.at[s], lrecv.at[s], lr_s.at[k], lr_r.at[s], (q, g * r + s)).wait_recv()
        mine = mine + lrecv[s].astype(F32)
    gsend[...] = mine.astype(BF16)
    for k in range(1, ng):
        t = lax.rem(g + k, ng)
        rcopy(gsend.at[t], grecv.at[g], g_s.at[k], g_r.at[g], (q, t * r + j)).start()
    row = lax.broadcasted_iota(jnp.int32, (tb, nreal), 0) + c * tb
    own_rows = (lax.broadcasted_iota(jnp.int32, (tb, nreal), 1) == row).astype(F32).astype(BF16)
    residual = jnp.concatenate([mm(own_rows, xall[i]) for i in range(r)], axis=1)
    residual = residual + gsend[g].astype(F32)
    for k in range(1, ng):
        s = lax.rem(g + k, ng)
        rcopy(gsend.at[s], grecv.at[s], g_s.at[k], g_r.at[s], (q, s * r + j)).wait_recv()
        residual = residual + grecv[s].astype(F32)

    t_send[...] = jnp.broadcast_to(jnp.sum(residual * residual, axis=1, keepdims=True), (tb, 128))
    for k in range(1, nq):
        rcopy(t_send, t_recv.at[q], t_s.at[k], t_r.at[q], (rq(k), c)).start()
    qrow = lax.broadcasted_iota(jnp.int32, (nqueries, total), 0)
    qslot = lax.broadcasted_iota(jnp.int32, (nqueries, total), 1)
    lens_b = jnp.broadcast_to(lens_row[:1], (nqueries, total)).astype(F32)
    vals_b = jnp.broadcast_to(valid.astype(F32)[:1], (nqueries, total))
    len_col = jnp.sum(jnp.where(qslot == qrow * SEQ, lens_b, 0.0), axis=1, keepdims=True)
    off_col = jnp.sum(jnp.where(qslot < qrow * SEQ, vals_b, 0.0), axis=1, keepdims=True)
    prow = (lax.broadcasted_iota(jnp.int32, (nqueries, tb), 1) + c * tb).astype(F32)
    member = jnp.where(jnp.logical_and(prow >= off_col, prow < off_col + len_col), 1.0, 0.0)
    tsum = t_send[...]
    for k in range(1, nq):
        s = rq(k)
        rcopy(t_send, t_recv.at[s], t_s.at[k], t_r.at[s], (s, c)).wait_recv()
        tsum = tsum + t_recv[s]
    final = residual * lax.rsqrt(tsum[:, :1] / d_all + epsilon)
    pooled_part = mm(member, final, lax.Precision.HIGHEST)
    for i in range(r):
        pp[i] = pooled_part[:, i * w:(i + 1) * w]
    for i in range(r):
        @pl.when(c != q * r + i)
        def _(i=i):
            rcopy(pp.at[i], prc.at[c], pp_s.at[i], pp_r.at[c], (q, q * r + i)).start()

    @pl.when(g == q)
    def _():
        pooled = pp[j]
        for k in range(1, nc):
            s = rc(k)
            rcopy(pp.at[j], prc.at[s], pp_s.at[0], pp_r.at[s], (q, s)).wait_recv()
            pooled = pooled + prc[s]
        pblk[...] = (pooled / len_col).astype(BF16)
        for k in range(1, nq):
            rcopy(pblk, pblk, pb_s.at[k], pb_r, (rq(k), c)).start()

    loads[3].wait()
    loads[4].wait()

    @pl.when(g != q)
    def _():
        rcopy(pblk, pblk, pb_s.at[0], pb_r, (g, c)).wait_recv()

    cpart[...] = mm(pblk[...], code[:, pl.ds(pl.multiple_of(q * bw, bw), bw)])
    for k in range(1, nc):
        rcopy(cpart, crecv.at[c], c_s.at[k], c_r.at[c], (q, rc(k))).start()
    crecv[c] = cpart[...]
    for k in range(1, nc):
        s = rc(k)
        rcopy(cpart, crecv.at[s], c_s.at[k], c_r.at[s], (q, s)).wait_recv()
    csum = crecv[0]
    for i in range(1, nc):
        csum = csum + crecv[i]
    codes[q] = csum.astype(BF16)
    for k in range(1, nq):
        rcopy(codes.at[q], codes.at[q], o_s.at[k], o_r.at[q], (rq(k), c)).start()
    for k in range(1, nq):
        s = rq(k)
        rcopy(codes.at[s], codes.at[s], o_s.at[k], o_r.at[s], (s, c)).wait_recv()
    qcodes = jnp.concatenate([codes[i] for i in range(nq)], axis=1)
    scale = 1.0 / math.sqrt(corp.shape[1])
    scores = lax.dot_general(qcodes, corp[...], (((1,), (1,)), ((), ())), preferred_element_type=F32) * scale

    blocks = corp.shape[0] // LANES
    lists = jnp.concatenate([scores[:, i * LANES:(i + 1) * LANES] for i in range(blocks)], axis=0)
    best = merge_all(sort_lanes(lists), nqueries, q >= nq // 2)
    top_q[q] = best
    for k in range(1, nq):
        rcopy(top_q.at[q], top_q.at[q], tq_s.at[k], tq_r.at[q], (rq(k), c)).start()
    for k in range(1, nq):
        s = rq(k)
        rcopy(top_q.at[s], top_q.at[s], tq_s.at[k], tq_r.at[s], (s, c)).wait_recv()
    best = merge_all(top_q[...].reshape(nq * nqueries, LANES), nqueries, c >= nc // 2)
    top_c[c] = best
    for k in range(1, nc):
        rcopy(top_c.at[c], top_c.at[c], tc_s.at[k], tc_r.at[c], (q, rc(k))).start()
    for k in range(1, nc):
        s = rc(k)
        rcopy(top_c.at[s], top_c.at[s], tc_s.at[k], tc_r.at[s], (q, s)).wait_recv()
    best = merge_all(top_c[...].reshape(nc * nqueries, LANES), nqueries, False)
    out[...] = best[:, :TOPK]

    for k in range(1, nq):
        rcopy(lens, lens_all.at[q], l_s.at[k], l_r.at[q], (rq(k), c)).wait_send()
        rcopy(inv_all.at[q], inv_all.at[q], iv_s.at[k], iv_r.at[q], (rq(k), c)).wait_send()
        rcopy(top_q.at[q], top_q.at[q], tq_s.at[k], tq_r.at[q], (rq(k), c)).wait_send()
        rcopy(t_send, t_recv.at[q], t_s.at[k], t_r.at[q], (rq(k), c)).wait_send()
        rcopy(codes.at[q], codes.at[q], o_s.at[k], o_r.at[q], (rq(k), c)).wait_send()

    @pl.when(q != g)
    def _():
        rcopy(hid, colbuf.at[q], a_s, a_r.at[q], (g, c)).wait_send()

    for i in range(nb):
        @pl.when(sends_up)
        def _(i=i):
            up_chain(i).wait_send()

        @pl.when(sends_down)
        def _(i=i):
            down_chain(i).wait_send()

        for k in range(1, r):
            rcopy(chunk(i, j), chunk(i, j), la_s.at[k, i], la_r.at[j, i], (q, g * r + lane(k))).wait_send()

    def drain(n, carry):
        far_part(n).wait_send()
        near_part(n).wait_send()
        passed_part(n).wait_send()
        h_near(n, 0).wait_send()
        h_near(n, 1).wait_send()
        h_pass(n).wait_send()
        return carry

    lax.fori_loop(0, nch, drain, 0)
    for k in range(1, r):
        rcopy(lsend.at[lane(k)], lrecv.at[j], lr_s.at[k], lr_r.at[j], (q, g * r + lane(k))).wait_send()
    for k in range(1, ng):
        t = lax.rem(g + k, ng)
        rcopy(gsend.at[t], grecv.at[g], g_s.at[k], g_r.at[g], (q, t * r + j)).wait_send()
    for i in range(r):
        @pl.when(c != q * r + i)
        def _(i=i):
            rcopy(pp.at[i], prc.at[c], pp_s.at[i], pp_r.at[c], (q, q * r + i)).wait_send()

    @pl.when(g == q)
    def _():
        for k in range(1, nq):
            rcopy(pblk, pblk, pb_s.at[k], pb_r, (rq(k), c)).wait_send()
    for k in range(1, nc):
        rcopy(cpart, crecv.at[c], c_s.at[k], c_r.at[c], (q, rc(k))).wait_send()
        rcopy(st_send, st_recv.at[c], st_s.at[k], st_r.at[c], (q, rc(k))).wait_send()
        rcopy(top_c.at[c], top_c.at[c], tc_s.at[k], tc_r.at[c], (q, rc(k))).wait_send()


def per_device_general(nq, nc, hidden_in, lengths, gate_weight, up_weight, down_weight, code_weight, corpus_codes):
    slots, w = hidden_in.shape
    r = nc // nq
    nreal = nq * slots * REAL_NUM // REAL_DEN
    tq, tb = nreal // nq, nreal // nc
    dq, ffc = gate_weight.shape
    cw = CHUNK if ffc % CHUNK == 0 else ffc
    nch = ffc // cw
    nb = nreal // PIECE if nreal % PIECE == 0 else nq
    nqueries = nq * lengths.shape[0]
    bits = code_weight.shape[1]
    bw = bits // nq
    ng = nc // r
    lens = jnp.broadcast_to(jnp.repeat(lengths, SEQ)[None, :], (8, slots))
    vm, dma = pltpu.VMEM, pltpu.SemaphoreType.DMA
    scratch = [
        vm(gate_weight.shape, BF16), vm(up_weight.shape, BF16), vm(down_weight.shape, BF16),
        vm(code_weight.shape, BF16), vm(corpus_codes.shape, BF16),
        vm((nq, slots, w), BF16), vm((nq, 8, slots), jnp.int32), vm((r, nreal, w), BF16),
        vm((nch, nq, 2, tq, cw), BF16), vm((nch, nq, 2, tq, cw), BF16),
        vm((8, slots), F32), vm((nc, 8, slots), F32), vm((nq, 8, slots), F32), vm((r, nreal, w), BF16),
        vm((nch, 2, tq, cw), F32), vm((nq, nqueries, LANES), F32), vm((nc, nqueries, LANES), F32),
        vm((nch, nq, tq, cw), BF16), vm((nreal, dq), F32),
        vm((r, ng, tb, dq), BF16), vm((r, ng, tb, dq), BF16), vm((ng, tb, dq), BF16), vm((ng, tb, dq), BF16),
        vm((tb, 128), F32), vm((nq, tb, 128), F32),
        vm((r, nqueries, w), F32), vm((nc, nqueries, w), F32), vm((nqueries, w), BF16),
        vm((nqueries, bw), F32), vm((nc, nqueries, bw), F32), vm((nq, nqueries, bw), BF16),
        dma((5,)), dma, dma((nq,)), dma((nq,)), dma((nq,)), dma((2, nb)), dma((nb,)), dma((r, nb)), dma((r, nb)),
        dma((nch, nq)), dma((nch, nq)), dma((nc,)), dma((nc,)), dma((nq,)), dma((nq,)),
        dma((nq,)), dma((nq,)), dma((nc,)), dma((nc,)), dma((nch, nq)), dma((nch, nq)),
        dma((r,)), dma((r,)), dma((ng,)), dma((ng,)), dma((nq,)), dma((nq,)),
        dma((r,)), dma((nc,)), dma((nq,)), dma, dma((nc,)), dma((nc,)), dma((nq,)), dma((nq,)),
    ]
    dims = (nq, nc, r, nreal, tq, tb, nch, cw, w * nc)
    vspec, aspec = pl.BlockSpec(memory_space=pltpu.VMEM), pl.BlockSpec(memory_space=pl.ANY)
    return pl.pallas_call(
        functools.partial(general_kernel, dims),
        out_shape=jax.ShapeDtypeStruct((nqueries, TOPK), F32),
        in_specs=[vspec, vspec] + [aspec] * 5,
        out_specs=vspec,
        scratch_shapes=scratch,
        compiler_params=pltpu.CompilerParams(
            collective_id=0, has_side_effects=True, vmem_limit_bytes=60 * 1024 * 1024),
    )(hidden_in, lens, gate_weight, up_weight, down_weight, code_weight, corpus_codes)


def fast_kernel(dims, names, hid, lens, gate_h, up_h, down_h, code_h, corp_h, out, *refs):
    nq, nc, r, nblk, bm, nh, hw, d_all = dims
    s = types.SimpleNamespace(**dict(zip(names, refs)))
    q = lax.axis_index("query")
    c = lax.axis_index("corpus")
    g = c // r
    j = lax.rem(c, r)
    ng = nc // r
    slots, w = hid.shape
    total = nq * slots
    nqueries = total // SEQ
    nreal = nblk * bm
    qm, lm, pm = bm // nq, bm // r, bm // nc
    nu = nblk * nh
    bw = s.code.shape[1] // nq
    drains = []

    loads = []
    for i, (a, b) in enumerate(((gate_h, s.gate), (up_h, s.up), (down_h, s.down), (code_h, s.code), (corp_h, s.corp))):
        cp = pltpu.make_async_copy(a, b, s.w_s.at[i])
        cp.start()
        loads.append(cp)

    slot_query = lax.broadcasted_iota(jnp.int32, (8, slots), 1) // SEQ
    own_lens = jnp.zeros((8, slots), jnp.int32)
    for k in range(slots // SEQ):
        own_lens = jnp.where(slot_query == k, lens[k], own_lens)
    s.lens_all[q] = own_lens

    def rq(k):
        return lax.rem(q + k, nq)

    def rc(k):
        return lax.rem(c + k, nc)

    def lane(k):
        return lax.rem(j + k, r)

    def send(cp):
        cp.start()
        drains.append(cp.wait_send)

    barrier = pltpu.get_barrier_semaphore()
    for k in range(1, nq):
        pl.semaphore_signal(barrier, inc=1, device_id=(rq(k), c), device_id_type=pl.DeviceIdType.MESH)
    for k in range(1, nc):
        pl.semaphore_signal(barrier, inc=1, device_id=(q, rc(k)), device_id_type=pl.DeviceIdType.MESH)
    pl.semaphore_wait(barrier, nq - 1 + nc - 1)

    for k in range(1, nq):
        send(rcopy(s.lens_all.at[q], s.lens_all.at[q], s.l_s.at[k], s.l_r.at[q], (rq(k), c)))

    @pl.when(q != g)
    def _():
        rcopy(hid, s.colbuf.at[q], s.a_s, s.a_r.at[q], (g, c)).start()

    squares = jnp.square(hid[...].astype(F32))
    s.st_send[...] = lax.dot_general(jnp.ones((8, w), F32), squares, (((1,), (1,)), ((), ())),
                                     precision=lax.Precision.HIGHEST, preferred_element_type=F32)
    for k in range(1, nc):
        send(rcopy(s.st_send, s.st_recv.at[c], s.st_s.at[k], s.st_r.at[c], (q, rc(k))))
    s.st_recv[c] = s.st_send[...]
    for k in range(1, nq):
        p = rq(k)
        rcopy(s.lens_all.at[p], s.lens_all.at[p], s.l_s.at[k], s.l_r.at[p], (p, c)).wait_recv()
    lens_row = jnp.concatenate([s.lens_all[i] for i in range(nq)], axis=1)
    slot = lax.broadcasted_iota(jnp.int32, (8, total), 1)
    valid = lax.rem(slot, SEQ) < lens_row
    before = lax.broadcasted_iota(jnp.int32, (total, total), 0) < lax.broadcasted_iota(jnp.int32, (total, total), 1)
    pos = mm(valid.astype(F32).astype(BF16), before.astype(F32).astype(BF16)).astype(jnp.int32)
    pos = jnp.where(valid, pos, -1)[:1]

    for k in range(1, nc):
        p = rc(k)
        rcopy(s.st_send, s.st_recv.at[p], s.st_s.at[k], s.st_r.at[p], (q, p)).wait_recv()
    stat = s.st_recv[0]
    for i in range(1, nc):
        stat = stat + s.st_recv[i]
    s.inv_all[q] = lax.rsqrt(stat / d_all + epsilon)
    for k in range(1, nq):
        send(rcopy(s.inv_all.at[q], s.inv_all.at[q], s.iv_s.at[k], s.iv_r.at[q], (rq(k), c)))

    def block(b, jj):
        return s.xall.at[jj, b]

    def down_chain(b):
        return rcopy(block(b, j), block(b, j), s.ch_s.at[0, b], s.ch_r.at[b], (q, jnp.maximum(c - r, 0)))

    def up_chain(b):
        return rcopy(block(b, j), block(b, j), s.ch_s.at[1, b], s.ch_r.at[b], (q, jnp.minimum(c + r, nc - 1)))

    def side(b, k):
        return rcopy(block(b, j), block(b, j), s.la_s.at[k, b], s.la_r.at[j, b], (q, g * r + lane(k)))

    def side_in(b, k):
        p = lane(k)
        return rcopy(block(b, p), block(b, p), s.la_s.at[k, b], s.la_r.at[p, b], (q, g * r + p))

    sends_up = jnp.logical_and(g >= q, g < ng - 1)
    sends_down = jnp.logical_and(g <= q, g > 0)

    def pass_on(b):
        @pl.when(sends_up)
        def _():
            up_chain(b).start()

        @pl.when(sends_down)
        def _():
            down_chain(b).start()

        for k in range(1, r):
            side(b, k).start()

    @pl.when(q == g)
    def _():
        s.colbuf[q] = hid[...]
        for k in range(1, nq):
            p = rq(k)
            rcopy(hid, s.colbuf.at[p], s.a_s, s.a_r.at[p], (p, c)).wait_recv()
        stacked = s.colbuf[...].reshape(total, w)
        for b in range(nblk):
            row = lax.broadcasted_iota(jnp.int32, (bm, total), 0) + b * bm
            pick = (pos == row).astype(F32).astype(BF16)
            s.xall[j, b] = mm(pick, stacked).astype(BF16)
            pass_on(b)

    for k in range(1, nq):
        p = rq(k)
        rcopy(s.inv_all.at[p], s.inv_all.at[p], s.iv_s.at[k], s.iv_r.at[p], (p, c)).wait_recv()
    inv_row = jnp.concatenate([s.inv_all[i] for i in range(nq)], axis=1)[:1]
    for b in range(nblk):
        row = lax.broadcasted_iota(jnp.int32, (bm, total), 0) + b * bm
        col = jnp.sum(jnp.where(pos == row, inv_row, 0.0), axis=1, keepdims=True)
        s.inv_c[b] = jnp.broadcast_to(col, (bm, LANES))

    loads[0].wait()
    loads[1].wait()

    side_a = q + 1 - 2 * lax.rem(q, 2)
    side_b = q + 2 - 4 * (q // 2)
    far = nq - 1 - q

    def sides(n):
        odd = lax.rem(n, 2)
        return side_a + (side_b - side_a) * odd, side_b + (side_a - side_b) * odd

    def near_part(n):
        one, _ = sides(n)
        return rcopy(s.psend.at[n, one], s.precv.at[n, 0], s.p_s.at[n, 0], s.p_r.at[n, 0], (one, c))

    def far_part(n):
        one, _ = sides(n)
        return rcopy(s.psend.at[n, far], s.precv.at[n, 1], s.p_s.at[n, 1], s.p_r.at[n, 1], (one, c))

    def passed_part(n):
        _, two = sides(n)
        return rcopy(s.precv.at[n, 3], s.precv.at[n, 2], s.p_s.at[n, 2], s.p_r.at[n, 2], (two, c))

    def h_near(n, k):
        to = sides(n)[k]
        return rcopy(s.hall.at[n, q], s.hall.at[n, q], s.h_s.at[n, k], s.h_r.at[n, k], (to, c))

    def h_near_in(n, k):
        to = sides(n)[k]
        return rcopy(s.hall.at[n, to], s.hall.at[n, to], s.h_s.at[n, k], s.h_r.at[n, k], (to, c))

    def h_pass(n):
        one, two = sides(n)
        return rcopy(s.hall.at[n, one], s.hall.at[n, one], s.h_s.at[n, 2], s.h_r.at[n, 2], (two, c))

    def h_pass_in(n):
        _, two = sides(n)
        return rcopy(s.hall.at[n, far], s.hall.at[n, far], s.h_s.at[n, 2], s.h_r.at[n, 2], (two, c))

    def products(b, carry):
        @pl.when(q != g)
        def _():
            up_chain(b).wait_recv()
            pass_on(b)

        for k in range(1, r):
            side_in(b, k).wait_recv()
        scale = s.inv_c[b][:, :1]
        for i in range(r):
            s.xn[:, i * w:(i + 1) * w] = (s.xall[i, b].astype(F32) * scale).astype(BF16)
        xb = s.xn[...]
        for h in range(nh):
            n = b * nh + h
            for e, wref in enumerate((s.gate, s.up)):
                full = mm(xb, wref[:, h * hw:(h + 1) * hw])
                for i in range(nq):
                    s.psend[n, i, e] = full[i * qm:(i + 1) * qm].astype(BF16)

                    @pl.when(q == i)
                    def _(i=i, e=e, full=full, n=n):
                        s.pown[n, e] = full[i * qm:(i + 1) * qm]
            far_part(n).start()
            near_part(n).start()
        return carry

    lax.fori_loop(0, nblk, products, 0)

    row = lax.broadcasted_iota(jnp.int32, (nblk * pm, nreal), 0)
    row = (row // pm) * bm + (j * ng + g) * pm + lax.rem(row, pm)
    own_rows = (lax.broadcasted_iota(jnp.int32, (nblk * pm, nreal), 1) == row).astype(F32).astype(BF16)
    for i in range(r):
        s.res[:, i * w:(i + 1) * w] = mm(own_rows, s.xall[i].reshape(nreal, w))

    loads[2].wait()

    def passes(n, carry):
        _, two = sides(n)
        far_part(n).wait_recv()
        s.precv[n, 3] = (s.psend[n, two].astype(F32) + s.precv[n, 1].astype(F32)).astype(BF16)
        passed_part(n).start()
        return carry

    def reduce_unit(n):
        near_part(n).wait_recv()
        passed_part(n).wait_recv()
        gsum = s.pown[n, 0] + s.precv[n, 0, 0].astype(F32) + s.precv[n, 2, 0].astype(F32)
        usum = s.pown[n, 1] + s.precv[n, 0, 1].astype(F32) + s.precv[n, 2, 1].astype(F32)
        s.hall[n, q] = (gsum / (1.0 + jnp.exp(-gsum)) * usum).astype(BF16)
        h_near(n, 0).start()
        h_near(n, 1).start()

    def relay_unit(n):
        h_near_in(n, 0).wait_recv()
        h_pass(n).start()

    def reduces(n, carry):
        reduce_unit(n)
        relay_unit(n - 1)
        return carry

    lax.fori_loop(0, nu, passes, 0)
    reduce_unit(0)
    lax.fori_loop(1, nu, reduces, 0)
    relay_unit(nu - 1)

    def lane_send(b, k):
        t = lane(k)
        return rcopy(s.lsend.at[b, t], s.lrecv.at[b, j], s.lr_s.at[b, k], s.lr_r.at[b, j], (q, g * r + t))

    def lane_in(b, k):
        p = lane(k)
        return rcopy(s.lsend.at[b, p], s.lrecv.at[b, p], s.lr_s.at[b, k], s.lr_r.at[b, p], (q, g * r + p))

    def group_send(b, k):
        t = lax.rem(g + k, ng)
        return rcopy(s.gsend.at[b, t], s.grecv.at[b, g], s.g_s.at[b, k], s.g_r.at[b, g], (q, t * r + j))

    def group_in(b, k):
        p = lax.rem(g + k, ng)
        return rcopy(s.gsend.at[b, p], s.grecv.at[b, p], s.g_s.at[b, k], s.g_r.at[b, p], (q, p * r + j))

    def down_block(b):
        part = None
        for h in range(nh):
            n = b * nh + h
            h_near_in(n, 1).wait_recv()
            h_pass_in(n).wait_recv()
            term = mm(s.hall[n].reshape(bm, hw), s.down[h * hw:(h + 1) * hw, :])
            part = term if part is None else part + term
        for t in range(r):
            s.lsend[b, t] = part[t * lm:(t + 1) * lm].astype(BF16)
        for k in range(1, r):
            lane_send(b, k).start()

    def sum_block(b):
        mine = s.lsend[b, j].astype(F32)
        for k in range(1, r):
            lane_in(b, k).wait_recv()
            mine = mine + s.lrecv[b, lane(k)].astype(F32)
        for t in range(ng):
            s.gsend[b, t] = mine[t * pm:(t + 1) * pm].astype(BF16)
        for k in range(1, ng):
            group_send(b, k).start()

    def downs(b, carry):
        down_block(b)
        sum_block(b - 1)
        return carry

    down_block(0)
    lax.fori_loop(1, nblk, downs, 0)
    sum_block(nblk - 1)
    for b in range(nblk):
        total_b = s.gsend[b, g].astype(F32)
        for k in range(1, ng):
            group_in(b, k).wait_recv()
            total_b = total_b + s.grecv[b, lax.rem(g + k, ng)].astype(F32)
        s.res[b * pm:(b + 1) * pm, :] = s.res[b * pm:(b + 1) * pm, :] + total_b
    residual = s.res[...]
    tb = nblk * pm

    s.t_send[...] = jnp.broadcast_to(jnp.sum(residual * residual, axis=1, keepdims=True), (tb, LANES))
    for k in range(1, nq):
        send(rcopy(s.t_send, s.t_recv.at[q], s.t_s.at[k], s.t_r.at[q], (rq(k), c)))
    qrow = lax.broadcasted_iota(jnp.int32, (nqueries, total), 0)
    qslot = lax.broadcasted_iota(jnp.int32, (nqueries, total), 1)
    lens_b = jnp.broadcast_to(lens_row[:1], (nqueries, total)).astype(F32)
    vals_b = jnp.broadcast_to(valid.astype(F32)[:1], (nqueries, total))
    len_col = jnp.sum(jnp.where(qslot == qrow * SEQ, lens_b, 0.0), axis=1, keepdims=True)
    off_col = jnp.sum(jnp.where(qslot < qrow * SEQ, vals_b, 0.0), axis=1, keepdims=True)
    prow = lax.broadcasted_iota(jnp.int32, (nqueries, tb), 1)
    prow = ((prow // pm) * bm + (j * ng + g) * pm + lax.rem(prow, pm)).astype(F32)
    member = jnp.where(jnp.logical_and(prow >= off_col, prow < off_col + len_col), 1.0, 0.0)
    tsum = s.t_send[...]
    for k in range(1, nq):
        p = rq(k)
        rcopy(s.t_send, s.t_recv.at[p], s.t_s.at[k], s.t_r.at[p], (p, c)).wait_recv()
        tsum = tsum + s.t_recv[p]
    final = residual * lax.rsqrt(tsum[:, :1] / d_all + epsilon)
    pooled_part = mm(member, final, lax.Precision.HIGHEST)
    for i in range(r):
        s.pp[i] = pooled_part[:, i * w:(i + 1) * w]
    for i in range(r):
        @pl.when(c != q * r + i)
        def _(i=i):
            rcopy(s.pp.at[i], s.prc.at[c], s.pp_s.at[i], s.pp_r.at[c], (q, q * r + i)).start()

    @pl.when(g == q)
    def _():
        pooled = s.pp[j]
        for k in range(1, nc):
            p = rc(k)
            rcopy(s.pp.at[j], s.prc.at[p], s.pp_s.at[0], s.pp_r.at[p], (q, p)).wait_recv()
            pooled = pooled + s.prc[p]
        s.pblk[...] = (pooled / len_col).astype(BF16)
        for k in range(1, nq):
            rcopy(s.pblk, s.pblk, s.pb_s.at[k], s.pb_r, (rq(k), c)).start()

    loads[3].wait()
    loads[4].wait()

    @pl.when(g != q)
    def _():
        rcopy(s.pblk, s.pblk, s.pb_s.at[0], s.pb_r, (g, c)).wait_recv()

    s.cpart[...] = mm(s.pblk[...], s.code[:, pl.ds(pl.multiple_of(q * bw, bw), bw)])
    for k in range(1, nc):
        send(rcopy(s.cpart, s.crecv.at[c], s.c_s.at[k], s.c_r.at[c], (q, rc(k))))
    s.crecv[c] = s.cpart[...]
    for k in range(1, nc):
        p = rc(k)
        rcopy(s.cpart, s.crecv.at[p], s.c_s.at[k], s.c_r.at[p], (q, p)).wait_recv()
    csum = s.crecv[0]
    for i in range(1, nc):
        csum = csum + s.crecv[i]
    s.codes[q] = csum.astype(BF16)
    for k in range(1, nq):
        send(rcopy(s.codes.at[q], s.codes.at[q], s.o_s.at[k], s.o_r.at[q], (rq(k), c)))
    for k in range(1, nq):
        p = rq(k)
        rcopy(s.codes.at[p], s.codes.at[p], s.o_s.at[k], s.o_r.at[p], (p, c)).wait_recv()
    qcodes = jnp.concatenate([s.codes[i] for i in range(nq)], axis=1)
    scale = 1.0 / math.sqrt(s.corp.shape[1])
    scores = lax.dot_general(qcodes, s.corp[...], (((1,), (1,)), ((), ())), preferred_element_type=F32) * scale

    blocks = s.corp.shape[0] // LANES
    lists = jnp.concatenate([scores[:, i * LANES:(i + 1) * LANES] for i in range(blocks)], axis=0)
    best = merge_all(sort_lanes(lists), nqueries, q >= nq // 2)
    s.top_q[q] = best
    for k in range(1, nq):
        send(rcopy(s.top_q.at[q], s.top_q.at[q], s.tq_s.at[k], s.tq_r.at[q], (rq(k), c)))
    for k in range(1, nq):
        p = rq(k)
        rcopy(s.top_q.at[p], s.top_q.at[p], s.tq_s.at[k], s.tq_r.at[p], (p, c)).wait_recv()
    best = merge_all(s.top_q[...].reshape(nq * nqueries, LANES), nqueries, c >= nc // 2)
    s.top_c[c] = best
    for k in range(1, nc):
        send(rcopy(s.top_c.at[c], s.top_c.at[c], s.tc_s.at[k], s.tc_r.at[c], (q, rc(k))))
    for k in range(1, nc):
        p = rc(k)
        rcopy(s.top_c.at[p], s.top_c.at[p], s.tc_s.at[k], s.tc_r.at[p], (q, p)).wait_recv()
    best = merge_all(s.top_c[...].reshape(nc * nqueries, LANES), nqueries, False)
    out[...] = best[:, :TOPK]

    for wait in drains:
        wait()

    @pl.when(q != g)
    def _():
        rcopy(hid, s.colbuf.at[q], s.a_s, s.a_r.at[q], (g, c)).wait_send()

    def drain_blocks(b, carry):
        @pl.when(sends_up)
        def _():
            up_chain(b).wait_send()

        @pl.when(sends_down)
        def _():
            down_chain(b).wait_send()

        for k in range(1, r):
            side(b, k).wait_send()
        for k in range(1, r):
            lane_send(b, k).wait_send()
        for k in range(1, ng):
            group_send(b, k).wait_send()
        return carry

    def drain_units(n, carry):
        far_part(n).wait_send()
        near_part(n).wait_send()
        passed_part(n).wait_send()
        h_near(n, 0).wait_send()
        h_near(n, 1).wait_send()
        h_pass(n).wait_send()
        return carry

    lax.fori_loop(0, nblk, drain_blocks, 0)
    lax.fori_loop(0, nu, drain_units, 0)
    for i in range(r):
        @pl.when(c != q * r + i)
        def _(i=i):
            rcopy(s.pp.at[i], s.prc.at[c], s.pp_s.at[i], s.pp_r.at[c], (q, q * r + i)).wait_send()

    @pl.when(g == q)
    def _():
        for k in range(1, nq):
            rcopy(s.pblk, s.pblk, s.pb_s.at[k], s.pb_r, (rq(k), c)).wait_send()


def halves_of(ffc):
    return 2 if ffc % (2 * LANES) == 0 else 1


def per_device_fast(nq, nc, hidden_in, lengths, gate_weight, up_weight, down_weight, code_weight, corpus_codes):
    slots, w = hidden_in.shape
    r = nc // nq
    ng = nc // r
    nreal = nq * slots * REAL_NUM // REAL_DEN
    dq, ffc = gate_weight.shape
    bm = 8 * nc
    nblk = nreal // bm
    nh = halves_of(ffc)
    hw = ffc // nh
    nu = nblk * nh
    qm, lm, pm = bm // nq, bm // r, bm // nc
    tb = nblk * pm
    nqueries = nq * lengths.shape[0]
    bits = code_weight.shape[1]
    bw = bits // nq
    vm, dma = pltpu.VMEM, pltpu.SemaphoreType.DMA
    scratch = dict(
        gate=vm(gate_weight.shape, BF16), up=vm(up_weight.shape, BF16), down=vm(down_weight.shape, BF16),
        code=vm(code_weight.shape, BF16), corp=vm(corpus_codes.shape, BF16),
        colbuf=vm((nq, slots, w), BF16), lens_all=vm((nq, 8, slots), jnp.int32), xall=vm((r, nblk, bm, w), BF16),
        xn=vm((bm, dq), BF16), inv_c=vm((nblk, bm, LANES), F32),
        st_send=vm((8, slots), F32), st_recv=vm((nc, 8, slots), F32), inv_all=vm((nq, 8, slots), F32),
        psend=vm((nu, nq, 2, qm, hw), BF16), precv=vm((nu, 4, 2, qm, hw), BF16), pown=vm((nu, 2, qm, hw), F32),
        hall=vm((nu, nq, qm, hw), BF16),
        lsend=vm((nblk, r, lm, dq), BF16), lrecv=vm((nblk, r, lm, dq), BF16),
        gsend=vm((nblk, ng, pm, dq), BF16), grecv=vm((nblk, ng, pm, dq), BF16), res=vm((tb, dq), F32),
        t_send=vm((tb, LANES), F32), t_recv=vm((nq, tb, LANES), F32),
        pp=vm((r, nqueries, w), F32), prc=vm((nc, nqueries, w), F32), pblk=vm((nqueries, w), BF16),
        cpart=vm((nqueries, bw), F32), crecv=vm((nc, nqueries, bw), F32), codes=vm((nq, nqueries, bw), BF16),
        top_q=vm((nq, nqueries, LANES), F32), top_c=vm((nc, nqueries, LANES), F32),
        w_s=dma((5,)), l_s=dma((nq,)), l_r=dma((nq,)), a_s=dma, a_r=dma((nq,)), st_s=dma((nc,)), st_r=dma((nc,)),
        iv_s=dma((nq,)), iv_r=dma((nq,)), ch_s=dma((2, nblk)), ch_r=dma((nblk,)), la_s=dma((r, nblk)), la_r=dma((r, nblk)),
        p_s=dma((nu, 3)), p_r=dma((nu, 3)), h_s=dma((nu, 3)), h_r=dma((nu, 3)),
        lr_s=dma((nblk, r)), lr_r=dma((nblk, r)), g_s=dma((nblk, ng)), g_r=dma((nblk, ng)),
        t_s=dma((nq,)), t_r=dma((nq,)), pp_s=dma((r,)), pp_r=dma((nc,)), pb_s=dma((nq,)), pb_r=dma,
        c_s=dma((nc,)), c_r=dma((nc,)), o_s=dma((nq,)), o_r=dma((nq,)),
        tq_s=dma((nq,)), tq_r=dma((nq,)), tc_s=dma((nc,)), tc_r=dma((nc,)),
    )
    dims = (nq, nc, r, nblk, bm, nh, hw, w * nc)
    vspec, aspec = pl.BlockSpec(memory_space=pltpu.VMEM), pl.BlockSpec(memory_space=pl.ANY)
    sspec = pl.BlockSpec(memory_space=pltpu.SMEM)
    return pl.pallas_call(
        functools.partial(fast_kernel, dims, tuple(scratch)),
        out_shape=jax.ShapeDtypeStruct((nqueries, TOPK), F32),
        in_specs=[vspec, sspec] + [aspec] * 5,
        out_specs=vspec,
        scratch_shapes=list(scratch.values()),
        compiler_params=pltpu.CompilerParams(
            collective_id=0, has_side_effects=True, vmem_limit_bytes=60 * 1024 * 1024),
    )(hidden_in, lengths, gate_weight, up_weight, down_weight, code_weight, corpus_codes)


def per_device(nq, nc, hidden_in, *rest):
    slots, w = hidden_in.shape
    nreal = nq * slots * REAL_NUM // REAL_DEN
    fits = nreal % (8 * nc) == 0 and w % LANES == 0
    body = per_device_fast if fits else per_device_general
    return body(nq, nc, hidden_in, *rest)


def solution(mesh):
    in_specs = (
        P("query", "corpus"),
        P("query"),
        P("query", "corpus"),
        P("query", "corpus"),
        P("corpus", "query"),
        P("corpus", None),
        P(("query", "corpus"), None),
    )
    body = functools.partial(per_device, mesh.shape["query"], mesh.shape["corpus"])
    return jax.shard_map(body, mesh=mesh, in_specs=in_specs, out_specs=P(), check_vma=False)
```

```python
import functools
import math
import types

import jax
import jax.numpy as jnp
from jax import lax
from jax.experimental import pallas as pl
from jax.experimental.pallas import tpu as pltpu
from jax.sharding import PartitionSpec as P

SEQ = 32
LANES = 128
TOPK = 100
REAL_NUM, REAL_DEN = 5, 8
CHUNK = 256
PIECE = 32

epsilon = 1e-05
F32, BF16 = jnp.float32, jnp.bfloat16


def mm(a, b, precision=None):
    return lax.dot_general(a, b, (((1,), (0,)), ((), ())), precision=precision, preferred_element_type=F32)


def rcopy(src, dst, send, recv, dev):
    return pltpu.make_async_remote_copy(
        src_ref=src, dst_ref=dst, send_sem=send, recv_sem=recv,
        device_id=dev, device_id_type=pl.DeviceIdType.MESH)


def exchange(x, s, keep_max):
    bit = (lax.broadcasted_iota(jnp.int32, x.shape, 1) & s) != 0
    other = jnp.where(bit, pltpu.roll(x, s, 1), pltpu.roll(x, LANES - s, 1))
    return jnp.where(keep_max, jnp.maximum(x, other), jnp.minimum(x, other))


def sort_lanes(x):
    lane = lax.broadcasted_iota(jnp.int32, x.shape, 1)
    flip = (lax.broadcasted_iota(jnp.int32, x.shape, 0) >= x.shape[0] // 2).astype(jnp.int32)
    size = 2
    while size <= LANES:
        up = ((lane & size) != 0).astype(jnp.int32) if size < LANES else jnp.zeros_like(lane)
        s = size // 2
        while s:
            low = ((lane & s) != 0).astype(jnp.int32)
            x = exchange(x, s, (low ^ up ^ flip) == 0)
            s //= 2
        size *= 2
    return x


def merge_all(x, rows, lone):
    while x.shape[0] > rows:
        half = x.shape[0] // 2
        x = jnp.maximum(x[:half], x[half:])
        lane = lax.broadcasted_iota(jnp.int32, x.shape, 1)
        if half > rows:
            flip = (lax.broadcasted_iota(jnp.int32, x.shape, 0) >= half // 2).astype(jnp.int32)
        else:
            flip = jnp.zeros_like(lane) + jnp.asarray(lone, jnp.int32)
        s = LANES // 2
        while s:
            low = ((lane & s) != 0).astype(jnp.int32)
            x = exchange(x, s, (low ^ flip) == 0)
            s //= 2
    return x


def general_kernel(dims, hid, lens, gate_h, up_h, down_h, code_h, corp_h, out,
                 gate, up, down, code, corp, colbuf, lens_all, xall, psend, precv,
                 st_send, st_recv, inv_all, xn, pown, top_q, top_c, hall, acc, lsend, lrecv, gsend, grecv, t_send, t_recv,
                 pp, prc, pblk, cpart, crecv, codes,
                 w_s, a_s, a_r, l_s, l_r, ch_s, ch_r, la_s, la_r, p_s, p_r, st_s, st_r, iv_s, iv_r, tq_s, tq_r, tc_s, tc_r, h_s, h_r,
                 lr_s, lr_r, g_s, g_r, t_s, t_r, pp_s, pp_r, pb_s, pb_r, c_s, c_r, o_s, o_r):
    nq, nc, r, nreal, tq, tb, nch, cw, d_all = dims
    q = lax.axis_index("query")
    c = lax.axis_index("corpus")
    g = c // r
    j = lax.rem(c, r)
    slots, w = hid.shape[0], hid.shape[1]
    total = nq * slots
    nqueries = total // SEQ
    bw = code.shape[1] // nq

    loads = []
    for i, (s, d) in enumerate(((gate_h, gate), (up_h, up), (down_h, down), (code_h, code), (corp_h, corp))):
        cp = pltpu.make_async_copy(s, d, w_s.at[i])
        cp.start()
        loads.append(cp)

    def rq(k):
        return lax.rem(q + k, nq)

    def rc(k):
        return lax.rem(c + k, nc)

    def lane(k):
        return lax.rem(j + k, r)

    barrier = pltpu.get_barrier_semaphore()
    for k in range(1, nq):
        pl.semaphore_signal(barrier, inc=1, device_id=(rq(k), c), device_id_type=pl.DeviceIdType.MESH)
    for k in range(1, nc):
        pl.semaphore_signal(barrier, inc=1, device_id=(q, rc(k)), device_id_type=pl.DeviceIdType.MESH)
    pl.semaphore_wait(barrier, nq - 1 + nc - 1)

    for k in range(1, nq):
        rcopy(lens, lens_all.at[q], l_s.at[k], l_r.at[q], (rq(k), c)).start()

    @pl.when(q != g)
    def _():
        rcopy(hid, colbuf.at[q], a_s, a_r.at[q], (g, c)).start()

    squares = jnp.square(hid[...].astype(F32))
    st_send[...] = lax.dot_general(jnp.ones((8, w), F32), squares, (((1,), (1,)), ((), ())),
                                   precision=lax.Precision.HIGHEST, preferred_element_type=F32)
    for k in range(1, nc):
        rcopy(st_send, st_recv.at[c], st_s.at[k], st_r.at[c], (q, rc(k))).start()
    st_recv[c] = st_send[...]
    lens_all[q] = lens[...]
    for k in range(1, nq):
        s = rq(k)
        rcopy(lens, lens_all.at[s], l_s.at[k], l_r.at[s], (s, c)).wait_recv()
    lens_row = jnp.concatenate([lens_all[i] for i in range(nq)], axis=1)
    slot = lax.broadcasted_iota(jnp.int32, (8, total), 1)
    valid = lax.rem(slot, SEQ) < lens_row
    before = lax.broadcasted_iota(jnp.int32, (total, total), 0) < lax.broadcasted_iota(jnp.int32, (total, total), 1)
    pos = mm(valid.astype(F32).astype(BF16), before.astype(F32).astype(BF16)).astype(jnp.int32)
    pos = jnp.where(valid, pos, -1)[:1]

    for k in range(1, nc):
        s = rc(k)
        rcopy(st_send, st_recv.at[s], st_s.at[k], st_r.at[s], (q, s)).wait_recv()
    stat = st_recv[0]
    for i in range(1, nc):
        stat = stat + st_recv[i]
    inv_all[q] = lax.rsqrt(stat / d_all + epsilon)
    for k in range(1, nq):
        rcopy(inv_all.at[q], inv_all.at[q], iv_s.at[k], iv_r.at[q], (rq(k), c)).start()

    nb = ch_r.shape[0]
    ct = nreal // nb

    def chunk(i, slot_j):
        return xall.at[slot_j, pl.ds(i * ct, ct)]

    def down_chain(i):
        return rcopy(chunk(i, j), chunk(i, j), ch_s.at[0, i], ch_r.at[i], (q, jnp.maximum(c - r, 0)))

    def up_chain(i):
        return rcopy(chunk(i, j), chunk(i, j), ch_s.at[1, i], ch_r.at[i], (q, jnp.minimum(c + r, nc - 1)))

    sends_up = jnp.logical_and(g >= q, g < nc // r - 1)
    sends_down = jnp.logical_and(g <= q, g > 0)

    @pl.when(q == g)
    def _():
        colbuf[q] = hid[...]
        for k in range(1, nq):
            s = rq(k)
            rcopy(hid, colbuf.at[s], a_s, a_r.at[s], (s, c)).wait_recv()
        stacked = colbuf[...].reshape(total, w)
        for i in range(nq):
            row = lax.broadcasted_iota(jnp.int32, (tq, total), 0) + i * tq
            pick = (pos == row).astype(F32).astype(BF16)
            xall[j, i * tq:(i + 1) * tq, :] = mm(pick, stacked).astype(BF16)

    for i in range(nb):
        @pl.when(q != g)
        def _(i=i):
            up_chain(i).wait_recv()

        @pl.when(sends_up)
        def _(i=i):
            up_chain(i).start()

        @pl.when(sends_down)
        def _(i=i):
            down_chain(i).start()

        for k in range(1, r):
            rcopy(chunk(i, j), chunk(i, j), la_s.at[k, i], la_r.at[j, i], (q, g * r + lane(k))).start()
    for k in range(1, nq):
        s = rq(k)
        rcopy(inv_all.at[s], inv_all.at[s], iv_s.at[k], iv_r.at[s], (s, c)).wait_recv()
    inv_row = jnp.concatenate([inv_all[i] for i in range(nq)], axis=1)[:1]
    inv_cols = []
    for i in range(nq):
        row = lax.broadcasted_iota(jnp.int32, (tq, total), 0) + i * tq
        inv_cols.append(jnp.sum(jnp.where(pos == row, inv_row, 0.0), axis=1, keepdims=True))
    inv = jnp.concatenate(inv_cols, axis=0)
    for i in range(nb):
        for k in range(1, r):
            s = lane(k)
            rcopy(chunk(i, s), chunk(i, s), la_s.at[k, i], la_r.at[s, i], (q, g * r + s)).wait_recv()

    loads[0].wait()
    loads[1].wait()

    for i in range(r):
        xn[i] = (xall[i].astype(F32) * inv).astype(BF16)

    side_a = q + 1 - 2 * lax.rem(q, 2)
    side_b = q + 2 - 4 * (q // 2)
    far = nq - 1 - q

    def sides(n):
        odd = lax.rem(n, 2)
        return side_a + (side_b - side_a) * odd, side_b + (side_a - side_b) * odd

    def near_part(n):
        one, _ = sides(n)
        return rcopy(psend.at[n, one], precv.at[n, 0], p_s.at[n, 0], p_r.at[n, 0], (one, c))

    def far_part(n):
        one, _ = sides(n)
        return rcopy(psend.at[n, far], precv.at[n, 1], p_s.at[n, 1], p_r.at[n, 1], (one, c))

    def passed_part(n):
        _, two = sides(n)
        return rcopy(precv.at[n, 3], precv.at[n, 2], p_s.at[n, 2], p_r.at[n, 2], (two, c))

    def h_near(n, k):
        to = sides(n)[k]
        return rcopy(hall.at[n, q], hall.at[n, q], h_s.at[n, k], h_r.at[n, k], (to, c))

    def h_near_in(n, k):
        to = sides(n)[k]
        return rcopy(hall.at[n, to], hall.at[n, to], h_s.at[n, k], h_r.at[n, k], (to, c))

    def h_pass(n):
        one, two = sides(n)
        return rcopy(hall.at[n, one], hall.at[n, one], h_s.at[n, 2], h_r.at[n, 2], (two, c))

    def h_pass_in(n):
        _, two = sides(n)
        return rcopy(hall.at[n, far], hall.at[n, far], h_s.at[n, 2], h_r.at[n, 2], (two, c))

    def matmuls(n, carry):
        cols = pl.ds(pl.multiple_of(n * cw, cw), cw)
        for e, wref in enumerate((gate, up)):
            full = sum(mm(xn[i], wref[i * w:(i + 1) * w, cols]) for i in range(r))
            for i in range(nq):
                psend[n, i, e] = full[i * tq:(i + 1) * tq].astype(BF16)

                @pl.when(q == i)
                def _(i=i, e=e, full=full):
                    pown[n, e] = full[i * tq:(i + 1) * tq]
        far_part(n).start()
        near_part(n).start()
        return carry

    lax.fori_loop(0, nch, matmuls, 0)

    loads[2].wait()
    acc[...] = jnp.zeros_like(acc)

    def pass_chunk(n):
        _, two = sides(n)
        far_part(n).wait_recv()
        precv[n, 3] = (psend[n, two].astype(F32) + precv[n, 1].astype(F32)).astype(BF16)
        passed_part(n).start()

    def reduce_chunk(n):
        near_part(n).wait_recv()
        passed_part(n).wait_recv()
        gsum = pown[n, 0] + precv[n, 0, 0].astype(F32) + precv[n, 2, 0].astype(F32)
        usum = pown[n, 1] + precv[n, 0, 1].astype(F32) + precv[n, 2, 1].astype(F32)
        hall[n, q] = (gsum / (1.0 + jnp.exp(-gsum)) * usum).astype(BF16)
        h_near(n, 0).start()
        h_near(n, 1).start()

    def relay_chunk(n):
        h_near_in(n, 0).wait_recv()
        h_pass(n).start()

    def down_chunk(n):
        h_near_in(n, 1).wait_recv()
        h_pass_in(n).wait_recv()
        acc[...] += mm(hall[n].reshape(nreal, cw), down[pl.ds(pl.multiple_of(n * cw, cw), cw), :])

    def passes(n, carry):
        pass_chunk(n)
        return carry

    lax.fori_loop(0, nch, passes, 0)
    reduce_chunk(0)

    def reduces(n, carry):
        reduce_chunk(n)
        relay_chunk(n - 1)
        return carry

    lax.fori_loop(1, nch, reduces, 0)
    relay_chunk(nch - 1)

    def downs(n, carry):
        down_chunk(n)
        return carry

    lax.fori_loop(0, nch, downs, 0)

    ng = nc // r
    for gg in range(ng):
        for jj in range(r):
            b = gg * r + jj
            lsend[jj, gg] = acc[b * tb:(b + 1) * tb].astype(BF16)
    for k in range(1, r):
        t = lane(k)
        rcopy(lsend.at[t], lrecv.at[j], lr_s.at[k], lr_r.at[j], (q, g * r + t)).start()
    mine = lsend[j].astype(F32)
    for k in range(1, r):
        s = lane(k)
        rcopy(lsend.at[s], lrecv.at[s], lr_s.at[k], lr_r.at[s], (q, g * r + s)).wait_recv()
        mine = mine + lrecv[s].astype(F32)
    gsend[...] = mine.astype(BF16)
    for k in range(1, ng):
        t = lax.rem(g + k, ng)
        rcopy(gsend.at[t], grecv.at[g], g_s.at[k], g_r.at[g], (q, t * r + j)).start()
    row = lax.broadcasted_iota(jnp.int32, (tb, nreal), 0) + c * tb
    own_rows = (lax.broadcasted_iota(jnp.int32, (tb, nreal), 1) == row).astype(F32).astype(BF16)
    residual = jnp.concatenate([mm(own_rows, xall[i]) for i in range(r)], axis=1)
    residual = residual + gsend[g].astype(F32)
    for k in range(1, ng):
        s = lax.rem(g + k, ng)
        rcopy(gsend.at[s], grecv.at[s], g_s.at[k], g_r.at[s], (q, s * r + j)).wait_recv()
        residual = residual + grecv[s].astype(F32)

    t_send[...] = jnp.broadcast_to(jnp.sum(residual * residual, axis=1, keepdims=True), (tb, 128))
    for k in range(1, nq):
        rcopy(t_send, t_recv.at[q], t_s.at[k], t_r.at[q], (rq(k), c)).start()
    qrow = lax.broadcasted_iota(jnp.int32, (nqueries, total), 0)
    qslot = lax.broadcasted_iota(jnp.int32, (nqueries, total), 1)
    lens_b = jnp.broadcast_to(lens_row[:1], (nqueries, total)).astype(F32)
    vals_b = jnp.broadcast_to(valid.astype(F32)[:1], (nqueries, total))
    len_col = jnp.sum(jnp.where(qslot == qrow * SEQ, lens_b, 0.0), axis=1, keepdims=True)
    off_col = jnp.sum(jnp.where(qslot < qrow * SEQ, vals_b, 0.0), axis=1, keepdims=True)
    prow = (lax.broadcasted_iota(jnp.int32, (nqueries, tb), 1) + c * tb).astype(F32)
    member = jnp.where(jnp.logical_and(prow >= off_col, prow < off_col + len_col), 1.0, 0.0)
    tsum = t_send[...]
    for k in range(1, nq):
        s = rq(k)
        rcopy(t_send, t_recv.at[s], t_s.at[k], t_r.at[s], (s, c)).wait_recv()
        tsum = tsum + t_recv[s]
    final = residual * lax.rsqrt(tsum[:, :1] / d_all + epsilon)
    pooled_part = mm(member, final, lax.Precision.HIGHEST)
    for i in range(r):
        pp[i] = pooled_part[:, i * w:(i + 1) * w]
    for i in range(r):
        @pl.when(c != q * r + i)
        def _(i=i):
            rcopy(pp.at[i], prc.at[c], pp_s.at[i], pp_r.at[c], (q, q * r + i)).start()

    @pl.when(g == q)
    def _():
        pooled = pp[j]
        for k in range(1, nc):
            s = rc(k)
            rcopy(pp.at[j], prc.at[s], pp_s.at[0], pp_r.at[s], (q, s)).wait_recv()
            pooled = pooled + prc[s]
        pblk[...] = (pooled / len_col).astype(BF16)
        for k in range(1, nq):
            rcopy(pblk, pblk, pb_s.at[k], pb_r, (rq(k), c)).start()

    loads[3].wait()
    loads[4].wait()

    @pl.when(g != q)
    def _():
        rcopy(pblk, pblk, pb_s.at[0], pb_r, (g, c)).wait_recv()

    cpart[...] = mm(pblk[...], code[:, pl.ds(pl.multiple_of(q * bw, bw), bw)])
    for k in range(1, nc):
        rcopy(cpart, crecv.at[c], c_s.at[k], c_r.at[c], (q, rc(k))).start()
    crecv[c] = cpart[...]
    for k in range(1, nc):
        s = rc(k)
        rcopy(cpart, crecv.at[s], c_s.at[k], c_r.at[s], (q, s)).wait_recv()
    csum = crecv[0]
    for i in range(1, nc):
        csum = csum + crecv[i]
    codes[q] = csum.astype(BF16)
    for k in range(1, nq):
        rcopy(codes.at[q], codes.at[q], o_s.at[k], o_r.at[q], (rq(k), c)).start()
    for k in range(1, nq):
        s = rq(k)
        rcopy(codes.at[s], codes.at[s], o_s.at[k], o_r.at[s], (s, c)).wait_recv()
    qcodes = jnp.concatenate([codes[i] for i in range(nq)], axis=1)
    scale = 1.0 / math.sqrt(corp.shape[1])
    scores = lax.dot_general(qcodes, corp[...], (((1,), (1,)), ((), ())), preferred_element_type=F32) * scale

    blocks = corp.shape[0] // LANES
    lists = jnp.concatenate([scores[:, i * LANES:(i + 1) * LANES] for i in range(blocks)], axis=0)
    best = merge_all(sort_lanes(lists), nqueries, q >= nq // 2)
    top_q[q] = best
    for k in range(1, nq):
        rcopy(top_q.at[q], top_q.at[q], tq_s.at[k], tq_r.at[q], (rq(k), c)).start()
    for k in range(1, nq):
        s = rq(k)
        rcopy(top_q.at[s], top_q.at[s], tq_s.at[k], tq_r.at[s], (s, c)).wait_recv()
    best = merge_all(top_q[...].reshape(nq * nqueries, LANES), nqueries, c >= nc // 2)
    top_c[c] = best
    for k in range(1, nc):
        rcopy(top_c.at[c], top_c.at[c], tc_s.at[k], tc_r.at[c], (q, rc(k))).start()
    for k in range(1, nc):
        s = rc(k)
        rcopy(top_c.at[s], top_c.at[s], tc_s.at[k], tc_r.at[s], (q, s)).wait_recv()
    best = merge_all(top_c[...].reshape(nc * nqueries, LANES), nqueries, False)
    out[...] = best[:, :TOPK]

    for k in range(1, nq):
        rcopy(lens, lens_all.at[q], l_s.at[k], l_r.at[q], (rq(k), c)).wait_send()
        rcopy(inv_all.at[q], inv_all.at[q], iv_s.at[k], iv_r.at[q], (rq(k), c)).wait_send()
        rcopy(top_q.at[q], top_q.at[q], tq_s.at[k], tq_r.at[q], (rq(k), c)).wait_send()
        rcopy(t_send, t_recv.at[q], t_s.at[k], t_r.at[q], (rq(k), c)).wait_send()
        rcopy(codes.at[q], codes.at[q], o_s.at[k], o_r.at[q], (rq(k), c)).wait_send()

    @pl.when(q != g)
    def _():
        rcopy(hid, colbuf.at[q], a_s, a_r.at[q], (g, c)).wait_send()

    for i in range(nb):
        @pl.when(sends_up)
        def _(i=i):
            up_chain(i).wait_send()

        @pl.when(sends_down)
        def _(i=i):
            down_chain(i).wait_send()

        for k in range(1, r):
            rcopy(chunk(i, j), chunk(i, j), la_s.at[k, i], la_r.at[j, i], (q, g * r + lane(k))).wait_send()

    def drain(n, carry):
        far_part(n).wait_send()
        near_part(n).wait_send()
        passed_part(n).wait_send()
        h_near(n, 0).wait_send()
        h_near(n, 1).wait_send()
        h_pass(n).wait_send()
        return carry

    lax.fori_loop(0, nch, drain, 0)
    for k in range(1, r):
        rcopy(lsend.at[lane(k)], lrecv.at[j], lr_s.at[k], lr_r.at[j], (q, g * r + lane(k))).wait_send()
    for k in range(1, ng):
        t = lax.rem(g + k, ng)
        rcopy(gsend.at[t], grecv.at[g], g_s.at[k], g_r.at[g], (q, t * r + j)).wait_send()
    for i in range(r):
        @pl.when(c != q * r + i)
        def _(i=i):
            rcopy(pp.at[i], prc.at[c], pp_s.at[i], pp_r.at[c], (q, q * r + i)).wait_send()

    @pl.when(g == q)
    def _():
        for k in range(1, nq):
            rcopy(pblk, pblk, pb_s.at[k], pb_r, (rq(k), c)).wait_send()
    for k in range(1, nc):
        rcopy(cpart, crecv.at[c], c_s.at[k], c_r.at[c], (q, rc(k))).wait_send()
        rcopy(st_send, st_recv.at[c], st_s.at[k], st_r.at[c], (q, rc(k))).wait_send()
        rcopy(top_c.at[c], top_c.at[c], tc_s.at[k], tc_r.at[c], (q, rc(k))).wait_send()


def per_device_general(nq, nc, hidden_in, lengths, gate_weight, up_weight, down_weight, code_weight, corpus_codes):
    slots, w = hidden_in.shape
    r = nc // nq
    nreal = nq * slots * REAL_NUM // REAL_DEN
    tq, tb = nreal // nq, nreal // nc
    dq, ffc = gate_weight.shape
    cw = CHUNK if ffc % CHUNK == 0 else ffc
    nch = ffc // cw
    nb = nreal // PIECE if nreal % PIECE == 0 else nq
    nqueries = nq * lengths.shape[0]
    bits = code_weight.shape[1]
    bw = bits // nq
    ng = nc // r
    lens = jnp.broadcast_to(jnp.repeat(lengths, SEQ)[None, :], (8, slots))
    vm, dma = pltpu.VMEM, pltpu.SemaphoreType.DMA
    scratch = [
        vm(gate_weight.shape, BF16), vm(up_weight.shape, BF16), vm(down_weight.shape, BF16),
        vm(code_weight.shape, BF16), vm(corpus_codes.shape, BF16),
        vm((nq, slots, w), BF16), vm((nq, 8, slots), jnp.int32), vm((r, nreal, w), BF16),
        vm((nch, nq, 2, tq, cw), BF16), vm((nch, nq, 2, tq, cw), BF16),
        vm((8, slots), F32), vm((nc, 8, slots), F32), vm((nq, 8, slots), F32), vm((r, nreal, w), BF16),
        vm((nch, 2, tq, cw), F32), vm((nq, nqueries, LANES), F32), vm((nc, nqueries, LANES), F32),
        vm((nch, nq, tq, cw), BF16), vm((nreal, dq), F32),
        vm((r, ng, tb, dq), BF16), vm((r, ng, tb, dq), BF16), vm((ng, tb, dq), BF16), vm((ng, tb, dq), BF16),
        vm((tb, 128), F32), vm((nq, tb, 128), F32),
        vm((r, nqueries, w), F32), vm((nc, nqueries, w), F32), vm((nqueries, w), BF16),
        vm((nqueries, bw), F32), vm((nc, nqueries, bw), F32), vm((nq, nqueries, bw), BF16),
        dma((5,)), dma, dma((nq,)), dma((nq,)), dma((nq,)), dma((2, nb)), dma((nb,)), dma((r, nb)), dma((r, nb)),
        dma((nch, nq)), dma((nch, nq)), dma((nc,)), dma((nc,)), dma((nq,)), dma((nq,)),
        dma((nq,)), dma((nq,)), dma((nc,)), dma((nc,)), dma((nch, nq)), dma((nch, nq)),
        dma((r,)), dma((r,)), dma((ng,)), dma((ng,)), dma((nq,)), dma((nq,)),
        dma((r,)), dma((nc,)), dma((nq,)), dma, dma((nc,)), dma((nc,)), dma((nq,)), dma((nq,)),
    ]
    dims = (nq, nc, r, nreal, tq, tb, nch, cw, w * nc)
    vspec, aspec = pl.BlockSpec(memory_space=pltpu.VMEM), pl.BlockSpec(memory_space=pl.ANY)
    return pl.pallas_call(
        functools.partial(general_kernel, dims),
        out_shape=jax.ShapeDtypeStruct((nqueries, TOPK), F32),
        in_specs=[vspec, vspec] + [aspec] * 5,
        out_specs=vspec,
        scratch_shapes=scratch,
        compiler_params=pltpu.CompilerParams(
            collective_id=0, has_side_effects=True, vmem_limit_bytes=60 * 1024 * 1024),
    )(hidden_in, lens, gate_weight, up_weight, down_weight, code_weight, corpus_codes)


def fast_kernel(dims, names, hid, lens, gate_h, up_h, down_h, code_h, corp_h, out, *refs):
    nq, nc, r, nblk, bm, nh, hw, lag, d_all = dims
    s = types.SimpleNamespace(**dict(zip(names, refs)))
    q = lax.axis_index("query")
    c = lax.axis_index("corpus")
    g = c // r
    j = lax.rem(c, r)
    ng = nc // r
    slots, w = hid.shape
    total = nq * slots
    nqueries = total // SEQ
    nreal = nblk * bm
    qm, lm, pm = bm // nq, bm // r, bm // nc
    nu = nblk * nh
    bw = s.codew.shape[2] // nq
    gate, up, code, corp = s.gu.at[0], s.gu.at[1], s.codew.at[0], s.codew.at[1]

    first = pltpu.make_async_copy(hid, s.colbuf.at[q], s.w_s.at[0])
    first.start()
    counts = pltpu.make_async_copy(lens, s.lens_s, s.w_s.at[1])
    counts.start()
    for a, b, k in ((gate_h, gate, 2), (up_h, up, 2), (down_h, s.down, 3), (code_h, code, 4), (corp_h, corp, 4)):
        pltpu.make_async_copy(a, b, s.w_s.at[k]).start()

    def loaded(ref, k):
        pltpu.make_async_copy(ref, ref, s.w_s.at[k]).wait()

    def rq(k):
        return lax.rem(q + k, nq)

    def rc(k):
        return lax.rem(c + k, nc)

    def lane(k):
        return lax.rem(j + k, r)

    def got(ref, sem):
        rcopy(ref, ref, sem, sem, (rq(1), c)).wait_recv()

    def sent(ref, sem):
        rcopy(ref, ref, sem, sem, (rq(1), c)).wait_send()

    def to_query(src, ref, ss, rs):
        for k in range(1, nq):
            rcopy(src, ref.at[q], ss, rs, (rq(k), c)).start()

    def to_corpus(src, ref, ss, rs):
        for k in range(1, nc):
            rcopy(src, ref.at[c], ss, rs, (q, rc(k))).start()

    barrier = pltpu.get_barrier_semaphore()
    for k in range(1, nq):
        pl.semaphore_signal(barrier, inc=1, device_id=(rq(k), c), device_id_type=pl.DeviceIdType.MESH)
    for k in range(1, nc):
        pl.semaphore_signal(barrier, inc=1, device_id=(q, rc(k)), device_id_type=pl.DeviceIdType.MESH)

    first.wait()
    squares = jnp.square(s.colbuf[q].astype(F32))
    s.st_send[...] = lax.dot_general(jnp.ones((8, w), F32), squares, (((1,), (1,)), ((), ())),
                                     precision=lax.Precision.HIGHEST, preferred_element_type=F32)
    counts.wait()
    slot_query = lax.broadcasted_iota(jnp.int32, (8, slots), 1) // SEQ
    own_lens = jnp.zeros((8, slots), jnp.int32)
    for k in range(slots // SEQ):
        own_lens = jnp.where(slot_query == k, s.lens_s[k], own_lens)
    s.lens_all[q] = own_lens

    pl.semaphore_wait(barrier, nq - 1 + nc - 1)

    @pl.when(q != g)
    def _():
        rcopy(s.colbuf.at[q], s.colbuf.at[q], s.a_s, s.a_r, (g, c)).start()

    to_query(s.lens_all.at[q], s.lens_all, s.l_s, s.l_r)
    to_corpus(s.st_send, s.st_recv, s.st_s, s.st_r)
    s.st_recv[c] = s.st_send[...]
    got(s.lens_all.at[pl.ds(0, nq - 1)], s.l_r)
    lens_row = jnp.concatenate([s.lens_all[i] for i in range(nq)], axis=1)
    slot = lax.broadcasted_iota(jnp.int32, (8, total), 1)
    valid = lax.rem(slot, SEQ) < lens_row
    before = lax.broadcasted_iota(jnp.int32, (total, total), 0) < lax.broadcasted_iota(jnp.int32, (total, total), 1)
    pos = mm(valid.astype(F32).astype(BF16), before.astype(F32).astype(BF16)).astype(jnp.int32)
    pos = jnp.where(valid, pos, -1)[:1]

    got(s.st_recv.at[pl.ds(0, nc - 1)], s.st_r)
    stat = s.st_recv[0]
    for i in range(1, nc):
        stat = stat + s.st_recv[i]
    s.inv_all[q] = lax.rsqrt(stat / d_all + epsilon)
    to_query(s.inv_all.at[q], s.inv_all, s.iv_s, s.iv_r)

    def block(b, jj):
        return s.xall.at[jj, b]

    def down_chain(b):
        return rcopy(block(b, j), block(b, j), s.ch_s.at[0], s.ch_r.at[b], (q, jnp.maximum(c - r, 0)))

    def up_chain(b):
        return rcopy(block(b, j), block(b, j), s.ch_s.at[1], s.ch_r.at[b], (q, jnp.minimum(c + r, nc - 1)))

    def side(b, k):
        return rcopy(block(b, j), block(b, j), s.la_s, s.la_r.at[b], (q, g * r + lane(k)))

    sends_up = jnp.logical_and(g >= q, g < ng - 1)
    sends_down = jnp.logical_and(g <= q, g > 0)

    def pass_on(b):
        @pl.when(sends_up)
        def _():
            up_chain(b).start()

        @pl.when(sends_down)
        def _():
            down_chain(b).start()

        for k in range(1, r):
            side(b, k).start()

    @pl.when(q == g)
    def _():
        got(s.colbuf.at[pl.ds(0, nq - 1)], s.a_r)
        stacked = s.colbuf[...].reshape(total, w)
        for b in range(nblk):
            row = lax.broadcasted_iota(jnp.int32, (bm, total), 0) + b * bm
            pick = (pos == row).astype(F32).astype(BF16)
            s.xall[j, b] = mm(pick, stacked).astype(BF16)
            pass_on(b)

    got(s.inv_all.at[pl.ds(0, nq - 1)], s.iv_r)
    inv_row = jnp.concatenate([s.inv_all[i] for i in range(nq)], axis=1)[:1]
    for b in range(nblk):
        row = lax.broadcasted_iota(jnp.int32, (bm, total), 0) + b * bm
        col = jnp.sum(jnp.where(pos == row, inv_row, 0.0), axis=1, keepdims=True)
        s.inv_c[b] = jnp.broadcast_to(col, (bm, LANES))

    loaded(s.gu, 2)

    side_a = q + 1 - 2 * lax.rem(q, 2)
    side_b = q + 2 - 4 * (q // 2)
    far = nq - 1 - q

    def sides(n):
        odd = lax.rem(n, 2)
        return side_a + (side_b - side_a) * odd, side_b + (side_a - side_b) * odd

    def near_part(n):
        one, _ = sides(n)
        return rcopy(s.psend.at[n, one], s.precv.at[n, 0], s.p_s, s.p_r.at[n], (one, c))

    def far_part(n):
        one, _ = sides(n)
        return rcopy(s.psend.at[n, far], s.precv.at[n, 2], s.p_s, s.pf_r.at[n], (one, c))

    def passed_part(n):
        _, two = sides(n)
        return rcopy(s.precv.at[n, 3], s.precv.at[n, 1], s.p_s, s.p_r.at[n], (two, c))

    def h_near(n, k, sem):
        return rcopy(s.hall.at[n, q], s.hall.at[n, q], s.h_s, sem, (sides(n)[k], c))

    def h_pass(n, sem):
        one, two = sides(n)
        return rcopy(s.hall.at[n, one], s.hall.at[n, one], s.h_s, sem, (two, c))

    def products(b, carry):
        @pl.when(q != g)
        def _():
            up_chain(b).wait_recv()
            pass_on(b)

        got(s.xall.at[pl.ds(0, r - 1), b], s.la_r.at[b])
        scale = s.inv_c[b][:, :1]
        for i in range(r):
            s.xn[:, i * w:(i + 1) * w] = (s.xall[i, b].astype(F32) * scale).astype(BF16)
        xb = s.xn[...]
        for h in range(nh):
            n = b * nh + h
            for e, wref in enumerate((gate, up)):
                full = mm(xb, wref[:, h * hw:(h + 1) * hw])
                for i in range(nq):
                    s.psend[n, i, e] = full[i * qm:(i + 1) * qm].astype(BF16)

                    @pl.when(q == i)
                    def _(i=i, e=e, full=full, n=n):
                        s.pown[n, e] = full[i * qm:(i + 1) * qm]
            far_part(n).start()
            near_part(n).start()
        return carry

    lax.fori_loop(0, nblk, products, 0)

    row = lax.broadcasted_iota(jnp.int32, (nblk * pm, nreal), 0)
    row = (row // pm) * bm + (j * ng + g) * pm + lax.rem(row, pm)
    own_rows = (lax.broadcasted_iota(jnp.int32, (nblk * pm, nreal), 1) == row).astype(F32).astype(BF16)
    for i in range(r):
        s.res[:, i * w:(i + 1) * w] = mm(own_rows, s.xall[i].reshape(nreal, w))

    loaded(s.down, 3)

    def passes(n, carry):
        _, two = sides(n)
        got(s.precv.at[n, 2], s.pf_r.at[n])
        s.precv[n, 3] = (s.psend[n, two].astype(F32) + s.precv[n, 2].astype(F32)).astype(BF16)
        passed_part(n).start()
        return carry

    def reduce_unit(n):
        got(s.precv.at[n, pl.ds(0, 2)], s.p_r.at[n])
        gsum = s.pown[n, 0] + s.precv[n, 0, 0].astype(F32) + s.precv[n, 1, 0].astype(F32)
        usum = s.pown[n, 1] + s.precv[n, 0, 1].astype(F32) + s.precv[n, 1, 1].astype(F32)
        s.hall[n, q] = (gsum / (1.0 + jnp.exp(-gsum)) * usum).astype(BF16)
        h_near(n, 0, s.hn_r.at[n]).start()
        h_near(n, 1, s.hb_r.at[n // nh]).start()

    def relay_unit(n):
        got(s.hall.at[n, 0], s.hn_r.at[n])
        h_pass(n, s.hb_r.at[n // nh]).start()

    def reduces(n, carry):
        reduce_unit(n)
        return carry

    def reduces_relays(n, carry):
        reduce_unit(n)
        relay_unit(n - lag)
        return carry

    def relays(n, carry):
        relay_unit(n)
        return carry

    lax.fori_loop(0, nu, passes, 0)
    lax.fori_loop(0, lag, reduces, 0)
    lax.fori_loop(lag, nu, reduces_relays, 0)
    lax.fori_loop(nu - lag, nu, relays, 0)

    def lane_send(b, k):
        t = lane(k)
        return rcopy(s.lsend.at[b, t], s.lrecv.at[b, j], s.lr_s, s.lr_r.at[b], (q, g * r + t))

    def group_send(b, k):
        t = lax.rem(g + k, ng)
        return rcopy(s.gsend.at[b, t], s.grecv.at[b, g], s.g_s, s.g_r.at[b], (q, t * r + j))

    def down_block(b):
        part = None
        got(s.hall.at[pl.ds(b * nh, nh), pl.ds(0, 2)], s.hb_r.at[b])
        for h in range(nh):
            n = b * nh + h
            term = mm(s.hall[n].reshape(bm, hw), s.down[h * hw:(h + 1) * hw, :])
            part = term if part is None else part + term
        for t in range(r):
            s.lsend[b, t] = part[t * lm:(t + 1) * lm].astype(BF16)
        for k in range(1, r):
            lane_send(b, k).start()

    def sum_block(b):
        mine = s.lsend[b, j].astype(F32)
        got(s.lrecv.at[b, pl.ds(0, r - 1)], s.lr_r.at[b])
        for k in range(1, r):
            mine = mine + s.lrecv[b, lane(k)].astype(F32)
        for t in range(ng):
            s.gsend[b, t] = mine[t * pm:(t + 1) * pm].astype(BF16)
        for k in range(1, ng):
            group_send(b, k).start()

    def downs(b, carry):
        down_block(b)
        sum_block(b - 1)
        return carry

    down_block(0)
    lax.fori_loop(1, nblk, downs, 0)
    sum_block(nblk - 1)
    for b in range(nblk):
        total_b = s.gsend[b, g].astype(F32)
        got(s.grecv.at[b, pl.ds(0, ng - 1)], s.g_r.at[b])
        for k in range(1, ng):
            total_b = total_b + s.grecv[b, lax.rem(g + k, ng)].astype(F32)
        s.res[b * pm:(b + 1) * pm, :] = s.res[b * pm:(b + 1) * pm, :] + total_b
    residual = s.res[...]
    tb = nblk * pm

    s.t_send[...] = jnp.broadcast_to(jnp.sum(residual * residual, axis=1, keepdims=True), (tb, LANES))
    to_query(s.t_send, s.t_recv, s.t_s, s.t_r)
    qrow = lax.broadcasted_iota(jnp.int32, (nqueries, total), 0)
    qslot = lax.broadcasted_iota(jnp.int32, (nqueries, total), 1)
    lens_b = jnp.broadcast_to(lens_row[:1], (nqueries, total)).astype(F32)
    vals_b = jnp.broadcast_to(valid.astype(F32)[:1], (nqueries, total))
    len_col = jnp.sum(jnp.where(qslot == qrow * SEQ, lens_b, 0.0), axis=1, keepdims=True)
    off_col = jnp.sum(jnp.where(qslot < qrow * SEQ, vals_b, 0.0), axis=1, keepdims=True)
    prow = lax.broadcasted_iota(jnp.int32, (nqueries, tb), 1)
    prow = ((prow // pm) * bm + (j * ng + g) * pm + lax.rem(prow, pm)).astype(F32)
    member = jnp.where(jnp.logical_and(prow >= off_col, prow < off_col + len_col), 1.0, 0.0)
    tsum = s.t_send[...]
    got(s.t_recv.at[pl.ds(0, nq - 1)], s.t_r)
    for k in range(1, nq):
        tsum = tsum + s.t_recv[rq(k)]
    final = residual * lax.rsqrt(tsum[:, :1] / d_all + epsilon)
    pooled_part = mm(member, final, lax.Precision.HIGHEST)
    for i in range(r):
        s.pp[i] = pooled_part[:, i * w:(i + 1) * w]
    for i in range(r):
        @pl.when(c != q * r + i)
        def _(i=i):
            rcopy(s.pp.at[i], s.prc.at[c], s.pp_s, s.pp_r, (q, q * r + i)).start()

    @pl.when(g == q)
    def _():
        pooled = s.pp[j]
        got(s.prc.at[pl.ds(0, nc - 1)], s.pp_r)
        for k in range(1, nc):
            pooled = pooled + s.prc[rc(k)]
        s.pblk[0] = (pooled / len_col).astype(BF16)
        for k in range(1, nq):
            rcopy(s.pblk.at[0], s.pblk.at[0], s.pb_s, s.pb_r, (rq(k), c)).start()

    loaded(s.codew, 4)

    @pl.when(g != q)
    def _():
        got(s.pblk.at[0], s.pb_r)

    s.cpart[...] = mm(s.pblk[0], code[:, pl.ds(pl.multiple_of(q * bw, bw), bw)])
    to_corpus(s.cpart, s.crecv, s.c_s, s.c_r)
    s.crecv[c] = s.cpart[...]
    got(s.crecv.at[pl.ds(0, nc - 1)], s.c_r)
    csum = s.crecv[0]
    for i in range(1, nc):
        csum = csum + s.crecv[i]
    s.codes[q] = csum.astype(BF16)
    to_query(s.codes.at[q], s.codes, s.o_s, s.o_r)
    got(s.codes.at[pl.ds(0, nq - 1)], s.o_r)
    qcodes = jnp.concatenate([s.codes[i] for i in range(nq)], axis=1)
    scale = 1.0 / math.sqrt(corp.shape[1])
    scores = lax.dot_general(qcodes, corp[...], (((1,), (1,)), ((), ())), preferred_element_type=F32) * scale

    blocks = corp.shape[0] // LANES
    lists = jnp.concatenate([scores[:, i * LANES:(i + 1) * LANES] for i in range(blocks)], axis=0)
    best = merge_all(sort_lanes(lists), nqueries, q >= nq // 2)
    s.top_q[q] = best
    to_query(s.top_q.at[q], s.top_q, s.tq_s, s.tq_r)
    got(s.top_q.at[pl.ds(0, nq - 1)], s.tq_r)
    best = merge_all(s.top_q[...].reshape(nq * nqueries, LANES), nqueries, c >= nc // 2)
    s.top_c[c] = best
    to_corpus(s.top_c.at[c], s.top_c, s.tc_s, s.tc_r)
    got(s.top_c.at[pl.ds(0, nc - 1)], s.tc_r)
    best = merge_all(s.top_c[...].reshape(nc * nqueries, LANES), nqueries, False)
    out[...] = best[:, :TOPK]

    sent(s.lens_all.at[pl.ds(0, nq - 1)], s.l_s)
    sent(s.st_recv.at[pl.ds(0, nc - 1)], s.st_s)
    sent(s.inv_all.at[pl.ds(0, nq - 1)], s.iv_s)

    @pl.when(q != g)
    def _():
        sent(s.colbuf.at[0], s.a_s)

    @pl.when(sends_down)
    def _():
        sent(s.xall.at[0], s.ch_s.at[0])

    @pl.when(sends_up)
    def _():
        sent(s.xall.at[0], s.ch_s.at[1])

    sent(s.xall.at[pl.ds(0, r - 1)], s.la_s)
    sent(s.psend.at[:, pl.ds(0, 3)], s.p_s)
    sent(s.hall.at[:, pl.ds(0, 3)], s.h_s)
    sent(s.lsend.at[:, pl.ds(0, r - 1)], s.lr_s)
    sent(s.gsend.at[:, pl.ds(0, ng - 1)], s.g_s)
    sent(s.t_recv.at[pl.ds(0, nq - 1)], s.t_s)

    @pl.when(g == q)
    def _():
        sent(s.pp.at[pl.ds(0, r - 1)], s.pp_s)
        sent(s.pblk.at[pl.ds(0, nq - 1)], s.pb_s)

    @pl.when(g != q)
    def _():
        sent(s.pp, s.pp_s)

    sent(s.crecv.at[pl.ds(0, nc - 1)], s.c_s)
    sent(s.codes.at[pl.ds(0, nq - 1)], s.o_s)
    sent(s.top_q.at[pl.ds(0, nq - 1)], s.tq_s)
    sent(s.top_c.at[pl.ds(0, nc - 1)], s.tc_s)


def halves_of(ffc):
    return 2 if ffc % (2 * LANES) == 0 else 1


def per_device_fast(nq, nc, hidden_in, lengths, gate_weight, up_weight, down_weight, code_weight, corpus_codes):
    slots, w = hidden_in.shape
    r = nc // nq
    ng = nc // r
    nreal = nq * slots * REAL_NUM // REAL_DEN
    dq, ffc = gate_weight.shape
    bm = 8 * nc
    nblk = nreal // bm
    nh = halves_of(ffc)
    hw = ffc // nh
    nu = nblk * nh
    qm, lm, pm = bm // nq, bm // r, bm // nc
    tb = nblk * pm
    nqueries = nq * lengths.shape[0]
    bits = code_weight.shape[1]
    bw = bits // nq
    vm, dma = pltpu.VMEM, pltpu.SemaphoreType.DMA
    scratch = dict(
        gu=vm((2,) + gate_weight.shape, BF16), down=vm(down_weight.shape, BF16), codew=vm((2,) + code_weight.shape, BF16),
        lens_s=pltpu.SMEM(lengths.shape, jnp.int32),
        colbuf=vm((nq, slots, w), BF16), lens_all=vm((nq, 8, slots), jnp.int32), xall=vm((r, nblk, bm, w), BF16),
        xn=vm((bm, dq), BF16), inv_c=vm((nblk, bm, LANES), F32),
        st_send=vm((8, slots), F32), st_recv=vm((nc, 8, slots), F32), inv_all=vm((nq, 8, slots), F32),
        psend=vm((nu, nq, 2, qm, hw), BF16), precv=vm((nu, 4, 2, qm, hw), BF16), pown=vm((nu, 2, qm, hw), F32),
        hall=vm((nu, nq, qm, hw), BF16),
        lsend=vm((nblk, r, lm, dq), BF16), lrecv=vm((nblk, r, lm, dq), BF16),
        gsend=vm((nblk, ng, pm, dq), BF16), grecv=vm((nblk, ng, pm, dq), BF16), res=vm((tb, dq), F32),
        t_send=vm((tb, LANES), F32), t_recv=vm((nq, tb, LANES), F32),
        pp=vm((r, nqueries, w), F32), prc=vm((nc, nqueries, w), F32), pblk=vm((nq, nqueries, w), BF16),
        cpart=vm((nqueries, bw), F32), crecv=vm((nc, nqueries, bw), F32), codes=vm((nq, nqueries, bw), BF16),
        top_q=vm((nq, nqueries, LANES), F32), top_c=vm((nc, nqueries, LANES), F32),
        w_s=dma((5,)), l_s=dma, l_r=dma, a_s=dma, a_r=dma, st_s=dma, st_r=dma, iv_s=dma, iv_r=dma,
        ch_s=dma((2,)), ch_r=dma((nblk,)), la_s=dma, la_r=dma((nblk,)),
        p_s=dma, p_r=dma((nu,)), pf_r=dma((nu,)), h_s=dma, hn_r=dma((nu,)), hb_r=dma((nblk,)),
        lr_s=dma, lr_r=dma((nblk,)), g_s=dma, g_r=dma((nblk,)),
        t_s=dma, t_r=dma, pp_s=dma, pp_r=dma, pb_s=dma, pb_r=dma, c_s=dma, c_r=dma, o_s=dma, o_r=dma,
        tq_s=dma, tq_r=dma, tc_s=dma, tc_r=dma,
    )
    dims = (nq, nc, r, nblk, bm, nh, hw, min(3, nu - 1), w * nc)
    vspec, aspec = pl.BlockSpec(memory_space=pltpu.VMEM), pl.BlockSpec(memory_space=pl.ANY)
    return pl.pallas_call(
        functools.partial(fast_kernel, dims, tuple(scratch)),
        out_shape=jax.ShapeDtypeStruct((nqueries, TOPK), F32),
        in_specs=[aspec] * 7,
        out_specs=vspec,
        scratch_shapes=list(scratch.values()),
        compiler_params=pltpu.CompilerParams(
            collective_id=0, has_side_effects=True, vmem_limit_bytes=60 * 1024 * 1024),
    )(hidden_in, lengths, gate_weight, up_weight, down_weight, code_weight, corpus_codes)


def per_device(nq, nc, hidden_in, *rest):
    slots, w = hidden_in.shape
    nreal = nq * slots * REAL_NUM // REAL_DEN
    fits = nreal % (8 * nc) == 0 and w % LANES == 0 and rest[4].shape == rest[5].shape
    body = per_device_fast if fits else per_device_general
    return body(nq, nc, hidden_in, *rest)


def solution(mesh):
    in_specs = (
        P("query", "corpus"),
        P("query"),
        P("query", "corpus"),
        P("query", "corpus"),
        P("corpus", "query"),
        P("corpus", None),
        P(("query", "corpus"), None),
    )
    body = functools.partial(per_device, mesh.shape["query"], mesh.shape["corpus"])
    return jax.shard_map(body, mesh=mesh, in_specs=in_specs, out_specs=P(), check_vma=False)
```

```python
import functools
import math
import types

import jax
import jax.numpy as jnp
from jax import lax
from jax.experimental import pallas as pl
from jax.experimental.pallas import tpu as pltpu
from jax.sharding import PartitionSpec as P

SEQ = 32
LANES = 128
TOPK = 100
REAL_NUM, REAL_DEN = 5, 8
CHUNK = 256
PIECE = 32

epsilon = 1e-05
F32, BF16 = jnp.float32, jnp.bfloat16


def mm(a, b, precision=None):
    return lax.dot_general(a, b, (((1,), (0,)), ((), ())), precision=precision, preferred_element_type=F32)


def rcopy(src, dst, send, recv, dev):
    return pltpu.make_async_remote_copy(
        src_ref=src, dst_ref=dst, send_sem=send, recv_sem=recv,
        device_id=dev, device_id_type=pl.DeviceIdType.MESH)


def exchange(x, s, keep_max):
    bit = (lax.broadcasted_iota(jnp.int32, x.shape, 1) & s) != 0
    other = jnp.where(bit, pltpu.roll(x, s, 1), pltpu.roll(x, LANES - s, 1))
    return jnp.where(keep_max, jnp.maximum(x, other), jnp.minimum(x, other))


def sort_lanes(x):
    lane = lax.broadcasted_iota(jnp.int32, x.shape, 1)
    flip = (lax.broadcasted_iota(jnp.int32, x.shape, 0) >= x.shape[0] // 2).astype(jnp.int32)
    size = 2
    while size <= LANES:
        up = ((lane & size) != 0).astype(jnp.int32) if size < LANES else jnp.zeros_like(lane)
        s = size // 2
        while s:
            low = ((lane & s) != 0).astype(jnp.int32)
            x = exchange(x, s, (low ^ up ^ flip) == 0)
            s //= 2
        size *= 2
    return x


def merge_all(x, rows, lone):
    while x.shape[0] > rows:
        half = x.shape[0] // 2
        x = jnp.maximum(x[:half], x[half:])
        lane = lax.broadcasted_iota(jnp.int32, x.shape, 1)
        if half > rows:
            flip = (lax.broadcasted_iota(jnp.int32, x.shape, 0) >= half // 2).astype(jnp.int32)
        else:
            flip = jnp.zeros_like(lane) + jnp.asarray(lone, jnp.int32)
        s = LANES // 2
        while s:
            low = ((lane & s) != 0).astype(jnp.int32)
            x = exchange(x, s, (low ^ flip) == 0)
            s //= 2
    return x


def general_kernel(dims, hid, lens, gate_h, up_h, down_h, code_h, corp_h, out,
                 gate, up, down, code, corp, colbuf, lens_all, xall, psend, precv,
                 st_send, st_recv, inv_all, xn, pown, top_q, top_c, hall, acc, lsend, lrecv, gsend, grecv, t_send, t_recv,
                 pp, prc, pblk, cpart, crecv, codes,
                 w_s, a_s, a_r, l_s, l_r, ch_s, ch_r, la_s, la_r, p_s, p_r, st_s, st_r, iv_s, iv_r, tq_s, tq_r, tc_s, tc_r, h_s, h_r,
                 lr_s, lr_r, g_s, g_r, t_s, t_r, pp_s, pp_r, pb_s, pb_r, c_s, c_r, o_s, o_r):
    nq, nc, r, nreal, tq, tb, nch, cw, d_all = dims
    q = lax.axis_index("query")
    c = lax.axis_index("corpus")
    g = c // r
    j = lax.rem(c, r)
    slots, w = hid.shape[0], hid.shape[1]
    total = nq * slots
    nqueries = total // SEQ
    bw = code.shape[1] // nq

    loads = []
    for i, (s, d) in enumerate(((gate_h, gate), (up_h, up), (down_h, down), (code_h, code), (corp_h, corp))):
        cp = pltpu.make_async_copy(s, d, w_s.at[i])
        cp.start()
        loads.append(cp)

    def rq(k):
        return lax.rem(q + k, nq)

    def rc(k):
        return lax.rem(c + k, nc)

    def lane(k):
        return lax.rem(j + k, r)

    barrier = pltpu.get_barrier_semaphore()
    for k in range(1, nq):
        pl.semaphore_signal(barrier, inc=1, device_id=(rq(k), c), device_id_type=pl.DeviceIdType.MESH)
    for k in range(1, nc):
        pl.semaphore_signal(barrier, inc=1, device_id=(q, rc(k)), device_id_type=pl.DeviceIdType.MESH)
    pl.semaphore_wait(barrier, nq - 1 + nc - 1)

    for k in range(1, nq):
        rcopy(lens, lens_all.at[q], l_s.at[k], l_r.at[q], (rq(k), c)).start()

    @pl.when(q != g)
    def _():
        rcopy(hid, colbuf.at[q], a_s, a_r.at[q], (g, c)).start()

    squares = jnp.square(hid[...].astype(F32))
    st_send[...] = lax.dot_general(jnp.ones((8, w), F32), squares, (((1,), (1,)), ((), ())),
                                   precision=lax.Precision.HIGHEST, preferred_element_type=F32)
    for k in range(1, nc):
        rcopy(st_send, st_recv.at[c], st_s.at[k], st_r.at[c], (q, rc(k))).start()
    st_recv[c] = st_send[...]
    lens_all[q] = lens[...]
    for k in range(1, nq):
        s = rq(k)
        rcopy(lens, lens_all.at[s], l_s.at[k], l_r.at[s], (s, c)).wait_recv()
    lens_row = jnp.concatenate([lens_all[i] for i in range(nq)], axis=1)
    slot = lax.broadcasted_iota(jnp.int32, (8, total), 1)
    valid = lax.rem(slot, SEQ) < lens_row
    before = lax.broadcasted_iota(jnp.int32, (total, total), 0) < lax.broadcasted_iota(jnp.int32, (total, total), 1)
    pos = mm(valid.astype(F32).astype(BF16), before.astype(F32).astype(BF16)).astype(jnp.int32)
    pos = jnp.where(valid, pos, -1)[:1]

    for k in range(1, nc):
        s = rc(k)
        rcopy(st_send, st_recv.at[s], st_s.at[k], st_r.at[s], (q, s)).wait_recv()
    stat = st_recv[0]
    for i in range(1, nc):
        stat = stat + st_recv[i]
    inv_all[q] = lax.rsqrt(stat / d_all + epsilon)
    for k in range(1, nq):
        rcopy(inv_all.at[q], inv_all.at[q], iv_s.at[k], iv_r.at[q], (rq(k), c)).start()

    nb = ch_r.shape[0]
    ct = nreal // nb

    def chunk(i, slot_j):
        return xall.at[slot_j, pl.ds(i * ct, ct)]

    def down_chain(i):
        return rcopy(chunk(i, j), chunk(i, j), ch_s.at[0, i], ch_r.at[i], (q, jnp.maximum(c - r, 0)))

    def up_chain(i):
        return rcopy(chunk(i, j), chunk(i, j), ch_s.at[1, i], ch_r.at[i], (q, jnp.minimum(c + r, nc - 1)))

    sends_up = jnp.logical_and(g >= q, g < nc // r - 1)
    sends_down = jnp.logical_and(g <= q, g > 0)

    @pl.when(q == g)
    def _():
        colbuf[q] = hid[...]
        for k in range(1, nq):
            s = rq(k)
            rcopy(hid, colbuf.at[s], a_s, a_r.at[s], (s, c)).wait_recv()
        stacked = colbuf[...].reshape(total, w)
        for i in range(nq):
            row = lax.broadcasted_iota(jnp.int32, (tq, total), 0) + i * tq
            pick = (pos == row).astype(F32).astype(BF16)
            xall[j, i * tq:(i + 1) * tq, :] = mm(pick, stacked).astype(BF16)

    for i in range(nb):
        @pl.when(q != g)
        def _(i=i):
            up_chain(i).wait_recv()

        @pl.when(sends_up)
        def _(i=i):
            up_chain(i).start()

        @pl.when(sends_down)
        def _(i=i):
            down_chain(i).start()

        for k in range(1, r):
            rcopy(chunk(i, j), chunk(i, j), la_s.at[k, i], la_r.at[j, i], (q, g * r + lane(k))).start()
    for k in range(1, nq):
        s = rq(k)
        rcopy(inv_all.at[s], inv_all.at[s], iv_s.at[k], iv_r.at[s], (s, c)).wait_recv()
    inv_row = jnp.concatenate([inv_all[i] for i in range(nq)], axis=1)[:1]
    inv_cols = []
    for i in range(nq):
        row = lax.broadcasted_iota(jnp.int32, (tq, total), 0) + i * tq
        inv_cols.append(jnp.sum(jnp.where(pos == row, inv_row, 0.0), axis=1, keepdims=True))
    inv = jnp.concatenate(inv_cols, axis=0)
    for i in range(nb):
        for k in range(1, r):
            s = lane(k)
            rcopy(chunk(i, s), chunk(i, s), la_s.at[k, i], la_r.at[s, i], (q, g * r + s)).wait_recv()

    loads[0].wait()
    loads[1].wait()

    for i in range(r):
        xn[i] = (xall[i].astype(F32) * inv).astype(BF16)

    side_a = q + 1 - 2 * lax.rem(q, 2)
    side_b = q + 2 - 4 * (q // 2)
    far = nq - 1 - q

    def sides(n):
        odd = lax.rem(n, 2)
        return side_a + (side_b - side_a) * odd, side_b + (side_a - side_b) * odd

    def near_part(n):
        one, _ = sides(n)
        return rcopy(psend.at[n, one], precv.at[n, 0], p_s.at[n, 0], p_r.at[n, 0], (one, c))

    def far_part(n):
        one, _ = sides(n)
        return rcopy(psend.at[n, far], precv.at[n, 1], p_s.at[n, 1], p_r.at[n, 1], (one, c))

    def passed_part(n):
        _, two = sides(n)
        return rcopy(precv.at[n, 3], precv.at[n, 2], p_s.at[n, 2], p_r.at[n, 2], (two, c))

    def h_near(n, k):
        to = sides(n)[k]
        return rcopy(hall.at[n, q], hall.at[n, q], h_s.at[n, k], h_r.at[n, k], (to, c))

    def h_near_in(n, k):
        to = sides(n)[k]
        return rcopy(hall.at[n, to], hall.at[n, to], h_s.at[n, k], h_r.at[n, k], (to, c))

    def h_pass(n):
        one, two = sides(n)
        return rcopy(hall.at[n, one], hall.at[n, one], h_s.at[n, 2], h_r.at[n, 2], (two, c))

    def h_pass_in(n):
        _, two = sides(n)
        return rcopy(hall.at[n, far], hall.at[n, far], h_s.at[n, 2], h_r.at[n, 2], (two, c))

    def matmuls(n, carry):
        cols = pl.ds(pl.multiple_of(n * cw, cw), cw)
        for e, wref in enumerate((gate, up)):
            full = sum(mm(xn[i], wref[i * w:(i + 1) * w, cols]) for i in range(r))
            for i in range(nq):
                psend[n, i, e] = full[i * tq:(i + 1) * tq].astype(BF16)

                @pl.when(q == i)
                def _(i=i, e=e, full=full):
                    pown[n, e] = full[i * tq:(i + 1) * tq]
        far_part(n).start()
        near_part(n).start()
        return carry

    lax.fori_loop(0, nch, matmuls, 0)

    loads[2].wait()
    acc[...] = jnp.zeros_like(acc)

    def pass_chunk(n):
        _, two = sides(n)
        far_part(n).wait_recv()
        precv[n, 3] = (psend[n, two].astype(F32) + precv[n, 1].astype(F32)).astype(BF16)
        passed_part(n).start()

    def reduce_chunk(n):
        near_part(n).wait_recv()
        passed_part(n).wait_recv()
        gsum = pown[n, 0] + precv[n, 0, 0].astype(F32) + precv[n, 2, 0].astype(F32)
        usum = pown[n, 1] + precv[n, 0, 1].astype(F32) + precv[n, 2, 1].astype(F32)
        hall[n, q] = (gsum / (1.0 + jnp.exp(-gsum)) * usum).astype(BF16)
        h_near(n, 0).start()
        h_near(n, 1).start()

    def relay_chunk(n):
        h_near_in(n, 0).wait_recv()
        h_pass(n).start()

    def down_chunk(n):
        h_near_in(n, 1).wait_recv()
        h_pass_in(n).wait_recv()
        acc[...] += mm(hall[n].reshape(nreal, cw), down[pl.ds(pl.multiple_of(n * cw, cw), cw), :])

    def passes(n, carry):
        pass_chunk(n)
        return carry

    lax.fori_loop(0, nch, passes, 0)
    reduce_chunk(0)

    def reduces(n, carry):
        reduce_chunk(n)
        relay_chunk(n - 1)
        return carry

    lax.fori_loop(1, nch, reduces, 0)
    relay_chunk(nch - 1)

    def downs(n, carry):
        down_chunk(n)
        return carry

    lax.fori_loop(0, nch, downs, 0)

    ng = nc // r
    for gg in range(ng):
        for jj in range(r):
            b = gg * r + jj
            lsend[jj, gg] = acc[b * tb:(b + 1) * tb].astype(BF16)
    for k in range(1, r):
        t = lane(k)
        rcopy(lsend.at[t], lrecv.at[j], lr_s.at[k], lr_r.at[j], (q, g * r + t)).start()
    mine = lsend[j].astype(F32)
    for k in range(1, r):
        s = lane(k)
        rcopy(lsend.at[s], lrecv.at[s], lr_s.at[k], lr_r.at[s], (q, g * r + s)).wait_recv()
        mine = mine + lrecv[s].astype(F32)
    gsend[...] = mine.astype(BF16)
    for k in range(1, ng):
        t = lax.rem(g + k, ng)
        rcopy(gsend.at[t], grecv.at[g], g_s.at[k], g_r.at[g], (q, t * r + j)).start()
    row = lax.broadcasted_iota(jnp.int32, (tb, nreal), 0) + c * tb
    own_rows = (lax.broadcasted_iota(jnp.int32, (tb, nreal), 1) == row).astype(F32).astype(BF16)
    residual = jnp.concatenate([mm(own_rows, xall[i]) for i in range(r)], axis=1)
    residual = residual + gsend[g].astype(F32)
    for k in range(1, ng):
        s = lax.rem(g + k, ng)
        rcopy(gsend.at[s], grecv.at[s], g_s.at[k], g_r.at[s], (q, s * r + j)).wait_recv()
        residual = residual + grecv[s].astype(F32)

    t_send[...] = jnp.broadcast_to(jnp.sum(residual * residual, axis=1, keepdims=True), (tb, 128))
    for k in range(1, nq):
        rcopy(t_send, t_recv.at[q], t_s.at[k], t_r.at[q], (rq(k), c)).start()
    qrow = lax.broadcasted_iota(jnp.int32, (nqueries, total), 0)
    qslot = lax.broadcasted_iota(jnp.int32, (nqueries, total), 1)
    lens_b = jnp.broadcast_to(lens_row[:1], (nqueries, total)).astype(F32)
    vals_b = jnp.broadcast_to(valid.astype(F32)[:1], (nqueries, total))
    len_col = jnp.sum(jnp.where(qslot == qrow * SEQ, lens_b, 0.0), axis=1, keepdims=True)
    off_col = jnp.sum(jnp.where(qslot < qrow * SEQ, vals_b, 0.0), axis=1, keepdims=True)
    prow = (lax.broadcasted_iota(jnp.int32, (nqueries, tb), 1) + c * tb).astype(F32)
    member = jnp.where(jnp.logical_and(prow >= off_col, prow < off_col + len_col), 1.0, 0.0)
    tsum = t_send[...]
    for k in range(1, nq):
        s = rq(k)
        rcopy(t_send, t_recv.at[s], t_s.at[k], t_r.at[s], (s, c)).wait_recv()
        tsum = tsum + t_recv[s]
    final = residual * lax.rsqrt(tsum[:, :1] / d_all + epsilon)
    pooled_part = mm(member, final, lax.Precision.HIGHEST)
    for i in range(r):
        pp[i] = pooled_part[:, i * w:(i + 1) * w]
    for i in range(r):
        @pl.when(c != q * r + i)
        def _(i=i):
            rcopy(pp.at[i], prc.at[c], pp_s.at[i], pp_r.at[c], (q, q * r + i)).start()

    @pl.when(g == q)
    def _():
        pooled = pp[j]
        for k in range(1, nc):
            s = rc(k)
            rcopy(pp.at[j], prc.at[s], pp_s.at[0], pp_r.at[s], (q, s)).wait_recv()
            pooled = pooled + prc[s]
        pblk[...] = (pooled / len_col).astype(BF16)
        for k in range(1, nq):
            rcopy(pblk, pblk, pb_s.at[k], pb_r, (rq(k), c)).start()

    loads[3].wait()
    loads[4].wait()

    @pl.when(g != q)
    def _():
        rcopy(pblk, pblk, pb_s.at[0], pb_r, (g, c)).wait_recv()

    cpart[...] = mm(pblk[...], code[:, pl.ds(pl.multiple_of(q * bw, bw), bw)])
    for k in range(1, nc):
        rcopy(cpart, crecv.at[c], c_s.at[k], c_r.at[c], (q, rc(k))).start()
    crecv[c] = cpart[...]
    for k in range(1, nc):
        s = rc(k)
        rcopy(cpart, crecv.at[s], c_s.at[k], c_r.at[s], (q, s)).wait_recv()
    csum = crecv[0]
    for i in range(1, nc):
        csum = csum + crecv[i]
    codes[q] = csum.astype(BF16)
    for k in range(1, nq):
        rcopy(codes.at[q], codes.at[q], o_s.at[k], o_r.at[q], (rq(k), c)).start()
    for k in range(1, nq):
        s = rq(k)
        rcopy(codes.at[s], codes.at[s], o_s.at[k], o_r.at[s], (s, c)).wait_recv()
    qcodes = jnp.concatenate([codes[i] for i in range(nq)], axis=1)
    scale = 1.0 / math.sqrt(corp.shape[1])
    scores = lax.dot_general(qcodes, corp[...], (((1,), (1,)), ((), ())), preferred_element_type=F32) * scale

    blocks = corp.shape[0] // LANES
    lists = jnp.concatenate([scores[:, i * LANES:(i + 1) * LANES] for i in range(blocks)], axis=0)
    best = merge_all(sort_lanes(lists), nqueries, q >= nq // 2)
    top_q[q] = best
    for k in range(1, nq):
        rcopy(top_q.at[q], top_q.at[q], tq_s.at[k], tq_r.at[q], (rq(k), c)).start()
    for k in range(1, nq):
        s = rq(k)
        rcopy(top_q.at[s], top_q.at[s], tq_s.at[k], tq_r.at[s], (s, c)).wait_recv()
    best = merge_all(top_q[...].reshape(nq * nqueries, LANES), nqueries, c >= nc // 2)
    top_c[c] = best
    for k in range(1, nc):
        rcopy(top_c.at[c], top_c.at[c], tc_s.at[k], tc_r.at[c], (q, rc(k))).start()
    for k in range(1, nc):
        s = rc(k)
        rcopy(top_c.at[s], top_c.at[s], tc_s.at[k], tc_r.at[s], (q, s)).wait_recv()
    best = merge_all(top_c[...].reshape(nc * nqueries, LANES), nqueries, False)
    out[...] = best[:, :TOPK]

    for k in range(1, nq):
        rcopy(lens, lens_all.at[q], l_s.at[k], l_r.at[q], (rq(k), c)).wait_send()
        rcopy(inv_all.at[q], inv_all.at[q], iv_s.at[k], iv_r.at[q], (rq(k), c)).wait_send()
        rcopy(top_q.at[q], top_q.at[q], tq_s.at[k], tq_r.at[q], (rq(k), c)).wait_send()
        rcopy(t_send, t_recv.at[q], t_s.at[k], t_r.at[q], (rq(k), c)).wait_send()
        rcopy(codes.at[q], codes.at[q], o_s.at[k], o_r.at[q], (rq(k), c)).wait_send()

    @pl.when(q != g)
    def _():
        rcopy(hid, colbuf.at[q], a_s, a_r.at[q], (g, c)).wait_send()

    for i in range(nb):
        @pl.when(sends_up)
        def _(i=i):
            up_chain(i).wait_send()

        @pl.when(sends_down)
        def _(i=i):
            down_chain(i).wait_send()

        for k in range(1, r):
            rcopy(chunk(i, j), chunk(i, j), la_s.at[k, i], la_r.at[j, i], (q, g * r + lane(k))).wait_send()

    def drain(n, carry):
        far_part(n).wait_send()
        near_part(n).wait_send()
        passed_part(n).wait_send()
        h_near(n, 0).wait_send()
        h_near(n, 1).wait_send()
        h_pass(n).wait_send()
        return carry

    lax.fori_loop(0, nch, drain, 0)
    for k in range(1, r):
        rcopy(lsend.at[lane(k)], lrecv.at[j], lr_s.at[k], lr_r.at[j], (q, g * r + lane(k))).wait_send()
    for k in range(1, ng):
        t = lax.rem(g + k, ng)
        rcopy(gsend.at[t], grecv.at[g], g_s.at[k], g_r.at[g], (q, t * r + j)).wait_send()
    for i in range(r):
        @pl.when(c != q * r + i)
        def _(i=i):
            rcopy(pp.at[i], prc.at[c], pp_s.at[i], pp_r.at[c], (q, q * r + i)).wait_send()

    @pl.when(g == q)
    def _():
        for k in range(1, nq):
            rcopy(pblk, pblk, pb_s.at[k], pb_r, (rq(k), c)).wait_send()
    for k in range(1, nc):
        rcopy(cpart, crecv.at[c], c_s.at[k], c_r.at[c], (q, rc(k))).wait_send()
        rcopy(st_send, st_recv.at[c], st_s.at[k], st_r.at[c], (q, rc(k))).wait_send()
        rcopy(top_c.at[c], top_c.at[c], tc_s.at[k], tc_r.at[c], (q, rc(k))).wait_send()


def per_device_general(nq, nc, hidden_in, lengths, gate_weight, up_weight, down_weight, code_weight, corpus_codes):
    slots, w = hidden_in.shape
    r = nc // nq
    nreal = nq * slots * REAL_NUM // REAL_DEN
    tq, tb = nreal // nq, nreal // nc
    dq, ffc = gate_weight.shape
    cw = CHUNK if ffc % CHUNK == 0 else ffc
    nch = ffc // cw
    nb = nreal // PIECE if nreal % PIECE == 0 else nq
    nqueries = nq * lengths.shape[0]
    bits = code_weight.shape[1]
    bw = bits // nq
    ng = nc // r
    lens = jnp.broadcast_to(jnp.repeat(lengths, SEQ)[None, :], (8, slots))
    vm, dma = pltpu.VMEM, pltpu.SemaphoreType.DMA
    scratch = [
        vm(gate_weight.shape, BF16), vm(up_weight.shape, BF16), vm(down_weight.shape, BF16),
        vm(code_weight.shape, BF16), vm(corpus_codes.shape, BF16),
        vm((nq, slots, w), BF16), vm((nq, 8, slots), jnp.int32), vm((r, nreal, w), BF16),
        vm((nch, nq, 2, tq, cw), BF16), vm((nch, nq, 2, tq, cw), BF16),
        vm((8, slots), F32), vm((nc, 8, slots), F32), vm((nq, 8, slots), F32), vm((r, nreal, w), BF16),
        vm((nch, 2, tq, cw), F32), vm((nq, nqueries, LANES), F32), vm((nc, nqueries, LANES), F32),
        vm((nch, nq, tq, cw), BF16), vm((nreal, dq), F32),
        vm((r, ng, tb, dq), BF16), vm((r, ng, tb, dq), BF16), vm((ng, tb, dq), BF16), vm((ng, tb, dq), BF16),
        vm((tb, 128), F32), vm((nq, tb, 128), F32),
        vm((r, nqueries, w), F32), vm((nc, nqueries, w), F32), vm((nqueries, w), BF16),
        vm((nqueries, bw), F32), vm((nc, nqueries, bw), F32), vm((nq, nqueries, bw), BF16),
        dma((5,)), dma, dma((nq,)), dma((nq,)), dma((nq,)), dma((2, nb)), dma((nb,)), dma((r, nb)), dma((r, nb)),
        dma((nch, nq)), dma((nch, nq)), dma((nc,)), dma((nc,)), dma((nq,)), dma((nq,)),
        dma((nq,)), dma((nq,)), dma((nc,)), dma((nc,)), dma((nch, nq)), dma((nch, nq)),
        dma((r,)), dma((r,)), dma((ng,)), dma((ng,)), dma((nq,)), dma((nq,)),
        dma((r,)), dma((nc,)), dma((nq,)), dma, dma((nc,)), dma((nc,)), dma((nq,)), dma((nq,)),
    ]
    dims = (nq, nc, r, nreal, tq, tb, nch, cw, w * nc)
    vspec, aspec = pl.BlockSpec(memory_space=pltpu.VMEM), pl.BlockSpec(memory_space=pl.ANY)
    return pl.pallas_call(
        functools.partial(general_kernel, dims),
        out_shape=jax.ShapeDtypeStruct((nqueries, TOPK), F32),
        in_specs=[vspec, vspec] + [aspec] * 5,
        out_specs=vspec,
        scratch_shapes=scratch,
        compiler_params=pltpu.CompilerParams(
            collective_id=0, has_side_effects=True, vmem_limit_bytes=60 * 1024 * 1024),
    )(hidden_in, lens, gate_weight, up_weight, down_weight, code_weight, corpus_codes)


def fast_kernel(dims, names, hid, lens, gate_h, up_h, down_h, code_h, corp_h, out, *refs):
    nq, nc, r, nblk, bm, pr, nh, hw, d_all = dims
    s = types.SimpleNamespace(**dict(zip(names, refs)))
    q = lax.axis_index("query")
    c = lax.axis_index("corpus")
    g = c // r
    j = lax.rem(c, r)
    ng = nc // r
    slots, w = hid.shape
    total = nq * slots
    nqueries = total // SEQ
    nreal = nblk * bm
    qm, lm, pm = bm // nq, bm // r, bm // nc
    nu = nblk * nh
    bw = s.codew.shape[2] // nq
    gate, up, code, corp = s.gu.at[0], s.gu.at[1], s.codew.at[0], s.codew.at[1]

    first = pltpu.make_async_copy(hid, s.colbuf.at[q], s.w_s.at[0])
    first.start()
    counts = pltpu.make_async_copy(lens, s.lens_s, s.w_s.at[1])
    counts.start()
    for a, b, k in ((gate_h, gate, 2), (up_h, up, 2), (down_h, s.down, 3), (code_h, code, 4), (corp_h, corp, 4)):
        pltpu.make_async_copy(a, b, s.w_s.at[k]).start()

    def loaded(ref, k):
        pltpu.make_async_copy(ref, ref, s.w_s.at[k]).wait()

    def rq(k):
        return lax.rem(q + k, nq)

    def rc(k):
        return lax.rem(c + k, nc)

    def lane(k):
        return lax.rem(j + k, r)

    def got(ref, sem):
        rcopy(ref, ref, sem, sem, (rq(1), c)).wait_recv()

    def sent(ref, sem):
        rcopy(ref, ref, sem, sem, (rq(1), c)).wait_send()

    def to_query(src, ref, ss, rs):
        for k in range(1, nq):
            rcopy(src, ref.at[q], ss, rs, (rq(k), c)).start()

    def to_corpus(src, ref, ss, rs):
        for k in range(1, nc):
            rcopy(src, ref.at[c], ss, rs, (q, rc(k))).start()

    barrier = pltpu.get_barrier_semaphore()
    for k in range(1, nq):
        pl.semaphore_signal(barrier, inc=1, device_id=(rq(k), c), device_id_type=pl.DeviceIdType.MESH)
    for k in range(1, nc):
        pl.semaphore_signal(barrier, inc=1, device_id=(q, rc(k)), device_id_type=pl.DeviceIdType.MESH)

    first.wait()
    squares = jnp.square(s.colbuf[q].astype(F32))
    s.st_send[...] = lax.dot_general(jnp.ones((8, w), F32), squares, (((1,), (1,)), ((), ())),
                                     precision=lax.Precision.HIGHEST, preferred_element_type=F32)
    counts.wait()
    slot_query = lax.broadcasted_iota(jnp.int32, (8, slots), 1) // SEQ
    own_lens = jnp.zeros((8, slots), jnp.int32)
    for k in range(slots // SEQ):
        own_lens = jnp.where(slot_query == k, s.lens_s[k], own_lens)
    s.lens_all[q] = own_lens

    pl.semaphore_wait(barrier, nq - 1 + nc - 1)

    side_a = q + 1 - 2 * lax.rem(q, 2)
    side_b = q + 2 - 4 * (q // 2)
    far = nq - 1 - q
    opposite = nq - 1 - g
    helper = g + 1 - 2 * lax.rem(g, 2)
    upper, lower = pl.ds(0, slots // 2), pl.ds(slots // 2, slots // 2)

    @pl.when(jnp.logical_and(q != g, q != opposite))
    def _():
        rcopy(s.colbuf.at[q], s.colbuf.at[q], s.a_s, s.a_r, (g, c)).start()

    @pl.when(q == opposite)
    def _():
        rcopy(s.colbuf.at[q, lower], s.colbuf.at[q, lower], s.a_s, s.ah_r, (helper, c)).start()
        rcopy(s.colbuf.at[q, upper], s.colbuf.at[q, upper], s.a_s, s.a_r, (g, c)).start()

    to_query(s.lens_all.at[q], s.lens_all, s.l_s, s.l_r)
    to_corpus(s.st_send, s.st_recv, s.st_s, s.st_r)
    s.st_recv[c] = s.st_send[...]
    got(s.lens_all.at[pl.ds(0, nq - 1)], s.l_r)
    lens_row = jnp.concatenate([s.lens_all[i] for i in range(nq)], axis=1)
    slot = lax.broadcasted_iota(jnp.int32, (8, total), 1)
    valid = lax.rem(slot, SEQ) < lens_row
    before = lax.broadcasted_iota(jnp.int32, (total, total), 0) < lax.broadcasted_iota(jnp.int32, (total, total), 1)
    pos = mm(valid.astype(F32).astype(BF16), before.astype(F32).astype(BF16)).astype(jnp.int32)
    pos = jnp.where(valid, pos, -1)[:1]

    @pl.when(q == helper)
    def _():
        got(s.colbuf.at[0, lower], s.ah_r)
        rcopy(s.colbuf.at[opposite, lower], s.colbuf.at[opposite, lower], s.ah_s, s.a_r, (g, c)).start()

    got(s.st_recv.at[pl.ds(0, nc - 1)], s.st_r)
    stat = s.st_recv[0]
    for i in range(1, nc):
        stat = stat + s.st_recv[i]
    s.inv_all[q] = lax.rsqrt(stat / d_all + epsilon)
    to_query(s.inv_all.at[q], s.inv_all, s.iv_s, s.iv_r)

    def piece(b, p):
        return s.xall.at[j, b, pl.ds(p * pr, pr)]

    def down_chain(b, p):
        return rcopy(piece(b, p), piece(b, p), s.ch_s.at[0], s.ch_r.at[b, p], (q, jnp.maximum(c - r, 0)))

    def up_chain(b, p):
        return rcopy(piece(b, p), piece(b, p), s.ch_s.at[1], s.ch_r.at[b, p], (q, jnp.minimum(c + r, nc - 1)))

    def side(b, p, k):
        return rcopy(piece(b, p), piece(b, p), s.la_s, s.la_r.at[b], (q, g * r + lane(k)))

    sends_up = jnp.logical_and(g >= q, g < ng - 1)
    sends_down = jnp.logical_and(g <= q, g > 0)

    def pass_on(b, p):
        @pl.when(sends_up)
        def _():
            up_chain(b, p).start()

        @pl.when(sends_down)
        def _():
            down_chain(b, p).start()

        for k in range(1, r):
            side(b, p, k).start()

    @pl.when(q == g)
    def _():
        got(s.colbuf.at[pl.ds(0, nq - 1)], s.a_r)
        stacked = s.colbuf[...].reshape(total, w)
        for b in range(nblk):
            row = lax.broadcasted_iota(jnp.int32, (bm, total), 0) + b * bm
            pick = (pos == row).astype(F32).astype(BF16)
            s.xall[j, b] = mm(pick, stacked).astype(BF16)
            for p in range(bm // pr):
                pass_on(b, p)

    got(s.inv_all.at[pl.ds(0, nq - 1)], s.iv_r)
    inv_row = jnp.concatenate([s.inv_all[i] for i in range(nq)], axis=1)[:1]
    for b in range(nblk):
        row = lax.broadcasted_iota(jnp.int32, (bm, total), 0) + b * bm
        col = jnp.sum(jnp.where(pos == row, inv_row, 0.0), axis=1, keepdims=True)
        s.inv_c[b] = jnp.broadcast_to(col, (bm, LANES))

    loaded(s.gu, 2)

    def sides(n):
        odd = lax.rem(n, 2)
        return side_a + (side_b - side_a) * odd, side_b + (side_a - side_b) * odd

    def near_part(n):
        one, _ = sides(n)
        return rcopy(s.psend.at[n, one], s.precv.at[n, 0], s.p_s, s.p_r.at[n], (one, c))

    def far_part(n):
        one, _ = sides(n)
        return rcopy(s.psend.at[n, far], s.precv.at[n, 2], s.p_s, s.pf_r.at[n], (one, c))

    def passed_part(n):
        _, two = sides(n)
        return rcopy(s.precv.at[n, 3], s.precv.at[n, 1], s.p_s, s.p_r.at[n], (two, c))

    def h_near(n, k, sem):
        return rcopy(s.hall.at[n, q], s.hall.at[n, q], s.h_s, sem, (sides(n)[k], c))

    def h_pass(n, sem):
        one, two = sides(n)
        return rcopy(s.hall.at[n, one], s.hall.at[n, one], s.h_s, sem, (two, c))

    def products(b):
        @pl.when(q != g)
        def _():
            for p in range(bm // pr):
                up_chain(b, p).wait_recv()
                pass_on(b, p)

        got(s.xall.at[pl.ds(0, r - 1), b], s.la_r.at[b])
        scale = s.inv_c[b][:, :1]
        for i in range(r):
            s.xn[:, i * w:(i + 1) * w] = (s.xall[i, b].astype(F32) * scale).astype(BF16)
        xb = s.xn[...]
        for h in range(nh):
            n = b * nh + h
            for e, wref in enumerate((gate, up)):
                full = mm(xb, wref[:, h * hw:(h + 1) * hw])
                s.full[h, e] = full
                for i in range(nq):
                    s.psend[n, i, e] = full[i * qm:(i + 1) * qm].astype(BF16)
            far_part(n).start()
            near_part(n).start()
            for e in range(2):
                s.pown[n, e] = s.full[h, e, pl.ds(pl.multiple_of(q * qm, qm), qm)]

    def pass_unit(n):
        _, two = sides(n)
        got(s.precv.at[n, 2], s.pf_r.at[n])
        s.precv[n, 3] = (s.psend[n, two].astype(F32) + s.precv[n, 2].astype(F32)).astype(BF16)
        passed_part(n).start()

    def reduce_unit(n):
        got(s.precv.at[n, pl.ds(0, 2)], s.p_r.at[n])
        gsum = s.pown[n, 0] + s.precv[n, 0, 0].astype(F32) + s.precv[n, 1, 0].astype(F32)
        usum = s.pown[n, 1] + s.precv[n, 0, 1].astype(F32) + s.precv[n, 1, 1].astype(F32)
        s.hall[n, q] = (gsum / (1.0 + jnp.exp(-gsum)) * usum).astype(BF16)
        h_near(n, 0, s.hn_r.at[n]).start()
        h_near(n, 1, s.hb_r.at[n // nh]).start()

    def relay_unit(n):
        got(s.hall.at[n, 0], s.hn_r.at[n])
        h_pass(n, s.hb_r.at[n // nh]).start()

    def lane_send(b, k):
        t = lane(k)
        return rcopy(s.lsend.at[b, t], s.lrecv.at[b, j], s.lr_s, s.lr_r.at[b], (q, g * r + t))

    def group_send(b, k):
        t = lax.rem(g + k, ng)
        return rcopy(s.gsend.at[b, t], s.grecv.at[b, g], s.g_s, s.g_r.at[b], (q, t * r + j))

    def down_block(b):
        part = None
        got(s.hall.at[pl.ds(b * nh, nh), pl.ds(0, 2)], s.hb_r.at[b])
        for h in range(nh):
            n = b * nh + h
            term = mm(s.hall[n].reshape(bm, hw), s.down[h * hw:(h + 1) * hw, :])
            part = term if part is None else part + term
        for t in range(r):
            s.lsend[b, t] = part[t * lm:(t + 1) * lm].astype(BF16)
        for k in range(1, r):
            lane_send(b, k).start()

    def sum_block(b):
        mine = s.lsend[b, j].astype(F32)
        got(s.lrecv.at[b, pl.ds(0, r - 1)], s.lr_r.at[b])
        for k in range(1, r):
            mine = mine + s.lrecv[b, lane(k)].astype(F32)
        for t in range(ng):
            s.gsend[b, t] = mine[t * pm:(t + 1) * pm].astype(BF16)
        for k in range(1, ng):
            group_send(b, k).start()

    def units(unit, b):
        for h in range(nh):
            unit(b * nh + h)

    stages = (products, functools.partial(units, pass_unit), functools.partial(units, reduce_unit),
              functools.partial(units, relay_unit), down_block, sum_block)
    delays = (0,1,3,4,6,7)

    def turn(t, carry):
        for stage, delay in zip(stages, delays):
            @pl.when(jnp.logical_and(t >= delay, t < nblk + delay))
            def _(stage=stage, delay=delay):
                stage(t - delay)
        return carry

    loaded(s.down, 3)
    lax.fori_loop(0, nblk + delays[-1], turn, 0)
    row = lax.broadcasted_iota(jnp.int32, (nblk * pm, nreal), 0)
    row = (row // pm) * bm + (j * ng + g) * pm + lax.rem(row, pm)
    own_rows = (lax.broadcasted_iota(jnp.int32, (nblk * pm, nreal), 1) == row).astype(F32).astype(BF16)
    for i in range(r):
        s.res[:, i * w:(i + 1) * w] = mm(own_rows, s.xall[i].reshape(nreal, w))

    for b in range(nblk):
        total_b = s.gsend[b, g].astype(F32)
        got(s.grecv.at[b, pl.ds(0, ng - 1)], s.g_r.at[b])
        for k in range(1, ng):
            total_b = total_b + s.grecv[b, lax.rem(g + k, ng)].astype(F32)
        s.res[b * pm:(b + 1) * pm, :] = s.res[b * pm:(b + 1) * pm, :] + total_b
    residual = s.res[...]
    tb = nblk * pm

    s.t_send[...] = jnp.broadcast_to(jnp.sum(residual * residual, axis=1, keepdims=True), (tb, LANES))
    to_query(s.t_send, s.t_recv, s.t_s, s.t_r)
    qrow = lax.broadcasted_iota(jnp.int32, (nqueries, total), 0)
    qslot = lax.broadcasted_iota(jnp.int32, (nqueries, total), 1)
    lens_b = jnp.broadcast_to(lens_row[:1], (nqueries, total)).astype(F32)
    vals_b = jnp.broadcast_to(valid.astype(F32)[:1], (nqueries, total))
    len_col = jnp.sum(jnp.where(qslot == qrow * SEQ, lens_b, 0.0), axis=1, keepdims=True)
    off_col = jnp.sum(jnp.where(qslot < qrow * SEQ, vals_b, 0.0), axis=1, keepdims=True)
    prow = lax.broadcasted_iota(jnp.int32, (nqueries, tb), 1)
    prow = ((prow // pm) * bm + (j * ng + g) * pm + lax.rem(prow, pm)).astype(F32)
    member = jnp.where(jnp.logical_and(prow >= off_col, prow < off_col + len_col), 1.0, 0.0)
    tsum = s.t_send[...]
    got(s.t_recv.at[pl.ds(0, nq - 1)], s.t_r)
    for k in range(1, nq):
        tsum = tsum + s.t_recv[rq(k)]
    final = residual * lax.rsqrt(tsum[:, :1] / d_all + epsilon)
    pooled_part = mm(member, final, lax.Precision.HIGHEST)
    for i in range(r):
        s.pp[i] = pooled_part[:, i * w:(i + 1) * w].astype(BF16)
    for i in range(r):
        @pl.when(c != q * r + i)
        def _(i=i):
            rcopy(s.pp.at[i], s.prc.at[c], s.pp_s, s.pp_r, (q, q * r + i)).start()

    @pl.when(g == q)
    def _():
        pooled = s.pp[j].astype(F32)
        got(s.prc.at[pl.ds(0, nc - 1)], s.pp_r)
        for k in range(1, nc):
            pooled = pooled + s.prc[rc(k)].astype(F32)
        s.pblk[0] = (pooled / len_col).astype(BF16)
        for k in range(1, nq):
            rcopy(s.pblk.at[0], s.pblk.at[0], s.pb_s, s.pb_r, (rq(k), c)).start()

    loaded(s.codew, 4)

    @pl.when(g != q)
    def _():
        got(s.pblk.at[0], s.pb_r)

    s.cpart[...] = mm(s.pblk[0], code[:, pl.ds(pl.multiple_of(q * bw, bw), bw)]).astype(BF16)
    to_corpus(s.cpart, s.crecv, s.c_s, s.c_r)
    s.crecv[c] = s.cpart[...]
    got(s.crecv.at[pl.ds(0, nc - 1)], s.c_r)
    csum = s.crecv[0].astype(F32)
    for i in range(1, nc):
        csum = csum + s.crecv[i].astype(F32)
    s.codes[q] = csum.astype(BF16)
    to_query(s.codes.at[q], s.codes, s.o_s, s.o_r)
    got(s.codes.at[pl.ds(0, nq - 1)], s.o_r)
    qcodes = jnp.concatenate([s.codes[i] for i in range(nq)], axis=1)
    scale = 1.0 / math.sqrt(corp.shape[1])
    scores = lax.dot_general(qcodes, corp[...], (((1,), (1,)), ((), ())), preferred_element_type=F32) * scale

    blocks = corp.shape[0] // LANES
    lists = jnp.concatenate([scores[:, i * LANES:(i + 1) * LANES] for i in range(blocks)], axis=0)
    best = merge_all(sort_lanes(lists), nqueries, q >= nq // 2)
    s.top_q[q] = best
    to_query(s.top_q.at[q], s.top_q, s.tq_s, s.tq_r)
    got(s.top_q.at[pl.ds(0, nq - 1)], s.tq_r)
    best = merge_all(s.top_q[...].reshape(nq * nqueries, LANES), nqueries, c >= nc // 2)
    s.top_c[c] = best
    to_corpus(s.top_c.at[c], s.top_c, s.tc_s, s.tc_r)
    got(s.top_c.at[pl.ds(0, nc - 1)], s.tc_r)
    best = merge_all(s.top_c[...].reshape(nc * nqueries, LANES), nqueries, False)
    out[...] = best[:, :TOPK]

    sent(s.lens_all.at[pl.ds(0, nq - 1)], s.l_s)
    sent(s.st_recv.at[pl.ds(0, nc - 1)], s.st_s)
    sent(s.inv_all.at[pl.ds(0, nq - 1)], s.iv_s)

    @pl.when(q != g)
    def _():
        sent(s.colbuf.at[0], s.a_s)

    @pl.when(q == helper)
    def _():
        sent(s.colbuf.at[0, lower], s.ah_s)

    @pl.when(sends_down)
    def _():
        sent(s.xall.at[0], s.ch_s.at[0])

    @pl.when(sends_up)
    def _():
        sent(s.xall.at[0], s.ch_s.at[1])

    sent(s.xall.at[pl.ds(0, r - 1)], s.la_s)
    sent(s.psend.at[:, pl.ds(0, 3)], s.p_s)
    sent(s.hall.at[:, pl.ds(0, 3)], s.h_s)
    sent(s.lsend.at[:, pl.ds(0, r - 1)], s.lr_s)
    sent(s.gsend.at[:, pl.ds(0, ng - 1)], s.g_s)
    sent(s.t_recv.at[pl.ds(0, nq - 1)], s.t_s)

    @pl.when(g == q)
    def _():
        sent(s.pp.at[pl.ds(0, r - 1)], s.pp_s)
        sent(s.pblk.at[pl.ds(0, nq - 1)], s.pb_s)

    @pl.when(g != q)
    def _():
        sent(s.pp, s.pp_s)

    sent(s.crecv.at[pl.ds(0, nc - 1)], s.c_s)
    sent(s.codes.at[pl.ds(0, nq - 1)], s.o_s)
    sent(s.top_q.at[pl.ds(0, nq - 1)], s.tq_s)
    sent(s.top_c.at[pl.ds(0, nc - 1)], s.tc_s)


def halves_of(ffc):
    return 2 if ffc % (2 * LANES) == 0 else 1


def per_device_fast(nq, nc, hidden_in, lengths, gate_weight, up_weight, down_weight, code_weight, corpus_codes):
    slots, w = hidden_in.shape
    r = nc // nq
    ng = nc // r
    nreal = nq * slots * REAL_NUM // REAL_DEN
    dq, ffc = gate_weight.shape
    bm = 8 * nc
    nblk = nreal // bm
    pr = PIECE if bm % PIECE == 0 else bm
    nh = halves_of(ffc)
    hw = ffc // nh
    nu = nblk * nh
    qm, lm, pm = bm // nq, bm // r, bm // nc
    tb = nblk * pm
    nqueries = nq * lengths.shape[0]
    bits = code_weight.shape[1]
    bw = bits // nq
    vm, dma = pltpu.VMEM, pltpu.SemaphoreType.DMA
    scratch = dict(
        gu=vm((2,) + gate_weight.shape, BF16), down=vm(down_weight.shape, BF16), codew=vm((2,) + code_weight.shape, BF16),
        lens_s=pltpu.SMEM(lengths.shape, jnp.int32),
        colbuf=vm((nq, slots, w), BF16), lens_all=vm((nq, 8, slots), jnp.int32), xall=vm((r, nblk, bm, w), BF16),
        xn=vm((bm, dq), BF16), inv_c=vm((nblk, bm, LANES), F32),
        st_send=vm((8, slots), F32), st_recv=vm((nc, 8, slots), F32), inv_all=vm((nq, 8, slots), F32),
        psend=vm((nu, nq, 2, qm, hw), BF16), precv=vm((nu, 4, 2, qm, hw), BF16), pown=vm((nu, 2, qm, hw), F32), full=vm((nh, 2, bm, hw), F32),
        hall=vm((nu, nq, qm, hw), BF16),
        lsend=vm((nblk, r, lm, dq), BF16), lrecv=vm((nblk, r, lm, dq), BF16),
        gsend=vm((nblk, ng, pm, dq), BF16), grecv=vm((nblk, ng, pm, dq), BF16), res=vm((tb, dq), F32),
        t_send=vm((tb, LANES), F32), t_recv=vm((nq, tb, LANES), F32),
        pp=vm((r, nqueries, w), BF16), prc=vm((nc, nqueries, w), BF16), pblk=vm((nq, nqueries, w), BF16),
        cpart=vm((nqueries, bw), BF16), crecv=vm((nc, nqueries, bw), BF16), codes=vm((nq, nqueries, bw), BF16),
        top_q=vm((nq, nqueries, LANES), F32), top_c=vm((nc, nqueries, LANES), F32),
        w_s=dma((5,)), l_s=dma, l_r=dma, a_s=dma, a_r=dma, ah_s=dma, ah_r=dma, st_s=dma, st_r=dma, iv_s=dma, iv_r=dma,
        ch_s=dma((2,)), ch_r=dma((nblk, bm // pr)), la_s=dma, la_r=dma((nblk,)),
        p_s=dma, p_r=dma((nu,)), pf_r=dma((nu,)), h_s=dma, hn_r=dma((nu,)), hb_r=dma((nblk,)),
        lr_s=dma, lr_r=dma((nblk,)), g_s=dma, g_r=dma((nblk,)),
        t_s=dma, t_r=dma, pp_s=dma, pp_r=dma, pb_s=dma, pb_r=dma, c_s=dma, c_r=dma, o_s=dma, o_r=dma,
        tq_s=dma, tq_r=dma, tc_s=dma, tc_r=dma,
    )
    dims = (nq, nc, r, nblk, bm, pr, nh, hw, w * nc)
    vspec, aspec = pl.BlockSpec(memory_space=pltpu.VMEM), pl.BlockSpec(memory_space=pl.ANY)
    return pl.pallas_call(
        functools.partial(fast_kernel, dims, tuple(scratch)),
        out_shape=jax.ShapeDtypeStruct((nqueries, TOPK), F32),
        in_specs=[aspec] * 7,
        out_specs=vspec,
        scratch_shapes=list(scratch.values()),
        compiler_params=pltpu.CompilerParams(
            collective_id=0, has_side_effects=True, vmem_limit_bytes=60 * 1024 * 1024),
    )(hidden_in, lengths, gate_weight, up_weight, down_weight, code_weight, corpus_codes)


def per_device(nq, nc, hidden_in, *rest):
    slots, w = hidden_in.shape
    nreal = nq * slots * REAL_NUM // REAL_DEN
    fits = nreal % (8 * nc) == 0 and w % LANES == 0 and rest[4].shape == rest[5].shape
    body = per_device_fast if fits else per_device_general
    return body(nq, nc, hidden_in, *rest)


def solution(mesh):
    in_specs = (
        P("query", "corpus"),
        P("query"),
        P("query", "corpus"),
        P("query", "corpus"),
        P("corpus", "query"),
        P("corpus", None),
        P(("query", "corpus"), None),
    )
    body = functools.partial(per_device, mesh.shape["query"], mesh.shape["corpus"])
    return jax.shard_map(body, mesh=mesh, in_specs=in_specs, out_specs=P(), check_vma=False)
```

```python
import functools
import math
import types

import jax
import jax.numpy as jnp
from jax import lax
from jax.experimental import pallas as pl
from jax.experimental.pallas import tpu as pltpu
from jax.sharding import PartitionSpec as P

SEQ = 32
LANES = 128
TOPK = 100
REAL_NUM, REAL_DEN = 5, 8
CHUNK = 256
PIECE = 32

epsilon = 1e-05
F32, BF16 = jnp.float32, jnp.bfloat16


def mm(a, b, precision=None):
    return lax.dot_general(a, b, (((1,), (0,)), ((), ())), precision=precision, preferred_element_type=F32)


def rcopy(src, dst, send, recv, dev):
    return pltpu.make_async_remote_copy(
        src_ref=src, dst_ref=dst, send_sem=send, recv_sem=recv,
        device_id=dev, device_id_type=pl.DeviceIdType.MESH)


def exchange(x, s, keep_max):
    bit = (lax.broadcasted_iota(jnp.int32, x.shape, 1) & s) != 0
    other = jnp.where(bit, pltpu.roll(x, s, 1), pltpu.roll(x, LANES - s, 1))
    return jnp.where(keep_max, jnp.maximum(x, other), jnp.minimum(x, other))


def sort_lanes(x):
    lane = lax.broadcasted_iota(jnp.int32, x.shape, 1)
    flip = (lax.broadcasted_iota(jnp.int32, x.shape, 0) >= x.shape[0] // 2).astype(jnp.int32)
    size = 2
    while size <= LANES:
        up = ((lane & size) != 0).astype(jnp.int32) if size < LANES else jnp.zeros_like(lane)
        s = size // 2
        while s:
            low = ((lane & s) != 0).astype(jnp.int32)
            x = exchange(x, s, (low ^ up ^ flip) == 0)
            s //= 2
        size *= 2
    return x


def merge_all(x, rows, lone):
    while x.shape[0] > rows:
        half = x.shape[0] // 2
        x = jnp.maximum(x[:half], x[half:])
        lane = lax.broadcasted_iota(jnp.int32, x.shape, 1)
        if half > rows:
            flip = (lax.broadcasted_iota(jnp.int32, x.shape, 0) >= half // 2).astype(jnp.int32)
        else:
            flip = jnp.zeros_like(lane) + jnp.asarray(lone, jnp.int32)
        s = LANES // 2
        while s:
            low = ((lane & s) != 0).astype(jnp.int32)
            x = exchange(x, s, (low ^ flip) == 0)
            s //= 2
    return x


def general_kernel(dims, hid, lens, gate_h, up_h, down_h, code_h, corp_h, out,
                 gate, up, down, code, corp, colbuf, lens_all, xall, psend, precv,
                 st_send, st_recv, inv_all, xn, pown, top_q, top_c, hall, acc, lsend, lrecv, gsend, grecv, t_send, t_recv,
                 pp, prc, pblk, cpart, crecv, codes,
                 w_s, a_s, a_r, l_s, l_r, ch_s, ch_r, la_s, la_r, p_s, p_r, st_s, st_r, iv_s, iv_r, tq_s, tq_r, tc_s, tc_r, h_s, h_r,
                 lr_s, lr_r, g_s, g_r, t_s, t_r, pp_s, pp_r, pb_s, pb_r, c_s, c_r, o_s, o_r):
    nq, nc, r, nreal, tq, tb, nch, cw, d_all = dims
    q = lax.axis_index("query")
    c = lax.axis_index("corpus")
    g = c // r
    j = lax.rem(c, r)
    slots, w = hid.shape[0], hid.shape[1]
    total = nq * slots
    nqueries = total // SEQ
    bw = code.shape[1] // nq

    loads = []
    for i, (s, d) in enumerate(((gate_h, gate), (up_h, up), (down_h, down), (code_h, code), (corp_h, corp))):
        cp = pltpu.make_async_copy(s, d, w_s.at[i])
        cp.start()
        loads.append(cp)

    def rq(k):
        return lax.rem(q + k, nq)

    def rc(k):
        return lax.rem(c + k, nc)

    def lane(k):
        return lax.rem(j + k, r)

    barrier = pltpu.get_barrier_semaphore()
    for k in range(1, nq):
        pl.semaphore_signal(barrier, inc=1, device_id=(rq(k), c), device_id_type=pl.DeviceIdType.MESH)
    for k in range(1, nc):
        pl.semaphore_signal(barrier, inc=1, device_id=(q, rc(k)), device_id_type=pl.DeviceIdType.MESH)
    pl.semaphore_wait(barrier, nq - 1 + nc - 1)

    for k in range(1, nq):
        rcopy(lens, lens_all.at[q], l_s.at[k], l_r.at[q], (rq(k), c)).start()

    @pl.when(q != g)
    def _():
        rcopy(hid, colbuf.at[q], a_s, a_r.at[q], (g, c)).start()

    squares = jnp.square(hid[...].astype(F32))
    st_send[...] = lax.dot_general(jnp.ones((8, w), F32), squares, (((1,), (1,)), ((), ())),
                                   precision=lax.Precision.HIGHEST, preferred_element_type=F32)
    for k in range(1, nc):
        rcopy(st_send, st_recv.at[c], st_s.at[k], st_r.at[c], (q, rc(k))).start()
    st_recv[c] = st_send[...]
    lens_all[q] = lens[...]
    for k in range(1, nq):
        s = rq(k)
        rcopy(lens, lens_all.at[s], l_s.at[k], l_r.at[s], (s, c)).wait_recv()
    lens_row = jnp.concatenate([lens_all[i] for i in range(nq)], axis=1)
    slot = lax.broadcasted_iota(jnp.int32, (8, total), 1)
    valid = lax.rem(slot, SEQ) < lens_row
    before = lax.broadcasted_iota(jnp.int32, (total, total), 0) < lax.broadcasted_iota(jnp.int32, (total, total), 1)
    pos = mm(valid.astype(F32).astype(BF16), before.astype(F32).astype(BF16)).astype(jnp.int32)
    pos = jnp.where(valid, pos, -1)[:1]

    for k in range(1, nc):
        s = rc(k)
        rcopy(st_send, st_recv.at[s], st_s.at[k], st_r.at[s], (q, s)).wait_recv()
    stat = st_recv[0]
    for i in range(1, nc):
        stat = stat + st_recv[i]
    inv_all[q] = lax.rsqrt(stat / d_all + epsilon)
    for k in range(1, nq):
        rcopy(inv_all.at[q], inv_all.at[q], iv_s.at[k], iv_r.at[q], (rq(k), c)).start()

    nb = ch_r.shape[0]
    ct = nreal // nb

    def chunk(i, slot_j):
        return xall.at[slot_j, pl.ds(i * ct, ct)]

    def down_chain(i):
        return rcopy(chunk(i, j), chunk(i, j), ch_s.at[0, i], ch_r.at[i], (q, jnp.maximum(c - r, 0)))

    def up_chain(i):
        return rcopy(chunk(i, j), chunk(i, j), ch_s.at[1, i], ch_r.at[i], (q, jnp.minimum(c + r, nc - 1)))

    sends_up = jnp.logical_and(g >= q, g < nc // r - 1)
    sends_down = jnp.logical_and(g <= q, g > 0)

    @pl.when(q == g)
    def _():
        colbuf[q] = hid[...]
        for k in range(1, nq):
            s = rq(k)
            rcopy(hid, colbuf.at[s], a_s, a_r.at[s], (s, c)).wait_recv()
        stacked = colbuf[...].reshape(total, w)
        for i in range(nq):
            row = lax.broadcasted_iota(jnp.int32, (tq, total), 0) + i * tq
            pick = (pos == row).astype(F32).astype(BF16)
            xall[j, i * tq:(i + 1) * tq, :] = mm(pick, stacked).astype(BF16)

    for i in range(nb):
        @pl.when(q != g)
        def _(i=i):
            up_chain(i).wait_recv()

        @pl.when(sends_up)
        def _(i=i):
            up_chain(i).start()

        @pl.when(sends_down)
        def _(i=i):
            down_chain(i).start()

        for k in range(1, r):
            rcopy(chunk(i, j), chunk(i, j), la_s.at[k, i], la_r.at[j, i], (q, g * r + lane(k))).start()
    for k in range(1, nq):
        s = rq(k)
        rcopy(inv_all.at[s], inv_all.at[s], iv_s.at[k], iv_r.at[s], (s, c)).wait_recv()
    inv_row = jnp.concatenate([inv_all[i] for i in range(nq)], axis=1)[:1]
    inv_cols = []
    for i in range(nq):
        row = lax.broadcasted_iota(jnp.int32, (tq, total), 0) + i * tq
        inv_cols.append(jnp.sum(jnp.where(pos == row, inv_row, 0.0), axis=1, keepdims=True))
    inv = jnp.concatenate(inv_cols, axis=0)
    for i in range(nb):
        for k in range(1, r):
            s = lane(k)
            rcopy(chunk(i, s), chunk(i, s), la_s.at[k, i], la_r.at[s, i], (q, g * r + s)).wait_recv()

    loads[0].wait()
    loads[1].wait()

    for i in range(r):
        xn[i] = (xall[i].astype(F32) * inv).astype(BF16)

    side_a = q + 1 - 2 * lax.rem(q, 2)
    side_b = q + 2 - 4 * (q // 2)
    far = nq - 1 - q

    def sides(n):
        odd = lax.rem(n, 2)
        return side_a + (side_b - side_a) * odd, side_b + (side_a - side_b) * odd

    def near_part(n):
        one, _ = sides(n)
        return rcopy(psend.at[n, one], precv.at[n, 0], p_s.at[n, 0], p_r.at[n, 0], (one, c))

    def far_part(n):
        one, _ = sides(n)
        return rcopy(psend.at[n, far], precv.at[n, 1], p_s.at[n, 1], p_r.at[n, 1], (one, c))

    def passed_part(n):
        _, two = sides(n)
        return rcopy(precv.at[n, 3], precv.at[n, 2], p_s.at[n, 2], p_r.at[n, 2], (two, c))

    def h_near(n, k):
        to = sides(n)[k]
        return rcopy(hall.at[n, q], hall.at[n, q], h_s.at[n, k], h_r.at[n, k], (to, c))

    def h_near_in(n, k):
        to = sides(n)[k]
        return rcopy(hall.at[n, to], hall.at[n, to], h_s.at[n, k], h_r.at[n, k], (to, c))

    def h_pass(n):
        one, two = sides(n)
        return rcopy(hall.at[n, one], hall.at[n, one], h_s.at[n, 2], h_r.at[n, 2], (two, c))

    def h_pass_in(n):
        _, two = sides(n)
        return rcopy(hall.at[n, far], hall.at[n, far], h_s.at[n, 2], h_r.at[n, 2], (two, c))

    def matmuls(n, carry):
        cols = pl.ds(pl.multiple_of(n * cw, cw), cw)
        for e, wref in enumerate((gate, up)):
            full = sum(mm(xn[i], wref[i * w:(i + 1) * w, cols]) for i in range(r))
            for i in range(nq):
                psend[n, i, e] = full[i * tq:(i + 1) * tq].astype(BF16)

                @pl.when(q == i)
                def _(i=i, e=e, full=full):
                    pown[n, e] = full[i * tq:(i + 1) * tq]
        far_part(n).start()
        near_part(n).start()
        return carry

    lax.fori_loop(0, nch, matmuls, 0)

    loads[2].wait()
    acc[...] = jnp.zeros_like(acc)

    def pass_chunk(n):
        _, two = sides(n)
        far_part(n).wait_recv()
        precv[n, 3] = (psend[n, two].astype(F32) + precv[n, 1].astype(F32)).astype(BF16)
        passed_part(n).start()

    def reduce_chunk(n):
        near_part(n).wait_recv()
        passed_part(n).wait_recv()
        gsum = pown[n, 0] + precv[n, 0, 0].astype(F32) + precv[n, 2, 0].astype(F32)
        usum = pown[n, 1] + precv[n, 0, 1].astype(F32) + precv[n, 2, 1].astype(F32)
        hall[n, q] = (gsum / (1.0 + jnp.exp(-gsum)) * usum).astype(BF16)
        h_near(n, 0).start()
        h_near(n, 1).start()

    def relay_chunk(n):
        h_near_in(n, 0).wait_recv()
        h_pass(n).start()

    def down_chunk(n):
        h_near_in(n, 1).wait_recv()
        h_pass_in(n).wait_recv()
        acc[...] += mm(hall[n].reshape(nreal, cw), down[pl.ds(pl.multiple_of(n * cw, cw), cw), :])

    def passes(n, carry):
        pass_chunk(n)
        return carry

    lax.fori_loop(0, nch, passes, 0)
    reduce_chunk(0)

    def reduces(n, carry):
        reduce_chunk(n)
        relay_chunk(n - 1)
        return carry

    lax.fori_loop(1, nch, reduces, 0)
    relay_chunk(nch - 1)

    def downs(n, carry):
        down_chunk(n)
        return carry

    lax.fori_loop(0, nch, downs, 0)

    ng = nc // r
    for gg in range(ng):
        for jj in range(r):
            b = gg * r + jj
            lsend[jj, gg] = acc[b * tb:(b + 1) * tb].astype(BF16)
    for k in range(1, r):
        t = lane(k)
        rcopy(lsend.at[t], lrecv.at[j], lr_s.at[k], lr_r.at[j], (q, g * r + t)).start()
    mine = lsend[j].astype(F32)
    for k in range(1, r):
        s = lane(k)
        rcopy(lsend.at[s], lrecv.at[s], lr_s.at[k], lr_r.at[s], (q, g * r + s)).wait_recv()
        mine = mine + lrecv[s].astype(F32)
    gsend[...] = mine.astype(BF16)
    for k in range(1, ng):
        t = lax.rem(g + k, ng)
        rcopy(gsend.at[t], grecv.at[g], g_s.at[k], g_r.at[g], (q, t * r + j)).start()
    row = lax.broadcasted_iota(jnp.int32, (tb, nreal), 0) + c * tb
    own_rows = (lax.broadcasted_iota(jnp.int32, (tb, nreal), 1) == row).astype(F32).astype(BF16)
    residual = jnp.concatenate([mm(own_rows, xall[i]) for i in range(r)], axis=1)
    residual = residual + gsend[g].astype(F32)
    for k in range(1, ng):
        s = lax.rem(g + k, ng)
        rcopy(gsend.at[s], grecv.at[s], g_s.at[k], g_r.at[s], (q, s * r + j)).wait_recv()
        residual = residual + grecv[s].astype(F32)

    t_send[...] = jnp.broadcast_to(jnp.sum(residual * residual, axis=1, keepdims=True), (tb, 128))
    for k in range(1, nq):
        rcopy(t_send, t_recv.at[q], t_s.at[k], t_r.at[q], (rq(k), c)).start()
    qrow = lax.broadcasted_iota(jnp.int32, (nqueries, total), 0)
    qslot = lax.broadcasted_iota(jnp.int32, (nqueries, total), 1)
    lens_b = jnp.broadcast_to(lens_row[:1], (nqueries, total)).astype(F32)
    vals_b = jnp.broadcast_to(valid.astype(F32)[:1], (nqueries, total))
    len_col = jnp.sum(jnp.where(qslot == qrow * SEQ, lens_b, 0.0), axis=1, keepdims=True)
    off_col = jnp.sum(jnp.where(qslot < qrow * SEQ, vals_b, 0.0), axis=1, keepdims=True)
    prow = (lax.broadcasted_iota(jnp.int32, (nqueries, tb), 1) + c * tb).astype(F32)
    member = jnp.where(jnp.logical_and(prow >= off_col, prow < off_col + len_col), 1.0, 0.0)
    tsum = t_send[...]
    for k in range(1, nq):
        s = rq(k)
        rcopy(t_send, t_recv.at[s], t_s.at[k], t_r.at[s], (s, c)).wait_recv()
        tsum = tsum + t_recv[s]
    final = residual * lax.rsqrt(tsum[:, :1] / d_all + epsilon)
    pooled_part = mm(member, final, lax.Precision.HIGHEST)
    for i in range(r):
        pp[i] = pooled_part[:, i * w:(i + 1) * w]
    for i in range(r):
        @pl.when(c != q * r + i)
        def _(i=i):
            rcopy(pp.at[i], prc.at[c], pp_s.at[i], pp_r.at[c], (q, q * r + i)).start()

    @pl.when(g == q)
    def _():
        pooled = pp[j]
        for k in range(1, nc):
            s = rc(k)
            rcopy(pp.at[j], prc.at[s], pp_s.at[0], pp_r.at[s], (q, s)).wait_recv()
            pooled = pooled + prc[s]
        pblk[...] = (pooled / len_col).astype(BF16)
        for k in range(1, nq):
            rcopy(pblk, pblk, pb_s.at[k], pb_r, (rq(k), c)).start()

    loads[3].wait()
    loads[4].wait()

    @pl.when(g != q)
    def _():
        rcopy(pblk, pblk, pb_s.at[0], pb_r, (g, c)).wait_recv()

    cpart[...] = mm(pblk[...], code[:, pl.ds(pl.multiple_of(q * bw, bw), bw)])
    for k in range(1, nc):
        rcopy(cpart, crecv.at[c], c_s.at[k], c_r.at[c], (q, rc(k))).start()
    crecv[c] = cpart[...]
    for k in range(1, nc):
        s = rc(k)
        rcopy(cpart, crecv.at[s], c_s.at[k], c_r.at[s], (q, s)).wait_recv()
    csum = crecv[0]
    for i in range(1, nc):
        csum = csum + crecv[i]
    codes[q] = csum.astype(BF16)
    for k in range(1, nq):
        rcopy(codes.at[q], codes.at[q], o_s.at[k], o_r.at[q], (rq(k), c)).start()
    for k in range(1, nq):
        s = rq(k)
        rcopy(codes.at[s], codes.at[s], o_s.at[k], o_r.at[s], (s, c)).wait_recv()
    qcodes = jnp.concatenate([codes[i] for i in range(nq)], axis=1)
    scale = 1.0 / math.sqrt(corp.shape[1])
    scores = lax.dot_general(qcodes, corp[...], (((1,), (1,)), ((), ())), preferred_element_type=F32) * scale

    blocks = corp.shape[0] // LANES
    lists = jnp.concatenate([scores[:, i * LANES:(i + 1) * LANES] for i in range(blocks)], axis=0)
    best = merge_all(sort_lanes(lists), nqueries, q >= nq // 2)
    top_q[q] = best
    for k in range(1, nq):
        rcopy(top_q.at[q], top_q.at[q], tq_s.at[k], tq_r.at[q], (rq(k), c)).start()
    for k in range(1, nq):
        s = rq(k)
        rcopy(top_q.at[s], top_q.at[s], tq_s.at[k], tq_r.at[s], (s, c)).wait_recv()
    best = merge_all(top_q[...].reshape(nq * nqueries, LANES), nqueries, c >= nc // 2)
    top_c[c] = best
    for k in range(1, nc):
        rcopy(top_c.at[c], top_c.at[c], tc_s.at[k], tc_r.at[c], (q, rc(k))).start()
    for k in range(1, nc):
        s = rc(k)
        rcopy(top_c.at[s], top_c.at[s], tc_s.at[k], tc_r.at[s], (q, s)).wait_recv()
    best = merge_all(top_c[...].reshape(nc * nqueries, LANES), nqueries, False)
    out[...] = best[:, :TOPK]

    for k in range(1, nq):
        rcopy(lens, lens_all.at[q], l_s.at[k], l_r.at[q], (rq(k), c)).wait_send()
        rcopy(inv_all.at[q], inv_all.at[q], iv_s.at[k], iv_r.at[q], (rq(k), c)).wait_send()
        rcopy(top_q.at[q], top_q.at[q], tq_s.at[k], tq_r.at[q], (rq(k), c)).wait_send()
        rcopy(t_send, t_recv.at[q], t_s.at[k], t_r.at[q], (rq(k), c)).wait_send()
        rcopy(codes.at[q], codes.at[q], o_s.at[k], o_r.at[q], (rq(k), c)).wait_send()

    @pl.when(q != g)
    def _():
        rcopy(hid, colbuf.at[q], a_s, a_r.at[q], (g, c)).wait_send()

    for i in range(nb):
        @pl.when(sends_up)
        def _(i=i):
            up_chain(i).wait_send()

        @pl.when(sends_down)
        def _(i=i):
            down_chain(i).wait_send()

        for k in range(1, r):
            rcopy(chunk(i, j), chunk(i, j), la_s.at[k, i], la_r.at[j, i], (q, g * r + lane(k))).wait_send()

    def drain(n, carry):
        far_part(n).wait_send()
        near_part(n).wait_send()
        passed_part(n).wait_send()
        h_near(n, 0).wait_send()
        h_near(n, 1).wait_send()
        h_pass(n).wait_send()
        return carry

    lax.fori_loop(0, nch, drain, 0)
    for k in range(1, r):
        rcopy(lsend.at[lane(k)], lrecv.at[j], lr_s.at[k], lr_r.at[j], (q, g * r + lane(k))).wait_send()
    for k in range(1, ng):
        t = lax.rem(g + k, ng)
        rcopy(gsend.at[t], grecv.at[g], g_s.at[k], g_r.at[g], (q, t * r + j)).wait_send()
    for i in range(r):
        @pl.when(c != q * r + i)
        def _(i=i):
            rcopy(pp.at[i], prc.at[c], pp_s.at[i], pp_r.at[c], (q, q * r + i)).wait_send()

    @pl.when(g == q)
    def _():
        for k in range(1, nq):
            rcopy(pblk, pblk, pb_s.at[k], pb_r, (rq(k), c)).wait_send()
    for k in range(1, nc):
        rcopy(cpart, crecv.at[c], c_s.at[k], c_r.at[c], (q, rc(k))).wait_send()
        rcopy(st_send, st_recv.at[c], st_s.at[k], st_r.at[c], (q, rc(k))).wait_send()
        rcopy(top_c.at[c], top_c.at[c], tc_s.at[k], tc_r.at[c], (q, rc(k))).wait_send()


def per_device_general(nq, nc, hidden_in, lengths, gate_weight, up_weight, down_weight, code_weight, corpus_codes):
    slots, w = hidden_in.shape
    r = nc // nq
    nreal = nq * slots * REAL_NUM // REAL_DEN
    tq, tb = nreal // nq, nreal // nc
    dq, ffc = gate_weight.shape
    cw = CHUNK if ffc % CHUNK == 0 else ffc
    nch = ffc // cw
    nb = nreal // PIECE if nreal % PIECE == 0 else nq
    nqueries = nq * lengths.shape[0]
    bits = code_weight.shape[1]
    bw = bits // nq
    ng = nc // r
    lens = jnp.broadcast_to(jnp.repeat(lengths, SEQ)[None, :], (8, slots))
    vm, dma = pltpu.VMEM, pltpu.SemaphoreType.DMA
    scratch = [
        vm(gate_weight.shape, BF16), vm(up_weight.shape, BF16), vm(down_weight.shape, BF16),
        vm(code_weight.shape, BF16), vm(corpus_codes.shape, BF16),
        vm((nq, slots, w), BF16), vm((nq, 8, slots), jnp.int32), vm((r, nreal, w), BF16),
        vm((nch, nq, 2, tq, cw), BF16), vm((nch, nq, 2, tq, cw), BF16),
        vm((8, slots), F32), vm((nc, 8, slots), F32), vm((nq, 8, slots), F32), vm((r, nreal, w), BF16),
        vm((nch, 2, tq, cw), F32), vm((nq, nqueries, LANES), F32), vm((nc, nqueries, LANES), F32),
        vm((nch, nq, tq, cw), BF16), vm((nreal, dq), F32),
        vm((r, ng, tb, dq), BF16), vm((r, ng, tb, dq), BF16), vm((ng, tb, dq), BF16), vm((ng, tb, dq), BF16),
        vm((tb, 128), F32), vm((nq, tb, 128), F32),
        vm((r, nqueries, w), F32), vm((nc, nqueries, w), F32), vm((nqueries, w), BF16),
        vm((nqueries, bw), F32), vm((nc, nqueries, bw), F32), vm((nq, nqueries, bw), BF16),
        dma((5,)), dma, dma((nq,)), dma((nq,)), dma((nq,)), dma((2, nb)), dma((nb,)), dma((r, nb)), dma((r, nb)),
        dma((nch, nq)), dma((nch, nq)), dma((nc,)), dma((nc,)), dma((nq,)), dma((nq,)),
        dma((nq,)), dma((nq,)), dma((nc,)), dma((nc,)), dma((nch, nq)), dma((nch, nq)),
        dma((r,)), dma((r,)), dma((ng,)), dma((ng,)), dma((nq,)), dma((nq,)),
        dma((r,)), dma((nc,)), dma((nq,)), dma, dma((nc,)), dma((nc,)), dma((nq,)), dma((nq,)),
    ]
    dims = (nq, nc, r, nreal, tq, tb, nch, cw, w * nc)
    vspec, aspec = pl.BlockSpec(memory_space=pltpu.VMEM), pl.BlockSpec(memory_space=pl.ANY)
    return pl.pallas_call(
        functools.partial(general_kernel, dims),
        out_shape=jax.ShapeDtypeStruct((nqueries, TOPK), F32),
        in_specs=[vspec, vspec] + [aspec] * 5,
        out_specs=vspec,
        scratch_shapes=scratch,
        compiler_params=pltpu.CompilerParams(
            collective_id=0, has_side_effects=True, vmem_limit_bytes=60 * 1024 * 1024),
    )(hidden_in, lens, gate_weight, up_weight, down_weight, code_weight, corpus_codes)


def fast_kernel(dims, names, hid, lens, gate_h, up_h, down_h, code_h, corp_h, out, *refs):
    nq, nc, r, nblk, bm, nh, hw, d_all = dims
    s = types.SimpleNamespace(**dict(zip(names, refs)))
    q = lax.axis_index("query")
    c = lax.axis_index("corpus")
    g = c // r
    j = lax.rem(c, r)
    ng = nc // r
    slots, w = hid.shape
    total = nq * slots
    nqueries = total // SEQ
    nreal = nblk * bm
    qm, lm, pm = bm // nq, bm // r, bm // nc
    nu = nblk * nh
    bw = s.codew.shape[2] // nq
    gate, up, code, corp = s.gu.at[0], s.gu.at[1], s.codew.at[0], s.codew.at[1]

    fq = w // nq
    for i in range(nq):
        pltpu.make_async_copy(hid.at[:, pl.ds(i * fq, fq)], s.hidq.at[i], s.w_s.at[0]).start()
    counts = pltpu.make_async_copy(lens, s.lens_s, s.w_s.at[1])
    counts.start()
    for a, b, k in ((gate_h, gate, 2), (up_h, up, 2), (down_h, s.down, 3), (code_h, code, 4), (corp_h, corp, 4)):
        pltpu.make_async_copy(a, b, s.w_s.at[k]).start()

    def loaded(ref, k):
        pltpu.make_async_copy(ref, ref, s.w_s.at[k]).wait()

    def rq(k):
        return lax.rem(q + k, nq)

    def rc(k):
        return lax.rem(c + k, nc)

    def lane(k):
        return lax.rem(j + k, r)

    def got(ref, sem):
        rcopy(ref, ref, sem, sem, (rq(1), c)).wait_recv()

    def sent(ref, sem):
        rcopy(ref, ref, sem, sem, (rq(1), c)).wait_send()

    def to_query(src, ref, ss, rs):
        for k in range(1, nq):
            rcopy(src, ref.at[q], ss, rs, (rq(k), c)).start()

    def to_corpus(src, ref, ss, rs):
        for k in range(1, nc):
            rcopy(src, ref.at[c], ss, rs, (q, rc(k))).start()

    barrier = pltpu.get_barrier_semaphore()
    for k in range(1, nq):
        pl.semaphore_signal(barrier, inc=1, device_id=(rq(k), c), device_id_type=pl.DeviceIdType.MESH)
    for k in range(1, nc):
        pl.semaphore_signal(barrier, inc=1, device_id=(q, rc(k)), device_id_type=pl.DeviceIdType.MESH)

    loaded(s.hidq, 0)
    squares = jnp.square(s.hidq[0].astype(F32))
    for i in range(1, nq):
        squares = squares + jnp.square(s.hidq[i].astype(F32))
    s.st_send[...] = lax.dot_general(jnp.ones((8, fq), F32), squares, (((1,), (1,)), ((), ())),
                                     precision=lax.Precision.HIGHEST, preferred_element_type=F32)
    counts.wait()
    slot_query = lax.broadcasted_iota(jnp.int32, (8, slots), 1) // SEQ
    own_lens = jnp.zeros((8, slots), jnp.int32)
    for k in range(slots // SEQ):
        own_lens = jnp.where(slot_query == k, s.lens_s[k], own_lens)
    s.lens_all[q] = own_lens

    pl.semaphore_wait(barrier, nq - 1 + nc - 1)

    side_a = q + 1 - 2 * lax.rem(q, 2)
    side_b = q + 2 - 4 * (q // 2)
    far = nq - 1 - q

    for k in range(1, nq):
        rcopy(s.hidq.at[rq(k)], s.colbuf.at[q], s.a_s, s.a_r, (rq(k), c)).start()
    s.colbuf[q] = s.hidq[q]

    to_query(s.lens_all.at[q], s.lens_all, s.l_s, s.l_r)
    to_corpus(s.st_send, s.st_recv, s.st_s, s.st_r)
    s.st_recv[c] = s.st_send[...]
    got(s.lens_all.at[pl.ds(0, nq - 1)], s.l_r)
    lens_row = jnp.concatenate([s.lens_all[i] for i in range(nq)], axis=1)
    slot = lax.broadcasted_iota(jnp.int32, (8, total), 1)
    valid = lax.rem(slot, SEQ) < lens_row
    before = lax.broadcasted_iota(jnp.int32, (total, total), 0) < lax.broadcasted_iota(jnp.int32, (total, total), 1)
    pos = mm(valid.astype(F32).astype(BF16), before.astype(F32).astype(BF16)).astype(jnp.int32)
    pos = jnp.where(valid, pos, -1)[:1]

    got(s.st_recv.at[pl.ds(0, nc - 1)], s.st_r)
    stat = s.st_recv[0]
    for i in range(1, nc):
        stat = stat + s.st_recv[i]
    s.inv_all[q] = lax.rsqrt(stat / d_all + epsilon)
    to_query(s.inv_all.at[q], s.inv_all, s.iv_s, s.iv_r)

    def side(b, k):
        return rcopy(s.xall.at[j, b], s.xall.at[j, b], s.la_s, s.la_r.at[b], (q, g * r + lane(k)))

    def spread(b, k):
        t = lax.rem(g + k, ng)
        return rcopy(s.xpk.at[b], s.xall.at[j, b, q], s.x_s, s.x_r.at[b], (g, t * r + j))

    got(s.colbuf.at[pl.ds(0, nq - 1)], s.a_r)
    stacked = s.colbuf[...].reshape(total, fq)
    for b in range(nblk):
        row = lax.broadcasted_iota(jnp.int32, (bm, total), 0) + b * bm
        pick = (pos == row).astype(F32).astype(BF16)
        s.xpk[b] = mm(pick, stacked).astype(BF16)
        for k in range(ng - 1, 0, -1):
            spread(b, k).start()

        @pl.when(q != g)
        def _(b=b):
            spread(b, 0).start()

        @pl.when(q == g)
        def _(b=b):
            s.xall[j, b, q] = s.xpk[b]

    got(s.inv_all.at[pl.ds(0, nq - 1)], s.iv_r)
    inv_row = jnp.concatenate([s.inv_all[i] for i in range(nq)], axis=1)[:1]
    for b in range(nblk):
        row = lax.broadcasted_iota(jnp.int32, (bm, total), 0) + b * bm
        col = jnp.sum(jnp.where(pos == row, inv_row, 0.0), axis=1, keepdims=True)
        s.inv_c[b] = jnp.broadcast_to(col, (bm, LANES))

    loaded(s.gu, 2)

    def sides(n):
        odd = lax.rem(n, 2)
        return side_a + (side_b - side_a) * odd, side_b + (side_a - side_b) * odd

    def near_part(n):
        one, _ = sides(n)
        return rcopy(s.psend.at[n, one], s.precv.at[n, 0], s.p_s, s.p_r.at[n], (one, c))

    def far_part(n):
        one, _ = sides(n)
        return rcopy(s.psend.at[n, far], s.precv.at[n, 2], s.p_s, s.pf_r.at[n], (one, c))

    def passed_part(n):
        _, two = sides(n)
        return rcopy(s.precv.at[n, 3], s.precv.at[n, 1], s.p_s, s.p_r.at[n], (two, c))

    def h_near(n, k, sem):
        return rcopy(s.hall.at[n, q], s.hall.at[n, q], s.h_s, sem, (sides(n)[k], c))

    def h_pass(n, sem):
        one, two = sides(n)
        return rcopy(s.hall.at[n, one], s.hall.at[n, one], s.h_s, sem, (two, c))

    def fetch(b):
        @pl.when(q != g)
        def _():
            got(s.xall.at[0, b], s.x_r.at[b])

        @pl.when(q == g)
        def _():
            got(s.xall.at[0, b, pl.ds(0, nq - 1)], s.x_r.at[b])

        for k in range(1, r):
            side(b, k).start()

    def products(b):
        got(s.xall.at[pl.ds(0, r - 1), b], s.la_r.at[b])
        scale = s.inv_c[b][:, :1]
        for i in range(r):
            for k in range(nq):
                at = i * w + k * fq
                s.xn[:, at:at + fq] = (s.xall[i, b, k].astype(F32) * scale).astype(BF16)
        xb = s.xn[...]
        for h in range(nh):
            n = b * nh + h
            for e, wref in enumerate((gate, up)):
                full = mm(xb, wref[:, h * hw:(h + 1) * hw])
                s.full[h, e] = full
                for i in range(nq):
                    s.psend[n, i, e] = full[i * qm:(i + 1) * qm].astype(BF16)
            far_part(n).start()
            near_part(n).start()
            for e in range(2):
                s.pown[n, e] = s.full[h, e, pl.ds(pl.multiple_of(q * qm, qm), qm)]

    def pass_unit(n):
        _, two = sides(n)
        got(s.precv.at[n, 2], s.pf_r.at[n])
        s.precv[n, 3] = (s.psend[n, two].astype(F32) + s.precv[n, 2].astype(F32)).astype(BF16)
        passed_part(n).start()

    def reduce_unit(n):
        got(s.precv.at[n, pl.ds(0, 2)], s.p_r.at[n])
        gsum = s.pown[n, 0] + s.precv[n, 0, 0].astype(F32) + s.precv[n, 1, 0].astype(F32)
        usum = s.pown[n, 1] + s.precv[n, 0, 1].astype(F32) + s.precv[n, 1, 1].astype(F32)
        s.hall[n, q] = (gsum / (1.0 + jnp.exp(-gsum)) * usum).astype(BF16)
        h_near(n, 0, s.hn_r.at[n]).start()
        h_near(n, 1, s.hb_r.at[n // nh]).start()

    def relay_unit(n):
        got(s.hall.at[n, 0], s.hn_r.at[n])
        h_pass(n, s.hb_r.at[n // nh]).start()

    def lane_send(b, k):
        t = lane(k)
        return rcopy(s.lsend.at[b, t], s.lrecv.at[b, j], s.lr_s, s.lr_r.at[b], (q, g * r + t))

    def group_send(b, k):
        t = lax.rem(g + k, ng)
        return rcopy(s.gsend.at[b, t], s.grecv.at[b, g], s.g_s, s.g_r.at[b], (q, t * r + j))

    def down_block(b):
        part = None
        got(s.hall.at[pl.ds(b * nh, nh), pl.ds(0, 2)], s.hb_r.at[b])
        for h in range(nh):
            n = b * nh + h
            term = mm(s.hall[n].reshape(bm, hw), s.down[h * hw:(h + 1) * hw, :])
            part = term if part is None else part + term
        for t in range(r):
            s.lsend[b, t] = part[t * lm:(t + 1) * lm].astype(BF16)
        for k in range(1, r):
            lane_send(b, k).start()

    def sum_block(b):
        mine = s.lsend[b, j].astype(F32)
        got(s.lrecv.at[b, pl.ds(0, r - 1)], s.lr_r.at[b])
        for k in range(1, r):
            mine = mine + s.lrecv[b, lane(k)].astype(F32)
        for t in range(ng):
            s.gsend[b, t] = mine[t * pm:(t + 1) * pm].astype(BF16)
        for k in range(1, ng):
            group_send(b, k).start()

    def units(unit, b):
        for h in range(nh):
            unit(b * nh + h)

    def fetch_next(b):
        @pl.when(b + 1 < nblk)
        def _():
            fetch(b + 1)

    fetch(0)
    stages = (products, fetch_next, functools.partial(units, pass_unit), functools.partial(units, reduce_unit),
              functools.partial(units, relay_unit), down_block, sum_block)
    delays = (0,0,1,2,3,4,5)

    def turn(t, carry):
        for stage, delay in zip(stages, delays):
            @pl.when(jnp.logical_and(t >= delay, t < nblk + delay))
            def _(stage=stage, delay=delay):
                stage(t - delay)
        return carry

    loaded(s.down, 3)
    lax.fori_loop(0, nblk + delays[-1], turn, 0)
    row = lax.broadcasted_iota(jnp.int32, (nblk * pm, nreal), 0)
    row = (row // pm) * bm + (j * ng + g) * pm + lax.rem(row, pm)
    own_rows = (lax.broadcasted_iota(jnp.int32, (nblk * pm, nreal), 1) == row).astype(F32).astype(BF16)
    for i in range(r):
        for k in range(nq):
            at = i * w + k * fq
            s.res[:, at:at + fq] = mm(own_rows, s.xall[i, :, k].reshape(nreal, fq))

    for b in range(nblk):
        total_b = s.gsend[b, g].astype(F32)
        got(s.grecv.at[b, pl.ds(0, ng - 1)], s.g_r.at[b])
        for k in range(1, ng):
            total_b = total_b + s.grecv[b, lax.rem(g + k, ng)].astype(F32)
        s.res[b * pm:(b + 1) * pm, :] = s.res[b * pm:(b + 1) * pm, :] + total_b
    residual = s.res[...]
    tb = nblk * pm

    s.t_send[...] = jnp.broadcast_to(jnp.sum(residual * residual, axis=1, keepdims=True), (tb, LANES))
    to_query(s.t_send, s.t_recv, s.t_s, s.t_r)
    qrow = lax.broadcasted_iota(jnp.int32, (nqueries, total), 0)
    qslot = lax.broadcasted_iota(jnp.int32, (nqueries, total), 1)
    lens_b = jnp.broadcast_to(lens_row[:1], (nqueries, total)).astype(F32)
    vals_b = jnp.broadcast_to(valid.astype(F32)[:1], (nqueries, total))
    len_col = jnp.sum(jnp.where(qslot == qrow * SEQ, lens_b, 0.0), axis=1, keepdims=True)
    off_col = jnp.sum(jnp.where(qslot < qrow * SEQ, vals_b, 0.0), axis=1, keepdims=True)
    prow = lax.broadcasted_iota(jnp.int32, (nqueries, tb), 1)
    prow = ((prow // pm) * bm + (j * ng + g) * pm + lax.rem(prow, pm)).astype(F32)
    member = jnp.where(jnp.logical_and(prow >= off_col, prow < off_col + len_col), 1.0, 0.0)
    tsum = s.t_send[...]
    got(s.t_recv.at[pl.ds(0, nq - 1)], s.t_r)
    for k in range(1, nq):
        tsum = tsum + s.t_recv[rq(k)]
    final = residual * lax.rsqrt(tsum[:, :1] / d_all + epsilon)
    pooled_part = mm(member, final, lax.Precision.HIGHEST)
    for i in range(r):
        s.pp[i] = pooled_part[:, i * w:(i + 1) * w].astype(BF16)
    for i in range(r):
        @pl.when(c != q * r + i)
        def _(i=i):
            rcopy(s.pp.at[i], s.prc.at[c], s.pp_s, s.pp_r, (q, q * r + i)).start()

    @pl.when(g == q)
    def _():
        pooled = s.pp[j].astype(F32)
        got(s.prc.at[pl.ds(0, nc - 1)], s.pp_r)
        for k in range(1, nc):
            pooled = pooled + s.prc[rc(k)].astype(F32)
        s.pblk[0] = (pooled / len_col).astype(BF16)
        for k in range(1, nq):
            rcopy(s.pblk.at[0], s.pblk.at[0], s.pb_s, s.pb_r, (rq(k), c)).start()

    loaded(s.codew, 4)

    @pl.when(g != q)
    def _():
        got(s.pblk.at[0], s.pb_r)

    s.cpart[...] = mm(s.pblk[0], code[:, pl.ds(pl.multiple_of(q * bw, bw), bw)])
    to_corpus(s.cpart, s.crecv, s.c_s, s.c_r)
    s.crecv[c] = s.cpart[...]
    got(s.crecv.at[pl.ds(0, nc - 1)], s.c_r)
    csum = s.crecv[0]
    for i in range(1, nc):
        csum = csum + s.crecv[i]
    s.codes[q] = csum.astype(BF16)
    to_query(s.codes.at[q], s.codes, s.o_s, s.o_r)
    got(s.codes.at[pl.ds(0, nq - 1)], s.o_r)
    qcodes = jnp.concatenate([s.codes[i] for i in range(nq)], axis=1)
    scale = 1.0 / math.sqrt(corp.shape[1])
    scores = lax.dot_general(qcodes, corp[...], (((1,), (1,)), ((), ())), preferred_element_type=F32) * scale

    blocks = corp.shape[0] // LANES
    lists = jnp.concatenate([scores[:, i * LANES:(i + 1) * LANES] for i in range(blocks)], axis=0)
    best = merge_all(sort_lanes(lists), nqueries, q >= nq // 2)
    s.top_q[q] = best
    to_query(s.top_q.at[q], s.top_q, s.tq_s, s.tq_r)
    got(s.top_q.at[pl.ds(0, nq - 1)], s.tq_r)
    best = merge_all(s.top_q[...].reshape(nq * nqueries, LANES), nqueries, c >= nc // 2)
    s.top_c[c] = best
    to_corpus(s.top_c.at[c], s.top_c, s.tc_s, s.tc_r)
    got(s.top_c.at[pl.ds(0, nc - 1)], s.tc_r)
    best = merge_all(s.top_c[...].reshape(nc * nqueries, LANES), nqueries, False)
    out[...] = best[:, :TOPK]

    sent(s.lens_all.at[pl.ds(0, nq - 1)], s.l_s)
    sent(s.st_recv.at[pl.ds(0, nc - 1)], s.st_s)
    sent(s.inv_all.at[pl.ds(0, nq - 1)], s.iv_s)

    sent(s.colbuf.at[pl.ds(0, nq - 1)], s.a_s)

    @pl.when(q != g)
    def _():
        sent(s.xall.at[0], s.x_s)

    @pl.when(q == g)
    def _():
        sent(s.xall.at[0, :, pl.ds(0, nq - 1)], s.x_s)

    sent(s.xall.at[pl.ds(0, r - 1)], s.la_s)
    sent(s.psend.at[:, pl.ds(0, 3)], s.p_s)
    sent(s.hall.at[:, pl.ds(0, 3)], s.h_s)
    sent(s.lsend.at[:, pl.ds(0, r - 1)], s.lr_s)
    sent(s.gsend.at[:, pl.ds(0, ng - 1)], s.g_s)
    sent(s.t_recv.at[pl.ds(0, nq - 1)], s.t_s)

    @pl.when(g == q)
    def _():
        sent(s.pp.at[pl.ds(0, r - 1)], s.pp_s)
        sent(s.pblk.at[pl.ds(0, nq - 1)], s.pb_s)

    @pl.when(g != q)
    def _():
        sent(s.pp, s.pp_s)

    sent(s.crecv.at[pl.ds(0, nc - 1)], s.c_s)
    sent(s.codes.at[pl.ds(0, nq - 1)], s.o_s)
    sent(s.top_q.at[pl.ds(0, nq - 1)], s.tq_s)
    sent(s.top_c.at[pl.ds(0, nc - 1)], s.tc_s)


def halves_of(ffc):
    return 2 if ffc % (2 * LANES) == 0 else 1


def per_device_fast(nq, nc, hidden_in, lengths, gate_weight, up_weight, down_weight, code_weight, corpus_codes):
    slots, w = hidden_in.shape
    r = nc // nq
    ng = nc // r
    nreal = nq * slots * REAL_NUM // REAL_DEN
    dq, ffc = gate_weight.shape
    bm = 8 * nc
    nblk = nreal // bm
    nh = halves_of(ffc)
    hw = ffc // nh
    nu = nblk * nh
    qm, lm, pm = bm // nq, bm // r, bm // nc
    tb = nblk * pm
    nqueries = nq * lengths.shape[0]
    bits = code_weight.shape[1]
    bw = bits // nq
    vm, dma = pltpu.VMEM, pltpu.SemaphoreType.DMA
    scratch = dict(
        gu=vm((2,) + gate_weight.shape, BF16), down=vm(down_weight.shape, BF16), codew=vm((2,) + code_weight.shape, BF16),
        lens_s=pltpu.SMEM(lengths.shape, jnp.int32),
        hidq=vm((nq, slots, w // nq), BF16), colbuf=vm((nq, slots, w // nq), BF16), xpk=vm((nblk, bm, w // nq), BF16), lens_all=vm((nq, 8, slots), jnp.int32), xall=vm((r, nblk, nq, bm, w // nq), BF16),
        xn=vm((bm, dq), BF16), inv_c=vm((nblk, bm, LANES), F32),
        st_send=vm((8, slots), F32), st_recv=vm((nc, 8, slots), F32), inv_all=vm((nq, 8, slots), F32),
        psend=vm((nu, nq, 2, qm, hw), BF16), precv=vm((nu, 4, 2, qm, hw), BF16), pown=vm((nu, 2, qm, hw), F32), full=vm((nh, 2, bm, hw), F32),
        hall=vm((nu, nq, qm, hw), BF16),
        lsend=vm((nblk, r, lm, dq), BF16), lrecv=vm((nblk, r, lm, dq), BF16),
        gsend=vm((nblk, ng, pm, dq), BF16), grecv=vm((nblk, ng, pm, dq), BF16), res=vm((tb, dq), F32),
        t_send=vm((tb, LANES), F32), t_recv=vm((nq, tb, LANES), F32),
        pp=vm((r, nqueries, w), BF16), prc=vm((nc, nqueries, w), BF16), pblk=vm((nq, nqueries, w), BF16),
        cpart=vm((nqueries, bw), F32), crecv=vm((nc, nqueries, bw), F32), codes=vm((nq, nqueries, bw), BF16),
        top_q=vm((nq, nqueries, LANES), F32), top_c=vm((nc, nqueries, LANES), F32),
        w_s=dma((5,)), l_s=dma, l_r=dma, a_s=dma, a_r=dma, st_s=dma, st_r=dma, iv_s=dma, iv_r=dma,
        x_s=dma, x_r=dma((nblk,)), la_s=dma, la_r=dma((nblk,)),
        p_s=dma, p_r=dma((nu,)), pf_r=dma((nu,)), h_s=dma, hn_r=dma((nu,)), hb_r=dma((nblk,)),
        lr_s=dma, lr_r=dma((nblk,)), g_s=dma, g_r=dma((nblk,)),
        t_s=dma, t_r=dma, pp_s=dma, pp_r=dma, pb_s=dma, pb_r=dma, c_s=dma, c_r=dma, o_s=dma, o_r=dma,
        tq_s=dma, tq_r=dma, tc_s=dma, tc_r=dma,
    )
    dims = (nq, nc, r, nblk, bm, nh, hw, w * nc)
    vspec, aspec = pl.BlockSpec(memory_space=pltpu.VMEM), pl.BlockSpec(memory_space=pl.ANY)
    return pl.pallas_call(
        functools.partial(fast_kernel, dims, tuple(scratch)),
        out_shape=jax.ShapeDtypeStruct((nqueries, TOPK), F32),
        in_specs=[aspec] * 7,
        out_specs=vspec,
        scratch_shapes=list(scratch.values()),
        compiler_params=pltpu.CompilerParams(
            collective_id=0, has_side_effects=True, vmem_limit_bytes=60 * 1024 * 1024),
    )(hidden_in, lengths, gate_weight, up_weight, down_weight, code_weight, corpus_codes)


def per_device(nq, nc, hidden_in, *rest):
    slots, w = hidden_in.shape
    nreal = nq * slots * REAL_NUM // REAL_DEN
    fits = nreal % (8 * nc) == 0 and w % (nq * LANES) == 0 and rest[4].shape == rest[5].shape
    body = per_device_fast if fits else per_device_general
    return body(nq, nc, hidden_in, *rest)


def solution(mesh):
    in_specs = (
        P("query", "corpus"),
        P("query"),
        P("query", "corpus"),
        P("query", "corpus"),
        P("corpus", "query"),
        P("corpus", None),
        P(("query", "corpus"), None),
    )
    body = functools.partial(per_device, mesh.shape["query"], mesh.shape["corpus"])
    return jax.shard_map(body, mesh=mesh, in_specs=in_specs, out_specs=P(), check_vma=False)
```

```python
import functools
import math
import types

import jax
import jax.numpy as jnp
from jax import lax
from jax.experimental import pallas as pl
from jax.experimental.pallas import tpu as pltpu
from jax.sharding import PartitionSpec as P

SEQ = 32
LANES = 128
TOPK = 100
REAL_NUM, REAL_DEN = 5, 8
CHUNK = 256
PIECE = 32

epsilon = 1e-05
F32, BF16 = jnp.float32, jnp.bfloat16


def mm(a, b, precision=None):
    return lax.dot_general(a, b, (((1,), (0,)), ((), ())), precision=precision, preferred_element_type=F32)


def rcopy(src, dst, send, recv, dev):
    return pltpu.make_async_remote_copy(
        src_ref=src, dst_ref=dst, send_sem=send, recv_sem=recv,
        device_id=dev, device_id_type=pl.DeviceIdType.MESH)


def exchange(x, s, keep_max):
    bit = (lax.broadcasted_iota(jnp.int32, x.shape, 1) & s) != 0
    other = jnp.where(bit, pltpu.roll(x, s, 1), pltpu.roll(x, LANES - s, 1))
    return jnp.where(keep_max, jnp.maximum(x, other), jnp.minimum(x, other))


def sort_lanes(x):
    lane = lax.broadcasted_iota(jnp.int32, x.shape, 1)
    flip = (lax.broadcasted_iota(jnp.int32, x.shape, 0) >= x.shape[0] // 2).astype(jnp.int32)
    size = 2
    while size <= LANES:
        up = ((lane & size) != 0).astype(jnp.int32) if size < LANES else jnp.zeros_like(lane)
        s = size // 2
        while s:
            low = ((lane & s) != 0).astype(jnp.int32)
            x = exchange(x, s, (low ^ up ^ flip) == 0)
            s //= 2
        size *= 2
    return x


def merge_all(x, rows, lone):
    while x.shape[0] > rows:
        half = x.shape[0] // 2
        x = jnp.maximum(x[:half], x[half:])
        lane = lax.broadcasted_iota(jnp.int32, x.shape, 1)
        if half > rows:
            flip = (lax.broadcasted_iota(jnp.int32, x.shape, 0) >= half // 2).astype(jnp.int32)
        else:
            flip = jnp.zeros_like(lane) + jnp.asarray(lone, jnp.int32)
        s = LANES // 2
        while s:
            low = ((lane & s) != 0).astype(jnp.int32)
            x = exchange(x, s, (low ^ flip) == 0)
            s //= 2
    return x


def general_kernel(dims, hid, lens, gate_h, up_h, down_h, code_h, corp_h, out,
                 gate, up, down, code, corp, colbuf, lens_all, xall, psend, precv,
                 st_send, st_recv, inv_all, xn, pown, top_q, top_c, hall, acc, lsend, lrecv, gsend, grecv, t_send, t_recv,
                 pp, prc, pblk, cpart, crecv, codes,
                 w_s, a_s, a_r, l_s, l_r, ch_s, ch_r, la_s, la_r, p_s, p_r, st_s, st_r, iv_s, iv_r, tq_s, tq_r, tc_s, tc_r, h_s, h_r,
                 lr_s, lr_r, g_s, g_r, t_s, t_r, pp_s, pp_r, pb_s, pb_r, c_s, c_r, o_s, o_r):
    nq, nc, r, nreal, tq, tb, nch, cw, d_all = dims
    q = lax.axis_index("query")
    c = lax.axis_index("corpus")
    g = c // r
    j = lax.rem(c, r)
    slots, w = hid.shape[0], hid.shape[1]
    total = nq * slots
    nqueries = total // SEQ
    bw = code.shape[1] // nq

    loads = []
    for i, (s, d) in enumerate(((gate_h, gate), (up_h, up), (down_h, down), (code_h, code), (corp_h, corp))):
        cp = pltpu.make_async_copy(s, d, w_s.at[i])
        cp.start()
        loads.append(cp)

    def rq(k):
        return lax.rem(q + k, nq)

    def rc(k):
        return lax.rem(c + k, nc)

    def lane(k):
        return lax.rem(j + k, r)

    barrier = pltpu.get_barrier_semaphore()
    for k in range(1, nq):
        pl.semaphore_signal(barrier, inc=1, device_id=(rq(k), c), device_id_type=pl.DeviceIdType.MESH)
    for k in range(1, nc):
        pl.semaphore_signal(barrier, inc=1, device_id=(q, rc(k)), device_id_type=pl.DeviceIdType.MESH)
    pl.semaphore_wait(barrier, nq - 1 + nc - 1)

    for k in range(1, nq):
        rcopy(lens, lens_all.at[q], l_s.at[k], l_r.at[q], (rq(k), c)).start()

    @pl.when(q != g)
    def _():
        rcopy(hid, colbuf.at[q], a_s, a_r.at[q], (g, c)).start()

    squares = jnp.square(hid[...].astype(F32))
    st_send[...] = lax.dot_general(jnp.ones((8, w), F32), squares, (((1,), (1,)), ((), ())),
                                   precision=lax.Precision.HIGHEST, preferred_element_type=F32)
    for k in range(1, nc):
        rcopy(st_send, st_recv.at[c], st_s.at[k], st_r.at[c], (q, rc(k))).start()
    st_recv[c] = st_send[...]
    lens_all[q] = lens[...]
    for k in range(1, nq):
        s = rq(k)
        rcopy(lens, lens_all.at[s], l_s.at[k], l_r.at[s], (s, c)).wait_recv()
    lens_row = jnp.concatenate([lens_all[i] for i in range(nq)], axis=1)
    slot = lax.broadcasted_iota(jnp.int32, (8, total), 1)
    valid = lax.rem(slot, SEQ) < lens_row
    before = lax.broadcasted_iota(jnp.int32, (total, total), 0) < lax.broadcasted_iota(jnp.int32, (total, total), 1)
    pos = mm(valid.astype(F32).astype(BF16), before.astype(F32).astype(BF16)).astype(jnp.int32)
    pos = jnp.where(valid, pos, -1)[:1]

    for k in range(1, nc):
        s = rc(k)
        rcopy(st_send, st_recv.at[s], st_s.at[k], st_r.at[s], (q, s)).wait_recv()
    stat = st_recv[0]
    for i in range(1, nc):
        stat = stat + st_recv[i]
    inv_all[q] = lax.rsqrt(stat / d_all + epsilon)
    for k in range(1, nq):
        rcopy(inv_all.at[q], inv_all.at[q], iv_s.at[k], iv_r.at[q], (rq(k), c)).start()

    nb = ch_r.shape[0]
    ct = nreal // nb

    def chunk(i, slot_j):
        return xall.at[slot_j, pl.ds(i * ct, ct)]

    def down_chain(i):
        return rcopy(chunk(i, j), chunk(i, j), ch_s.at[0, i], ch_r.at[i], (q, jnp.maximum(c - r, 0)))

    def up_chain(i):
        return rcopy(chunk(i, j), chunk(i, j), ch_s.at[1, i], ch_r.at[i], (q, jnp.minimum(c + r, nc - 1)))

    sends_up = jnp.logical_and(g >= q, g < nc // r - 1)
    sends_down = jnp.logical_and(g <= q, g > 0)

    @pl.when(q == g)
    def _():
        colbuf[q] = hid[...]
        for k in range(1, nq):
            s = rq(k)
            rcopy(hid, colbuf.at[s], a_s, a_r.at[s], (s, c)).wait_recv()
        stacked = colbuf[...].reshape(total, w)
        for i in range(nq):
            row = lax.broadcasted_iota(jnp.int32, (tq, total), 0) + i * tq
            pick = (pos == row).astype(F32).astype(BF16)
            xall[j, i * tq:(i + 1) * tq, :] = mm(pick, stacked).astype(BF16)

    for i in range(nb):
        @pl.when(q != g)
        def _(i=i):
            up_chain(i).wait_recv()

        @pl.when(sends_up)
        def _(i=i):
            up_chain(i).start()

        @pl.when(sends_down)
        def _(i=i):
            down_chain(i).start()

        for k in range(1, r):
            rcopy(chunk(i, j), chunk(i, j), la_s.at[k, i], la_r.at[j, i], (q, g * r + lane(k))).start()
    for k in range(1, nq):
        s = rq(k)
        rcopy(inv_all.at[s], inv_all.at[s], iv_s.at[k], iv_r.at[s], (s, c)).wait_recv()
    inv_row = jnp.concatenate([inv_all[i] for i in range(nq)], axis=1)[:1]
    inv_cols = []
    for i in range(nq):
        row = lax.broadcasted_iota(jnp.int32, (tq, total), 0) + i * tq
        inv_cols.append(jnp.sum(jnp.where(pos == row, inv_row, 0.0), axis=1, keepdims=True))
    inv = jnp.concatenate(inv_cols, axis=0)
    for i in range(nb):
        for k in range(1, r):
            s = lane(k)
            rcopy(chunk(i, s), chunk(i, s), la_s.at[k, i], la_r.at[s, i], (q, g * r + s)).wait_recv()

    loads[0].wait()
    loads[1].wait()

    for i in range(r):
        xn[i] = (xall[i].astype(F32) * inv).astype(BF16)

    side_a = q + 1 - 2 * lax.rem(q, 2)
    side_b = q + 2 - 4 * (q // 2)
    far = nq - 1 - q

    def sides(n):
        odd = lax.rem(n, 2)
        return side_a + (side_b - side_a) * odd, side_b + (side_a - side_b) * odd

    def near_part(n):
        one, _ = sides(n)
        return rcopy(psend.at[n, one], precv.at[n, 0], p_s.at[n, 0], p_r.at[n, 0], (one, c))

    def far_part(n):
        one, _ = sides(n)
        return rcopy(psend.at[n, far], precv.at[n, 1], p_s.at[n, 1], p_r.at[n, 1], (one, c))

    def passed_part(n):
        _, two = sides(n)
        return rcopy(precv.at[n, 3], precv.at[n, 2], p_s.at[n, 2], p_r.at[n, 2], (two, c))

    def h_near(n, k):
        to = sides(n)[k]
        return rcopy(hall.at[n, q], hall.at[n, q], h_s.at[n, k], h_r.at[n, k], (to, c))

    def h_near_in(n, k):
        to = sides(n)[k]
        return rcopy(hall.at[n, to], hall.at[n, to], h_s.at[n, k], h_r.at[n, k], (to, c))

    def h_pass(n):
        one, two = sides(n)
        return rcopy(hall.at[n, one], hall.at[n, one], h_s.at[n, 2], h_r.at[n, 2], (two, c))

    def h_pass_in(n):
        _, two = sides(n)
        return rcopy(hall.at[n, far], hall.at[n, far], h_s.at[n, 2], h_r.at[n, 2], (two, c))

    def matmuls(n, carry):
        cols = pl.ds(pl.multiple_of(n * cw, cw), cw)
        for e, wref in enumerate((gate, up)):
            full = sum(mm(xn[i], wref[i * w:(i + 1) * w, cols]) for i in range(r))
            for i in range(nq):
                psend[n, i, e] = full[i * tq:(i + 1) * tq].astype(BF16)

                @pl.when(q == i)
                def _(i=i, e=e, full=full):
                    pown[n, e] = full[i * tq:(i + 1) * tq]
        far_part(n).start()
        near_part(n).start()
        return carry

    lax.fori_loop(0, nch, matmuls, 0)

    loads[2].wait()
    acc[...] = jnp.zeros_like(acc)

    def pass_chunk(n):
        _, two = sides(n)
        far_part(n).wait_recv()
        precv[n, 3] = (psend[n, two].astype(F32) + precv[n, 1].astype(F32)).astype(BF16)
        passed_part(n).start()

    def reduce_chunk(n):
        near_part(n).wait_recv()
        passed_part(n).wait_recv()
        gsum = pown[n, 0] + precv[n, 0, 0].astype(F32) + precv[n, 2, 0].astype(F32)
        usum = pown[n, 1] + precv[n, 0, 1].astype(F32) + precv[n, 2, 1].astype(F32)
        hall[n, q] = (gsum / (1.0 + jnp.exp(-gsum)) * usum).astype(BF16)
        h_near(n, 0).start()
        h_near(n, 1).start()

    def relay_chunk(n):
        h_near_in(n, 0).wait_recv()
        h_pass(n).start()

    def down_chunk(n):
        h_near_in(n, 1).wait_recv()
        h_pass_in(n).wait_recv()
        acc[...] += mm(hall[n].reshape(nreal, cw), down[pl.ds(pl.multiple_of(n * cw, cw), cw), :])

    def passes(n, carry):
        pass_chunk(n)
        return carry

    lax.fori_loop(0, nch, passes, 0)
    reduce_chunk(0)

    def reduces(n, carry):
        reduce_chunk(n)
        relay_chunk(n - 1)
        return carry

    lax.fori_loop(1, nch, reduces, 0)
    relay_chunk(nch - 1)

    def downs(n, carry):
        down_chunk(n)
        return carry

    lax.fori_loop(0, nch, downs, 0)

    ng = nc // r
    for gg in range(ng):
        for jj in range(r):
            b = gg * r + jj
            lsend[jj, gg] = acc[b * tb:(b + 1) * tb].astype(BF16)
    for k in range(1, r):
        t = lane(k)
        rcopy(lsend.at[t], lrecv.at[j], lr_s.at[k], lr_r.at[j], (q, g * r + t)).start()
    mine = lsend[j].astype(F32)
    for k in range(1, r):
        s = lane(k)
        rcopy(lsend.at[s], lrecv.at[s], lr_s.at[k], lr_r.at[s], (q, g * r + s)).wait_recv()
        mine = mine + lrecv[s].astype(F32)
    gsend[...] = mine.astype(BF16)
    for k in range(1, ng):
        t = lax.rem(g + k, ng)
        rcopy(gsend.at[t], grecv.at[g], g_s.at[k], g_r.at[g], (q, t * r + j)).start()
    row = lax.broadcasted_iota(jnp.int32, (tb, nreal), 0) + c * tb
    own_rows = (lax.broadcasted_iota(jnp.int32, (tb, nreal), 1) == row).astype(F32).astype(BF16)
    residual = jnp.concatenate([mm(own_rows, xall[i]) for i in range(r)], axis=1)
    residual = residual + gsend[g].astype(F32)
    for k in range(1, ng):
        s = lax.rem(g + k, ng)
        rcopy(gsend.at[s], grecv.at[s], g_s.at[k], g_r.at[s], (q, s * r + j)).wait_recv()
        residual = residual + grecv[s].astype(F32)

    t_send[...] = jnp.broadcast_to(jnp.sum(residual * residual, axis=1, keepdims=True), (tb, 128))
    for k in range(1, nq):
        rcopy(t_send, t_recv.at[q], t_s.at[k], t_r.at[q], (rq(k), c)).start()
    qrow = lax.broadcasted_iota(jnp.int32, (nqueries, total), 0)
    qslot = lax.broadcasted_iota(jnp.int32, (nqueries, total), 1)
    lens_b = jnp.broadcast_to(lens_row[:1], (nqueries, total)).astype(F32)
    vals_b = jnp.broadcast_to(valid.astype(F32)[:1], (nqueries, total))
    len_col = jnp.sum(jnp.where(qslot == qrow * SEQ, lens_b, 0.0), axis=1, keepdims=True)
    off_col = jnp.sum(jnp.where(qslot < qrow * SEQ, vals_b, 0.0), axis=1, keepdims=True)
    prow = (lax.broadcasted_iota(jnp.int32, (nqueries, tb), 1) + c * tb).astype(F32)
    member = jnp.where(jnp.logical_and(prow >= off_col, prow < off_col + len_col), 1.0, 0.0)
    tsum = t_send[...]
    for k in range(1, nq):
        s = rq(k)
        rcopy(t_send, t_recv.at[s], t_s.at[k], t_r.at[s], (s, c)).wait_recv()
        tsum = tsum + t_recv[s]
    final = residual * lax.rsqrt(tsum[:, :1] / d_all + epsilon)
    pooled_part = mm(member, final, lax.Precision.HIGHEST)
    for i in range(r):
        pp[i] = pooled_part[:, i * w:(i + 1) * w]
    for i in range(r):
        @pl.when(c != q * r + i)
        def _(i=i):
            rcopy(pp.at[i], prc.at[c], pp_s.at[i], pp_r.at[c], (q, q * r + i)).start()

    @pl.when(g == q)
    def _():
        pooled = pp[j]
        for k in range(1, nc):
            s = rc(k)
            rcopy(pp.at[j], prc.at[s], pp_s.at[0], pp_r.at[s], (q, s)).wait_recv()
            pooled = pooled + prc[s]
        pblk[...] = (pooled / len_col).astype(BF16)
        for k in range(1, nq):
            rcopy(pblk, pblk, pb_s.at[k], pb_r, (rq(k), c)).start()

    loads[3].wait()
    loads[4].wait()

    @pl.when(g != q)
    def _():
        rcopy(pblk, pblk, pb_s.at[0], pb_r, (g, c)).wait_recv()

    cpart[...] = mm(pblk[...], code[:, pl.ds(pl.multiple_of(q * bw, bw), bw)])
    for k in range(1, nc):
        rcopy(cpart, crecv.at[c], c_s.at[k], c_r.at[c], (q, rc(k))).start()
    crecv[c] = cpart[...]
    for k in range(1, nc):
        s = rc(k)
        rcopy(cpart, crecv.at[s], c_s.at[k], c_r.at[s], (q, s)).wait_recv()
    csum = crecv[0]
    for i in range(1, nc):
        csum = csum + crecv[i]
    codes[q] = csum.astype(BF16)
    for k in range(1, nq):
        rcopy(codes.at[q], codes.at[q], o_s.at[k], o_r.at[q], (rq(k), c)).start()
    for k in range(1, nq):
        s = rq(k)
        rcopy(codes.at[s], codes.at[s], o_s.at[k], o_r.at[s], (s, c)).wait_recv()
    qcodes = jnp.concatenate([codes[i] for i in range(nq)], axis=1)
    scale = 1.0 / math.sqrt(corp.shape[1])
    scores = lax.dot_general(qcodes, corp[...], (((1,), (1,)), ((), ())), preferred_element_type=F32) * scale

    blocks = corp.shape[0] // LANES
    lists = jnp.concatenate([scores[:, i * LANES:(i + 1) * LANES] for i in range(blocks)], axis=0)
    best = merge_all(sort_lanes(lists), nqueries, q >= nq // 2)
    top_q[q] = best
    for k in range(1, nq):
        rcopy(top_q.at[q], top_q.at[q], tq_s.at[k], tq_r.at[q], (rq(k), c)).start()
    for k in range(1, nq):
        s = rq(k)
        rcopy(top_q.at[s], top_q.at[s], tq_s.at[k], tq_r.at[s], (s, c)).wait_recv()
    best = merge_all(top_q[...].reshape(nq * nqueries, LANES), nqueries, c >= nc // 2)
    top_c[c] = best
    for k in range(1, nc):
        rcopy(top_c.at[c], top_c.at[c], tc_s.at[k], tc_r.at[c], (q, rc(k))).start()
    for k in range(1, nc):
        s = rc(k)
        rcopy(top_c.at[s], top_c.at[s], tc_s.at[k], tc_r.at[s], (q, s)).wait_recv()
    best = merge_all(top_c[...].reshape(nc * nqueries, LANES), nqueries, False)
    out[...] = best[:, :TOPK]

    for k in range(1, nq):
        rcopy(lens, lens_all.at[q], l_s.at[k], l_r.at[q], (rq(k), c)).wait_send()
        rcopy(inv_all.at[q], inv_all.at[q], iv_s.at[k], iv_r.at[q], (rq(k), c)).wait_send()
        rcopy(top_q.at[q], top_q.at[q], tq_s.at[k], tq_r.at[q], (rq(k), c)).wait_send()
        rcopy(t_send, t_recv.at[q], t_s.at[k], t_r.at[q], (rq(k), c)).wait_send()
        rcopy(codes.at[q], codes.at[q], o_s.at[k], o_r.at[q], (rq(k), c)).wait_send()

    @pl.when(q != g)
    def _():
        rcopy(hid, colbuf.at[q], a_s, a_r.at[q], (g, c)).wait_send()

    for i in range(nb):
        @pl.when(sends_up)
        def _(i=i):
            up_chain(i).wait_send()

        @pl.when(sends_down)
        def _(i=i):
            down_chain(i).wait_send()

        for k in range(1, r):
            rcopy(chunk(i, j), chunk(i, j), la_s.at[k, i], la_r.at[j, i], (q, g * r + lane(k))).wait_send()

    def drain(n, carry):
        far_part(n).wait_send()
        near_part(n).wait_send()
        passed_part(n).wait_send()
        h_near(n, 0).wait_send()
        h_near(n, 1).wait_send()
        h_pass(n).wait_send()
        return carry

    lax.fori_loop(0, nch, drain, 0)
    for k in range(1, r):
        rcopy(lsend.at[lane(k)], lrecv.at[j], lr_s.at[k], lr_r.at[j], (q, g * r + lane(k))).wait_send()
    for k in range(1, ng):
        t = lax.rem(g + k, ng)
        rcopy(gsend.at[t], grecv.at[g], g_s.at[k], g_r.at[g], (q, t * r + j)).wait_send()
    for i in range(r):
        @pl.when(c != q * r + i)
        def _(i=i):
            rcopy(pp.at[i], prc.at[c], pp_s.at[i], pp_r.at[c], (q, q * r + i)).wait_send()

    @pl.when(g == q)
    def _():
        for k in range(1, nq):
            rcopy(pblk, pblk, pb_s.at[k], pb_r, (rq(k), c)).wait_send()
    for k in range(1, nc):
        rcopy(cpart, crecv.at[c], c_s.at[k], c_r.at[c], (q, rc(k))).wait_send()
        rcopy(st_send, st_recv.at[c], st_s.at[k], st_r.at[c], (q, rc(k))).wait_send()
        rcopy(top_c.at[c], top_c.at[c], tc_s.at[k], tc_r.at[c], (q, rc(k))).wait_send()


def per_device_general(nq, nc, hidden_in, lengths, gate_weight, up_weight, down_weight, code_weight, corpus_codes):
    slots, w = hidden_in.shape
    r = nc // nq
    nreal = nq * slots * REAL_NUM // REAL_DEN
    tq, tb = nreal // nq, nreal // nc
    dq, ffc = gate_weight.shape
    cw = CHUNK if ffc % CHUNK == 0 else ffc
    nch = ffc // cw
    nb = nreal // PIECE if nreal % PIECE == 0 else nq
    nqueries = nq * lengths.shape[0]
    bits = code_weight.shape[1]
    bw = bits // nq
    ng = nc // r
    lens = jnp.broadcast_to(jnp.repeat(lengths, SEQ)[None, :], (8, slots))
    vm, dma = pltpu.VMEM, pltpu.SemaphoreType.DMA
    scratch = [
        vm(gate_weight.shape, BF16), vm(up_weight.shape, BF16), vm(down_weight.shape, BF16),
        vm(code_weight.shape, BF16), vm(corpus_codes.shape, BF16),
        vm((nq, slots, w), BF16), vm((nq, 8, slots), jnp.int32), vm((r, nreal, w), BF16),
        vm((nch, nq, 2, tq, cw), BF16), vm((nch, nq, 2, tq, cw), BF16),
        vm((8, slots), F32), vm((nc, 8, slots), F32), vm((nq, 8, slots), F32), vm((r, nreal, w), BF16),
        vm((nch, 2, tq, cw), F32), vm((nq, nqueries, LANES), F32), vm((nc, nqueries, LANES), F32),
        vm((nch, nq, tq, cw), BF16), vm((nreal, dq), F32),
        vm((r, ng, tb, dq), BF16), vm((r, ng, tb, dq), BF16), vm((ng, tb, dq), BF16), vm((ng, tb, dq), BF16),
        vm((tb, 128), F32), vm((nq, tb, 128), F32),
        vm((r, nqueries, w), F32), vm((nc, nqueries, w), F32), vm((nqueries, w), BF16),
        vm((nqueries, bw), F32), vm((nc, nqueries, bw), F32), vm((nq, nqueries, bw), BF16),
        dma((5,)), dma, dma((nq,)), dma((nq,)), dma((nq,)), dma((2, nb)), dma((nb,)), dma((r, nb)), dma((r, nb)),
        dma((nch, nq)), dma((nch, nq)), dma((nc,)), dma((nc,)), dma((nq,)), dma((nq,)),
        dma((nq,)), dma((nq,)), dma((nc,)), dma((nc,)), dma((nch, nq)), dma((nch, nq)),
        dma((r,)), dma((r,)), dma((ng,)), dma((ng,)), dma((nq,)), dma((nq,)),
        dma((r,)), dma((nc,)), dma((nq,)), dma, dma((nc,)), dma((nc,)), dma((nq,)), dma((nq,)),
    ]
    dims = (nq, nc, r, nreal, tq, tb, nch, cw, w * nc)
    vspec, aspec = pl.BlockSpec(memory_space=pltpu.VMEM), pl.BlockSpec(memory_space=pl.ANY)
    return pl.pallas_call(
        functools.partial(general_kernel, dims),
        out_shape=jax.ShapeDtypeStruct((nqueries, TOPK), F32),
        in_specs=[vspec, vspec] + [aspec] * 5,
        out_specs=vspec,
        scratch_shapes=scratch,
        compiler_params=pltpu.CompilerParams(
            collective_id=0, has_side_effects=True, vmem_limit_bytes=60 * 1024 * 1024),
    )(hidden_in, lens, gate_weight, up_weight, down_weight, code_weight, corpus_codes)


def compare(v, size, step, flip, inner):
    part = len(v)
    sub = lax.broadcasted_iota(jnp.int32, v[0].shape, 0)
    across = step < part if inner else step >= 8
    if size >= LANES:
        up = [0] * part
    elif size < part:
        up = [int((i & size) != 0) for i in range(part)]
    else:
        up = [((sub & (size // part)) != 0).astype(jnp.int32)] * part
    masks = {}

    def high(i, low, name):
        key = (name, up[i] if isinstance(up[i], int) else -1)
        if key not in masks:
            masks[key] = (flip ^ up[i] ^ low) == 0
        return masks[key]

    v = list(v)
    if across:
        hop = step if inner else step // 8
        for i in range(part):
            if i & hop == 0:
                a, b = v[i], v[i | hop]
                most, least = jnp.maximum(a, b), jnp.minimum(a, b)
                pick = high(i, 0, 0)
                v[i], v[i | hop] = jnp.where(pick, most, least), jnp.where(pick, least, most)
        return v
    s = step // part if inner else step
    bit = (sub & s) != 0
    low = bit.astype(jnp.int32)
    for i in range(part):
        x = v[i]
        other = pltpu.roll(x, 4, 0) if s == 4 else jnp.where(bit, pltpu.roll(x, s, 0), pltpu.roll(x, 8 - s, 0))
        v[i] = jnp.where(high(i, low, 1), jnp.maximum(x, other), jnp.minimum(x, other))
    return v


def columns(lists):
    cols = jnp.concatenate([lists] * (LANES // lists.shape[0]), axis=0).T
    return [cols[i:i + 8] for i in range(0, LANES, 8)]


def merge_columns(v, count, rows, lone, inner):
    lane = lax.broadcasted_iota(jnp.int32, v[0].shape, 1)
    half = count // 2
    while half >= rows:
        v = [jnp.maximum(x, pltpu.roll(x, LANES - half, 1)) for x in v]
        if half > rows:
            flip = (lax.rem(lane, half) >= half // 2).astype(jnp.int32)
        else:
            flip = jnp.zeros_like(lane) + jnp.asarray(lone, jnp.int32)
        step = LANES // 2
        while step:
            v = compare(v, LANES, step, flip, inner)
            step //= 2
        half //= 2
    return v


def top_rows(lists, rows, lone, board):
    count = lists.shape[0]
    v = columns(lists)
    lane = lax.broadcasted_iota(jnp.int32, v[0].shape, 1)
    flip = (lax.rem(lane, count) >= count // 2).astype(jnp.int32)
    size = 2
    while size <= LANES:
        step = size // 2
        while step:
            v = compare(v, size, step, flip, True)
            step //= 2
        size *= 2
    v = merge_columns(v, count, rows, lone, True)
    for i, x in enumerate(v):
        board[pl.ds(i, 8, stride=len(v)), :] = x
    return board[...].T[:rows]


def merge_rows(lists, rows, lone):
    v = merge_columns(columns(lists), lists.shape[0], rows, lone, False)
    return jnp.concatenate(v, axis=0).T[:rows]


def fast_kernel(dims, names, hid, lens, gate_h, up_h, down_h, code_h, corp_h, out, *refs):
    nq, nc, r, nblk, bm, nh, hw, d_all = dims
    s = types.SimpleNamespace(**dict(zip(names, refs)))
    q = lax.axis_index("query")
    c = lax.axis_index("corpus")
    g = c // r
    j = lax.rem(c, r)
    ng = nc // r
    slots, w = hid.shape
    total = nq * slots
    nqueries = total // SEQ
    nreal = nblk * bm
    qm, lm, pm = bm // nq, bm // r, bm // nc
    nu = nblk * nh
    bw = s.codew.shape[2] // nq
    gate, up, code, corp = s.gu.at[0], s.gu.at[1], s.codew.at[0], s.codew.at[1]

    fq = w // nq
    for i in range(nq):
        pltpu.make_async_copy(hid.at[:, pl.ds(i * fq, fq)], s.hidq.at[i], s.w_s.at[0]).start()
    counts = pltpu.make_async_copy(lens, s.lens_s, s.w_s.at[1])
    counts.start()
    for a, b, k in ((gate_h, gate, 2), (up_h, up, 2), (down_h, s.down, 3), (code_h, code, 4), (corp_h, corp, 4)):
        pltpu.make_async_copy(a, b, s.w_s.at[k]).start()

    def loaded(ref, k):
        pltpu.make_async_copy(ref, ref, s.w_s.at[k]).wait()

    def rq(k):
        return lax.rem(q + k, nq)

    def rc(k):
        return lax.rem(c + k, nc)

    def lane(k):
        return lax.rem(j + k, r)

    def got(ref, sem):
        rcopy(ref, ref, sem, sem, (rq(1), c)).wait_recv()

    def sent(ref, sem):
        rcopy(ref, ref, sem, sem, (rq(1), c)).wait_send()

    def to_query(src, ref, ss, rs):
        for k in range(1, nq):
            rcopy(src, ref.at[q], ss, rs, (rq(k), c)).start()

    def to_corpus(src, ref, ss, rs):
        for k in range(1, nc):
            rcopy(src, ref.at[c], ss, rs, (q, rc(k))).start()

    barrier = pltpu.get_barrier_semaphore()
    for k in range(1, nq):
        pl.semaphore_signal(barrier, inc=1, device_id=(rq(k), c), device_id_type=pl.DeviceIdType.MESH)
    for k in range(1, nc):
        pl.semaphore_signal(barrier, inc=1, device_id=(q, rc(k)), device_id_type=pl.DeviceIdType.MESH)

    loaded(s.hidq, 0)
    squares = jnp.square(s.hidq[0].astype(F32))
    for i in range(1, nq):
        squares = squares + jnp.square(s.hidq[i].astype(F32))
    s.st_send[...] = lax.dot_general(jnp.ones((8, fq), F32), squares, (((1,), (1,)), ((), ())),
                                     precision=lax.Precision.HIGHEST, preferred_element_type=F32)
    counts.wait()
    slot_query = lax.broadcasted_iota(jnp.int32, (8, slots), 1) // SEQ
    own_lens = jnp.zeros((8, slots), jnp.int32)
    for k in range(slots // SEQ):
        own_lens = jnp.where(slot_query == k, s.lens_s[k], own_lens)
    s.lens_all[q] = own_lens

    pl.semaphore_wait(barrier, nq - 1 + nc - 1)

    side_a = q + 1 - 2 * lax.rem(q, 2)
    side_b = q + 2 - 4 * (q // 2)
    far = nq - 1 - q

    for k in range(1, nq):
        rcopy(s.hidq.at[rq(k)], s.colbuf.at[q], s.a_s, s.a_r, (rq(k), c)).start()
    s.colbuf[q] = s.hidq[q]

    to_query(s.lens_all.at[q], s.lens_all, s.l_s, s.l_r)
    to_corpus(s.st_send, s.st_recv, s.st_s, s.st_r)
    s.st_recv[c] = s.st_send[...]
    got(s.lens_all.at[pl.ds(0, nq - 1)], s.l_r)
    lens_row = jnp.concatenate([s.lens_all[i] for i in range(nq)], axis=1)
    slot = lax.broadcasted_iota(jnp.int32, (8, total), 1)
    valid = lax.rem(slot, SEQ) < lens_row
    before = lax.broadcasted_iota(jnp.int32, (total, total), 0) < lax.broadcasted_iota(jnp.int32, (total, total), 1)
    pos = mm(valid.astype(F32).astype(BF16), before.astype(F32).astype(BF16)).astype(jnp.int32)
    pos = jnp.where(valid, pos, -1)[:1]

    got(s.st_recv.at[pl.ds(0, nc - 1)], s.st_r)
    stat = s.st_recv[0]
    for i in range(1, nc):
        stat = stat + s.st_recv[i]
    s.inv_all[q] = lax.rsqrt(stat / d_all + epsilon)
    to_query(s.inv_all.at[q], s.inv_all, s.iv_s, s.iv_r)

    def side(b, k):
        return rcopy(s.xall.at[j, b], s.xall.at[j, b], s.la_s, s.la_r.at[b], (q, g * r + lane(k)))

    def spread(b, k):
        t = lax.rem(g + k, ng)
        return rcopy(s.xpk.at[b], s.xall.at[j, b, q], s.x_s, s.x_r.at[b], (g, t * r + j))

    got(s.colbuf.at[pl.ds(0, nq - 1)], s.a_r)
    stacked = s.colbuf[...].reshape(total, fq)
    for b in range(nblk):
        row = lax.broadcasted_iota(jnp.int32, (bm, total), 0) + b * bm
        pick = (pos == row).astype(F32).astype(BF16)
        s.xpk[b] = mm(pick, stacked).astype(BF16)
        for k in range(ng - 1, 0, -1):
            spread(b, k).start()

        @pl.when(q != g)
        def _(b=b):
            spread(b, 0).start()

        @pl.when(q == g)
        def _(b=b):
            s.xall[j, b, q] = s.xpk[b]

    got(s.inv_all.at[pl.ds(0, nq - 1)], s.iv_r)
    inv_row = jnp.concatenate([s.inv_all[i] for i in range(nq)], axis=1)[:1]
    for b in range(nblk):
        row = lax.broadcasted_iota(jnp.int32, (bm, total), 0) + b * bm
        col = jnp.sum(jnp.where(pos == row, inv_row, 0.0), axis=1, keepdims=True)
        s.inv_c[b] = jnp.broadcast_to(col, (bm, LANES))

    loaded(s.gu, 2)

    def sides(n):
        odd = lax.rem(n, 2)
        return side_a + (side_b - side_a) * odd, side_b + (side_a - side_b) * odd

    def near_part(n):
        one, _ = sides(n)
        return rcopy(s.psend.at[n, one], s.precv.at[n, 0], s.p_s, s.p_r.at[n], (one, c))

    def far_part(n):
        one, _ = sides(n)
        return rcopy(s.psend.at[n, far], s.precv.at[n, 2], s.p_s, s.pf_r.at[n], (one, c))

    def passed_part(n):
        _, two = sides(n)
        return rcopy(s.precv.at[n, 3], s.precv.at[n, 1], s.p_s, s.p_r.at[n], (two, c))

    def h_near(n, k, sem):
        return rcopy(s.hall.at[n, q], s.hall.at[n, q], s.h_s, sem, (sides(n)[k], c))

    def h_pass(n, sem):
        one, two = sides(n)
        return rcopy(s.hall.at[n, one], s.hall.at[n, one], s.h_s, sem, (two, c))

    def fetch(b):
        @pl.when(q != g)
        def _():
            got(s.xall.at[0, b], s.x_r.at[b])

        @pl.when(q == g)
        def _():
            got(s.xall.at[0, b, pl.ds(0, nq - 1)], s.x_r.at[b])

        for k in range(1, r):
            side(b, k).start()

    def products(b):
        got(s.xall.at[pl.ds(0, r - 1), b], s.la_r.at[b])
        scale = s.inv_c[b][:, :1]
        for i in range(r):
            for k in range(nq):
                at = i * w + k * fq
                s.xn[:, at:at + fq] = (s.xall[i, b, k].astype(F32) * scale).astype(BF16)
        xb = s.xn[...]
        for h in range(nh):
            n = b * nh + h
            for e, wref in enumerate((gate, up)):
                full = mm(xb, wref[:, h * hw:(h + 1) * hw])
                s.full[h, e] = full
                for i in range(nq):
                    s.psend[n, i, e] = full[i * qm:(i + 1) * qm].astype(BF16)
            far_part(n).start()
            near_part(n).start()
            for e in range(2):
                s.pown[n, e] = s.full[h, e, pl.ds(pl.multiple_of(q * qm, qm), qm)]

    def pass_unit(n):
        _, two = sides(n)
        got(s.precv.at[n, 2], s.pf_r.at[n])
        s.precv[n, 3] = (s.psend[n, two].astype(F32) + s.precv[n, 2].astype(F32)).astype(BF16)
        passed_part(n).start()

    def reduce_unit(n):
        got(s.precv.at[n, pl.ds(0, 2)], s.p_r.at[n])
        gsum = s.pown[n, 0] + s.precv[n, 0, 0].astype(F32) + s.precv[n, 1, 0].astype(F32)
        usum = s.pown[n, 1] + s.precv[n, 0, 1].astype(F32) + s.precv[n, 1, 1].astype(F32)
        s.hall[n, q] = (gsum / (1.0 + jnp.exp(-gsum)) * usum).astype(BF16)
        h_near(n, 0, s.hn_r.at[n]).start()
        h_near(n, 1, s.hb_r.at[n // nh]).start()

    def relay_unit(n):
        got(s.hall.at[n, 0], s.hn_r.at[n])
        h_pass(n, s.hb_r.at[n // nh]).start()

    def lane_send(b, k):
        t = lane(k)
        return rcopy(s.lsend.at[b, t], s.lrecv.at[b, j], s.lr_s, s.lr_r.at[b], (q, g * r + t))

    def group_send(b, k):
        t = lax.rem(g + k, ng)
        return rcopy(s.gsend.at[b, t], s.grecv.at[b, g], s.g_s, s.g_r.at[b], (q, t * r + j))

    def down_block(b):
        part = None
        got(s.hall.at[pl.ds(b * nh, nh), pl.ds(0, 2)], s.hb_r.at[b])
        for h in range(nh):
            n = b * nh + h
            term = mm(s.hall[n].reshape(bm, hw), s.down[h * hw:(h + 1) * hw, :])
            part = term if part is None else part + term
        for t in range(r):
            s.lsend[b, t] = part[t * lm:(t + 1) * lm].astype(BF16)
        for k in range(1, r):
            lane_send(b, k).start()

    def sum_block(b):
        mine = s.lsend[b, j].astype(F32)
        got(s.lrecv.at[b, pl.ds(0, r - 1)], s.lr_r.at[b])
        for k in range(1, r):
            mine = mine + s.lrecv[b, lane(k)].astype(F32)
        for t in range(ng):
            s.gsend[b, t] = mine[t * pm:(t + 1) * pm].astype(BF16)
        for k in range(1, ng):
            group_send(b, k).start()

    def units(unit, b):
        for h in range(nh):
            unit(b * nh + h)

    def fetch_next(b):
        @pl.when(b + 1 < nblk)
        def _():
            fetch(b + 1)

    fetch(0)
    stages = (products, fetch_next, functools.partial(units, pass_unit), functools.partial(units, reduce_unit),
              functools.partial(units, relay_unit), down_block, sum_block)
    delays = (0, 0, 1, 2, 3, 4, 5)

    def turn(t, carry):
        for stage, delay in zip(stages, delays):
            @pl.when(jnp.logical_and(t >= delay, t < nblk + delay))
            def _(stage=stage, delay=delay):
                stage(t - delay)
        return carry

    loaded(s.down, 3)
    lax.fori_loop(0, nblk + delays[-1], turn, 0)
    row = lax.broadcasted_iota(jnp.int32, (nblk * pm, nreal), 0)
    row = (row // pm) * bm + (j * ng + g) * pm + lax.rem(row, pm)
    own_rows = (lax.broadcasted_iota(jnp.int32, (nblk * pm, nreal), 1) == row).astype(F32).astype(BF16)
    for i in range(r):
        for k in range(nq):
            at = i * w + k * fq
            s.res[:, at:at + fq] = mm(own_rows, s.xall[i, :, k].reshape(nreal, fq))

    for b in range(nblk):
        total_b = s.gsend[b, g].astype(F32)
        got(s.grecv.at[b, pl.ds(0, ng - 1)], s.g_r.at[b])
        for k in range(1, ng):
            total_b = total_b + s.grecv[b, lax.rem(g + k, ng)].astype(F32)
        s.res[b * pm:(b + 1) * pm, :] = s.res[b * pm:(b + 1) * pm, :] + total_b
    residual = s.res[...]
    tb = nblk * pm

    s.t_send[...] = jnp.broadcast_to(jnp.sum(residual * residual, axis=1, keepdims=True), (tb, LANES))
    to_query(s.t_send, s.t_recv, s.t_s, s.t_r)
    qrow = lax.broadcasted_iota(jnp.int32, (nqueries, total), 0)
    qslot = lax.broadcasted_iota(jnp.int32, (nqueries, total), 1)
    lens_b = jnp.broadcast_to(lens_row[:1], (nqueries, total)).astype(F32)
    vals_b = jnp.broadcast_to(valid.astype(F32)[:1], (nqueries, total))
    len_col = jnp.sum(jnp.where(qslot == qrow * SEQ, lens_b, 0.0), axis=1, keepdims=True)
    off_col = jnp.sum(jnp.where(qslot < qrow * SEQ, vals_b, 0.0), axis=1, keepdims=True)
    prow = lax.broadcasted_iota(jnp.int32, (nqueries, tb), 1)
    prow = ((prow // pm) * bm + (j * ng + g) * pm + lax.rem(prow, pm)).astype(F32)
    member = jnp.where(jnp.logical_and(prow >= off_col, prow < off_col + len_col), 1.0, 0.0)
    tsum = s.t_send[...]
    got(s.t_recv.at[pl.ds(0, nq - 1)], s.t_r)
    for k in range(1, nq):
        tsum = tsum + s.t_recv[rq(k)]
    final = residual * lax.rsqrt(tsum[:, :1] / d_all + epsilon)
    pooled_part = mm(member, final, lax.Precision.HIGHEST)
    for i in range(r):
        s.pp[i] = pooled_part[:, i * w:(i + 1) * w].astype(BF16)
    for i in range(r):
        @pl.when(c != q * r + i)
        def _(i=i):
            rcopy(s.pp.at[i], s.prc.at[c], s.pp_s, s.pp_r, (q, q * r + i)).start()

    @pl.when(g == q)
    def _():
        pooled = s.pp[j].astype(F32)
        got(s.prc.at[pl.ds(0, nc - 1)], s.pp_r)
        for k in range(1, nc):
            pooled = pooled + s.prc[rc(k)].astype(F32)
        s.pblk[0] = (pooled / len_col).astype(BF16)
        for k in range(1, nq):
            rcopy(s.pblk.at[0], s.pblk.at[0], s.pb_s, s.pb_r, (rq(k), c)).start()

    loaded(s.codew, 4)

    @pl.when(g != q)
    def _():
        got(s.pblk.at[0], s.pb_r)

    s.cpart[...] = mm(s.pblk[0], code[:, pl.ds(pl.multiple_of(q * bw, bw), bw)])
    to_corpus(s.cpart, s.crecv, s.c_s, s.c_r)
    s.crecv[c] = s.cpart[...]
    got(s.crecv.at[pl.ds(0, nc - 1)], s.c_r)
    csum = s.crecv[0]
    for i in range(1, nc):
        csum = csum + s.crecv[i]
    s.codes[q] = csum.astype(BF16)
    to_query(s.codes.at[q], s.codes, s.o_s, s.o_r)
    got(s.codes.at[pl.ds(0, nq - 1)], s.o_r)
    qcodes = jnp.concatenate([s.codes[i] for i in range(nq)], axis=1)
    scale = 1.0 / math.sqrt(corp.shape[1])
    scores = lax.dot_general(qcodes, corp[...], (((1,), (1,)), ((), ())), preferred_element_type=F32) * scale

    blocks = corp.shape[0] // LANES
    lists = jnp.concatenate([scores[:, i * LANES:(i + 1) * LANES] for i in range(blocks)], axis=0)
    best = top_rows(lists, nqueries, q >= nq // 2, s.board)
    s.top_q[q] = best
    to_query(s.top_q.at[q], s.top_q, s.tq_s, s.tq_r)
    got(s.top_q.at[pl.ds(0, nq - 1)], s.tq_r)
    best = merge_rows(s.top_q[...].reshape(nq * nqueries, LANES), nqueries, c >= nc // 2)
    s.top_c[c] = best
    to_corpus(s.top_c.at[c], s.top_c, s.tc_s, s.tc_r)
    got(s.top_c.at[pl.ds(0, nc - 1)], s.tc_r)
    best = merge_rows(s.top_c[...].reshape(nc * nqueries, LANES), nqueries, False)
    out[...] = best[:, :TOPK]

    sent(s.lens_all.at[pl.ds(0, nq - 1)], s.l_s)
    sent(s.st_recv.at[pl.ds(0, nc - 1)], s.st_s)
    sent(s.inv_all.at[pl.ds(0, nq - 1)], s.iv_s)

    sent(s.colbuf.at[pl.ds(0, nq - 1)], s.a_s)

    @pl.when(q != g)
    def _():
        sent(s.xall.at[0], s.x_s)

    @pl.when(q == g)
    def _():
        sent(s.xall.at[0, :, pl.ds(0, nq - 1)], s.x_s)

    sent(s.xall.at[pl.ds(0, r - 1)], s.la_s)
    sent(s.psend.at[:, pl.ds(0, 3)], s.p_s)
    sent(s.hall.at[:, pl.ds(0, 3)], s.h_s)
    sent(s.lsend.at[:, pl.ds(0, r - 1)], s.lr_s)
    sent(s.gsend.at[:, pl.ds(0, ng - 1)], s.g_s)
    sent(s.t_recv.at[pl.ds(0, nq - 1)], s.t_s)

    @pl.when(g == q)
    def _():
        sent(s.pp.at[pl.ds(0, r - 1)], s.pp_s)
        sent(s.pblk.at[pl.ds(0, nq - 1)], s.pb_s)

    @pl.when(g != q)
    def _():
        sent(s.pp, s.pp_s)

    sent(s.crecv.at[pl.ds(0, nc - 1)], s.c_s)
    sent(s.codes.at[pl.ds(0, nq - 1)], s.o_s)
    sent(s.top_q.at[pl.ds(0, nq - 1)], s.tq_s)
    sent(s.top_c.at[pl.ds(0, nc - 1)], s.tc_s)


def halves_of(ffc):
    return 2 if ffc % (2 * LANES) == 0 else 1


def per_device_fast(nq, nc, hidden_in, lengths, gate_weight, up_weight, down_weight, code_weight, corpus_codes):
    slots, w = hidden_in.shape
    r = nc // nq
    ng = nc // r
    nreal = nq * slots * REAL_NUM // REAL_DEN
    dq, ffc = gate_weight.shape
    bm = 8 * nc
    nblk = nreal // bm
    nh = halves_of(ffc)
    hw = ffc // nh
    nu = nblk * nh
    qm, lm, pm = bm // nq, bm // r, bm // nc
    tb = nblk * pm
    nqueries = nq * lengths.shape[0]
    bits = code_weight.shape[1]
    bw = bits // nq
    vm, dma = pltpu.VMEM, pltpu.SemaphoreType.DMA
    scratch = dict(
        gu=vm((2,) + gate_weight.shape, BF16), down=vm(down_weight.shape, BF16), codew=vm((2,) + code_weight.shape, BF16),
        lens_s=pltpu.SMEM(lengths.shape, jnp.int32),
        hidq=vm((nq, slots, w // nq), BF16), colbuf=vm((nq, slots, w // nq), BF16), xpk=vm((nblk, bm, w // nq), BF16), lens_all=vm((nq, 8, slots), jnp.int32), xall=vm((r, nblk, nq, bm, w // nq), BF16),
        xn=vm((bm, dq), BF16), inv_c=vm((nblk, bm, LANES), F32),
        st_send=vm((8, slots), F32), st_recv=vm((nc, 8, slots), F32), inv_all=vm((nq, 8, slots), F32),
        psend=vm((nu, nq, 2, qm, hw), BF16), precv=vm((nu, 4, 2, qm, hw), BF16), pown=vm((nu, 2, qm, hw), F32), full=vm((nh, 2, bm, hw), F32),
        hall=vm((nu, nq, qm, hw), BF16),
        lsend=vm((nblk, r, lm, dq), BF16), lrecv=vm((nblk, r, lm, dq), BF16),
        gsend=vm((nblk, ng, pm, dq), BF16), grecv=vm((nblk, ng, pm, dq), BF16), res=vm((tb, dq), F32),
        t_send=vm((tb, LANES), F32), t_recv=vm((nq, tb, LANES), F32),
        pp=vm((r, nqueries, w), BF16), prc=vm((nc, nqueries, w), BF16), pblk=vm((nq, nqueries, w), BF16),
        cpart=vm((nqueries, bw), F32), crecv=vm((nc, nqueries, bw), F32), codes=vm((nq, nqueries, bw), BF16),
        top_q=vm((nq, nqueries, LANES), F32), top_c=vm((nc, nqueries, LANES), F32), board=vm((LANES, LANES), F32),
        w_s=dma((5,)), l_s=dma, l_r=dma, a_s=dma, a_r=dma, st_s=dma, st_r=dma, iv_s=dma, iv_r=dma,
        x_s=dma, x_r=dma((nblk,)), la_s=dma, la_r=dma((nblk,)),
        p_s=dma, p_r=dma((nu,)), pf_r=dma((nu,)), h_s=dma, hn_r=dma((nu,)), hb_r=dma((nblk,)),
        lr_s=dma, lr_r=dma((nblk,)), g_s=dma, g_r=dma((nblk,)),
        t_s=dma, t_r=dma, pp_s=dma, pp_r=dma, pb_s=dma, pb_r=dma, c_s=dma, c_r=dma, o_s=dma, o_r=dma,
        tq_s=dma, tq_r=dma, tc_s=dma, tc_r=dma,
    )
    dims = (nq, nc, r, nblk, bm, nh, hw, w * nc)
    vspec, aspec = pl.BlockSpec(memory_space=pltpu.VMEM), pl.BlockSpec(memory_space=pl.ANY)
    return pl.pallas_call(
        functools.partial(fast_kernel, dims, tuple(scratch)),
        out_shape=jax.ShapeDtypeStruct((nqueries, TOPK), F32),
        in_specs=[aspec] * 7,
        out_specs=vspec,
        scratch_shapes=list(scratch.values()),
        compiler_params=pltpu.CompilerParams(
            collective_id=0, has_side_effects=True, vmem_limit_bytes=60 * 1024 * 1024),
    )(hidden_in, lengths, gate_weight, up_weight, down_weight, code_weight, corpus_codes)


def per_device(nq, nc, hidden_in, *rest):
    slots, w = hidden_in.shape
    nreal = nq * slots * REAL_NUM // REAL_DEN
    nqueries = nq * rest[0].shape[0]
    lists = nqueries * max(nc, nq, rest[5].shape[0] // LANES)
    fits = lists <= LANES and LANES % lists == 0 and nreal % (8 * nc) == 0 and w % (nq * LANES) == 0 and rest[4].shape == rest[5].shape
    body = per_device_fast if fits else per_device_general
    return body(nq, nc, hidden_in, *rest)


def solution(mesh):
    in_specs = (
        P("query", "corpus"),
        P("query"),
        P("query", "corpus"),
        P("query", "corpus"),
        P("corpus", "query"),
        P("corpus", None),
        P(("query", "corpus"), None),
    )
    body = functools.partial(per_device, mesh.shape["query"], mesh.shape["corpus"])
    return jax.shard_map(body, mesh=mesh, in_specs=in_specs, out_specs=P(), check_vma=False)
```

```python
import functools
import math
import types

import jax
import jax.numpy as jnp
from jax import lax
from jax.experimental import pallas as pl
from jax.experimental.pallas import tpu as pltpu
from jax.sharding import PartitionSpec as P

SEQ = 32
LANES = 128
TOPK = 100
REAL_NUM, REAL_DEN = 5, 8
CHUNK = 256
PIECE = 32

epsilon = 1e-05
F32, BF16 = jnp.float32, jnp.bfloat16


def mm(a, b, precision=None):
    return lax.dot_general(a, b, (((1,), (0,)), ((), ())), precision=precision, preferred_element_type=F32)


def rcopy(src, dst, send, recv, dev):
    return pltpu.make_async_remote_copy(
        src_ref=src, dst_ref=dst, send_sem=send, recv_sem=recv,
        device_id=dev, device_id_type=pl.DeviceIdType.MESH)


def exchange(x, s, keep_max):
    bit = (lax.broadcasted_iota(jnp.int32, x.shape, 1) & s) != 0
    other = jnp.where(bit, pltpu.roll(x, s, 1), pltpu.roll(x, LANES - s, 1))
    return jnp.where(keep_max, jnp.maximum(x, other), jnp.minimum(x, other))


def sort_lanes(x):
    lane = lax.broadcasted_iota(jnp.int32, x.shape, 1)
    flip = (lax.broadcasted_iota(jnp.int32, x.shape, 0) >= x.shape[0] // 2).astype(jnp.int32)
    size = 2
    while size <= LANES:
        up = ((lane & size) != 0).astype(jnp.int32) if size < LANES else jnp.zeros_like(lane)
        s = size // 2
        while s:
            low = ((lane & s) != 0).astype(jnp.int32)
            x = exchange(x, s, (low ^ up ^ flip) == 0)
            s //= 2
        size *= 2
    return x


def merge_all(x, rows, lone):
    while x.shape[0] > rows:
        half = x.shape[0] // 2
        x = jnp.maximum(x[:half], x[half:])
        lane = lax.broadcasted_iota(jnp.int32, x.shape, 1)
        if half > rows:
            flip = (lax.broadcasted_iota(jnp.int32, x.shape, 0) >= half // 2).astype(jnp.int32)
        else:
            flip = jnp.zeros_like(lane) + jnp.asarray(lone, jnp.int32)
        s = LANES // 2
        while s:
            low = ((lane & s) != 0).astype(jnp.int32)
            x = exchange(x, s, (low ^ flip) == 0)
            s //= 2
    return x


def general_kernel(dims, hid, lens, gate_h, up_h, down_h, code_h, corp_h, out,
                 gate, up, down, code, corp, colbuf, lens_all, xall, psend, precv,
                 st_send, st_recv, inv_all, xn, pown, top_q, top_c, hall, acc, lsend, lrecv, gsend, grecv, t_send, t_recv,
                 pp, prc, pblk, cpart, crecv, codes,
                 w_s, a_s, a_r, l_s, l_r, ch_s, ch_r, la_s, la_r, p_s, p_r, st_s, st_r, iv_s, iv_r, tq_s, tq_r, tc_s, tc_r, h_s, h_r,
                 lr_s, lr_r, g_s, g_r, t_s, t_r, pp_s, pp_r, pb_s, pb_r, c_s, c_r, o_s, o_r):
    nq, nc, r, nreal, tq, tb, nch, cw, d_all = dims
    q = lax.axis_index("query")
    c = lax.axis_index("corpus")
    g = c // r
    j = lax.rem(c, r)
    slots, w = hid.shape[0], hid.shape[1]
    total = nq * slots
    nqueries = total // SEQ
    bw = code.shape[1] // nq

    loads = []
    for i, (s, d) in enumerate(((gate_h, gate), (up_h, up), (down_h, down), (code_h, code), (corp_h, corp))):
        cp = pltpu.make_async_copy(s, d, w_s.at[i])
        cp.start()
        loads.append(cp)

    def rq(k):
        return lax.rem(q + k, nq)

    def rc(k):
        return lax.rem(c + k, nc)

    def lane(k):
        return lax.rem(j + k, r)

    barrier = pltpu.get_barrier_semaphore()
    for k in range(1, nq):
        pl.semaphore_signal(barrier, inc=1, device_id=(rq(k), c), device_id_type=pl.DeviceIdType.MESH)
    for k in range(1, nc):
        pl.semaphore_signal(barrier, inc=1, device_id=(q, rc(k)), device_id_type=pl.DeviceIdType.MESH)
    pl.semaphore_wait(barrier, nq - 1 + nc - 1)

    for k in range(1, nq):
        rcopy(lens, lens_all.at[q], l_s.at[k], l_r.at[q], (rq(k), c)).start()

    @pl.when(q != g)
    def _():
        rcopy(hid, colbuf.at[q], a_s, a_r.at[q], (g, c)).start()

    squares = jnp.square(hid[...].astype(F32))
    st_send[...] = lax.dot_general(jnp.ones((8, w), F32), squares, (((1,), (1,)), ((), ())),
                                   precision=lax.Precision.HIGHEST, preferred_element_type=F32)
    for k in range(1, nc):
        rcopy(st_send, st_recv.at[c], st_s.at[k], st_r.at[c], (q, rc(k))).start()
    st_recv[c] = st_send[...]
    lens_all[q] = lens[...]
    for k in range(1, nq):
        s = rq(k)
        rcopy(lens, lens_all.at[s], l_s.at[k], l_r.at[s], (s, c)).wait_recv()
    lens_row = jnp.concatenate([lens_all[i] for i in range(nq)], axis=1)
    slot = lax.broadcasted_iota(jnp.int32, (8, total), 1)
    valid = lax.rem(slot, SEQ) < lens_row
    before = lax.broadcasted_iota(jnp.int32, (total, total), 0) < lax.broadcasted_iota(jnp.int32, (total, total), 1)
    pos = mm(valid.astype(F32).astype(BF16), before.astype(F32).astype(BF16)).astype(jnp.int32)
    pos = jnp.where(valid, pos, -1)[:1]

    for k in range(1, nc):
        s = rc(k)
        rcopy(st_send, st_recv.at[s], st_s.at[k], st_r.at[s], (q, s)).wait_recv()
    stat = st_recv[0]
    for i in range(1, nc):
        stat = stat + st_recv[i]
    inv_all[q] = lax.rsqrt(stat / d_all + epsilon)
    for k in range(1, nq):
        rcopy(inv_all.at[q], inv_all.at[q], iv_s.at[k], iv_r.at[q], (rq(k), c)).start()

    nb = ch_r.shape[0]
    ct = nreal // nb

    def chunk(i, slot_j):
        return xall.at[slot_j, pl.ds(i * ct, ct)]

    def down_chain(i):
        return rcopy(chunk(i, j), chunk(i, j), ch_s.at[0, i], ch_r.at[i], (q, jnp.maximum(c - r, 0)))

    def up_chain(i):
        return rcopy(chunk(i, j), chunk(i, j), ch_s.at[1, i], ch_r.at[i], (q, jnp.minimum(c + r, nc - 1)))

    sends_up = jnp.logical_and(g >= q, g < nc // r - 1)
    sends_down = jnp.logical_and(g <= q, g > 0)

    @pl.when(q == g)
    def _():
        colbuf[q] = hid[...]
        for k in range(1, nq):
            s = rq(k)
            rcopy(hid, colbuf.at[s], a_s, a_r.at[s], (s, c)).wait_recv()
        stacked = colbuf[...].reshape(total, w)
        for i in range(nq):
            row = lax.broadcasted_iota(jnp.int32, (tq, total), 0) + i * tq
            pick = (pos == row).astype(F32).astype(BF16)
            xall[j, i * tq:(i + 1) * tq, :] = mm(pick, stacked).astype(BF16)

    for i in range(nb):
        @pl.when(q != g)
        def _(i=i):
            up_chain(i).wait_recv()

        @pl.when(sends_up)
        def _(i=i):
            up_chain(i).start()

        @pl.when(sends_down)
        def _(i=i):
            down_chain(i).start()

        for k in range(1, r):
            rcopy(chunk(i, j), chunk(i, j), la_s.at[k, i], la_r.at[j, i], (q, g * r + lane(k))).start()
    for k in range(1, nq):
        s = rq(k)
        rcopy(inv_all.at[s], inv_all.at[s], iv_s.at[k], iv_r.at[s], (s, c)).wait_recv()
    inv_row = jnp.concatenate([inv_all[i] for i in range(nq)], axis=1)[:1]
    inv_cols = []
    for i in range(nq):
        row = lax.broadcasted_iota(jnp.int32, (tq, total), 0) + i * tq
        inv_cols.append(jnp.sum(jnp.where(pos == row, inv_row, 0.0), axis=1, keepdims=True))
    inv = jnp.concatenate(inv_cols, axis=0)
    for i in range(nb):
        for k in range(1, r):
            s = lane(k)
            rcopy(chunk(i, s), chunk(i, s), la_s.at[k, i], la_r.at[s, i], (q, g * r + s)).wait_recv()

    loads[0].wait()
    loads[1].wait()

    for i in range(r):
        xn[i] = (xall[i].astype(F32) * inv).astype(BF16)

    side_a = q + 1 - 2 * lax.rem(q, 2)
    side_b = q + 2 - 4 * (q // 2)
    far = nq - 1 - q

    def sides(n):
        odd = lax.rem(n, 2)
        return side_a + (side_b - side_a) * odd, side_b + (side_a - side_b) * odd

    def near_part(n):
        one, _ = sides(n)
        return rcopy(psend.at[n, one], precv.at[n, 0], p_s.at[n, 0], p_r.at[n, 0], (one, c))

    def far_part(n):
        one, _ = sides(n)
        return rcopy(psend.at[n, far], precv.at[n, 1], p_s.at[n, 1], p_r.at[n, 1], (one, c))

    def passed_part(n):
        _, two = sides(n)
        return rcopy(precv.at[n, 3], precv.at[n, 2], p_s.at[n, 2], p_r.at[n, 2], (two, c))

    def h_near(n, k):
        to = sides(n)[k]
        return rcopy(hall.at[n, q], hall.at[n, q], h_s.at[n, k], h_r.at[n, k], (to, c))

    def h_near_in(n, k):
        to = sides(n)[k]
        return rcopy(hall.at[n, to], hall.at[n, to], h_s.at[n, k], h_r.at[n, k], (to, c))

    def h_pass(n):
        one, two = sides(n)
        return rcopy(hall.at[n, one], hall.at[n, one], h_s.at[n, 2], h_r.at[n, 2], (two, c))

    def h_pass_in(n):
        _, two = sides(n)
        return rcopy(hall.at[n, far], hall.at[n, far], h_s.at[n, 2], h_r.at[n, 2], (two, c))

    def matmuls(n, carry):
        cols = pl.ds(pl.multiple_of(n * cw, cw), cw)
        for e, wref in enumerate((gate, up)):
            full = sum(mm(xn[i], wref[i * w:(i + 1) * w, cols]) for i in range(r))
            for i in range(nq):
                psend[n, i, e] = full[i * tq:(i + 1) * tq].astype(BF16)

                @pl.when(q == i)
                def _(i=i, e=e, full=full):
                    pown[n, e] = full[i * tq:(i + 1) * tq]
        far_part(n).start()
        near_part(n).start()
        return carry

    lax.fori_loop(0, nch, matmuls, 0)

    loads[2].wait()
    acc[...] = jnp.zeros_like(acc)

    def pass_chunk(n):
        _, two = sides(n)
        far_part(n).wait_recv()
        precv[n, 3] = (psend[n, two].astype(F32) + precv[n, 1].astype(F32)).astype(BF16)
        passed_part(n).start()

    def reduce_chunk(n):
        near_part(n).wait_recv()
        passed_part(n).wait_recv()
        gsum = pown[n, 0] + precv[n, 0, 0].astype(F32) + precv[n, 2, 0].astype(F32)
        usum = pown[n, 1] + precv[n, 0, 1].astype(F32) + precv[n, 2, 1].astype(F32)
        hall[n, q] = (gsum / (1.0 + jnp.exp(-gsum)) * usum).astype(BF16)
        h_near(n, 0).start()
        h_near(n, 1).start()

    def relay_chunk(n):
        h_near_in(n, 0).wait_recv()
        h_pass(n).start()

    def down_chunk(n):
        h_near_in(n, 1).wait_recv()
        h_pass_in(n).wait_recv()
        acc[...] += mm(hall[n].reshape(nreal, cw), down[pl.ds(pl.multiple_of(n * cw, cw), cw), :])

    def passes(n, carry):
        pass_chunk(n)
        return carry

    lax.fori_loop(0, nch, passes, 0)
    reduce_chunk(0)

    def reduces(n, carry):
        reduce_chunk(n)
        relay_chunk(n - 1)
        return carry

    lax.fori_loop(1, nch, reduces, 0)
    relay_chunk(nch - 1)

    def downs(n, carry):
        down_chunk(n)
        return carry

    lax.fori_loop(0, nch, downs, 0)

    ng = nc // r
    for gg in range(ng):
        for jj in range(r):
            b = gg * r + jj
            lsend[jj, gg] = acc[b * tb:(b + 1) * tb].astype(BF16)
    for k in range(1, r):
        t = lane(k)
        rcopy(lsend.at[t], lrecv.at[j], lr_s.at[k], lr_r.at[j], (q, g * r + t)).start()
    mine = lsend[j].astype(F32)
    for k in range(1, r):
        s = lane(k)
        rcopy(lsend.at[s], lrecv.at[s], lr_s.at[k], lr_r.at[s], (q, g * r + s)).wait_recv()
        mine = mine + lrecv[s].astype(F32)
    gsend[...] = mine.astype(BF16)
    for k in range(1, ng):
        t = lax.rem(g + k, ng)
        rcopy(gsend.at[t], grecv.at[g], g_s.at[k], g_r.at[g], (q, t * r + j)).start()
    row = lax.broadcasted_iota(jnp.int32, (tb, nreal), 0) + c * tb
    own_rows = (lax.broadcasted_iota(jnp.int32, (tb, nreal), 1) == row).astype(F32).astype(BF16)
    residual = jnp.concatenate([mm(own_rows, xall[i]) for i in range(r)], axis=1)
    residual = residual + gsend[g].astype(F32)
    for k in range(1, ng):
        s = lax.rem(g + k, ng)
        rcopy(gsend.at[s], grecv.at[s], g_s.at[k], g_r.at[s], (q, s * r + j)).wait_recv()
        residual = residual + grecv[s].astype(F32)

    t_send[...] = jnp.broadcast_to(jnp.sum(residual * residual, axis=1, keepdims=True), (tb, 128))
    for k in range(1, nq):
        rcopy(t_send, t_recv.at[q], t_s.at[k], t_r.at[q], (rq(k), c)).start()
    qrow = lax.broadcasted_iota(jnp.int32, (nqueries, total), 0)
    qslot = lax.broadcasted_iota(jnp.int32, (nqueries, total), 1)
    lens_b = jnp.broadcast_to(lens_row[:1], (nqueries, total)).astype(F32)
    vals_b = jnp.broadcast_to(valid.astype(F32)[:1], (nqueries, total))
    len_col = jnp.sum(jnp.where(qslot == qrow * SEQ, lens_b, 0.0), axis=1, keepdims=True)
    off_col = jnp.sum(jnp.where(qslot < qrow * SEQ, vals_b, 0.0), axis=1, keepdims=True)
    prow = (lax.broadcasted_iota(jnp.int32, (nqueries, tb), 1) + c * tb).astype(F32)
    member = jnp.where(jnp.logical_and(prow >= off_col, prow < off_col + len_col), 1.0, 0.0)
    tsum = t_send[...]
    for k in range(1, nq):
        s = rq(k)
        rcopy(t_send, t_recv.at[s], t_s.at[k], t_r.at[s], (s, c)).wait_recv()
        tsum = tsum + t_recv[s]
    final = residual * lax.rsqrt(tsum[:, :1] / d_all + epsilon)
    pooled_part = mm(member, final, lax.Precision.HIGHEST)
    for i in range(r):
        pp[i] = pooled_part[:, i * w:(i + 1) * w]
    for i in range(r):
        @pl.when(c != q * r + i)
        def _(i=i):
            rcopy(pp.at[i], prc.at[c], pp_s.at[i], pp_r.at[c], (q, q * r + i)).start()

    @pl.when(g == q)
    def _():
        pooled = pp[j]
        for k in range(1, nc):
            s = rc(k)
            rcopy(pp.at[j], prc.at[s], pp_s.at[0], pp_r.at[s], (q, s)).wait_recv()
            pooled = pooled + prc[s]
        pblk[...] = (pooled / len_col).astype(BF16)
        for k in range(1, nq):
            rcopy(pblk, pblk, pb_s.at[k], pb_r, (rq(k), c)).start()

    loads[3].wait()
    loads[4].wait()

    @pl.when(g != q)
    def _():
        rcopy(pblk, pblk, pb_s.at[0], pb_r, (g, c)).wait_recv()

    cpart[...] = mm(pblk[...], code[:, pl.ds(pl.multiple_of(q * bw, bw), bw)])
    for k in range(1, nc):
        rcopy(cpart, crecv.at[c], c_s.at[k], c_r.at[c], (q, rc(k))).start()
    crecv[c] = cpart[...]
    for k in range(1, nc):
        s = rc(k)
        rcopy(cpart, crecv.at[s], c_s.at[k], c_r.at[s], (q, s)).wait_recv()
    csum = crecv[0]
    for i in range(1, nc):
        csum = csum + crecv[i]
    codes[q] = csum.astype(BF16)
    for k in range(1, nq):
        rcopy(codes.at[q], codes.at[q], o_s.at[k], o_r.at[q], (rq(k), c)).start()
    for k in range(1, nq):
        s = rq(k)
        rcopy(codes.at[s], codes.at[s], o_s.at[k], o_r.at[s], (s, c)).wait_recv()
    qcodes = jnp.concatenate([codes[i] for i in range(nq)], axis=1)
    scale = 1.0 / math.sqrt(corp.shape[1])
    scores = lax.dot_general(qcodes, corp[...], (((1,), (1,)), ((), ())), preferred_element_type=F32) * scale

    blocks = corp.shape[0] // LANES
    lists = jnp.concatenate([scores[:, i * LANES:(i + 1) * LANES] for i in range(blocks)], axis=0)
    best = merge_all(sort_lanes(lists), nqueries, q >= nq // 2)
    top_q[q] = best
    for k in range(1, nq):
        rcopy(top_q.at[q], top_q.at[q], tq_s.at[k], tq_r.at[q], (rq(k), c)).start()
    for k in range(1, nq):
        s = rq(k)
        rcopy(top_q.at[s], top_q.at[s], tq_s.at[k], tq_r.at[s], (s, c)).wait_recv()
    best = merge_all(top_q[...].reshape(nq * nqueries, LANES), nqueries, c >= nc // 2)
    top_c[c] = best
    for k in range(1, nc):
        rcopy(top_c.at[c], top_c.at[c], tc_s.at[k], tc_r.at[c], (q, rc(k))).start()
    for k in range(1, nc):
        s = rc(k)
        rcopy(top_c.at[s], top_c.at[s], tc_s.at[k], tc_r.at[s], (q, s)).wait_recv()
    best = merge_all(top_c[...].reshape(nc * nqueries, LANES), nqueries, False)
    out[...] = best[:, :TOPK]

    for k in range(1, nq):
        rcopy(lens, lens_all.at[q], l_s.at[k], l_r.at[q], (rq(k), c)).wait_send()
        rcopy(inv_all.at[q], inv_all.at[q], iv_s.at[k], iv_r.at[q], (rq(k), c)).wait_send()
        rcopy(top_q.at[q], top_q.at[q], tq_s.at[k], tq_r.at[q], (rq(k), c)).wait_send()
        rcopy(t_send, t_recv.at[q], t_s.at[k], t_r.at[q], (rq(k), c)).wait_send()
        rcopy(codes.at[q], codes.at[q], o_s.at[k], o_r.at[q], (rq(k), c)).wait_send()

    @pl.when(q != g)
    def _():
        rcopy(hid, colbuf.at[q], a_s, a_r.at[q], (g, c)).wait_send()

    for i in range(nb):
        @pl.when(sends_up)
        def _(i=i):
            up_chain(i).wait_send()

        @pl.when(sends_down)
        def _(i=i):
            down_chain(i).wait_send()

        for k in range(1, r):
            rcopy(chunk(i, j), chunk(i, j), la_s.at[k, i], la_r.at[j, i], (q, g * r + lane(k))).wait_send()

    def drain(n, carry):
        far_part(n).wait_send()
        near_part(n).wait_send()
        passed_part(n).wait_send()
        h_near(n, 0).wait_send()
        h_near(n, 1).wait_send()
        h_pass(n).wait_send()
        return carry

    lax.fori_loop(0, nch, drain, 0)
    for k in range(1, r):
        rcopy(lsend.at[lane(k)], lrecv.at[j], lr_s.at[k], lr_r.at[j], (q, g * r + lane(k))).wait_send()
    for k in range(1, ng):
        t = lax.rem(g + k, ng)
        rcopy(gsend.at[t], grecv.at[g], g_s.at[k], g_r.at[g], (q, t * r + j)).wait_send()
    for i in range(r):
        @pl.when(c != q * r + i)
        def _(i=i):
            rcopy(pp.at[i], prc.at[c], pp_s.at[i], pp_r.at[c], (q, q * r + i)).wait_send()

    @pl.when(g == q)
    def _():
        for k in range(1, nq):
            rcopy(pblk, pblk, pb_s.at[k], pb_r, (rq(k), c)).wait_send()
    for k in range(1, nc):
        rcopy(cpart, crecv.at[c], c_s.at[k], c_r.at[c], (q, rc(k))).wait_send()
        rcopy(st_send, st_recv.at[c], st_s.at[k], st_r.at[c], (q, rc(k))).wait_send()
        rcopy(top_c.at[c], top_c.at[c], tc_s.at[k], tc_r.at[c], (q, rc(k))).wait_send()


def per_device_general(nq, nc, hidden_in, lengths, gate_weight, up_weight, down_weight, code_weight, corpus_codes):
    slots, w = hidden_in.shape
    r = nc // nq
    nreal = nq * slots * REAL_NUM // REAL_DEN
    tq, tb = nreal // nq, nreal // nc
    dq, ffc = gate_weight.shape
    cw = CHUNK if ffc % CHUNK == 0 else ffc
    nch = ffc // cw
    nb = nreal // PIECE if nreal % PIECE == 0 else nq
    nqueries = nq * lengths.shape[0]
    bits = code_weight.shape[1]
    bw = bits // nq
    ng = nc // r
    lens = jnp.broadcast_to(jnp.repeat(lengths, SEQ)[None, :], (8, slots))
    vm, dma = pltpu.VMEM, pltpu.SemaphoreType.DMA
    scratch = [
        vm(gate_weight.shape, BF16), vm(up_weight.shape, BF16), vm(down_weight.shape, BF16),
        vm(code_weight.shape, BF16), vm(corpus_codes.shape, BF16),
        vm((nq, slots, w), BF16), vm((nq, 8, slots), jnp.int32), vm((r, nreal, w), BF16),
        vm((nch, nq, 2, tq, cw), BF16), vm((nch, nq, 2, tq, cw), BF16),
        vm((8, slots), F32), vm((nc, 8, slots), F32), vm((nq, 8, slots), F32), vm((r, nreal, w), BF16),
        vm((nch, 2, tq, cw), F32), vm((nq, nqueries, LANES), F32), vm((nc, nqueries, LANES), F32),
        vm((nch, nq, tq, cw), BF16), vm((nreal, dq), F32),
        vm((r, ng, tb, dq), BF16), vm((r, ng, tb, dq), BF16), vm((ng, tb, dq), BF16), vm((ng, tb, dq), BF16),
        vm((tb, 128), F32), vm((nq, tb, 128), F32),
        vm((r, nqueries, w), F32), vm((nc, nqueries, w), F32), vm((nqueries, w), BF16),
        vm((nqueries, bw), F32), vm((nc, nqueries, bw), F32), vm((nq, nqueries, bw), BF16),
        dma((5,)), dma, dma((nq,)), dma((nq,)), dma((nq,)), dma((2, nb)), dma((nb,)), dma((r, nb)), dma((r, nb)),
        dma((nch, nq)), dma((nch, nq)), dma((nc,)), dma((nc,)), dma((nq,)), dma((nq,)),
        dma((nq,)), dma((nq,)), dma((nc,)), dma((nc,)), dma((nch, nq)), dma((nch, nq)),
        dma((r,)), dma((r,)), dma((ng,)), dma((ng,)), dma((nq,)), dma((nq,)),
        dma((r,)), dma((nc,)), dma((nq,)), dma, dma((nc,)), dma((nc,)), dma((nq,)), dma((nq,)),
    ]
    dims = (nq, nc, r, nreal, tq, tb, nch, cw, w * nc)
    vspec, aspec = pl.BlockSpec(memory_space=pltpu.VMEM), pl.BlockSpec(memory_space=pl.ANY)
    return pl.pallas_call(
        functools.partial(general_kernel, dims),
        out_shape=jax.ShapeDtypeStruct((nqueries, TOPK), F32),
        in_specs=[vspec, vspec] + [aspec] * 5,
        out_specs=vspec,
        scratch_shapes=scratch,
        compiler_params=pltpu.CompilerParams(
            collective_id=0, has_side_effects=True, vmem_limit_bytes=60 * 1024 * 1024),
    )(hidden_in, lens, gate_weight, up_weight, down_weight, code_weight, corpus_codes)


def compare(v, size, step, flip, inner):
    part = len(v)
    sub = lax.broadcasted_iota(jnp.int32, v[0].shape, 0)
    across = step < part if inner else step >= 8
    if size >= LANES:
        up = [0] * part
    elif size < part:
        up = [int((i & size) != 0) for i in range(part)]
    else:
        up = [((sub & (size // part)) != 0).astype(jnp.int32)] * part
    masks = {}

    def high(i, low, name):
        key = (name, up[i] if isinstance(up[i], int) else -1)
        if key not in masks:
            masks[key] = (flip ^ up[i] ^ low) == 0
        return masks[key]

    v = list(v)
    if across:
        hop = step if inner else step // 8
        for i in range(part):
            if i & hop == 0:
                a, b = v[i], v[i | hop]
                most, least = jnp.maximum(a, b), jnp.minimum(a, b)
                pick = high(i, 0, 0)
                v[i], v[i | hop] = jnp.where(pick, most, least), jnp.where(pick, least, most)
        return v
    s = step // part if inner else step
    bit = (sub & s) != 0
    low = bit.astype(jnp.int32)
    for i in range(part):
        x = v[i]
        other = pltpu.roll(x, 4, 0) if s == 4 else jnp.where(bit, pltpu.roll(x, s, 0), pltpu.roll(x, 8 - s, 0))
        v[i] = jnp.where(high(i, low, 1), jnp.maximum(x, other), jnp.minimum(x, other))
    return v


def columns(lists):
    cols = jnp.concatenate([lists] * (LANES // lists.shape[0]), axis=0).T
    return [cols[i:i + 8] for i in range(0, LANES, 8)]


def merge_columns(v, count, rows, lone, inner):
    lane = lax.broadcasted_iota(jnp.int32, v[0].shape, 1)
    half = count // 2
    while half >= rows:
        v = [jnp.maximum(x, pltpu.roll(x, LANES - half, 1)) for x in v]
        if half > rows:
            flip = (lax.rem(lane, half) >= half // 2).astype(jnp.int32)
        else:
            flip = jnp.zeros_like(lane) + jnp.asarray(lone, jnp.int32)
        step = LANES // 2
        while step:
            v = compare(v, LANES, step, flip, inner)
            step //= 2
        half //= 2
    return v


def top_rows(lists, rows, lone, board):
    count = lists.shape[0]
    v = columns(lists)
    lane = lax.broadcasted_iota(jnp.int32, v[0].shape, 1)
    flip = (lax.rem(lane, count) >= count // 2).astype(jnp.int32)
    size = 2
    while size <= LANES:
        step = size // 2
        while step:
            v = compare(v, size, step, flip, True)
            step //= 2
        size *= 2
    v = merge_columns(v, count, rows, lone, True)
    for i, x in enumerate(v):
        board[pl.ds(i, 8, stride=len(v)), :] = x
    return board[...].T[:rows]


def merge_rows(lists, rows, lone):
    v = merge_columns(columns(lists), lists.shape[0], rows, lone, False)
    return jnp.concatenate(v, axis=0).T[:rows]


def fast_kernel(dims, names, hid, lens, gate_h, up_h, down_h, code_h, corp_h, out, *refs):
    nq, nc, r, nblk, bm, nh, hw, d_all = dims
    s = types.SimpleNamespace(**dict(zip(names, refs)))
    q = lax.axis_index("query")
    c = lax.axis_index("corpus")
    g = c // r
    j = lax.rem(c, r)
    ng = nc // r
    slots, w = hid.shape
    total = nq * slots
    nqueries = total // SEQ
    nreal = nblk * bm
    qm, gm = bm // nq, bm // ng
    nu = nblk * nh
    bw = s.codeq.shape[1]
    gate, up, corp = s.gu.at[0], s.gu.at[1], s.corp

    fq = w // nq
    for i in range(nq):
        pltpu.make_async_copy(hid.at[:, pl.ds(i * fq, fq)], s.hidq.at[i], s.w_s.at[0]).start()
    counts = pltpu.make_async_copy(lens, s.lens_s, s.w_s.at[1])
    counts.start()
    for a, b, k in ((gate_h, gate, 2), (up_h, up, 2), (down_h, s.down, 3), (code_h.at[:, pl.ds(pl.multiple_of(q * bw, bw), bw)], s.codeq, 4), (corp_h, corp, 5)):
        pltpu.make_async_copy(a, b, s.w_s.at[k]).start()

    def loaded(ref, k):
        pltpu.make_async_copy(ref, ref, s.w_s.at[k]).wait()

    def rq(k):
        return lax.rem(q + k, nq)

    def rc(k):
        return lax.rem(c + k, nc)

    def lane(k):
        return lax.rem(j + k, r)

    def got(ref, sem):
        rcopy(ref, ref, sem, sem, (rq(1), c)).wait_recv()

    def sent(ref, sem):
        rcopy(ref, ref, sem, sem, (rq(1), c)).wait_send()

    def to_query(src, ref, ss, rs):
        for k in range(1, nq):
            rcopy(src, ref.at[q], ss, rs, (rq(k), c)).start()

    def to_corpus(src, ref, ss, rs):
        for k in range(1, nc):
            rcopy(src, ref.at[c], ss, rs, (q, rc(k))).start()

    others = [(n, k) for n in range(nq) for k in range(r) if n or k]
    barrier = pltpu.get_barrier_semaphore()
    for n, k in others:
        if n and k:
            pl.semaphore_signal(barrier, inc=1, device_id=(rq(n), g * r + lane(k)), device_id_type=pl.DeviceIdType.MESH)
    for k in range(1, nq):
        pl.semaphore_signal(barrier, inc=1, device_id=(rq(k), c), device_id_type=pl.DeviceIdType.MESH)
    for k in range(1, nc):
        pl.semaphore_signal(barrier, inc=1, device_id=(q, rc(k)), device_id_type=pl.DeviceIdType.MESH)

    loaded(s.hidq, 0)
    squares = jnp.square(s.hidq[0].astype(F32))
    for i in range(1, nq):
        squares = squares + jnp.square(s.hidq[i].astype(F32))
    s.st_send[...] = lax.dot_general(jnp.ones((8, fq), F32), squares, (((1,), (1,)), ((), ())),
                                     precision=lax.Precision.HIGHEST, preferred_element_type=F32)
    counts.wait()
    slot_query = lax.broadcasted_iota(jnp.int32, (8, slots), 1) // SEQ
    own_lens = jnp.zeros((8, slots), jnp.int32)
    for k in range(slots // SEQ):
        own_lens = jnp.where(slot_query == k, s.lens_s[k], own_lens)
    s.lens_all[q] = own_lens

    pl.semaphore_wait(barrier, nq - 1 + nc - 1 + (nq - 1) * (r - 1))

    side_a = q + 1 - 2 * lax.rem(q, 2)
    side_b = q + 2 - 4 * (q // 2)
    far = nq - 1 - q

    for k in range(1, nq):
        rcopy(s.hidq.at[rq(k)], s.colbuf.at[q], s.a_s, s.a_r, (rq(k), c)).start()
    s.colbuf[q] = s.hidq[q]

    to_query(s.lens_all.at[q], s.lens_all, s.l_s, s.l_r)
    to_corpus(s.st_send, s.st_recv, s.st_s, s.st_r)
    s.st_recv[c] = s.st_send[...]
    got(s.lens_all.at[pl.ds(0, nq - 1)], s.l_r)
    lens_row = jnp.concatenate([s.lens_all[i] for i in range(nq)], axis=1)
    slot = lax.broadcasted_iota(jnp.int32, (8, total), 1)
    valid = lax.rem(slot, SEQ) < lens_row
    before = lax.broadcasted_iota(jnp.int32, (total, total), 0) < lax.broadcasted_iota(jnp.int32, (total, total), 1)
    pos = mm(valid.astype(F32).astype(BF16), before.astype(F32).astype(BF16)).astype(jnp.int32)
    pos = jnp.where(valid, pos, -1)[:1]

    got(s.st_recv.at[pl.ds(0, nc - 1)], s.st_r)
    stat = s.st_recv[0]
    for i in range(1, nc):
        stat = stat + s.st_recv[i]
    s.inv_all[q] = lax.rsqrt(stat / d_all + epsilon)
    to_query(s.inv_all.at[q], s.inv_all, s.iv_s, s.iv_r)

    def side(b, k):
        return rcopy(s.xall.at[j, b], s.xall.at[j, b], s.la_s, s.la_r.at[b], (q, g * r + lane(k)))

    def spread(b, k):
        t = lax.rem(g + k, ng)
        return rcopy(s.xpk.at[b], s.xall.at[j, b, q], s.x_s, s.x_r.at[b], (g, t * r + j))

    got(s.colbuf.at[pl.ds(0, nq - 1)], s.a_r)
    stacked = s.colbuf[...].reshape(total, fq)
    for b in range(nblk):
        row = lax.broadcasted_iota(jnp.int32, (bm, total), 0) + b * bm
        pick = (pos == row).astype(F32).astype(BF16)
        s.xpk[b] = mm(pick, stacked).astype(BF16)
        for k in range(ng - 1, 0, -1):
            spread(b, k).start()

        @pl.when(q != g)
        def _(b=b):
            spread(b, 0).start()

        @pl.when(q == g)
        def _(b=b):
            s.xall[j, b, q] = s.xpk[b]

    got(s.inv_all.at[pl.ds(0, nq - 1)], s.iv_r)
    inv_row = jnp.concatenate([s.inv_all[i] for i in range(nq)], axis=1)[:1]
    for b in range(nblk):
        row = lax.broadcasted_iota(jnp.int32, (bm, total), 0) + b * bm
        col = jnp.sum(jnp.where(pos == row, inv_row, 0.0), axis=1, keepdims=True)
        s.inv_c[b] = jnp.broadcast_to(col, (bm, LANES))

    loaded(s.gu, 2)

    def sides(n):
        odd = lax.rem(n, 2)
        return side_a + (side_b - side_a) * odd, side_b + (side_a - side_b) * odd

    def near_part(n):
        one, _ = sides(n)
        return rcopy(s.psend.at[n, one], s.precv.at[n, 0], s.p_s, s.p_r.at[n], (one, c))

    def far_part(n):
        one, _ = sides(n)
        return rcopy(s.psend.at[n, far], s.precv.at[n, 2], s.p_s, s.pf_r.at[n], (one, c))

    def passed_part(n):
        _, two = sides(n)
        return rcopy(s.precv.at[n, 3], s.precv.at[n, 1], s.p_s, s.p_r.at[n], (two, c))

    def h_near(n, k, sem):
        return rcopy(s.hall.at[n, q], s.hall.at[n, q], s.h_s, sem, (sides(n)[k], c))

    def h_pass(n, sem):
        one, two = sides(n)
        return rcopy(s.hall.at[n, one], s.hall.at[n, one], s.h_s, sem, (two, c))

    def fetch(b):
        @pl.when(q != g)
        def _():
            got(s.xall.at[0, b], s.x_r.at[b])

        @pl.when(q == g)
        def _():
            got(s.xall.at[0, b, pl.ds(0, nq - 1)], s.x_r.at[b])

        for k in range(1, r):
            side(b, k).start()

    def products(b):
        got(s.xall.at[pl.ds(0, r - 1), b], s.la_r.at[b])
        scale = s.inv_c[b][:, :1]
        for i in range(r):
            for k in range(nq):
                at = i * w + k * fq
                s.xn[:, at:at + fq] = (s.xall[i, b, k].astype(F32) * scale).astype(BF16)
        xb = s.xn[...]
        for h in range(nh):
            n = b * nh + h
            for e, wref in enumerate((gate, up)):
                full = mm(xb, wref[:, h * hw:(h + 1) * hw])
                s.full[h, e] = full
                for i in range(nq):
                    s.psend[n, i, e] = full[i * qm:(i + 1) * qm].astype(BF16)
            far_part(n).start()
            near_part(n).start()
            for e in range(2):
                s.pown[n, e] = s.full[h, e, pl.ds(pl.multiple_of(q * qm, qm), qm)]

    def pass_unit(n):
        _, two = sides(n)
        got(s.precv.at[n, 2], s.pf_r.at[n])
        s.precv[n, 3] = (s.psend[n, two].astype(F32) + s.precv[n, 2].astype(F32)).astype(BF16)
        passed_part(n).start()

    def reduce_unit(n):
        got(s.precv.at[n, pl.ds(0, 2)], s.p_r.at[n])
        gsum = s.pown[n, 0] + s.precv[n, 0, 0].astype(F32) + s.precv[n, 1, 0].astype(F32)
        usum = s.pown[n, 1] + s.precv[n, 0, 1].astype(F32) + s.precv[n, 1, 1].astype(F32)
        s.hall[n, q] = (gsum / (1.0 + jnp.exp(-gsum)) * usum).astype(BF16)
        h_near(n, 0, s.hn_r.at[n]).start()
        h_near(n, 1, s.hb_r.at[n // nh]).start()

    def relay_unit(n):
        got(s.hall.at[n, 0], s.hn_r.at[n])
        h_pass(n, s.hb_r.at[n // nh]).start()

    def lane_send(b, k):
        t = lane(k)
        return rcopy(s.lsend.at[b, t], s.lrecv.at[b, j], s.lr_s, s.lr_r.at[b], (q, g * r + t))

    def group_send(b, k):
        t = lax.rem(g + k, ng)
        return rcopy(s.gsend.at[b, t], s.grecv.at[b, g], s.g_s, s.g_r.at[b], (q, t * r + j))

    def down_block(b):
        part = None
        got(s.hall.at[pl.ds(b * nh, nh), pl.ds(0, 2)], s.hb_r.at[b])
        for h in range(nh):
            n = b * nh + h
            term = mm(s.hall[n].reshape(bm, hw), s.down[h * hw:(h + 1) * hw, :])
            part = term if part is None else part + term
        s.acc[b] = part
        for t in range(r):
            s.lsend[b, t] = part[:, t * w:(t + 1) * w].astype(BF16)
        for k in range(1, r):
            lane_send(b, k).start()

    def sum_block(b):
        mine = s.acc[b, :, pl.ds(pl.multiple_of(j * w, w), w)]
        got(s.lrecv.at[b, pl.ds(0, r - 1)], s.lr_r.at[b])
        for k in range(1, r):
            mine = mine + s.lrecv[b, lane(k)].astype(F32)
        s.mine[b] = mine
        for t in range(ng):
            s.gsend[b, t] = mine[t * gm:(t + 1) * gm].astype(BF16)
        for k in range(1, ng):
            group_send(b, k).start()

    def units(unit, b):
        for h in range(nh):
            unit(b * nh + h)

    def fetch_next(b):
        @pl.when(b + 1 < nblk)
        def _():
            fetch(b + 1)

    fetch(0)
    stages = (products, fetch_next, functools.partial(units, pass_unit), functools.partial(units, reduce_unit),
              functools.partial(units, relay_unit), down_block, sum_block)
    delays = (0, 0, 1, 2, 3, 4, 5)

    def turn(t, carry):
        for stage, delay in zip(stages, delays):
            @pl.when(jnp.logical_and(t >= delay, t < nblk + delay))
            def _(stage=stage, delay=delay):
                stage(t - delay)
        return carry

    loaded(s.down, 3)
    lax.fori_loop(0, nblk + delays[-1], turn, 0)
    own = pl.ds(pl.multiple_of(g * gm, gm), gm)
    for b in range(nblk):
        for k in range(nq):
            s.res[b * gm:(b + 1) * gm, k * fq:(k + 1) * fq] = s.xall[j, b, k, own].astype(F32)
    for b in range(nblk):
        total_b = s.mine[b, own]
        got(s.grecv.at[b, pl.ds(0, ng - 1)], s.g_r.at[b])
        for k in range(1, ng):
            total_b = total_b + s.grecv[b, lax.rem(g + k, ng)].astype(F32)
        s.res[b * gm:(b + 1) * gm] = s.res[b * gm:(b + 1) * gm] + total_b
    residual = s.res[...]
    tb = nblk * gm

    sums = lax.dot_general(jnp.ones((8, w), F32), residual * residual, (((1,), (1,)), ((), ())),
                           precision=lax.Precision.HIGHEST, preferred_element_type=F32)
    s.t_send[...] = jnp.concatenate([sums, jnp.zeros((8, LANES - tb), F32)], axis=1)
    for n, k in others:
        rcopy(s.t_send, s.t_recv.at[q * r + j], s.t_s, s.t_r, (rq(n), g * r + lane(k))).start()
    qrow = lax.broadcasted_iota(jnp.int32, (nqueries, total), 0)
    qslot = lax.broadcasted_iota(jnp.int32, (nqueries, total), 1)
    lens_b = jnp.broadcast_to(lens_row[:1], (nqueries, total)).astype(F32)
    vals_b = jnp.broadcast_to(valid.astype(F32)[:1], (nqueries, total))
    len_col = jnp.sum(jnp.where(qslot == qrow * SEQ, lens_b, 0.0), axis=1, keepdims=True)
    off_col = jnp.sum(jnp.where(qslot < qrow * SEQ, vals_b, 0.0), axis=1, keepdims=True)
    prow = lax.broadcasted_iota(jnp.int32, (nqueries, tb), 1)
    prow = ((prow // gm) * bm + g * gm + lax.rem(prow, gm)).astype(F32)
    member = jnp.where(jnp.logical_and(prow >= off_col, prow < off_col + len_col), 1.0, 0.0)
    tsum = s.t_send[...]
    got(s.t_recv.at[pl.ds(0, len(others))], s.t_r)
    for n, k in others:
        tsum = tsum + s.t_recv[rq(n) * r + lane(k)]
    inv_own = lax.rsqrt(tsum[:1, :tb] / d_all + epsilon)
    pooled_part = mm(member * inv_own, residual, lax.Precision.HIGHEST)
    s.pp[...] = pooled_part

    @pl.when(g != q)
    def _():
        rcopy(s.pp, s.prc.at[g], s.pp_s, s.pp_r, (q, q * r + j)).start()

    @pl.when(g == q)
    def _():
        pooled = pooled_part
        got(s.prc.at[pl.ds(0, ng - 1)], s.pp_r)
        for k in range(1, ng):
            pooled = pooled + s.prc[lax.rem(g + k, ng)]
        s.pblk[0] = (pooled / len_col).astype(BF16)
        for k in range(1, nq):
            rcopy(s.pblk.at[0], s.pblk.at[0], s.pb_s, s.pb_r, (rq(k), c)).start()

    loaded(s.codeq, 4)
    loaded(s.corp, 5)

    @pl.when(g != q)
    def _():
        got(s.pblk.at[0], s.pb_r)

    s.cpart[...] = mm(s.pblk[0], s.codeq[...])
    to_corpus(s.cpart, s.crecv, s.c_s, s.c_r)
    s.crecv[c] = s.cpart[...]
    got(s.crecv.at[pl.ds(0, nc - 1)], s.c_r)
    csum = s.crecv[0]
    for i in range(1, nc):
        csum = csum + s.crecv[i]
    s.codes[q] = csum.astype(BF16)
    to_query(s.codes.at[q], s.codes, s.o_s, s.o_r)
    got(s.codes.at[pl.ds(0, nq - 1)], s.o_r)
    qcodes = jnp.concatenate([s.codes[i] for i in range(nq)], axis=1)
    scale = 1.0 / math.sqrt(corp.shape[1])
    scores = lax.dot_general(qcodes, corp[...], (((1,), (1,)), ((), ())), preferred_element_type=F32) * scale

    blocks = corp.shape[0] // LANES
    lists = jnp.concatenate([scores[:, i * LANES:(i + 1) * LANES] for i in range(blocks)], axis=0)
    best = top_rows(lists, nqueries, q >= nq // 2, s.board)
    s.top_q[q] = best
    to_query(s.top_q.at[q], s.top_q, s.tq_s, s.tq_r)
    got(s.top_q.at[pl.ds(0, nq - 1)], s.tq_r)
    best = merge_rows(s.top_q[...].reshape(nq * nqueries, LANES), nqueries, c >= nc // 2)
    s.top_c[c] = best
    to_corpus(s.top_c.at[c], s.top_c, s.tc_s, s.tc_r)
    got(s.top_c.at[pl.ds(0, nc - 1)], s.tc_r)
    best = merge_rows(s.top_c[...].reshape(nc * nqueries, LANES), nqueries, False)
    out[...] = best[:, :TOPK]

    sent(s.lens_all.at[pl.ds(0, nq - 1)], s.l_s)
    sent(s.st_recv.at[pl.ds(0, nc - 1)], s.st_s)
    sent(s.inv_all.at[pl.ds(0, nq - 1)], s.iv_s)

    sent(s.colbuf.at[pl.ds(0, nq - 1)], s.a_s)

    @pl.when(q != g)
    def _():
        sent(s.xall.at[0], s.x_s)

    @pl.when(q == g)
    def _():
        sent(s.xall.at[0, :, pl.ds(0, nq - 1)], s.x_s)

    sent(s.xall.at[pl.ds(0, r - 1)], s.la_s)
    sent(s.psend.at[:, pl.ds(0, 3)], s.p_s)
    sent(s.hall.at[:, pl.ds(0, 3)], s.h_s)
    sent(s.lsend.at[:, pl.ds(0, r - 1)], s.lr_s)
    sent(s.gsend.at[:, pl.ds(0, ng - 1)], s.g_s)
    sent(s.t_recv.at[pl.ds(0, len(others))], s.t_s)

    @pl.when(g == q)
    def _():
        sent(s.pblk.at[pl.ds(0, nq - 1)], s.pb_s)

    @pl.when(g != q)
    def _():
        sent(s.pp, s.pp_s)

    sent(s.crecv.at[pl.ds(0, nc - 1)], s.c_s)
    sent(s.codes.at[pl.ds(0, nq - 1)], s.o_s)
    sent(s.top_q.at[pl.ds(0, nq - 1)], s.tq_s)
    sent(s.top_c.at[pl.ds(0, nc - 1)], s.tc_s)


def halves_of(ffc):
    return 2 if ffc % (2 * LANES) == 0 else 1


def per_device_fast(nq, nc, hidden_in, lengths, gate_weight, up_weight, down_weight, code_weight, corpus_codes):
    slots, w = hidden_in.shape
    r = nc // nq
    ng = nc // r
    nreal = nq * slots * REAL_NUM // REAL_DEN
    dq, ffc = gate_weight.shape
    bm = 8 * nc
    nblk = nreal // bm
    nh = halves_of(ffc)
    hw = ffc // nh
    nu = nblk * nh
    qm, gm = bm // nq, bm // ng
    tb = nblk * gm
    nqueries = nq * lengths.shape[0]
    bits = code_weight.shape[1]
    bw = bits // nq
    vm, dma = pltpu.VMEM, pltpu.SemaphoreType.DMA
    scratch = dict(
        gu=vm((2,) + gate_weight.shape, BF16), down=vm(down_weight.shape, BF16), codeq=vm((w, bw), BF16), corp=vm(corpus_codes.shape, BF16),
        lens_s=pltpu.SMEM(lengths.shape, jnp.int32),
        hidq=vm((nq, slots, w // nq), BF16), colbuf=vm((nq, slots, w // nq), BF16), xpk=vm((nblk, bm, w // nq), BF16), lens_all=vm((nq, 8, slots), jnp.int32), xall=vm((r, nblk, nq, bm, w // nq), BF16),
        xn=vm((bm, dq), BF16), inv_c=vm((nblk, bm, LANES), F32),
        st_send=vm((8, slots), F32), st_recv=vm((nc, 8, slots), F32), inv_all=vm((nq, 8, slots), F32),
        psend=vm((nu, nq, 2, qm, hw), BF16), precv=vm((nu, 4, 2, qm, hw), BF16), pown=vm((nu, 2, qm, hw), F32), full=vm((nh, 2, bm, hw), F32),
        hall=vm((nu, nq, qm, hw), BF16),
        acc=vm((nblk, bm, dq), F32), lsend=vm((nblk, r, bm, w), BF16), lrecv=vm((nblk, r, bm, w), BF16),
        mine=vm((nblk, bm, w), F32), gsend=vm((nblk, ng, gm, w), BF16), grecv=vm((nblk, ng, gm, w), BF16), res=vm((tb, w), F32),
        t_send=vm((8, LANES), F32), t_recv=vm((nq * r, 8, LANES), F32),
        pp=vm((nqueries, w), F32), prc=vm((ng, nqueries, w), F32), pblk=vm((nq, nqueries, w), BF16),
        cpart=vm((nqueries, bw), F32), crecv=vm((nc, nqueries, bw), F32), codes=vm((nq, nqueries, bw), BF16),
        top_q=vm((nq, nqueries, LANES), F32), top_c=vm((nc, nqueries, LANES), F32), board=vm((LANES, LANES), F32),
        w_s=dma((6,)), l_s=dma, l_r=dma, a_s=dma, a_r=dma, st_s=dma, st_r=dma, iv_s=dma, iv_r=dma,
        x_s=dma, x_r=dma((nblk,)), la_s=dma, la_r=dma((nblk,)),
        p_s=dma, p_r=dma((nu,)), pf_r=dma((nu,)), h_s=dma, hn_r=dma((nu,)), hb_r=dma((nblk,)),
        lr_s=dma, lr_r=dma((nblk,)), g_s=dma, g_r=dma((nblk,)),
        t_s=dma, t_r=dma, pp_s=dma, pp_r=dma, pb_s=dma, pb_r=dma, c_s=dma, c_r=dma, o_s=dma, o_r=dma,
        tq_s=dma, tq_r=dma, tc_s=dma, tc_r=dma,
    )
    dims = (nq, nc, r, nblk, bm, nh, hw, w * nc)
    vspec, aspec = pl.BlockSpec(memory_space=pltpu.VMEM), pl.BlockSpec(memory_space=pl.ANY)
    return pl.pallas_call(
        functools.partial(fast_kernel, dims, tuple(scratch)),
        out_shape=jax.ShapeDtypeStruct((nqueries, TOPK), F32),
        in_specs=[aspec] * 7,
        out_specs=vspec,
        scratch_shapes=list(scratch.values()),
        compiler_params=pltpu.CompilerParams(
            collective_id=0, has_side_effects=True, vmem_limit_bytes=60 * 1024 * 1024),
    )(hidden_in, lengths, gate_weight, up_weight, down_weight, code_weight, corpus_codes)


def per_device(nq, nc, hidden_in, *rest):
    slots, w = hidden_in.shape
    nreal = nq * slots * REAL_NUM // REAL_DEN
    nqueries = nq * rest[0].shape[0]
    lists = nqueries * max(nc, nq, rest[5].shape[0] // LANES)
    fits = nreal // nq <= LANES and lists <= LANES and LANES % lists == 0 and nreal % (8 * nc) == 0 and w % (nq * LANES) == 0
    body = per_device_fast if fits else per_device_general
    return body(nq, nc, hidden_in, *rest)


def solution(mesh):
    in_specs = (
        P("query", "corpus"),
        P("query"),
        P("query", "corpus"),
        P("query", "corpus"),
        P("corpus", "query"),
        P("corpus", None),
        P(("query", "corpus"), None),
    )
    body = functools.partial(per_device, mesh.shape["query"], mesh.shape["corpus"])
    return jax.shard_map(body, mesh=mesh, in_specs=in_specs, out_specs=P(), check_vma=False)
```

```python
import functools
import math
import types

import jax
import jax.numpy as jnp
from jax import lax
from jax.experimental import pallas as pl
from jax.experimental.pallas import tpu as pltpu
from jax.sharding import PartitionSpec as P

SEQ = 32
LANES = 128
TOPK = 100
REAL_NUM, REAL_DEN = 5, 8
CHUNK = 256
PIECE = 32

epsilon = 1e-05
F32, BF16 = jnp.float32, jnp.bfloat16


def mm(a, b, precision=None):
    return lax.dot_general(a, b, (((1,), (0,)), ((), ())), precision=precision, preferred_element_type=F32)


def rcopy(src, dst, send, recv, dev):
    return pltpu.make_async_remote_copy(
        src_ref=src, dst_ref=dst, send_sem=send, recv_sem=recv,
        device_id=dev, device_id_type=pl.DeviceIdType.MESH)


def exchange(x, s, keep_max):
    bit = (lax.broadcasted_iota(jnp.int32, x.shape, 1) & s) != 0
    other = jnp.where(bit, pltpu.roll(x, s, 1), pltpu.roll(x, LANES - s, 1))
    return jnp.where(keep_max, jnp.maximum(x, other), jnp.minimum(x, other))


def sort_lanes(x):
    lane = lax.broadcasted_iota(jnp.int32, x.shape, 1)
    flip = (lax.broadcasted_iota(jnp.int32, x.shape, 0) >= x.shape[0] // 2).astype(jnp.int32)
    size = 2
    while size <= LANES:
        up = ((lane & size) != 0).astype(jnp.int32) if size < LANES else jnp.zeros_like(lane)
        s = size // 2
        while s:
            low = ((lane & s) != 0).astype(jnp.int32)
            x = exchange(x, s, (low ^ up ^ flip) == 0)
            s //= 2
        size *= 2
    return x


def merge_all(x, rows, lone):
    while x.shape[0] > rows:
        half = x.shape[0] // 2
        x = jnp.maximum(x[:half], x[half:])
        lane = lax.broadcasted_iota(jnp.int32, x.shape, 1)
        if half > rows:
            flip = (lax.broadcasted_iota(jnp.int32, x.shape, 0) >= half // 2).astype(jnp.int32)
        else:
            flip = jnp.zeros_like(lane) + jnp.asarray(lone, jnp.int32)
        s = LANES // 2
        while s:
            low = ((lane & s) != 0).astype(jnp.int32)
            x = exchange(x, s, (low ^ flip) == 0)
            s //= 2
    return x


def general_kernel(dims, hid, lens, gate_h, up_h, down_h, code_h, corp_h, out,
                 gate, up, down, code, corp, colbuf, lens_all, xall, psend, precv,
                 st_send, st_recv, inv_all, xn, pown, top_q, top_c, hall, acc, lsend, lrecv, gsend, grecv, t_send, t_recv,
                 pp, prc, pblk, cpart, crecv, codes,
                 w_s, a_s, a_r, l_s, l_r, ch_s, ch_r, la_s, la_r, p_s, p_r, st_s, st_r, iv_s, iv_r, tq_s, tq_r, tc_s, tc_r, h_s, h_r,
                 lr_s, lr_r, g_s, g_r, t_s, t_r, pp_s, pp_r, pb_s, pb_r, c_s, c_r, o_s, o_r):
    nq, nc, r, nreal, tq, tb, nch, cw, d_all = dims
    q = lax.axis_index("query")
    c = lax.axis_index("corpus")
    g = c // r
    j = lax.rem(c, r)
    slots, w = hid.shape[0], hid.shape[1]
    total = nq * slots
    nqueries = total // SEQ
    bw = code.shape[1] // nq

    loads = []
    for i, (s, d) in enumerate(((gate_h, gate), (up_h, up), (down_h, down), (code_h, code), (corp_h, corp))):
        cp = pltpu.make_async_copy(s, d, w_s.at[i])
        cp.start()
        loads.append(cp)

    def rq(k):
        return lax.rem(q + k, nq)

    def rc(k):
        return lax.rem(c + k, nc)

    def lane(k):
        return lax.rem(j + k, r)

    barrier = pltpu.get_barrier_semaphore()
    for k in range(1, nq):
        pl.semaphore_signal(barrier, inc=1, device_id=(rq(k), c), device_id_type=pl.DeviceIdType.MESH)
    for k in range(1, nc):
        pl.semaphore_signal(barrier, inc=1, device_id=(q, rc(k)), device_id_type=pl.DeviceIdType.MESH)
    pl.semaphore_wait(barrier, nq - 1 + nc - 1)

    for k in range(1, nq):
        rcopy(lens, lens_all.at[q], l_s.at[k], l_r.at[q], (rq(k), c)).start()

    @pl.when(q != g)
    def _():
        rcopy(hid, colbuf.at[q], a_s, a_r.at[q], (g, c)).start()

    squares = jnp.square(hid[...].astype(F32))
    st_send[...] = lax.dot_general(jnp.ones((8, w), F32), squares, (((1,), (1,)), ((), ())),
                                   precision=lax.Precision.HIGHEST, preferred_element_type=F32)
    for k in range(1, nc):
        rcopy(st_send, st_recv.at[c], st_s.at[k], st_r.at[c], (q, rc(k))).start()
    st_recv[c] = st_send[...]
    lens_all[q] = lens[...]
    for k in range(1, nq):
        s = rq(k)
        rcopy(lens, lens_all.at[s], l_s.at[k], l_r.at[s], (s, c)).wait_recv()
    lens_row = jnp.concatenate([lens_all[i] for i in range(nq)], axis=1)
    slot = lax.broadcasted_iota(jnp.int32, (8, total), 1)
    valid = lax.rem(slot, SEQ) < lens_row
    before = lax.broadcasted_iota(jnp.int32, (total, total), 0) < lax.broadcasted_iota(jnp.int32, (total, total), 1)
    pos = mm(valid.astype(F32).astype(BF16), before.astype(F32).astype(BF16)).astype(jnp.int32)
    pos = jnp.where(valid, pos, -1)[:1]

    for k in range(1, nc):
        s = rc(k)
        rcopy(st_send, st_recv.at[s], st_s.at[k], st_r.at[s], (q, s)).wait_recv()
    stat = st_recv[0]
    for i in range(1, nc):
        stat = stat + st_recv[i]
    inv_all[q] = lax.rsqrt(stat / d_all + epsilon)
    for k in range(1, nq):
        rcopy(inv_all.at[q], inv_all.at[q], iv_s.at[k], iv_r.at[q], (rq(k), c)).start()

    nb = ch_r.shape[0]
    ct = nreal // nb

    def chunk(i, slot_j):
        return xall.at[slot_j, pl.ds(i * ct, ct)]

    def down_chain(i):
        return rcopy(chunk(i, j), chunk(i, j), ch_s.at[0, i], ch_r.at[i], (q, jnp.maximum(c - r, 0)))

    def up_chain(i):
        return rcopy(chunk(i, j), chunk(i, j), ch_s.at[1, i], ch_r.at[i], (q, jnp.minimum(c + r, nc - 1)))

    sends_up = jnp.logical_and(g >= q, g < nc // r - 1)
    sends_down = jnp.logical_and(g <= q, g > 0)

    @pl.when(q == g)
    def _():
        colbuf[q] = hid[...]
        for k in range(1, nq):
            s = rq(k)
            rcopy(hid, colbuf.at[s], a_s, a_r.at[s], (s, c)).wait_recv()
        stacked = colbuf[...].reshape(total, w)
        for i in range(nq):
            row = lax.broadcasted_iota(jnp.int32, (tq, total), 0) + i * tq
            pick = (pos == row).astype(F32).astype(BF16)
            xall[j, i * tq:(i + 1) * tq, :] = mm(pick, stacked).astype(BF16)

    for i in range(nb):
        @pl.when(q != g)
        def _(i=i):
            up_chain(i).wait_recv()

        @pl.when(sends_up)
        def _(i=i):
            up_chain(i).start()

        @pl.when(sends_down)
        def _(i=i):
            down_chain(i).start()

        for k in range(1, r):
            rcopy(chunk(i, j), chunk(i, j), la_s.at[k, i], la_r.at[j, i], (q, g * r + lane(k))).start()
    for k in range(1, nq):
        s = rq(k)
        rcopy(inv_all.at[s], inv_all.at[s], iv_s.at[k], iv_r.at[s], (s, c)).wait_recv()
    inv_row = jnp.concatenate([inv_all[i] for i in range(nq)], axis=1)[:1]
    inv_cols = []
    for i in range(nq):
        row = lax.broadcasted_iota(jnp.int32, (tq, total), 0) + i * tq
        inv_cols.append(jnp.sum(jnp.where(pos == row, inv_row, 0.0), axis=1, keepdims=True))
    inv = jnp.concatenate(inv_cols, axis=0)
    for i in range(nb):
        for k in range(1, r):
            s = lane(k)
            rcopy(chunk(i, s), chunk(i, s), la_s.at[k, i], la_r.at[s, i], (q, g * r + s)).wait_recv()

    loads[0].wait()
    loads[1].wait()

    for i in range(r):
        xn[i] = (xall[i].astype(F32) * inv).astype(BF16)

    side_a = q + 1 - 2 * lax.rem(q, 2)
    side_b = q + 2 - 4 * (q // 2)
    far = nq - 1 - q

    def sides(n):
        odd = lax.rem(n, 2)
        return side_a + (side_b - side_a) * odd, side_b + (side_a - side_b) * odd

    def near_part(n):
        one, _ = sides(n)
        return rcopy(psend.at[n, one], precv.at[n, 0], p_s.at[n, 0], p_r.at[n, 0], (one, c))

    def far_part(n):
        one, _ = sides(n)
        return rcopy(psend.at[n, far], precv.at[n, 1], p_s.at[n, 1], p_r.at[n, 1], (one, c))

    def passed_part(n):
        _, two = sides(n)
        return rcopy(precv.at[n, 3], precv.at[n, 2], p_s.at[n, 2], p_r.at[n, 2], (two, c))

    def h_near(n, k):
        to = sides(n)[k]
        return rcopy(hall.at[n, q], hall.at[n, q], h_s.at[n, k], h_r.at[n, k], (to, c))

    def h_near_in(n, k):
        to = sides(n)[k]
        return rcopy(hall.at[n, to], hall.at[n, to], h_s.at[n, k], h_r.at[n, k], (to, c))

    def h_pass(n):
        one, two = sides(n)
        return rcopy(hall.at[n, one], hall.at[n, one], h_s.at[n, 2], h_r.at[n, 2], (two, c))

    def h_pass_in(n):
        _, two = sides(n)
        return rcopy(hall.at[n, far], hall.at[n, far], h_s.at[n, 2], h_r.at[n, 2], (two, c))

    def matmuls(n, carry):
        cols = pl.ds(pl.multiple_of(n * cw, cw), cw)
        for e, wref in enumerate((gate, up)):
            full = sum(mm(xn[i], wref[i * w:(i + 1) * w, cols]) for i in range(r))
            for i in range(nq):
                psend[n, i, e] = full[i * tq:(i + 1) * tq].astype(BF16)

                @pl.when(q == i)
                def _(i=i, e=e, full=full):
                    pown[n, e] = full[i * tq:(i + 1) * tq]
        far_part(n).start()
        near_part(n).start()
        return carry

    lax.fori_loop(0, nch, matmuls, 0)

    loads[2].wait()
    acc[...] = jnp.zeros_like(acc)

    def pass_chunk(n):
        _, two = sides(n)
        far_part(n).wait_recv()
        precv[n, 3] = (psend[n, two].astype(F32) + precv[n, 1].astype(F32)).astype(BF16)
        passed_part(n).start()

    def reduce_chunk(n):
        near_part(n).wait_recv()
        passed_part(n).wait_recv()
        gsum = pown[n, 0] + precv[n, 0, 0].astype(F32) + precv[n, 2, 0].astype(F32)
        usum = pown[n, 1] + precv[n, 0, 1].astype(F32) + precv[n, 2, 1].astype(F32)
        hall[n, q] = (gsum / (1.0 + jnp.exp(-gsum)) * usum).astype(BF16)
        h_near(n, 0).start()
        h_near(n, 1).start()

    def relay_chunk(n):
        h_near_in(n, 0).wait_recv()
        h_pass(n).start()

    def down_chunk(n):
        h_near_in(n, 1).wait_recv()
        h_pass_in(n).wait_recv()
        acc[...] += mm(hall[n].reshape(nreal, cw), down[pl.ds(pl.multiple_of(n * cw, cw), cw), :])

    def passes(n, carry):
        pass_chunk(n)
        return carry

    lax.fori_loop(0, nch, passes, 0)
    reduce_chunk(0)

    def reduces(n, carry):
        reduce_chunk(n)
        relay_chunk(n - 1)
        return carry

    lax.fori_loop(1, nch, reduces, 0)
    relay_chunk(nch - 1)

    def downs(n, carry):
        down_chunk(n)
        return carry

    lax.fori_loop(0, nch, downs, 0)

    ng = nc // r
    for gg in range(ng):
        for jj in range(r):
            b = gg * r + jj
            lsend[jj, gg] = acc[b * tb:(b + 1) * tb].astype(BF16)
    for k in range(1, r):
        t = lane(k)
        rcopy(lsend.at[t], lrecv.at[j], lr_s.at[k], lr_r.at[j], (q, g * r + t)).start()
    mine = lsend[j].astype(F32)
    for k in range(1, r):
        s = lane(k)
        rcopy(lsend.at[s], lrecv.at[s], lr_s.at[k], lr_r.at[s], (q, g * r + s)).wait_recv()
        mine = mine + lrecv[s].astype(F32)
    gsend[...] = mine.astype(BF16)
    for k in range(1, ng):
        t = lax.rem(g + k, ng)
        rcopy(gsend.at[t], grecv.at[g], g_s.at[k], g_r.at[g], (q, t * r + j)).start()
    row = lax.broadcasted_iota(jnp.int32, (tb, nreal), 0) + c * tb
    own_rows = (lax.broadcasted_iota(jnp.int32, (tb, nreal), 1) == row).astype(F32).astype(BF16)
    residual = jnp.concatenate([mm(own_rows, xall[i]) for i in range(r)], axis=1)
    residual = residual + gsend[g].astype(F32)
    for k in range(1, ng):
        s = lax.rem(g + k, ng)
        rcopy(gsend.at[s], grecv.at[s], g_s.at[k], g_r.at[s], (q, s * r + j)).wait_recv()
        residual = residual + grecv[s].astype(F32)

    t_send[...] = jnp.broadcast_to(jnp.sum(residual * residual, axis=1, keepdims=True), (tb, 128))
    for k in range(1, nq):
        rcopy(t_send, t_recv.at[q], t_s.at[k], t_r.at[q], (rq(k), c)).start()
    qrow = lax.broadcasted_iota(jnp.int32, (nqueries, total), 0)
    qslot = lax.broadcasted_iota(jnp.int32, (nqueries, total), 1)
    lens_b = jnp.broadcast_to(lens_row[:1], (nqueries, total)).astype(F32)
    vals_b = jnp.broadcast_to(valid.astype(F32)[:1], (nqueries, total))
    len_col = jnp.sum(jnp.where(qslot == qrow * SEQ, lens_b, 0.0), axis=1, keepdims=True)
    off_col = jnp.sum(jnp.where(qslot < qrow * SEQ, vals_b, 0.0), axis=1, keepdims=True)
    prow = (lax.broadcasted_iota(jnp.int32, (nqueries, tb), 1) + c * tb).astype(F32)
    member = jnp.where(jnp.logical_and(prow >= off_col, prow < off_col + len_col), 1.0, 0.0)
    tsum = t_send[...]
    for k in range(1, nq):
        s = rq(k)
        rcopy(t_send, t_recv.at[s], t_s.at[k], t_r.at[s], (s, c)).wait_recv()
        tsum = tsum + t_recv[s]
    final = residual * lax.rsqrt(tsum[:, :1] / d_all + epsilon)
    pooled_part = mm(member, final, lax.Precision.HIGHEST)
    for i in range(r):
        pp[i] = pooled_part[:, i * w:(i + 1) * w]
    for i in range(r):
        @pl.when(c != q * r + i)
        def _(i=i):
            rcopy(pp.at[i], prc.at[c], pp_s.at[i], pp_r.at[c], (q, q * r + i)).start()

    @pl.when(g == q)
    def _():
        pooled = pp[j]
        for k in range(1, nc):
            s = rc(k)
            rcopy(pp.at[j], prc.at[s], pp_s.at[0], pp_r.at[s], (q, s)).wait_recv()
            pooled = pooled + prc[s]
        pblk[...] = (pooled / len_col).astype(BF16)
        for k in range(1, nq):
            rcopy(pblk, pblk, pb_s.at[k], pb_r, (rq(k), c)).start()

    loads[3].wait()
    loads[4].wait()

    @pl.when(g != q)
    def _():
        rcopy(pblk, pblk, pb_s.at[0], pb_r, (g, c)).wait_recv()

    cpart[...] = mm(pblk[...], code[:, pl.ds(pl.multiple_of(q * bw, bw), bw)])
    for k in range(1, nc):
        rcopy(cpart, crecv.at[c], c_s.at[k], c_r.at[c], (q, rc(k))).start()
    crecv[c] = cpart[...]
    for k in range(1, nc):
        s = rc(k)
        rcopy(cpart, crecv.at[s], c_s.at[k], c_r.at[s], (q, s)).wait_recv()
    csum = crecv[0]
    for i in range(1, nc):
        csum = csum + crecv[i]
    codes[q] = csum.astype(BF16)
    for k in range(1, nq):
        rcopy(codes.at[q], codes.at[q], o_s.at[k], o_r.at[q], (rq(k), c)).start()
    for k in range(1, nq):
        s = rq(k)
        rcopy(codes.at[s], codes.at[s], o_s.at[k], o_r.at[s], (s, c)).wait_recv()
    qcodes = jnp.concatenate([codes[i] for i in range(nq)], axis=1)
    scale = 1.0 / math.sqrt(corp.shape[1])
    scores = lax.dot_general(qcodes, corp[...], (((1,), (1,)), ((), ())), preferred_element_type=F32) * scale

    blocks = corp.shape[0] // LANES
    lists = jnp.concatenate([scores[:, i * LANES:(i + 1) * LANES] for i in range(blocks)], axis=0)
    best = merge_all(sort_lanes(lists), nqueries, q >= nq // 2)
    top_q[q] = best
    for k in range(1, nq):
        rcopy(top_q.at[q], top_q.at[q], tq_s.at[k], tq_r.at[q], (rq(k), c)).start()
    for k in range(1, nq):
        s = rq(k)
        rcopy(top_q.at[s], top_q.at[s], tq_s.at[k], tq_r.at[s], (s, c)).wait_recv()
    best = merge_all(top_q[...].reshape(nq * nqueries, LANES), nqueries, c >= nc // 2)
    top_c[c] = best
    for k in range(1, nc):
        rcopy(top_c.at[c], top_c.at[c], tc_s.at[k], tc_r.at[c], (q, rc(k))).start()
    for k in range(1, nc):
        s = rc(k)
        rcopy(top_c.at[s], top_c.at[s], tc_s.at[k], tc_r.at[s], (q, s)).wait_recv()
    best = merge_all(top_c[...].reshape(nc * nqueries, LANES), nqueries, False)
    out[...] = best[:, :TOPK]

    for k in range(1, nq):
        rcopy(lens, lens_all.at[q], l_s.at[k], l_r.at[q], (rq(k), c)).wait_send()
        rcopy(inv_all.at[q], inv_all.at[q], iv_s.at[k], iv_r.at[q], (rq(k), c)).wait_send()
        rcopy(top_q.at[q], top_q.at[q], tq_s.at[k], tq_r.at[q], (rq(k), c)).wait_send()
        rcopy(t_send, t_recv.at[q], t_s.at[k], t_r.at[q], (rq(k), c)).wait_send()
        rcopy(codes.at[q], codes.at[q], o_s.at[k], o_r.at[q], (rq(k), c)).wait_send()

    @pl.when(q != g)
    def _():
        rcopy(hid, colbuf.at[q], a_s, a_r.at[q], (g, c)).wait_send()

    for i in range(nb):
        @pl.when(sends_up)
        def _(i=i):
            up_chain(i).wait_send()

        @pl.when(sends_down)
        def _(i=i):
            down_chain(i).wait_send()

        for k in range(1, r):
            rcopy(chunk(i, j), chunk(i, j), la_s.at[k, i], la_r.at[j, i], (q, g * r + lane(k))).wait_send()

    def drain(n, carry):
        far_part(n).wait_send()
        near_part(n).wait_send()
        passed_part(n).wait_send()
        h_near(n, 0).wait_send()
        h_near(n, 1).wait_send()
        h_pass(n).wait_send()
        return carry

    lax.fori_loop(0, nch, drain, 0)
    for k in range(1, r):
        rcopy(lsend.at[lane(k)], lrecv.at[j], lr_s.at[k], lr_r.at[j], (q, g * r + lane(k))).wait_send()
    for k in range(1, ng):
        t = lax.rem(g + k, ng)
        rcopy(gsend.at[t], grecv.at[g], g_s.at[k], g_r.at[g], (q, t * r + j)).wait_send()
    for i in range(r):
        @pl.when(c != q * r + i)
        def _(i=i):
            rcopy(pp.at[i], prc.at[c], pp_s.at[i], pp_r.at[c], (q, q * r + i)).wait_send()

    @pl.when(g == q)
    def _():
        for k in range(1, nq):
            rcopy(pblk, pblk, pb_s.at[k], pb_r, (rq(k), c)).wait_send()
    for k in range(1, nc):
        rcopy(cpart, crecv.at[c], c_s.at[k], c_r.at[c], (q, rc(k))).wait_send()
        rcopy(st_send, st_recv.at[c], st_s.at[k], st_r.at[c], (q, rc(k))).wait_send()
        rcopy(top_c.at[c], top_c.at[c], tc_s.at[k], tc_r.at[c], (q, rc(k))).wait_send()


def per_device_general(nq, nc, hidden_in, lengths, gate_weight, up_weight, down_weight, code_weight, corpus_codes):
    slots, w = hidden_in.shape
    r = nc // nq
    nreal = nq * slots * REAL_NUM // REAL_DEN
    tq, tb = nreal // nq, nreal // nc
    dq, ffc = gate_weight.shape
    cw = CHUNK if ffc % CHUNK == 0 else ffc
    nch = ffc // cw
    nb = nreal // PIECE if nreal % PIECE == 0 else nq
    nqueries = nq * lengths.shape[0]
    bits = code_weight.shape[1]
    bw = bits // nq
    ng = nc // r
    lens = jnp.broadcast_to(jnp.repeat(lengths, SEQ)[None, :], (8, slots))
    vm, dma = pltpu.VMEM, pltpu.SemaphoreType.DMA
    scratch = [
        vm(gate_weight.shape, BF16), vm(up_weight.shape, BF16), vm(down_weight.shape, BF16),
        vm(code_weight.shape, BF16), vm(corpus_codes.shape, BF16),
        vm((nq, slots, w), BF16), vm((nq, 8, slots), jnp.int32), vm((r, nreal, w), BF16),
        vm((nch, nq, 2, tq, cw), BF16), vm((nch, nq, 2, tq, cw), BF16),
        vm((8, slots), F32), vm((nc, 8, slots), F32), vm((nq, 8, slots), F32), vm((r, nreal, w), BF16),
        vm((nch, 2, tq, cw), F32), vm((nq, nqueries, LANES), F32), vm((nc, nqueries, LANES), F32),
        vm((nch, nq, tq, cw), BF16), vm((nreal, dq), F32),
        vm((r, ng, tb, dq), BF16), vm((r, ng, tb, dq), BF16), vm((ng, tb, dq), BF16), vm((ng, tb, dq), BF16),
        vm((tb, 128), F32), vm((nq, tb, 128), F32),
        vm((r, nqueries, w), F32), vm((nc, nqueries, w), F32), vm((nqueries, w), BF16),
        vm((nqueries, bw), F32), vm((nc, nqueries, bw), F32), vm((nq, nqueries, bw), BF16),
        dma((5,)), dma, dma((nq,)), dma((nq,)), dma((nq,)), dma((2, nb)), dma((nb,)), dma((r, nb)), dma((r, nb)),
        dma((nch, nq)), dma((nch, nq)), dma((nc,)), dma((nc,)), dma((nq,)), dma((nq,)),
        dma((nq,)), dma((nq,)), dma((nc,)), dma((nc,)), dma((nch, nq)), dma((nch, nq)),
        dma((r,)), dma((r,)), dma((ng,)), dma((ng,)), dma((nq,)), dma((nq,)),
        dma((r,)), dma((nc,)), dma((nq,)), dma, dma((nc,)), dma((nc,)), dma((nq,)), dma((nq,)),
    ]
    dims = (nq, nc, r, nreal, tq, tb, nch, cw, w * nc)
    vspec, aspec = pl.BlockSpec(memory_space=pltpu.VMEM), pl.BlockSpec(memory_space=pl.ANY)
    return pl.pallas_call(
        functools.partial(general_kernel, dims),
        out_shape=jax.ShapeDtypeStruct((nqueries, TOPK), F32),
        in_specs=[vspec, vspec] + [aspec] * 5,
        out_specs=vspec,
        scratch_shapes=scratch,
        compiler_params=pltpu.CompilerParams(
            collective_id=0, has_side_effects=True, vmem_limit_bytes=60 * 1024 * 1024),
    )(hidden_in, lens, gate_weight, up_weight, down_weight, code_weight, corpus_codes)


def compare(v, size, step, flip, inner):
    part = len(v)
    sub = lax.broadcasted_iota(jnp.int32, v[0].shape, 0)
    across = step < part if inner else step >= 8
    if size >= LANES:
        up = [0] * part
    elif size < part:
        up = [int((i & size) != 0) for i in range(part)]
    else:
        up = [((sub & (size // part)) != 0).astype(jnp.int32)] * part
    masks = {}

    def high(i, low, name):
        key = (name, up[i] if isinstance(up[i], int) else -1)
        if key not in masks:
            masks[key] = (flip ^ up[i] ^ low) == 0
        return masks[key]

    v = list(v)
    if across:
        hop = step if inner else step // 8
        for i in range(part):
            if i & hop == 0:
                a, b = v[i], v[i | hop]
                most, least = jnp.maximum(a, b), jnp.minimum(a, b)
                pick = high(i, 0, 0)
                v[i], v[i | hop] = jnp.where(pick, most, least), jnp.where(pick, least, most)
        return v
    s = step // part if inner else step
    bit = (sub & s) != 0
    low = bit.astype(jnp.int32)
    for i in range(part):
        x = v[i]
        other = pltpu.roll(x, 4, 0) if s == 4 else jnp.where(bit, pltpu.roll(x, s, 0), pltpu.roll(x, 8 - s, 0))
        v[i] = jnp.where(high(i, low, 1), jnp.maximum(x, other), jnp.minimum(x, other))
    return v


def columns(lists):
    cols = jnp.concatenate([lists] * (LANES // lists.shape[0]), axis=0).T
    return [cols[i:i + 8] for i in range(0, LANES, 8)]


def merge_columns(v, count, rows, lone, inner):
    lane = lax.broadcasted_iota(jnp.int32, v[0].shape, 1)
    half = count // 2
    while half >= rows:
        v = [jnp.maximum(x, pltpu.roll(x, LANES - half, 1)) for x in v]
        if half > rows:
            flip = (lax.rem(lane, half) >= half // 2).astype(jnp.int32)
        else:
            flip = jnp.zeros_like(lane) + jnp.asarray(lone, jnp.int32)
        step = LANES // 2
        while step:
            v = compare(v, LANES, step, flip, inner)
            step //= 2
        half //= 2
    return v


def top_rows(lists, rows, lone, board):
    count = lists.shape[0]
    v = columns(lists)
    lane = lax.broadcasted_iota(jnp.int32, v[0].shape, 1)
    flip = (lax.rem(lane, count) >= count // 2).astype(jnp.int32)
    size = 2
    while size <= LANES:
        step = size // 2
        while step:
            v = compare(v, size, step, flip, True)
            step //= 2
        size *= 2
    v = merge_columns(v, count, rows, lone, True)
    for i, x in enumerate(v):
        board[pl.ds(i, 8, stride=len(v)), :] = x
    return board[...].T[:rows]


def merge_rows(lists, rows, lone):
    v = merge_columns(columns(lists), lists.shape[0], rows, lone, False)
    return jnp.concatenate(v, axis=0).T[:rows]


def fast_kernel(dims, names, hid, lens, gate_h, up_h, down_h, code_h, corp_h, out, *refs):
    nq, nc, r, nblk, bm, nh, hw, d_all = dims
    s = types.SimpleNamespace(**dict(zip(names, refs)))
    q = lax.axis_index("query")
    c = lax.axis_index("corpus")
    g = c // r
    j = lax.rem(c, r)
    ng = nc // r
    slots, w = hid.shape
    total = nq * slots
    nqueries = total // SEQ
    nreal = nblk * bm
    qm, gm = bm // nq, bm // ng
    nu = nblk * nh
    bw = s.codeq.shape[1]
    gate, up, corp = s.gu.at[0], s.gu.at[1], s.corp

    fq = w // nq
    for i in range(nq):
        pltpu.make_async_copy(hid.at[:, pl.ds(i * fq, fq)], s.hidq.at[i], s.w_s.at[0]).start()
    counts = pltpu.make_async_copy(lens, s.lens_s, s.w_s.at[1])
    counts.start()
    for a, b, k in ((gate_h, gate, 2), (up_h, up, 2), (down_h, s.down, 3), (code_h.at[:, pl.ds(pl.multiple_of(q * bw, bw), bw)], s.codeq, 4), (corp_h, corp, 5)):
        pltpu.make_async_copy(a, b, s.w_s.at[k]).start()

    def loaded(ref, k):
        pltpu.make_async_copy(ref, ref, s.w_s.at[k]).wait()

    def rq(k):
        return lax.rem(q + k, nq)

    def rc(k):
        return lax.rem(c + k, nc)

    def lane(k):
        return lax.rem(j + k, r)

    def got(ref, sem):
        rcopy(ref, ref, sem, sem, (rq(1), c)).wait_recv()

    def sent(ref, sem):
        rcopy(ref, ref, sem, sem, (rq(1), c)).wait_send()

    def to_query(src, ref, ss, rs):
        for k in range(1, nq):
            rcopy(src, ref.at[q], ss, rs, (rq(k), c)).start()

    def to_corpus(src, ref, ss, rs):
        for k in range(1, nc):
            rcopy(src, ref.at[c], ss, rs, (q, rc(k))).start()

    others = [(n, k) for n in range(nq) for k in range(r) if n or k]
    barrier = pltpu.get_barrier_semaphore()
    for n, k in others:
        if n and k:
            pl.semaphore_signal(barrier, inc=1, device_id=(rq(n), g * r + lane(k)), device_id_type=pl.DeviceIdType.MESH)
    for k in range(1, nq):
        pl.semaphore_signal(barrier, inc=1, device_id=(rq(k), c), device_id_type=pl.DeviceIdType.MESH)
    for k in range(1, nc):
        pl.semaphore_signal(barrier, inc=1, device_id=(q, rc(k)), device_id_type=pl.DeviceIdType.MESH)

    loaded(s.hidq, 0)
    squares = jnp.square(s.hidq[0].astype(F32))
    for i in range(1, nq):
        squares = squares + jnp.square(s.hidq[i].astype(F32))
    s.st_send[...] = lax.dot_general(jnp.ones((8, fq), F32), squares, (((1,), (1,)), ((), ())),
                                     precision=lax.Precision.HIGHEST, preferred_element_type=F32)
    counts.wait()
    slot_query = lax.broadcasted_iota(jnp.int32, (8, slots), 1) // SEQ
    own_lens = jnp.zeros((8, slots), jnp.int32)
    for k in range(slots // SEQ):
        own_lens = jnp.where(slot_query == k, s.lens_s[k], own_lens)
    s.lens_all[q] = own_lens

    pl.semaphore_wait(barrier, nq - 1 + nc - 1 + (nq - 1) * (r - 1))

    side_a = q + 1 - 2 * lax.rem(q, 2)
    side_b = q + 2 - 4 * (q // 2)
    far = nq - 1 - q

    for k in range(1, nq):
        rcopy(s.hidq.at[rq(k)], s.colbuf.at[q], s.a_s, s.a_r, (rq(k), c)).start()
    s.colbuf[q] = s.hidq[q]

    to_query(s.lens_all.at[q], s.lens_all, s.l_s, s.l_r)
    to_corpus(s.st_send, s.st_recv, s.st_s, s.st_r)
    s.st_recv[c] = s.st_send[...]
    got(s.lens_all.at[pl.ds(0, nq - 1)], s.l_r)
    lens_row = jnp.concatenate([s.lens_all[i] for i in range(nq)], axis=1)
    slot = lax.broadcasted_iota(jnp.int32, (8, total), 1)
    valid = lax.rem(slot, SEQ) < lens_row
    before = lax.broadcasted_iota(jnp.int32, (total, total), 0) < lax.broadcasted_iota(jnp.int32, (total, total), 1)
    pos = mm(valid.astype(F32).astype(BF16), before.astype(F32).astype(BF16)).astype(jnp.int32)
    pos = jnp.where(valid, pos, -1)[:1]

    got(s.st_recv.at[pl.ds(0, nc - 1)], s.st_r)
    stat = s.st_recv[0]
    for i in range(1, nc):
        stat = stat + s.st_recv[i]
    s.inv_all[q] = lax.rsqrt(stat / d_all + epsilon)
    to_query(s.inv_all.at[q], s.inv_all, s.iv_s, s.iv_r)

    def side(b, k):
        return rcopy(s.xall.at[j, b], s.xall.at[j, b], s.la_s, s.la_r.at[b], (q, g * r + lane(k)))

    def spread(b, k):
        t = lax.rem(g + k, ng)
        return rcopy(s.xpk.at[b], s.xall.at[j, b, q], s.x_s, s.x_r.at[b], (g, t * r + j))

    got(s.colbuf.at[pl.ds(0, nq - 1)], s.a_r)
    stacked = s.colbuf[...].reshape(total, fq)
    for b in range(nblk):
        row = lax.broadcasted_iota(jnp.int32, (bm, total), 0) + b * bm
        pick = (pos == row).astype(F32).astype(BF16)
        s.xpk[b] = mm(pick, stacked).astype(BF16)
        for k in range(ng - 1, 0, -1):
            spread(b, k).start()

        @pl.when(q != g)
        def _(b=b):
            spread(b, 0).start()

        @pl.when(q == g)
        def _(b=b):
            s.xall[j, b, q] = s.xpk[b]

    got(s.inv_all.at[pl.ds(0, nq - 1)], s.iv_r)
    inv_row = jnp.concatenate([s.inv_all[i] for i in range(nq)], axis=1)[:1]
    for b in range(nblk):
        row = lax.broadcasted_iota(jnp.int32, (bm, total), 0) + b * bm
        col = jnp.sum(jnp.where(pos == row, inv_row, 0.0), axis=1, keepdims=True)
        s.inv_c[b] = jnp.broadcast_to(col, (bm, LANES))

    loaded(s.gu, 2)

    def sides(n):
        odd = lax.rem(n, 2)
        return side_a + (side_b - side_a) * odd, side_b + (side_a - side_b) * odd

    def near_part(n):
        one, _ = sides(n)
        return rcopy(s.psend.at[n, one], s.precv.at[n, 0], s.p_s, s.p_r.at[n], (one, c))

    def far_part(n):
        one, _ = sides(n)
        return rcopy(s.psend.at[n, far], s.precv.at[n, 2], s.p_s, s.pf_r.at[n], (one, c))

    def passed_part(n):
        _, two = sides(n)
        return rcopy(s.precv.at[n, 3], s.precv.at[n, 1], s.p_s, s.p_r.at[n], (two, c))

    def h_near(n, k, sem):
        return rcopy(s.hall.at[n, q], s.hall.at[n, q], s.h_s, sem, (sides(n)[k], c))

    def h_pass(n, sem):
        one, two = sides(n)
        return rcopy(s.hall.at[n, one], s.hall.at[n, one], s.h_s, sem, (two, c))

    def fetch(b):
        @pl.when(q != g)
        def _():
            got(s.xall.at[0, b], s.x_r.at[b])

        @pl.when(q == g)
        def _():
            got(s.xall.at[0, b, pl.ds(0, nq - 1)], s.x_r.at[b])

        for k in range(1, r):
            side(b, k).start()

    def products(b):
        got(s.xall.at[pl.ds(0, r - 1), b], s.la_r.at[b])
        scale = s.inv_c[b][:, :1]
        for i in range(r):
            for k in range(nq):
                at = i * w + k * fq
                s.xn[:, at:at + fq] = (s.xall[i, b, k].astype(F32) * scale).astype(BF16)
        xb = s.xn[...]
        for h in range(nh):
            n = b * nh + h
            for e, wref in enumerate((gate, up)):
                full = mm(xb, wref[:, h * hw:(h + 1) * hw])
                s.full[h, e] = full
                for i in range(nq):
                    s.psend[n, i, e] = full[i * qm:(i + 1) * qm].astype(BF16)
            far_part(n).start()
            near_part(n).start()
            for e in range(2):
                s.pown[n, e] = s.full[h, e, pl.ds(pl.multiple_of(q * qm, qm), qm)]

    def pass_unit(n):
        _, two = sides(n)
        got(s.precv.at[n, 2], s.pf_r.at[n])
        s.precv[n, 3] = (s.psend[n, two].astype(F32) + s.precv[n, 2].astype(F32)).astype(BF16)
        passed_part(n).start()

    split = (nh + 1) // 2

    def landing(n):
        return s.hb_r.at[2 * (n // nh) + lax.rem(n, nh) // split]

    def reduce_unit(n):
        got(s.precv.at[n, pl.ds(0, 2)], s.p_r.at[n])
        gsum = s.pown[n, 0] + s.precv[n, 0, 0].astype(F32) + s.precv[n, 1, 0].astype(F32)
        usum = s.pown[n, 1] + s.precv[n, 0, 1].astype(F32) + s.precv[n, 1, 1].astype(F32)
        s.hall[n, q] = (gsum / (1.0 + jnp.exp(-gsum)) * usum).astype(BF16)
        h_near(n, 0, s.hn_r.at[n]).start()
        h_near(n, 1, landing(n)).start()

    def relay_unit(n):
        got(s.hall.at[n, 0], s.hn_r.at[n])
        h_pass(n, landing(n)).start()

    def lane_send(b, k):
        t = lane(k)
        return rcopy(s.lsend.at[b, t], s.lrecv.at[b, j], s.lr_s, s.lr_r.at[b], (q, g * r + t))

    def group_send(b, k):
        t = lax.rem(g + k, ng)
        return rcopy(s.gsend.at[b, t], s.grecv.at[b, g], s.g_s, s.g_r.at[b], (q, t * r + j))

    def down_block(b):
        part = None
        for h in range(nh):
            n = b * nh + h
            if h % split == 0:
                got(s.hall.at[pl.ds(n, min(split, nh - h)), pl.ds(0, 2)], s.hb_r.at[2 * b + h // split])
            term = mm(s.hall[n].reshape(bm, hw), s.down[h * hw:(h + 1) * hw, :])
            part = term if part is None else part + term
        s.acc[b] = part
        for t in range(r):
            s.lsend[b, t] = part[:, t * w:(t + 1) * w].astype(BF16)
        for k in range(1, r):
            lane_send(b, k).start()

    def sum_block(b):
        mine = s.acc[b, :, pl.ds(pl.multiple_of(j * w, w), w)]
        got(s.lrecv.at[b, pl.ds(0, r - 1)], s.lr_r.at[b])
        for k in range(1, r):
            mine = mine + s.lrecv[b, lane(k)].astype(F32)
        s.mine[b] = mine
        for t in range(ng):
            s.gsend[b, t] = mine[t * gm:(t + 1) * gm].astype(BF16)
        for k in range(1, ng):
            group_send(b, k).start()

    def units(unit, b):
        for h in range(nh):
            unit(b * nh + h)

    def fetch_next(b):
        @pl.when(b + 1 < nblk)
        def _():
            fetch(b + 1)

    fetch(0)
    stages = (products, fetch_next, functools.partial(units, pass_unit), functools.partial(units, reduce_unit), functools.partial(units, relay_unit), sum_block, down_block)
    delays = (0, 0, 1, 2, 3, 5, 4)

    def turn(t, carry):
        for stage, delay in zip(stages, delays):
            @pl.when(jnp.logical_and(t >= delay, t < nblk + delay))
            def _(stage=stage, delay=delay):
                stage(t - delay)
        return carry

    loaded(s.down, 3)
    lax.fori_loop(0, nblk + max(delays), turn, 0)
    own = pl.ds(pl.multiple_of(g * gm, gm), gm)
    for b in range(nblk):
        for k in range(nq):
            s.res[b * gm:(b + 1) * gm, k * fq:(k + 1) * fq] = s.xall[j, b, k, own].astype(F32)
    for b in range(nblk):
        total_b = s.mine[b, own]
        got(s.grecv.at[b, pl.ds(0, ng - 1)], s.g_r.at[b])
        for k in range(1, ng):
            total_b = total_b + s.grecv[b, lax.rem(g + k, ng)].astype(F32)
        s.res[b * gm:(b + 1) * gm] = s.res[b * gm:(b + 1) * gm] + total_b
    residual = s.res[...]
    tb = nblk * gm

    sums = lax.dot_general(jnp.ones((8, w), F32), residual * residual, (((1,), (1,)), ((), ())),
                           precision=lax.Precision.HIGHEST, preferred_element_type=F32)
    s.t_send[...] = jnp.concatenate([sums, jnp.zeros((8, LANES - tb), F32)], axis=1)
    for n, k in others:
        rcopy(s.t_send, s.t_recv.at[q * r + j], s.t_s, s.t_r, (rq(n), g * r + lane(k))).start()
    qrow = lax.broadcasted_iota(jnp.int32, (nqueries, total), 0)
    qslot = lax.broadcasted_iota(jnp.int32, (nqueries, total), 1)
    lens_b = jnp.broadcast_to(lens_row[:1], (nqueries, total)).astype(F32)
    vals_b = jnp.broadcast_to(valid.astype(F32)[:1], (nqueries, total))
    len_col = jnp.sum(jnp.where(qslot == qrow * SEQ, lens_b, 0.0), axis=1, keepdims=True)
    off_col = jnp.sum(jnp.where(qslot < qrow * SEQ, vals_b, 0.0), axis=1, keepdims=True)
    prow = lax.broadcasted_iota(jnp.int32, (nqueries, tb), 1)
    prow = ((prow // gm) * bm + g * gm + lax.rem(prow, gm)).astype(F32)
    member = jnp.where(jnp.logical_and(prow >= off_col, prow < off_col + len_col), 1.0, 0.0)
    tsum = s.t_send[...]
    got(s.t_recv.at[pl.ds(0, len(others))], s.t_r)
    for n, k in others:
        tsum = tsum + s.t_recv[rq(n) * r + lane(k)]
    inv_own = lax.rsqrt(tsum[:1, :tb] / d_all + epsilon)
    pooled_part = mm(member * inv_own, residual, lax.Precision.HIGHEST)
    s.pp[...] = pooled_part

    @pl.when(g != q)
    def _():
        rcopy(s.pp, s.prc.at[g], s.pp_s, s.pp_r, (q, q * r + j)).start()

    @pl.when(g == q)
    def _():
        pooled = pooled_part
        got(s.prc.at[pl.ds(0, ng - 1)], s.pp_r)
        for k in range(1, ng):
            pooled = pooled + s.prc[lax.rem(g + k, ng)]
        s.pblk[0] = (pooled / len_col).astype(BF16)
        for k in range(1, nq):
            rcopy(s.pblk.at[0], s.pblk.at[0], s.pb_s, s.pb_r, (rq(k), c)).start()

    loaded(s.codeq, 4)
    loaded(s.corp, 5)

    @pl.when(g != q)
    def _():
        got(s.pblk.at[0], s.pb_r)

    s.cpart[...] = mm(s.pblk[0], s.codeq[...])
    to_corpus(s.cpart, s.crecv, s.c_s, s.c_r)
    s.crecv[c] = s.cpart[...]
    got(s.crecv.at[pl.ds(0, nc - 1)], s.c_r)
    csum = s.crecv[0]
    for i in range(1, nc):
        csum = csum + s.crecv[i]
    s.codes[q] = csum.astype(BF16)
    to_query(s.codes.at[q], s.codes, s.o_s, s.o_r)
    got(s.codes.at[pl.ds(0, nq - 1)], s.o_r)
    qcodes = jnp.concatenate([s.codes[i] for i in range(nq)], axis=1)
    scale = 1.0 / math.sqrt(corp.shape[1])
    scores = lax.dot_general(qcodes, corp[...], (((1,), (1,)), ((), ())), preferred_element_type=F32) * scale

    blocks = corp.shape[0] // LANES
    lists = jnp.concatenate([scores[:, i * LANES:(i + 1) * LANES] for i in range(blocks)], axis=0)
    best = top_rows(lists, nqueries, q >= nq // 2, s.board)
    s.top_q[q] = best
    to_query(s.top_q.at[q], s.top_q, s.tq_s, s.tq_r)
    got(s.top_q.at[pl.ds(0, nq - 1)], s.tq_r)
    best = merge_rows(s.top_q[...].reshape(nq * nqueries, LANES), nqueries, c >= nc // 2)
    s.top_c[c] = best
    to_corpus(s.top_c.at[c], s.top_c, s.tc_s, s.tc_r)
    got(s.top_c.at[pl.ds(0, nc - 1)], s.tc_r)
    best = merge_rows(s.top_c[...].reshape(nc * nqueries, LANES), nqueries, False)
    out[...] = best[:, :TOPK]

    sent(s.lens_all.at[pl.ds(0, nq - 1)], s.l_s)
    sent(s.st_recv.at[pl.ds(0, nc - 1)], s.st_s)
    sent(s.inv_all.at[pl.ds(0, nq - 1)], s.iv_s)

    sent(s.colbuf.at[pl.ds(0, nq - 1)], s.a_s)

    @pl.when(q != g)
    def _():
        sent(s.xall.at[0], s.x_s)

    @pl.when(q == g)
    def _():
        sent(s.xall.at[0, :, pl.ds(0, nq - 1)], s.x_s)

    sent(s.xall.at[pl.ds(0, r - 1)], s.la_s)
    sent(s.psend.at[:, pl.ds(0, 3)], s.p_s)
    sent(s.hall.at[:, pl.ds(0, 3)], s.h_s)
    sent(s.lsend.at[:, pl.ds(0, r - 1)], s.lr_s)
    sent(s.gsend.at[:, pl.ds(0, ng - 1)], s.g_s)
    sent(s.t_recv.at[pl.ds(0, len(others))], s.t_s)

    @pl.when(g == q)
    def _():
        sent(s.pblk.at[pl.ds(0, nq - 1)], s.pb_s)

    @pl.when(g != q)
    def _():
        sent(s.pp, s.pp_s)

    sent(s.crecv.at[pl.ds(0, nc - 1)], s.c_s)
    sent(s.codes.at[pl.ds(0, nq - 1)], s.o_s)
    sent(s.top_q.at[pl.ds(0, nq - 1)], s.tq_s)
    sent(s.top_c.at[pl.ds(0, nc - 1)], s.tc_s)


def chunks_of(ffc):
    return ffc // CHUNK if ffc % CHUNK == 0 else 1


def per_device_fast(nq, nc, hidden_in, lengths, gate_weight, up_weight, down_weight, code_weight, corpus_codes):
    slots, w = hidden_in.shape
    r = nc // nq
    ng = nc // r
    nreal = nq * slots * REAL_NUM // REAL_DEN
    dq, ffc = gate_weight.shape
    bm = 8 * nc
    nblk = nreal // bm
    nh = chunks_of(ffc)
    hw = ffc // nh
    nu = nblk * nh
    qm, gm = bm // nq, bm // ng
    tb = nblk * gm
    nqueries = nq * lengths.shape[0]
    bits = code_weight.shape[1]
    bw = bits // nq
    vm, dma = pltpu.VMEM, pltpu.SemaphoreType.DMA
    scratch = dict(
        gu=vm((2,) + gate_weight.shape, BF16), down=vm(down_weight.shape, BF16), codeq=vm((w, bw), BF16), corp=vm(corpus_codes.shape, BF16),
        lens_s=pltpu.SMEM(lengths.shape, jnp.int32),
        hidq=vm((nq, slots, w // nq), BF16), colbuf=vm((nq, slots, w // nq), BF16), xpk=vm((nblk, bm, w // nq), BF16), lens_all=vm((nq, 8, slots), jnp.int32), xall=vm((r, nblk, nq, bm, w // nq), BF16),
        xn=vm((bm, dq), BF16), inv_c=vm((nblk, bm, LANES), F32),
        st_send=vm((8, slots), F32), st_recv=vm((nc, 8, slots), F32), inv_all=vm((nq, 8, slots), F32),
        psend=vm((nu, nq, 2, qm, hw), BF16), precv=vm((nu, 4, 2, qm, hw), BF16), pown=vm((nu, 2, qm, hw), F32), full=vm((nh, 2, bm, hw), F32),
        hall=vm((nu, nq, qm, hw), BF16),
        acc=vm((nblk, bm, dq), F32), lsend=vm((nblk, r, bm, w), BF16), lrecv=vm((nblk, r, bm, w), BF16),
        mine=vm((nblk, bm, w), F32), gsend=vm((nblk, ng, gm, w), BF16), grecv=vm((nblk, ng, gm, w), BF16), res=vm((tb, w), F32),
        t_send=vm((8, LANES), F32), t_recv=vm((nq * r, 8, LANES), F32),
        pp=vm((nqueries, w), F32), prc=vm((ng, nqueries, w), F32), pblk=vm((nq, nqueries, w), BF16),
        cpart=vm((nqueries, bw), F32), crecv=vm((nc, nqueries, bw), F32), codes=vm((nq, nqueries, bw), BF16),
        top_q=vm((nq, nqueries, LANES), F32), top_c=vm((nc, nqueries, LANES), F32), board=vm((LANES, LANES), F32),
        w_s=dma((6,)), l_s=dma, l_r=dma, a_s=dma, a_r=dma, st_s=dma, st_r=dma, iv_s=dma, iv_r=dma,
        x_s=dma, x_r=dma((nblk,)), la_s=dma, la_r=dma((nblk,)),
        p_s=dma, p_r=dma((nu,)), pf_r=dma((nu,)), h_s=dma, hn_r=dma((nu,)), hb_r=dma((2 * nblk,)),
        lr_s=dma, lr_r=dma((nblk,)), g_s=dma, g_r=dma((nblk,)),
        t_s=dma, t_r=dma, pp_s=dma, pp_r=dma, pb_s=dma, pb_r=dma, c_s=dma, c_r=dma, o_s=dma, o_r=dma,
        tq_s=dma, tq_r=dma, tc_s=dma, tc_r=dma,
    )
    dims = (nq, nc, r, nblk, bm, nh, hw, w * nc)
    vspec, aspec = pl.BlockSpec(memory_space=pltpu.VMEM), pl.BlockSpec(memory_space=pl.ANY)
    return pl.pallas_call(
        functools.partial(fast_kernel, dims, tuple(scratch)),
        out_shape=jax.ShapeDtypeStruct((nqueries, TOPK), F32),
        in_specs=[aspec] * 7,
        out_specs=vspec,
        scratch_shapes=list(scratch.values()),
        compiler_params=pltpu.CompilerParams(
            collective_id=0, has_side_effects=True, vmem_limit_bytes=60 * 1024 * 1024),
    )(hidden_in, lengths, gate_weight, up_weight, down_weight, code_weight, corpus_codes)


def per_device(nq, nc, hidden_in, *rest):
    slots, w = hidden_in.shape
    nreal = nq * slots * REAL_NUM // REAL_DEN
    nqueries = nq * rest[0].shape[0]
    lists = nqueries * max(nc, nq, rest[5].shape[0] // LANES)
    fits = nreal // nq <= LANES and lists <= LANES and LANES % lists == 0 and nreal % (8 * nc) == 0 and w % (nq * LANES) == 0
    body = per_device_fast if fits else per_device_general
    return body(nq, nc, hidden_in, *rest)


def solution(mesh):
    in_specs = (
        P("query", "corpus"),
        P("query"),
        P("query", "corpus"),
        P("query", "corpus"),
        P("corpus", "query"),
        P("corpus", None),
        P(("query", "corpus"), None),
    )
    body = functools.partial(per_device, mesh.shape["query"], mesh.shape["corpus"])
    return jax.shard_map(body, mesh=mesh, in_specs=in_specs, out_specs=P(), check_vma=False)
```

```python
import functools
import math
import types

import jax
import jax.numpy as jnp
from jax import lax
from jax.experimental import pallas as pl
from jax.experimental.pallas import tpu as pltpu
from jax.sharding import PartitionSpec as P

SEQ = 32
LANES = 128
TOPK = 100
REAL_NUM, REAL_DEN = 5, 8
CHUNK = 256
PIECE = 32

epsilon = 1e-05
F32, BF16 = jnp.float32, jnp.bfloat16


def mm(a, b, precision=None):
    return lax.dot_general(a, b, (((1,), (0,)), ((), ())), precision=precision, preferred_element_type=F32)


def rcopy(src, dst, send, recv, dev):
    return pltpu.make_async_remote_copy(
        src_ref=src, dst_ref=dst, send_sem=send, recv_sem=recv,
        device_id=dev, device_id_type=pl.DeviceIdType.MESH)


def exchange(x, s, keep_max):
    bit = (lax.broadcasted_iota(jnp.int32, x.shape, 1) & s) != 0
    other = jnp.where(bit, pltpu.roll(x, s, 1), pltpu.roll(x, LANES - s, 1))
    return jnp.where(keep_max, jnp.maximum(x, other), jnp.minimum(x, other))


def sort_lanes(x):
    lane = lax.broadcasted_iota(jnp.int32, x.shape, 1)
    flip = (lax.broadcasted_iota(jnp.int32, x.shape, 0) >= x.shape[0] // 2).astype(jnp.int32)
    size = 2
    while size <= LANES:
        up = ((lane & size) != 0).astype(jnp.int32) if size < LANES else jnp.zeros_like(lane)
        s = size // 2
        while s:
            low = ((lane & s) != 0).astype(jnp.int32)
            x = exchange(x, s, (low ^ up ^ flip) == 0)
            s //= 2
        size *= 2
    return x


def merge_all(x, rows, lone):
    while x.shape[0] > rows:
        half = x.shape[0] // 2
        x = jnp.maximum(x[:half], x[half:])
        lane = lax.broadcasted_iota(jnp.int32, x.shape, 1)
        if half > rows:
            flip = (lax.broadcasted_iota(jnp.int32, x.shape, 0) >= half // 2).astype(jnp.int32)
        else:
            flip = jnp.zeros_like(lane) + jnp.asarray(lone, jnp.int32)
        s = LANES // 2
        while s:
            low = ((lane & s) != 0).astype(jnp.int32)
            x = exchange(x, s, (low ^ flip) == 0)
            s //= 2
    return x


def general_kernel(dims, hid, lens, gate_h, up_h, down_h, code_h, corp_h, out,
                 gate, up, down, code, corp, colbuf, lens_all, xall, psend, precv,
                 st_send, st_recv, inv_all, xn, pown, top_q, top_c, hall, acc, lsend, lrecv, gsend, grecv, t_send, t_recv,
                 pp, prc, pblk, cpart, crecv, codes,
                 w_s, a_s, a_r, l_s, l_r, ch_s, ch_r, la_s, la_r, p_s, p_r, st_s, st_r, iv_s, iv_r, tq_s, tq_r, tc_s, tc_r, h_s, h_r,
                 lr_s, lr_r, g_s, g_r, t_s, t_r, pp_s, pp_r, pb_s, pb_r, c_s, c_r, o_s, o_r):
    nq, nc, r, nreal, tq, tb, nch, cw, d_all = dims
    q = lax.axis_index("query")
    c = lax.axis_index("corpus")
    g = c // r
    j = lax.rem(c, r)
    slots, w = hid.shape[0], hid.shape[1]
    total = nq * slots
    nqueries = total // SEQ
    bw = code.shape[1] // nq

    loads = []
    for i, (s, d) in enumerate(((gate_h, gate), (up_h, up), (down_h, down), (code_h, code), (corp_h, corp))):
        cp = pltpu.make_async_copy(s, d, w_s.at[i])
        cp.start()
        loads.append(cp)

    def rq(k):
        return lax.rem(q + k, nq)

    def rc(k):
        return lax.rem(c + k, nc)

    def lane(k):
        return lax.rem(j + k, r)

    barrier = pltpu.get_barrier_semaphore()
    for k in range(1, nq):
        pl.semaphore_signal(barrier, inc=1, device_id=(rq(k), c), device_id_type=pl.DeviceIdType.MESH)
    for k in range(1, nc):
        pl.semaphore_signal(barrier, inc=1, device_id=(q, rc(k)), device_id_type=pl.DeviceIdType.MESH)
    pl.semaphore_wait(barrier, nq - 1 + nc - 1)

    for k in range(1, nq):
        rcopy(lens, lens_all.at[q], l_s.at[k], l_r.at[q], (rq(k), c)).start()

    @pl.when(q != g)
    def _():
        rcopy(hid, colbuf.at[q], a_s, a_r.at[q], (g, c)).start()

    squares = jnp.square(hid[...].astype(F32))
    st_send[...] = lax.dot_general(jnp.ones((8, w), F32), squares, (((1,), (1,)), ((), ())),
                                   precision=lax.Precision.HIGHEST, preferred_element_type=F32)
    for k in range(1, nc):
        rcopy(st_send, st_recv.at[c], st_s.at[k], st_r.at[c], (q, rc(k))).start()
    st_recv[c] = st_send[...]
    lens_all[q] = lens[...]
    for k in range(1, nq):
        s = rq(k)
        rcopy(lens, lens_all.at[s], l_s.at[k], l_r.at[s], (s, c)).wait_recv()
    lens_row = jnp.concatenate([lens_all[i] for i in range(nq)], axis=1)
    slot = lax.broadcasted_iota(jnp.int32, (8, total), 1)
    valid = lax.rem(slot, SEQ) < lens_row
    before = lax.broadcasted_iota(jnp.int32, (total, total), 0) < lax.broadcasted_iota(jnp.int32, (total, total), 1)
    pos = mm(valid.astype(F32).astype(BF16), before.astype(F32).astype(BF16)).astype(jnp.int32)
    pos = jnp.where(valid, pos, -1)[:1]

    for k in range(1, nc):
        s = rc(k)
        rcopy(st_send, st_recv.at[s], st_s.at[k], st_r.at[s], (q, s)).wait_recv()
    stat = st_recv[0]
    for i in range(1, nc):
        stat = stat + st_recv[i]
    inv_all[q] = lax.rsqrt(stat / d_all + epsilon)
    for k in range(1, nq):
        rcopy(inv_all.at[q], inv_all.at[q], iv_s.at[k], iv_r.at[q], (rq(k), c)).start()

    nb = ch_r.shape[0]
    ct = nreal // nb

    def chunk(i, slot_j):
        return xall.at[slot_j, pl.ds(i * ct, ct)]

    def down_chain(i):
        return rcopy(chunk(i, j), chunk(i, j), ch_s.at[0, i], ch_r.at[i], (q, jnp.maximum(c - r, 0)))

    def up_chain(i):
        return rcopy(chunk(i, j), chunk(i, j), ch_s.at[1, i], ch_r.at[i], (q, jnp.minimum(c + r, nc - 1)))

    sends_up = jnp.logical_and(g >= q, g < nc // r - 1)
    sends_down = jnp.logical_and(g <= q, g > 0)

    @pl.when(q == g)
    def _():
        colbuf[q] = hid[...]
        for k in range(1, nq):
            s = rq(k)
            rcopy(hid, colbuf.at[s], a_s, a_r.at[s], (s, c)).wait_recv()
        stacked = colbuf[...].reshape(total, w)
        for i in range(nq):
            row = lax.broadcasted_iota(jnp.int32, (tq, total), 0) + i * tq
            pick = (pos == row).astype(F32).astype(BF16)
            xall[j, i * tq:(i + 1) * tq, :] = mm(pick, stacked).astype(BF16)

    for i in range(nb):
        @pl.when(q != g)
        def _(i=i):
            up_chain(i).wait_recv()

        @pl.when(sends_up)
        def _(i=i):
            up_chain(i).start()

        @pl.when(sends_down)
        def _(i=i):
            down_chain(i).start()

        for k in range(1, r):
            rcopy(chunk(i, j), chunk(i, j), la_s.at[k, i], la_r.at[j, i], (q, g * r + lane(k))).start()
    for k in range(1, nq):
        s = rq(k)
        rcopy(inv_all.at[s], inv_all.at[s], iv_s.at[k], iv_r.at[s], (s, c)).wait_recv()
    inv_row = jnp.concatenate([inv_all[i] for i in range(nq)], axis=1)[:1]
    inv_cols = []
    for i in range(nq):
        row = lax.broadcasted_iota(jnp.int32, (tq, total), 0) + i * tq
        inv_cols.append(jnp.sum(jnp.where(pos == row, inv_row, 0.0), axis=1, keepdims=True))
    inv = jnp.concatenate(inv_cols, axis=0)
    for i in range(nb):
        for k in range(1, r):
            s = lane(k)
            rcopy(chunk(i, s), chunk(i, s), la_s.at[k, i], la_r.at[s, i], (q, g * r + s)).wait_recv()

    loads[0].wait()
    loads[1].wait()

    for i in range(r):
        xn[i] = (xall[i].astype(F32) * inv).astype(BF16)

    side_a = q + 1 - 2 * lax.rem(q, 2)
    side_b = q + 2 - 4 * (q // 2)
    far = nq - 1 - q

    def sides(n):
        odd = lax.rem(n, 2)
        return side_a + (side_b - side_a) * odd, side_b + (side_a - side_b) * odd

    def near_part(n):
        one, _ = sides(n)
        return rcopy(psend.at[n, one], precv.at[n, 0], p_s.at[n, 0], p_r.at[n, 0], (one, c))

    def far_part(n):
        one, _ = sides(n)
        return rcopy(psend.at[n, far], precv.at[n, 1], p_s.at[n, 1], p_r.at[n, 1], (one, c))

    def passed_part(n):
        _, two = sides(n)
        return rcopy(precv.at[n, 3], precv.at[n, 2], p_s.at[n, 2], p_r.at[n, 2], (two, c))

    def h_near(n, k):
        to = sides(n)[k]
        return rcopy(hall.at[n, q], hall.at[n, q], h_s.at[n, k], h_r.at[n, k], (to, c))

    def h_near_in(n, k):
        to = sides(n)[k]
        return rcopy(hall.at[n, to], hall.at[n, to], h_s.at[n, k], h_r.at[n, k], (to, c))

    def h_pass(n):
        one, two = sides(n)
        return rcopy(hall.at[n, one], hall.at[n, one], h_s.at[n, 2], h_r.at[n, 2], (two, c))

    def h_pass_in(n):
        _, two = sides(n)
        return rcopy(hall.at[n, far], hall.at[n, far], h_s.at[n, 2], h_r.at[n, 2], (two, c))

    def matmuls(n, carry):
        cols = pl.ds(pl.multiple_of(n * cw, cw), cw)
        for e, wref in enumerate((gate, up)):
            full = sum(mm(xn[i], wref[i * w:(i + 1) * w, cols]) for i in range(r))
            for i in range(nq):
                psend[n, i, e] = full[i * tq:(i + 1) * tq].astype(BF16)

                @pl.when(q == i)
                def _(i=i, e=e, full=full):
                    pown[n, e] = full[i * tq:(i + 1) * tq]
        far_part(n).start()
        near_part(n).start()
        return carry

    lax.fori_loop(0, nch, matmuls, 0)

    loads[2].wait()
    acc[...] = jnp.zeros_like(acc)

    def pass_chunk(n):
        _, two = sides(n)
        far_part(n).wait_recv()
        precv[n, 3] = (psend[n, two].astype(F32) + precv[n, 1].astype(F32)).astype(BF16)
        passed_part(n).start()

    def reduce_chunk(n):
        near_part(n).wait_recv()
        passed_part(n).wait_recv()
        gsum = pown[n, 0] + precv[n, 0, 0].astype(F32) + precv[n, 2, 0].astype(F32)
        usum = pown[n, 1] + precv[n, 0, 1].astype(F32) + precv[n, 2, 1].astype(F32)
        hall[n, q] = (gsum / (1.0 + jnp.exp(-gsum)) * usum).astype(BF16)
        h_near(n, 0).start()
        h_near(n, 1).start()

    def relay_chunk(n):
        h_near_in(n, 0).wait_recv()
        h_pass(n).start()

    def down_chunk(n):
        h_near_in(n, 1).wait_recv()
        h_pass_in(n).wait_recv()
        acc[...] += mm(hall[n].reshape(nreal, cw), down[pl.ds(pl.multiple_of(n * cw, cw), cw), :])

    def passes(n, carry):
        pass_chunk(n)
        return carry

    lax.fori_loop(0, nch, passes, 0)
    reduce_chunk(0)

    def reduces(n, carry):
        reduce_chunk(n)
        relay_chunk(n - 1)
        return carry

    lax.fori_loop(1, nch, reduces, 0)
    relay_chunk(nch - 1)

    def downs(n, carry):
        down_chunk(n)
        return carry

    lax.fori_loop(0, nch, downs, 0)

    ng = nc // r
    for gg in range(ng):
        for jj in range(r):
            b = gg * r + jj
            lsend[jj, gg] = acc[b * tb:(b + 1) * tb].astype(BF16)
    for k in range(1, r):
        t = lane(k)
        rcopy(lsend.at[t], lrecv.at[j], lr_s.at[k], lr_r.at[j], (q, g * r + t)).start()
    mine = lsend[j].astype(F32)
    for k in range(1, r):
        s = lane(k)
        rcopy(lsend.at[s], lrecv.at[s], lr_s.at[k], lr_r.at[s], (q, g * r + s)).wait_recv()
        mine = mine + lrecv[s].astype(F32)
    gsend[...] = mine.astype(BF16)
    for k in range(1, ng):
        t = lax.rem(g + k, ng)
        rcopy(gsend.at[t], grecv.at[g], g_s.at[k], g_r.at[g], (q, t * r + j)).start()
    row = lax.broadcasted_iota(jnp.int32, (tb, nreal), 0) + c * tb
    own_rows = (lax.broadcasted_iota(jnp.int32, (tb, nreal), 1) == row).astype(F32).astype(BF16)
    residual = jnp.concatenate([mm(own_rows, xall[i]) for i in range(r)], axis=1)
    residual = residual + gsend[g].astype(F32)
    for k in range(1, ng):
        s = lax.rem(g + k, ng)
        rcopy(gsend.at[s], grecv.at[s], g_s.at[k], g_r.at[s], (q, s * r + j)).wait_recv()
        residual = residual + grecv[s].astype(F32)

    t_send[...] = jnp.broadcast_to(jnp.sum(residual * residual, axis=1, keepdims=True), (tb, 128))
    for k in range(1, nq):
        rcopy(t_send, t_recv.at[q], t_s.at[k], t_r.at[q], (rq(k), c)).start()
    qrow = lax.broadcasted_iota(jnp.int32, (nqueries, total), 0)
    qslot = lax.broadcasted_iota(jnp.int32, (nqueries, total), 1)
    lens_b = jnp.broadcast_to(lens_row[:1], (nqueries, total)).astype(F32)
    vals_b = jnp.broadcast_to(valid.astype(F32)[:1], (nqueries, total))
    len_col = jnp.sum(jnp.where(qslot == qrow * SEQ, lens_b, 0.0), axis=1, keepdims=True)
    off_col = jnp.sum(jnp.where(qslot < qrow * SEQ, vals_b, 0.0), axis=1, keepdims=True)
    prow = (lax.broadcasted_iota(jnp.int32, (nqueries, tb), 1) + c * tb).astype(F32)
    member = jnp.where(jnp.logical_and(prow >= off_col, prow < off_col + len_col), 1.0, 0.0)
    tsum = t_send[...]
    for k in range(1, nq):
        s = rq(k)
        rcopy(t_send, t_recv.at[s], t_s.at[k], t_r.at[s], (s, c)).wait_recv()
        tsum = tsum + t_recv[s]
    final = residual * lax.rsqrt(tsum[:, :1] / d_all + epsilon)
    pooled_part = mm(member, final, lax.Precision.HIGHEST)
    for i in range(r):
        pp[i] = pooled_part[:, i * w:(i + 1) * w]
    for i in range(r):
        @pl.when(c != q * r + i)
        def _(i=i):
            rcopy(pp.at[i], prc.at[c], pp_s.at[i], pp_r.at[c], (q, q * r + i)).start()

    @pl.when(g == q)
    def _():
        pooled = pp[j]
        for k in range(1, nc):
            s = rc(k)
            rcopy(pp.at[j], prc.at[s], pp_s.at[0], pp_r.at[s], (q, s)).wait_recv()
            pooled = pooled + prc[s]
        pblk[...] = (pooled / len_col).astype(BF16)
        for k in range(1, nq):
            rcopy(pblk, pblk, pb_s.at[k], pb_r, (rq(k), c)).start()

    loads[3].wait()
    loads[4].wait()

    @pl.when(g != q)
    def _():
        rcopy(pblk, pblk, pb_s.at[0], pb_r, (g, c)).wait_recv()

    cpart[...] = mm(pblk[...], code[:, pl.ds(pl.multiple_of(q * bw, bw), bw)])
    for k in range(1, nc):
        rcopy(cpart, crecv.at[c], c_s.at[k], c_r.at[c], (q, rc(k))).start()
    crecv[c] = cpart[...]
    for k in range(1, nc):
        s = rc(k)
        rcopy(cpart, crecv.at[s], c_s.at[k], c_r.at[s], (q, s)).wait_recv()
    csum = crecv[0]
    for i in range(1, nc):
        csum = csum + crecv[i]
    codes[q] = csum.astype(BF16)
    for k in range(1, nq):
        rcopy(codes.at[q], codes.at[q], o_s.at[k], o_r.at[q], (rq(k), c)).start()
    for k in range(1, nq):
        s = rq(k)
        rcopy(codes.at[s], codes.at[s], o_s.at[k], o_r.at[s], (s, c)).wait_recv()
    qcodes = jnp.concatenate([codes[i] for i in range(nq)], axis=1)
    scale = 1.0 / math.sqrt(corp.shape[1])
    scores = lax.dot_general(qcodes, corp[...], (((1,), (1,)), ((), ())), preferred_element_type=F32) * scale

    blocks = corp.shape[0] // LANES
    lists = jnp.concatenate([scores[:, i * LANES:(i + 1) * LANES] for i in range(blocks)], axis=0)
    best = merge_all(sort_lanes(lists), nqueries, q >= nq // 2)
    top_q[q] = best
    for k in range(1, nq):
        rcopy(top_q.at[q], top_q.at[q], tq_s.at[k], tq_r.at[q], (rq(k), c)).start()
    for k in range(1, nq):
        s = rq(k)
        rcopy(top_q.at[s], top_q.at[s], tq_s.at[k], tq_r.at[s], (s, c)).wait_recv()
    best = merge_all(top_q[...].reshape(nq * nqueries, LANES), nqueries, c >= nc // 2)
    top_c[c] = best
    for k in range(1, nc):
        rcopy(top_c.at[c], top_c.at[c], tc_s.at[k], tc_r.at[c], (q, rc(k))).start()
    for k in range(1, nc):
        s = rc(k)
        rcopy(top_c.at[s], top_c.at[s], tc_s.at[k], tc_r.at[s], (q, s)).wait_recv()
    best = merge_all(top_c[...].reshape(nc * nqueries, LANES), nqueries, False)
    out[...] = best[:, :TOPK]

    for k in range(1, nq):
        rcopy(lens, lens_all.at[q], l_s.at[k], l_r.at[q], (rq(k), c)).wait_send()
        rcopy(inv_all.at[q], inv_all.at[q], iv_s.at[k], iv_r.at[q], (rq(k), c)).wait_send()
        rcopy(top_q.at[q], top_q.at[q], tq_s.at[k], tq_r.at[q], (rq(k), c)).wait_send()
        rcopy(t_send, t_recv.at[q], t_s.at[k], t_r.at[q], (rq(k), c)).wait_send()
        rcopy(codes.at[q], codes.at[q], o_s.at[k], o_r.at[q], (rq(k), c)).wait_send()

    @pl.when(q != g)
    def _():
        rcopy(hid, colbuf.at[q], a_s, a_r.at[q], (g, c)).wait_send()

    for i in range(nb):
        @pl.when(sends_up)
        def _(i=i):
            up_chain(i).wait_send()

        @pl.when(sends_down)
        def _(i=i):
            down_chain(i).wait_send()

        for k in range(1, r):
            rcopy(chunk(i, j), chunk(i, j), la_s.at[k, i], la_r.at[j, i], (q, g * r + lane(k))).wait_send()

    def drain(n, carry):
        far_part(n).wait_send()
        near_part(n).wait_send()
        passed_part(n).wait_send()
        h_near(n, 0).wait_send()
        h_near(n, 1).wait_send()
        h_pass(n).wait_send()
        return carry

    lax.fori_loop(0, nch, drain, 0)
    for k in range(1, r):
        rcopy(lsend.at[lane(k)], lrecv.at[j], lr_s.at[k], lr_r.at[j], (q, g * r + lane(k))).wait_send()
    for k in range(1, ng):
        t = lax.rem(g + k, ng)
        rcopy(gsend.at[t], grecv.at[g], g_s.at[k], g_r.at[g], (q, t * r + j)).wait_send()
    for i in range(r):
        @pl.when(c != q * r + i)
        def _(i=i):
            rcopy(pp.at[i], prc.at[c], pp_s.at[i], pp_r.at[c], (q, q * r + i)).wait_send()

    @pl.when(g == q)
    def _():
        for k in range(1, nq):
            rcopy(pblk, pblk, pb_s.at[k], pb_r, (rq(k), c)).wait_send()
    for k in range(1, nc):
        rcopy(cpart, crecv.at[c], c_s.at[k], c_r.at[c], (q, rc(k))).wait_send()
        rcopy(st_send, st_recv.at[c], st_s.at[k], st_r.at[c], (q, rc(k))).wait_send()
        rcopy(top_c.at[c], top_c.at[c], tc_s.at[k], tc_r.at[c], (q, rc(k))).wait_send()


def per_device_general(nq, nc, hidden_in, lengths, gate_weight, up_weight, down_weight, code_weight, corpus_codes):
    slots, w = hidden_in.shape
    r = nc // nq
    nreal = nq * slots * REAL_NUM // REAL_DEN
    tq, tb = nreal // nq, nreal // nc
    dq, ffc = gate_weight.shape
    cw = CHUNK if ffc % CHUNK == 0 else ffc
    nch = ffc // cw
    nb = nreal // PIECE if nreal % PIECE == 0 else nq
    nqueries = nq * lengths.shape[0]
    bits = code_weight.shape[1]
    bw = bits // nq
    ng = nc // r
    lens = jnp.broadcast_to(jnp.repeat(lengths, SEQ)[None, :], (8, slots))
    vm, dma = pltpu.VMEM, pltpu.SemaphoreType.DMA
    scratch = [
        vm(gate_weight.shape, BF16), vm(up_weight.shape, BF16), vm(down_weight.shape, BF16),
        vm(code_weight.shape, BF16), vm(corpus_codes.shape, BF16),
        vm((nq, slots, w), BF16), vm((nq, 8, slots), jnp.int32), vm((r, nreal, w), BF16),
        vm((nch, nq, 2, tq, cw), BF16), vm((nch, nq, 2, tq, cw), BF16),
        vm((8, slots), F32), vm((nc, 8, slots), F32), vm((nq, 8, slots), F32), vm((r, nreal, w), BF16),
        vm((nch, 2, tq, cw), F32), vm((nq, nqueries, LANES), F32), vm((nc, nqueries, LANES), F32),
        vm((nch, nq, tq, cw), BF16), vm((nreal, dq), F32),
        vm((r, ng, tb, dq), BF16), vm((r, ng, tb, dq), BF16), vm((ng, tb, dq), BF16), vm((ng, tb, dq), BF16),
        vm((tb, 128), F32), vm((nq, tb, 128), F32),
        vm((r, nqueries, w), F32), vm((nc, nqueries, w), F32), vm((nqueries, w), BF16),
        vm((nqueries, bw), F32), vm((nc, nqueries, bw), F32), vm((nq, nqueries, bw), BF16),
        dma((5,)), dma, dma((nq,)), dma((nq,)), dma((nq,)), dma((2, nb)), dma((nb,)), dma((r, nb)), dma((r, nb)),
        dma((nch, nq)), dma((nch, nq)), dma((nc,)), dma((nc,)), dma((nq,)), dma((nq,)),
        dma((nq,)), dma((nq,)), dma((nc,)), dma((nc,)), dma((nch, nq)), dma((nch, nq)),
        dma((r,)), dma((r,)), dma((ng,)), dma((ng,)), dma((nq,)), dma((nq,)),
        dma((r,)), dma((nc,)), dma((nq,)), dma, dma((nc,)), dma((nc,)), dma((nq,)), dma((nq,)),
    ]
    dims = (nq, nc, r, nreal, tq, tb, nch, cw, w * nc)
    vspec, aspec = pl.BlockSpec(memory_space=pltpu.VMEM), pl.BlockSpec(memory_space=pl.ANY)
    return pl.pallas_call(
        functools.partial(general_kernel, dims),
        out_shape=jax.ShapeDtypeStruct((nqueries, TOPK), F32),
        in_specs=[vspec, vspec] + [aspec] * 5,
        out_specs=vspec,
        scratch_shapes=scratch,
        compiler_params=pltpu.CompilerParams(
            collective_id=0, has_side_effects=True, vmem_limit_bytes=60 * 1024 * 1024),
    )(hidden_in, lens, gate_weight, up_weight, down_weight, code_weight, corpus_codes)


def compare(v, size, step, flip, inner):
    part = len(v)
    sub = lax.broadcasted_iota(jnp.int32, v[0].shape, 0)
    across = step < part if inner else step >= 8
    if size >= LANES:
        up = [0] * part
    elif size < part:
        up = [int((i & size) != 0) for i in range(part)]
    else:
        up = [((sub & (size // part)) != 0).astype(jnp.int32)] * part
    masks = {}

    def high(i, low, name):
        key = (name, up[i] if isinstance(up[i], int) else -1)
        if key not in masks:
            masks[key] = (flip ^ up[i] ^ low) == 0
        return masks[key]

    v = list(v)
    if across:
        hop = step if inner else step // 8
        for i in range(part):
            if i & hop == 0:
                a, b = v[i], v[i | hop]
                most, least = jnp.maximum(a, b), jnp.minimum(a, b)
                pick = high(i, 0, 0)
                v[i], v[i | hop] = jnp.where(pick, most, least), jnp.where(pick, least, most)
        return v
    s = step // part if inner else step
    bit = (sub & s) != 0
    low = bit.astype(jnp.int32)
    for i in range(part):
        x = v[i]
        other = pltpu.roll(x, 4, 0) if s == 4 else jnp.where(bit, pltpu.roll(x, s, 0), pltpu.roll(x, 8 - s, 0))
        v[i] = jnp.where(high(i, low, 1), jnp.maximum(x, other), jnp.minimum(x, other))
    return v


def columns(lists):
    cols = jnp.concatenate([lists] * (LANES // lists.shape[0]), axis=0).T
    return [cols[i:i + 8] for i in range(0, LANES, 8)]


def merge_columns(v, count, rows, lone, inner):
    lane = lax.broadcasted_iota(jnp.int32, v[0].shape, 1)
    half = count // 2
    while half >= rows:
        v = [jnp.maximum(x, pltpu.roll(x, LANES - half, 1)) for x in v]
        if half > rows:
            flip = (lax.rem(lane, half) >= half // 2).astype(jnp.int32)
        else:
            flip = jnp.zeros_like(lane) + jnp.asarray(lone, jnp.int32)
        step = LANES // 2
        while step:
            v = compare(v, LANES, step, flip, inner)
            step //= 2
        half //= 2
    return v


def top_rows(lists, rows, lone, board):
    count = lists.shape[0]
    v = columns(lists)
    lane = lax.broadcasted_iota(jnp.int32, v[0].shape, 1)
    flip = (lax.rem(lane, count) >= count // 2).astype(jnp.int32)
    size = 2
    while size <= LANES:
        step = size // 2
        while step:
            v = compare(v, size, step, flip, True)
            step //= 2
        size *= 2
    v = merge_columns(v, count, rows, lone, True)
    for i, x in enumerate(v):
        board[pl.ds(i, 8, stride=len(v)), :] = x
    return board[...].T[:rows]


def merge_rows(lists, rows, lone):
    v = merge_columns(columns(lists), lists.shape[0], rows, lone, False)
    return jnp.concatenate(v, axis=0).T[:rows]


def fast_kernel(dims, names, hid, lens, gate_h, up_h, down_h, code_h, corp_h, out, *refs):
    nq, nc, r, nblk, bm, nh, hw, d_all = dims
    s = types.SimpleNamespace(**dict(zip(names, refs)))
    q = lax.axis_index("query")
    c = lax.axis_index("corpus")
    g = c // r
    j = lax.rem(c, r)
    ng = nc // r
    slots, w = hid.shape
    total = nq * slots
    nqueries = total // SEQ
    nreal = nblk * bm
    qm, gm = bm // nq, bm // ng
    nu = nblk * nh
    bw = s.codeq.shape[1]
    gate, up, corp = s.gu.at[0], s.gu.at[1], s.corp

    fq = w // nq
    for i in range(nq):
        pltpu.make_async_copy(hid.at[:, pl.ds(i * fq, fq)], s.hidq.at[i], s.w_s.at[0]).start()
    counts = pltpu.make_async_copy(lens, s.lens_s, s.w_s.at[1])
    counts.start()
    for a, b, k in ((gate_h, gate, 2), (up_h, up, 2), (down_h, s.down, 3), (code_h.at[:, pl.ds(pl.multiple_of(q * bw, bw), bw)], s.codeq, 4), (corp_h, corp, 5)):
        pltpu.make_async_copy(a, b, s.w_s.at[k]).start()

    def loaded(ref, k):
        pltpu.make_async_copy(ref, ref, s.w_s.at[k]).wait()

    def rq(k):
        return lax.rem(q + k, nq)

    def rc(k):
        return lax.rem(c + k, nc)

    def lane(k):
        return lax.rem(j + k, r)

    def got(ref, sem):
        rcopy(ref, ref, sem, sem, (rq(1), c)).wait_recv()

    def sent(ref, sem):
        rcopy(ref, ref, sem, sem, (rq(1), c)).wait_send()

    def to_query(src, ref, ss, rs):
        for k in range(1, nq):
            rcopy(src, ref.at[q], ss, rs, (rq(k), c)).start()

    def to_corpus(src, ref, ss, rs):
        for k in range(1, nc):
            rcopy(src, ref.at[c], ss, rs, (q, rc(k))).start()

    others = [(n, k) for n in range(nq) for k in range(r) if n or k]
    barrier = pltpu.get_barrier_semaphore()
    for n, k in others:
        if n and k:
            pl.semaphore_signal(barrier, inc=1, device_id=(rq(n), g * r + lane(k)), device_id_type=pl.DeviceIdType.MESH)
    for k in range(1, nq):
        pl.semaphore_signal(barrier, inc=1, device_id=(rq(k), c), device_id_type=pl.DeviceIdType.MESH)
    for k in range(1, nc):
        pl.semaphore_signal(barrier, inc=1, device_id=(q, rc(k)), device_id_type=pl.DeviceIdType.MESH)

    loaded(s.hidq, 0)
    squares = jnp.square(s.hidq[0].astype(F32))
    for i in range(1, nq):
        squares = squares + jnp.square(s.hidq[i].astype(F32))
    s.st_send[...] = lax.dot_general(jnp.ones((8, fq), F32), squares, (((1,), (1,)), ((), ())),
                                     precision=lax.Precision.HIGHEST, preferred_element_type=F32)
    counts.wait()
    slot_query = lax.broadcasted_iota(jnp.int32, (8, slots), 1) // SEQ
    own_lens = jnp.zeros((8, slots), jnp.int32)
    for k in range(slots // SEQ):
        own_lens = jnp.where(slot_query == k, s.lens_s[k], own_lens)
    s.lens_all[q] = own_lens

    pl.semaphore_wait(barrier, nq - 1 + nc - 1 + (nq - 1) * (r - 1))

    side_a = q + 1 - 2 * lax.rem(q, 2)
    side_b = q + 2 - 4 * (q // 2)
    far = nq - 1 - q

    for k in range(1, nq):
        rcopy(s.hidq.at[rq(k)], s.colbuf.at[q], s.a_s, s.a_r, (rq(k), c)).start()
    s.colbuf[q] = s.hidq[q]

    to_query(s.lens_all.at[q], s.lens_all, s.l_s, s.l_r)
    to_corpus(s.st_send, s.st_recv, s.st_s, s.st_r)
    s.st_recv[c] = s.st_send[...]
    got(s.lens_all.at[pl.ds(0, nq - 1)], s.l_r)
    lens_row = jnp.concatenate([s.lens_all[i] for i in range(nq)], axis=1)
    slot = lax.broadcasted_iota(jnp.int32, (8, total), 1)
    valid = lax.rem(slot, SEQ) < lens_row
    before = lax.broadcasted_iota(jnp.int32, (total, total), 0) < lax.broadcasted_iota(jnp.int32, (total, total), 1)
    pos = mm(valid.astype(F32).astype(BF16), before.astype(F32).astype(BF16)).astype(jnp.int32)
    pos = jnp.where(valid, pos, -1)[:1]

    got(s.st_recv.at[pl.ds(0, nc - 1)], s.st_r)
    stat = s.st_recv[0]
    for i in range(1, nc):
        stat = stat + s.st_recv[i]
    s.inv_all[q] = lax.rsqrt(stat / d_all + epsilon)
    to_query(s.inv_all.at[q], s.inv_all, s.iv_s, s.iv_r)

    def side(b, k):
        return rcopy(s.xall.at[j, b], s.xall.at[j, b], s.la_s, s.la_r.at[b], (q, g * r + lane(k)))

    def spread(b, k):
        t = lax.rem(g + k, ng)
        return rcopy(s.xpk.at[b], s.xall.at[j, b, q], s.x_s, s.x_r.at[b], (g, t * r + j))

    got(s.colbuf.at[pl.ds(0, nq - 1)], s.a_r)
    stacked = s.colbuf[...].reshape(total, fq)
    for b in range(nblk):
        row = lax.broadcasted_iota(jnp.int32, (bm, total), 0) + b * bm
        pick = (pos == row).astype(F32).astype(BF16)
        s.xpk[b] = mm(pick, stacked).astype(BF16)
        for k in range(ng - 1, 0, -1):
            spread(b, k).start()

        @pl.when(q != g)
        def _(b=b):
            spread(b, 0).start()

        @pl.when(q == g)
        def _(b=b):
            s.xall[j, b, q] = s.xpk[b]

    got(s.inv_all.at[pl.ds(0, nq - 1)], s.iv_r)
    inv_row = jnp.concatenate([s.inv_all[i] for i in range(nq)], axis=1)[:1]
    for b in range(nblk):
        row = lax.broadcasted_iota(jnp.int32, (bm, total), 0) + b * bm
        col = jnp.sum(jnp.where(pos == row, inv_row, 0.0), axis=1, keepdims=True)
        s.inv_c[b] = jnp.broadcast_to(col, (bm, LANES))

    loaded(s.gu, 2)

    def sides(n):
        odd = lax.rem(n, 2)
        return side_a + (side_b - side_a) * odd, side_b + (side_a - side_b) * odd

    split = (nh + 1) // 2

    def group(n):
        return 2 * (n // nh) + lax.rem(n, nh) // split

    def several(n, h):
        return pl.ds(n, min(split, nh - h))

    def near_part(n):
        one, _ = sides(n)
        return rcopy(s.psend.at[n, one], s.precv.at[n, 0], s.p_s, s.p_r.at[group(n)], (one, c))

    def far_part(n):
        one, _ = sides(n)
        return rcopy(s.psend.at[n, far], s.precv.at[n, 2], s.p_s, s.pf_r.at[group(n)], (one, c))

    def passed_part(n):
        _, two = sides(n)
        return rcopy(s.precv.at[n, 3], s.precv.at[n, 1], s.p_s, s.p_r.at[group(n)], (two, c))

    def h_near(n, k, sem):
        return rcopy(s.hall.at[n, q], s.hall.at[n, q], s.h_s, sem, (sides(n)[k], c))

    def h_pass(n, sem):
        one, two = sides(n)
        return rcopy(s.hall.at[n, one], s.hall.at[n, one], s.h_s, sem, (two, c))

    def fetch(b):
        @pl.when(q != g)
        def _():
            got(s.xall.at[0, b], s.x_r.at[b])

        @pl.when(q == g)
        def _():
            got(s.xall.at[0, b, pl.ds(0, nq - 1)], s.x_r.at[b])

        for k in range(1, r):
            side(b, k).start()

    def products(b):
        got(s.xall.at[pl.ds(0, r - 1), b], s.la_r.at[b])
        scale = s.inv_c[b][:, :1]
        for i in range(r):
            for k in range(nq):
                at = i * w + k * fq
                s.xn[:, at:at + fq] = (s.xall[i, b, k].astype(F32) * scale).astype(BF16)
        xb = s.xn[...]
        for h in range(nh):
            n = b * nh + h
            for e, wref in enumerate((gate, up)):
                full = mm(xb, wref[:, h * hw:(h + 1) * hw])
                s.full[h, e] = full
                for i in range(nq):
                    s.psend[n, i, e] = full[i * qm:(i + 1) * qm].astype(BF16)
            far_part(n).start()
            near_part(n).start()
            for e in range(2):
                s.pown[n, e] = s.full[h, e, pl.ds(pl.multiple_of(q * qm, qm), qm)]

    def pass_unit(n, h):
        _, two = sides(n)
        if h % split == 0:
            got(s.precv.at[several(n, h), 2], s.pf_r.at[group(n)])
        s.precv[n, 3] = (s.psend[n, two].astype(F32) + s.precv[n, 2].astype(F32)).astype(BF16)
        passed_part(n).start()

    def reduce_unit(n, h):
        if h % split == 0:
            got(s.precv.at[several(n, h), pl.ds(0, 2)], s.p_r.at[group(n)])
        gsum = s.pown[n, 0] + s.precv[n, 0, 0].astype(F32) + s.precv[n, 1, 0].astype(F32)
        usum = s.pown[n, 1] + s.precv[n, 0, 1].astype(F32) + s.precv[n, 1, 1].astype(F32)
        s.hall[n, q] = (gsum / (1.0 + jnp.exp(-gsum)) * usum).astype(BF16)
        h_near(n, 0, s.hn_r.at[group(n)]).start()
        h_near(n, 1, s.hb_r.at[group(n)]).start()

    def relay_unit(n, h):
        if h % split == 0:
            got(s.hall.at[several(n, h), 0], s.hn_r.at[group(n)])
        h_pass(n, s.hb_r.at[group(n)]).start()

    def lane_send(b, k):
        t = lane(k)
        return rcopy(s.lsend.at[b, t], s.lrecv.at[b, j], s.lr_s, s.lr_r.at[b], (q, g * r + t))

    def group_send(b, k):
        t = lax.rem(g + k, ng)
        return rcopy(s.gsend.at[b, t], s.grecv.at[b, g], s.g_s, s.g_r.at[b], (q, t * r + j))

    def down_block(b):
        part = None
        for h in range(nh):
            n = b * nh + h
            if h % split == 0:
                got(s.hall.at[several(n, h), pl.ds(0, 2)], s.hb_r.at[group(n)])
            term = mm(s.hall[n].reshape(bm, hw), s.down[h * hw:(h + 1) * hw, :])
            part = term if part is None else part + term
        s.acc[b] = part
        for t in range(r):
            s.lsend[b, t] = part[:, t * w:(t + 1) * w].astype(BF16)
        for k in range(1, r):
            lane_send(b, k).start()

    def sum_block(b):
        mine = s.acc[b, :, pl.ds(pl.multiple_of(j * w, w), w)]
        got(s.lrecv.at[b, pl.ds(0, r - 1)], s.lr_r.at[b])
        for k in range(1, r):
            mine = mine + s.lrecv[b, lane(k)].astype(F32)
        s.mine[b] = mine
        for t in range(ng):
            s.gsend[b, t] = mine[t * gm:(t + 1) * gm].astype(BF16)
        for k in range(1, ng):
            group_send(b, k).start()

    def units(unit, b):
        for h in range(nh):
            unit(b * nh + h, h)

    def fetch_next(b):
        @pl.when(b + 1 < nblk)
        def _():
            fetch(b + 1)

    fetch(0)
    stages = (products, fetch_next, functools.partial(units, pass_unit), functools.partial(units, reduce_unit), functools.partial(units, relay_unit), sum_block, down_block)
    delays = (0, 0, 1, 2, 3, 5, 4)

    def turn(t, carry):
        for stage, delay in zip(stages, delays):
            @pl.when(jnp.logical_and(t >= delay, t < nblk + delay))
            def _(stage=stage, delay=delay):
                stage(t - delay)
        return carry

    loaded(s.down, 3)
    lax.fori_loop(0, nblk + max(delays), turn, 0)
    own = pl.ds(pl.multiple_of(g * gm, gm), gm)
    for b in range(nblk):
        for k in range(nq):
            s.res[b * gm:(b + 1) * gm, k * fq:(k + 1) * fq] = s.xall[j, b, k, own].astype(F32)
    for b in range(nblk):
        total_b = s.mine[b, own]
        got(s.grecv.at[b, pl.ds(0, ng - 1)], s.g_r.at[b])
        for k in range(1, ng):
            total_b = total_b + s.grecv[b, lax.rem(g + k, ng)].astype(F32)
        s.res[b * gm:(b + 1) * gm] = s.res[b * gm:(b + 1) * gm] + total_b
    residual = s.res[...]
    tb = nblk * gm

    sums = lax.dot_general(jnp.ones((8, w), F32), residual * residual, (((1,), (1,)), ((), ())),
                           precision=lax.Precision.HIGHEST, preferred_element_type=F32)
    s.t_send[...] = jnp.concatenate([sums, jnp.zeros((8, LANES - tb), F32)], axis=1)
    for n, k in others:
        rcopy(s.t_send, s.t_recv.at[q * r + j], s.t_s, s.t_r, (rq(n), g * r + lane(k))).start()
    qrow = lax.broadcasted_iota(jnp.int32, (nqueries, total), 0)
    qslot = lax.broadcasted_iota(jnp.int32, (nqueries, total), 1)
    lens_b = jnp.broadcast_to(lens_row[:1], (nqueries, total)).astype(F32)
    vals_b = jnp.broadcast_to(valid.astype(F32)[:1], (nqueries, total))
    len_col = jnp.sum(jnp.where(qslot == qrow * SEQ, lens_b, 0.0), axis=1, keepdims=True)
    off_col = jnp.sum(jnp.where(qslot < qrow * SEQ, vals_b, 0.0), axis=1, keepdims=True)
    prow = lax.broadcasted_iota(jnp.int32, (nqueries, tb), 1)
    prow = ((prow // gm) * bm + g * gm + lax.rem(prow, gm)).astype(F32)
    member = jnp.where(jnp.logical_and(prow >= off_col, prow < off_col + len_col), 1.0, 0.0)
    tsum = s.t_send[...]
    got(s.t_recv.at[pl.ds(0, len(others))], s.t_r)
    for n, k in others:
        tsum = tsum + s.t_recv[rq(n) * r + lane(k)]
    inv_own = lax.rsqrt(tsum[:1, :tb] / d_all + epsilon)
    pooled_part = mm(member * inv_own, residual, lax.Precision.HIGHEST)
    s.pp[...] = pooled_part

    @pl.when(g != q)
    def _():
        rcopy(s.pp, s.prc.at[g], s.pp_s, s.pp_r, (q, q * r + j)).start()

    @pl.when(g == q)
    def _():
        pooled = pooled_part
        got(s.prc.at[pl.ds(0, ng - 1)], s.pp_r)
        for k in range(1, ng):
            pooled = pooled + s.prc[lax.rem(g + k, ng)]
        s.pblk[0] = (pooled / len_col).astype(BF16)
        for k in range(1, nq):
            rcopy(s.pblk.at[0], s.pblk.at[0], s.pb_s, s.pb_r, (rq(k), c)).start()

    loaded(s.codeq, 4)
    loaded(s.corp, 5)

    @pl.when(g != q)
    def _():
        got(s.pblk.at[0], s.pb_r)

    s.cpart[...] = mm(s.pblk[0], s.codeq[...])
    to_corpus(s.cpart, s.crecv, s.c_s, s.c_r)
    s.crecv[c] = s.cpart[...]
    got(s.crecv.at[pl.ds(0, nc - 1)], s.c_r)
    csum = s.crecv[0]
    for i in range(1, nc):
        csum = csum + s.crecv[i]
    s.codes[q] = csum.astype(BF16)
    to_query(s.codes.at[q], s.codes, s.o_s, s.o_r)
    got(s.codes.at[pl.ds(0, nq - 1)], s.o_r)
    qcodes = jnp.concatenate([s.codes[i] for i in range(nq)], axis=1)
    scale = 1.0 / math.sqrt(corp.shape[1])
    scores = lax.dot_general(qcodes, corp[...], (((1,), (1,)), ((), ())), preferred_element_type=F32) * scale

    blocks = corp.shape[0] // LANES
    lists = jnp.concatenate([scores[:, i * LANES:(i + 1) * LANES] for i in range(blocks)], axis=0)
    best = top_rows(lists, nqueries, q >= nq // 2, s.board)
    s.top_q[q] = best
    to_query(s.top_q.at[q], s.top_q, s.tq_s, s.tq_r)
    got(s.top_q.at[pl.ds(0, nq - 1)], s.tq_r)
    best = merge_rows(s.top_q[...].reshape(nq * nqueries, LANES), nqueries, c >= nc // 2)
    s.top_c[c] = best
    to_corpus(s.top_c.at[c], s.top_c, s.tc_s, s.tc_r)
    got(s.top_c.at[pl.ds(0, nc - 1)], s.tc_r)
    best = merge_rows(s.top_c[...].reshape(nc * nqueries, LANES), nqueries, False)
    out[...] = best[:, :TOPK]

    sent(s.lens_all.at[pl.ds(0, nq - 1)], s.l_s)
    sent(s.st_recv.at[pl.ds(0, nc - 1)], s.st_s)
    sent(s.inv_all.at[pl.ds(0, nq - 1)], s.iv_s)

    sent(s.colbuf.at[pl.ds(0, nq - 1)], s.a_s)

    @pl.when(q != g)
    def _():
        sent(s.xall.at[0], s.x_s)

    @pl.when(q == g)
    def _():
        sent(s.xall.at[0, :, pl.ds(0, nq - 1)], s.x_s)

    sent(s.xall.at[pl.ds(0, r - 1)], s.la_s)
    sent(s.psend.at[:, pl.ds(0, 3)], s.p_s)
    sent(s.hall.at[:, pl.ds(0, 3)], s.h_s)
    sent(s.lsend.at[:, pl.ds(0, r - 1)], s.lr_s)
    sent(s.gsend.at[:, pl.ds(0, ng - 1)], s.g_s)
    sent(s.t_recv.at[pl.ds(0, len(others))], s.t_s)

    @pl.when(g == q)
    def _():
        sent(s.pblk.at[pl.ds(0, nq - 1)], s.pb_s)

    @pl.when(g != q)
    def _():
        sent(s.pp, s.pp_s)

    sent(s.crecv.at[pl.ds(0, nc - 1)], s.c_s)
    sent(s.codes.at[pl.ds(0, nq - 1)], s.o_s)
    sent(s.top_q.at[pl.ds(0, nq - 1)], s.tq_s)
    sent(s.top_c.at[pl.ds(0, nc - 1)], s.tc_s)


def chunks_of(ffc):
    return ffc // CHUNK if ffc % CHUNK == 0 else 1


def per_device_fast(nq, nc, hidden_in, lengths, gate_weight, up_weight, down_weight, code_weight, corpus_codes):
    slots, w = hidden_in.shape
    r = nc // nq
    ng = nc // r
    nreal = nq * slots * REAL_NUM // REAL_DEN
    dq, ffc = gate_weight.shape
    bm = 8 * nc
    nblk = nreal // bm
    nh = chunks_of(ffc)
    hw = ffc // nh
    nu = nblk * nh
    qm, gm = bm // nq, bm // ng
    tb = nblk * gm
    nqueries = nq * lengths.shape[0]
    bits = code_weight.shape[1]
    bw = bits // nq
    vm, dma = pltpu.VMEM, pltpu.SemaphoreType.DMA
    scratch = dict(
        gu=vm((2,) + gate_weight.shape, BF16), down=vm(down_weight.shape, BF16), codeq=vm((w, bw), BF16), corp=vm(corpus_codes.shape, BF16),
        lens_s=pltpu.SMEM(lengths.shape, jnp.int32),
        hidq=vm((nq, slots, w // nq), BF16), colbuf=vm((nq, slots, w // nq), BF16), xpk=vm((nblk, bm, w // nq), BF16), lens_all=vm((nq, 8, slots), jnp.int32), xall=vm((r, nblk, nq, bm, w // nq), BF16),
        xn=vm((bm, dq), BF16), inv_c=vm((nblk, bm, LANES), F32),
        st_send=vm((8, slots), F32), st_recv=vm((nc, 8, slots), F32), inv_all=vm((nq, 8, slots), F32),
        psend=vm((nu, nq, 2, qm, hw), BF16), precv=vm((nu, 4, 2, qm, hw), BF16), pown=vm((nu, 2, qm, hw), F32), full=vm((nh, 2, bm, hw), F32),
        hall=vm((nu, nq, qm, hw), BF16),
        acc=vm((nblk, bm, dq), F32), lsend=vm((nblk, r, bm, w), BF16), lrecv=vm((nblk, r, bm, w), BF16),
        mine=vm((nblk, bm, w), F32), gsend=vm((nblk, ng, gm, w), BF16), grecv=vm((nblk, ng, gm, w), BF16), res=vm((tb, w), F32),
        t_send=vm((8, LANES), F32), t_recv=vm((nq * r, 8, LANES), F32),
        pp=vm((nqueries, w), F32), prc=vm((ng, nqueries, w), F32), pblk=vm((nq, nqueries, w), BF16),
        cpart=vm((nqueries, bw), F32), crecv=vm((nc, nqueries, bw), F32), codes=vm((nq, nqueries, bw), BF16),
        top_q=vm((nq, nqueries, LANES), F32), top_c=vm((nc, nqueries, LANES), F32), board=vm((LANES, LANES), F32),
        w_s=dma((6,)), l_s=dma, l_r=dma, a_s=dma, a_r=dma, st_s=dma, st_r=dma, iv_s=dma, iv_r=dma,
        x_s=dma, x_r=dma((nblk,)), la_s=dma, la_r=dma((nblk,)),
        p_s=dma, p_r=dma((2 * nblk,)), pf_r=dma((2 * nblk,)), h_s=dma, hn_r=dma((2 * nblk,)), hb_r=dma((2 * nblk,)),
        lr_s=dma, lr_r=dma((nblk,)), g_s=dma, g_r=dma((nblk,)),
        t_s=dma, t_r=dma, pp_s=dma, pp_r=dma, pb_s=dma, pb_r=dma, c_s=dma, c_r=dma, o_s=dma, o_r=dma,
        tq_s=dma, tq_r=dma, tc_s=dma, tc_r=dma,
    )
    dims = (nq, nc, r, nblk, bm, nh, hw, w * nc)
    vspec, aspec = pl.BlockSpec(memory_space=pltpu.VMEM), pl.BlockSpec(memory_space=pl.ANY)
    return pl.pallas_call(
        functools.partial(fast_kernel, dims, tuple(scratch)),
        out_shape=jax.ShapeDtypeStruct((nqueries, TOPK), F32),
        in_specs=[aspec] * 7,
        out_specs=vspec,
        scratch_shapes=list(scratch.values()),
        compiler_params=pltpu.CompilerParams(
            collective_id=0, has_side_effects=True, vmem_limit_bytes=60 * 1024 * 1024),
    )(hidden_in, lengths, gate_weight, up_weight, down_weight, code_weight, corpus_codes)


def per_device(nq, nc, hidden_in, *rest):
    slots, w = hidden_in.shape
    nreal = nq * slots * REAL_NUM // REAL_DEN
    nqueries = nq * rest[0].shape[0]
    lists = nqueries * max(nc, nq, rest[5].shape[0] // LANES)
    fits = nreal // nq <= LANES and lists <= LANES and LANES % lists == 0 and nreal % (8 * nc) == 0 and w % (nq * LANES) == 0
    body = per_device_fast if fits else per_device_general
    return body(nq, nc, hidden_in, *rest)


def solution(mesh):
    in_specs = (
        P("query", "corpus"),
        P("query"),
        P("query", "corpus"),
        P("query", "corpus"),
        P("corpus", "query"),
        P("corpus", None),
        P(("query", "corpus"), None),
    )
    body = functools.partial(per_device, mesh.shape["query"], mesh.shape["corpus"])
    return jax.shard_map(body, mesh=mesh, in_specs=in_specs, out_specs=P(), check_vma=False)
```
